32 devices in a mesh: wide: 8 (over z, x), narrow: 4 (over y, core).
Axes of the slice: x: 2, y: 2, z: 4, core: 2. Of those that a mesh axis runs over, the one named last changes fastest.
Arguments:
- encoder_input: bfloat16 [32, 128, 768], P(('wide', 'narrow')), may hold values from -6 to 6
- decoder_input: bfloat16 [32, 448, 768], P(('wide', 'narrow')), may hold values from -6 to 6
- segments: int32 [32, 448], P(('wide', 'narrow')), may hold values from 0 to 7, never falling along the last dimension, each value on 1 to 224 neighbouring positions
- encoder_cotangent: bfloat16 [32, 128, 768], P(('wide', 'narrow')), may hold values from -6 to 6
- decoder_cotangent: bfloat16 [32, 448, 768], P(('wide', 'narrow')), may hold values from -6 to 6
- encoder_master: float32 [7087104], P(('wide', 'narrow')), may hold values from -2 to 2
- encoder_first: float32 [7087104], P(('wide', 'narrow')), may hold values from -0.01 to 0.01
- encoder_second: float32 [7087104], P(('wide', 'narrow')), may hold values from 0 to 0.0001, as said below
- decoder_master: float32 [9450240], P(('wide', 'narrow')), may hold values from -2 to 2
- decoder_first: float32 [9450240], P(('wide', 'narrow')), may hold values from -0.01 to 0.01
- decoder_second: float32 [9450240], P(('wide', 'narrow')), may hold values from 0 to 0.0001, as said below
- step_count: int32 [], replicated, may hold values from 1 to 10
Outputs:
- encoder_out: bfloat16 [32, 128, 768], P(('wide', 'narrow'))
- decoder_out: bfloat16 [32, 448, 768], P(('wide', 'narrow'))
- encoder_gradient: float32 [32, 128, 768], P(('wide', 'narrow'))
- decoder_gradient: float32 [32, 448, 768], P(('wide', 'narrow'))
- gradient_norm: float32 [], replicated
- encoder_weights: float32 [7087104], P(('wide', 'narrow'))
- encoder_moment: float32 [7087104], P(('wide', 'narrow'))
- encoder_variance: float32 [7087104], P(('wide', 'narrow'))
- encoder_copy: bfloat16 [7087104], P(('wide', 'narrow'))
- decoder_weights: float32 [9450240], P(('wide', 'narrow'))
- decoder_moment: float32 [9450240], P(('wide', 'narrow'))
- decoder_variance: float32 [9450240], P(('wide', 'narrow'))
- decoder_copy: bfloat16 [9450240], P(('wide', 'narrow'))
The draws below stay inside these ranges and needn't reach their ends.
Inputs may be any that keep to these rules, and one draw needn't show every extreme that they name: `segments`: segment numbers never fall along a row. `encoder_second`: positive. `decoder_second`: positive.
All inputs are finite; a program needn't handle non-finite values.
Results may differ from the reference program's by a relative error of at most 0.019.
Values may be sent and summed in bfloat16 or wider, within the bound.
A program may use at most 320 MiB of HBM per device.

```python
import math
import jax
import jax.numpy as jnp
import numpy as np
from jax import lax

D = 768
HEAD_DIM = 64
FF = 3072
FRAMES = 128
DEC_LEN = 448
CLIPS = 32
P_ENC = 7087104
P_DEC = 9450240


def attention_plan_drawn(prefix, width):
    return [(prefix + 'wq', width, width), (prefix + 'bq', width, 0), (prefix + 'wk', width, width), (prefix + 'wv', width, width), (prefix + 'bv', width, 0), (prefix + 'wo', width, width), (prefix + 'bo', width, 0)]


def feed_plan_drawn(width, hidden):
    return [('fc1_weight', width, hidden), ('fc1_bias', hidden, 0), ('fc2_weight', hidden, width), ('fc2_bias', width, 0)]


def encoder_layout_drawn(width, hidden):
    return [('ln1_gain', width, 0), ('ln1_bias', width, 0)] + attention_plan_drawn('att_', width) + [('ln2_gain', width, 0), ('ln2_bias', width, 0)] + feed_plan_drawn(width, hidden)


def decoder_layout_drawn(width, hidden):
    return [('ln1_gain', width, 0), ('ln1_bias', width, 0)] + attention_plan_drawn('self_', width) + [('ln2_gain', width, 0), ('ln2_bias', width, 0)] + attention_plan_drawn('cross_', width) + [('ln3_gain', width, 0), ('ln3_bias', width, 0)] + feed_plan_drawn(width, hidden)


def draw_packed(key, layout, factors):
    pieces = []
    for index, entry in enumerate(layout):
        name, rows, cols = entry
        sub = jax.random.fold_in(key, index + 11)
        if cols > 0:
            scale = factors.get(name, 1.0) / math.sqrt(rows)
            normal = jnp.clip(jax.random.normal(sub, (rows * cols,), jnp.float32), -4.0, 4.0)
            pieces.append(normal * scale)
        elif name[-4:] == 'gain':
            pieces.append(1.0 + 0.3 * jax.random.uniform(sub, (rows,), jnp.float32, -1.0, 1.0))
        else:
            pieces.append(0.2 * jnp.clip(jax.random.normal(sub, (rows,), jnp.float32), -4.0, 4.0))
    return jnp.concatenate(pieces)


def moment_scale():
    return 1.0 / math.sqrt(P_ENC + P_DEC)


def draw_first(key, count):
    normal = jnp.clip(jax.random.normal(jax.random.fold_in(key, 5), (count,), jnp.float32), -4.0, 4.0)
    return moment_scale() * normal


def draw_second(key, count):
    spread = jax.random.uniform(jax.random.fold_in(key, 7), (count,), jnp.float32, 0.0, math.log(4.0))
    return moment_scale() * moment_scale() * jnp.exp(spread)


def draw_encoder_master(key, part):
    factors = {'att_wo': max(1.0, math.sqrt(FRAMES) / 4.0)}
    return draw_packed(key, encoder_layout_drawn(D, FF), factors)


def draw_decoder_master(key, part):
    factors = {'self_wo': max(1.0, math.sqrt(DEC_LEN) / 6.0), 'cross_wo': max(1.0, math.sqrt(FRAMES) / 4.0)}
    return draw_packed(key, decoder_layout_drawn(D, FF), factors)


def draw_encoder_first(key, part):
    return draw_first(key, P_ENC)


def draw_decoder_first(key, part):
    return draw_first(key, P_DEC)


def draw_encoder_second(key, part):
    return draw_second(key, P_ENC)


def draw_decoder_second(key, part):
    return draw_second(key, P_DEC)


def steps_of(stream_key, shape, cuts, low, high):
    level, own = 1.0, jax.random.fold_in(stream_key, 6)
    for dim, blocks in cuts:
        steps = jnp.exp(jax.random.uniform(jax.random.fold_in(own, dim), (blocks,), jnp.float32, low / len(cuts), high / len(cuts)))
        level = level * jnp.repeat(steps, shape[dim] // blocks).reshape([-1 if axis == dim else 1 for axis in range(len(shape))])
    return level


def profile(count, total, reach, slope):
    weights = [(1 << 20) // math.isqrt(standing ** slope) + 1 for standing in range(2, count + 1)]
    spare, holding = total - reach - (count - 1), [1] * (count - 1)
    while spare > 0:
        candidates = [i for i in range(count - 1) if holding[i] < reach]
        pool, left = sum([weights[i] for i in candidates]), spare
        for i in candidates:
            addition = min(reach - holding[i], max(1, left * weights[i] // pool), spare)
            holding[i] = holding[i] + addition
            spare = spare - addition
    return np.array([reach] + holding)


def uneven(rng, number_of, total, reach, lean):
    if number_of == 2:
        one = jax.random.randint(rng, (), max(1, total - reach), min(reach, total - 1) + 1)
        return jnp.stack([one, total - one])
    sizes = jnp.asarray(profile(number_of, total, reach, lean), jnp.int32)
    pairs = (number_of - 1) // 2
    source_of, taker = sizes[1:1 + 2 * pairs:2], sizes[2:2 + 2 * pairs:2]
    margin = jnp.minimum(source_of - 1, reach - taker)
    moved = jax.random.randint(jax.random.fold_in(rng, 1), (pairs,), 0, 1 << 20) % (margin + 1)
    sizes = sizes.at[1:1 + 2 * pairs:2].set(source_of - moved).at[2:2 + 2 * pairs:2].set(taker + moved)
    return sizes[jax.random.permutation(jax.random.fold_in(rng, 2), number_of)]


def bell_draw(own_key, dims, scale, limit, cuts=(), held_as=jnp.bfloat16):
    factor_of = steps_of(own_key, dims, cuts, -0.22, 0.18) if cuts else 1.0
    array = jax.random.normal(own_key, dims, jnp.float32) * scale * factor_of
    return jnp.minimum(jnp.maximum(array, -limit), limit).astype(held_as)


def setup_inputs(seed: int = 0) -> dict:
    splits = jax.random.split(jax.random.key(seed), 13)
    return {
        "encoder_input": bell_draw(splits[0], (CLIPS, FRAMES, D), 1.0, 6.0, ((0, 32),)),
        "decoder_input": bell_draw(splits[1], (CLIPS, DEC_LEN, D), 1.0, 6.0, ((0, 32),)),
        "segments": jax.vmap(lambda own: jnp.searchsorted(jnp.cumsum(uneven(own, max(3, DEC_LEN // 56), DEC_LEN, DEC_LEN // 2, 2)), jnp.arange(DEC_LEN), side="right"))(jax.random.split(splits[2], CLIPS)).reshape((CLIPS, DEC_LEN)).astype(jnp.int32),
        "encoder_cotangent": bell_draw(splits[3], (CLIPS, FRAMES, D), 1.0, 6.0, ((0, 32),)),
        "decoder_cotangent": bell_draw(splits[4], (CLIPS, DEC_LEN, D), 1.0, 6.0, ((0, 32),)),
        "encoder_master": draw_encoder_master(jax.random.fold_in(splits[12], 71), 0),
        "encoder_first": draw_encoder_first(jax.random.fold_in(splits[12], 71), 0),
        "encoder_second": draw_encoder_second(jax.random.fold_in(splits[12], 71), 0),
        "decoder_master": draw_decoder_master(jax.random.fold_in(splits[12], 71), 0),
        "decoder_first": draw_decoder_first(jax.random.fold_in(splits[12], 71), 0),
        "decoder_second": draw_decoder_second(jax.random.fold_in(splits[12], 71), 0),
        "step_count": jax.random.randint(splits[11], (), 1, 11).astype(jnp.int32),
    }


@jax.custom_vjp
def low(v):
    return lax.optimization_barrier(v.astype(jnp.bfloat16)).astype(jnp.float32)

@jax.custom_vjp
def low_back(v):
    return v

def low_keep(v):
    return (low(v), None)

def low_pass(kept, grad):
    return (grad,)

def back_keep(v):
    return (v, None)

def back_low(kept, grad):
    return (low(grad),)
low.defvjp(low_keep, low_pass)
low_back.defvjp(back_keep, back_low)

def attention_plan(prefix, width):
    return [(prefix + 'wq', width, width), (prefix + 'bq', width, 0), (prefix + 'wk', width, width), (prefix + 'wv', width, width), (prefix + 'bv', width, 0), (prefix + 'wo', width, width), (prefix + 'bo', width, 0)]

def feed_plan(width, hidden):
    return [('fc1_weight', width, hidden), ('fc1_bias', hidden, 0), ('fc2_weight', hidden, width), ('fc2_bias', width, 0)]

def encoder_layout(width, hidden):
    return [('ln1_gain', width, 0), ('ln1_bias', width, 0)] + attention_plan('att_', width) + [('ln2_gain', width, 0), ('ln2_bias', width, 0)] + feed_plan(width, hidden)

def decoder_layout(width, hidden):
    return [('ln1_gain', width, 0), ('ln1_bias', width, 0)] + attention_plan('self_', width) + [('ln2_gain', width, 0), ('ln2_bias', width, 0)] + attention_plan('cross_', width) + [('ln3_gain', width, 0), ('ln3_bias', width, 0)] + feed_plan(width, hidden)

def unpack(flat, layout):
    params = {}
    offset = 0
    for name, rows, cols in layout:
        count = rows * cols if cols > 0 else rows
        piece = flat[offset:offset + count]
        params[name] = piece.reshape(rows, cols) if cols > 0 else piece
        offset = offset + count
    return params

def matmul(left, right):
    return jnp.dot(left, right, precision=lax.Precision.HIGHEST)

def layer_norm(values, gain, shift):
    centred = values - lax.optimization_barrier(jnp.mean(values, axis=-1, keepdims=True))
    spread = lax.optimization_barrier(jnp.mean(centred * centred, axis=-1, keepdims=True))
    return centred * lax.rsqrt(spread + 1e-05) * gain + shift

def attention(params, prefix, query_rows, key_rows, allowed):
    heads = query_rows.shape[1] // HEAD_DIM
    queries = low(low_back(matmul(query_rows, params[prefix + 'wq'])) + params[prefix + 'bq'])
    keys_low = low(low_back(matmul(key_rows, params[prefix + 'wk'])))
    values = low(low_back(matmul(key_rows, params[prefix + 'wv'])) + params[prefix + 'bv'])
    query_heads = queries.reshape(queries.shape[0], heads, HEAD_DIM)
    key_heads = keys_low.reshape(keys_low.shape[0], heads, HEAD_DIM)
    value_heads = values.reshape(values.shape[0], heads, HEAD_DIM)
    raw = jnp.einsum('qhd,khd->hqk', query_heads, key_heads, precision=lax.Precision.HIGHEST)
    scores = low_back(raw) * HEAD_DIM ** (-0.5)
    if allowed is not None:
        scores = jnp.where(allowed[None], scores, -1000000000.0)
    probs = low(jax.nn.softmax(scores, axis=-1))
    mixed = jnp.einsum('hqk,khd->qhd', probs, value_heads, precision=lax.Precision.HIGHEST)
    mixed = low(low_back(mixed.reshape(query_rows.shape[0], -1)))
    return low_back(matmul(mixed, params[prefix + 'wo'])) + params[prefix + 'bo']

def feed_forward(params, normed):
    pre = low_back(matmul(normed, params['fc1_weight'])) + params['fc1_bias']
    activated = low(jax.nn.gelu(pre, approximate=False))
    return low_back(matmul(activated, params['fc2_weight'])) + params['fc2_bias']

def encoder_block(params, frames):
    normed = low(layer_norm(frames, params['ln1_gain'], params['ln1_bias']))
    after = frames + attention(params, 'att_', normed, normed, None)
    normed_two = low(layer_norm(after, params['ln2_gain'], params['ln2_bias']))
    return after + feed_forward(params, normed_two)

def decoder_block(params, tokens, memory, segment_row):
    places = jnp.arange(tokens.shape[0], dtype=jnp.int32)
    allowed = (segment_row[:, None] == segment_row[None, :]) & (places[None, :] <= places[:, None])
    normed = low(layer_norm(tokens, params['ln1_gain'], params['ln1_bias']))
    after = tokens + attention(params, 'self_', normed, normed, allowed)
    normed_two = low(layer_norm(after, params['ln2_gain'], params['ln2_bias']))
    after_two = after + attention(params, 'cross_', normed_two, low(memory), None)
    normed_three = low(layer_norm(after_two, params['ln3_gain'], params['ln3_bias']))
    return after_two + feed_forward(params, normed_three)

def reference(encoder_input, decoder_input, segments, encoder_cotangent, decoder_cotangent, encoder_master, encoder_first, encoder_second, decoder_master, decoder_first, decoder_second, step_count):
    encoder_plan = encoder_layout(D, FF)
    decoder_plan = decoder_layout(D, FF)

    def one_clip(totals, items):
        frames, tokens, segment_row, encoder_cot, decoder_cot = items

        def forward(encoder_flat, decoder_flat, frame_rows, token_rows):
            encoder_params = unpack(low(encoder_flat), encoder_plan)
            decoder_params = unpack(low(decoder_flat), decoder_plan)
            memory = encoder_block(encoder_params, frame_rows)
            return (memory, decoder_block(decoder_params, token_rows, memory, segment_row))
        outputs, pullback = jax.vjp(forward, encoder_master, decoder_master, frames.astype(jnp.float32), tokens.astype(jnp.float32))
        encoder_grad, decoder_grad, frame_grad, token_grad = pullback((encoder_cot.astype(jnp.float32), decoder_cot.astype(jnp.float32)))
        return ((totals[0] + encoder_grad, totals[1] + decoder_grad), (outputs[0].astype(jnp.bfloat16), outputs[1].astype(jnp.bfloat16), frame_grad, token_grad))
    start = (jnp.zeros(encoder_master.shape, jnp.float32), jnp.zeros(decoder_master.shape, jnp.float32))
    (encoder_grad, decoder_grad), (encoder_out, decoder_out, encoder_gradient, decoder_gradient) = lax.scan(one_clip, start, (encoder_input, decoder_input, segments, encoder_cotangent, decoder_cotangent))
    gradient_norm = jnp.sqrt(jnp.sum(encoder_grad * encoder_grad) + jnp.sum(decoder_grad * decoder_grad))
    factor = 1.0 / jnp.maximum(gradient_norm, 1.0)
    correction = 1.0 - jnp.power(0.5, step_count.astype(jnp.float32))

    def adamw(master, first, second, grad):
        clipped = grad * factor
        moment = 0.5 * first + 0.5 * clipped
        variance = 0.5 * second + 0.5 * clipped * clipped
        update = moment / correction / (jnp.sqrt(variance / correction) + 1e-08) + 0.01 * master
        weights = master - 0.02 * update
        return (weights, moment, variance, weights.astype(jnp.bfloat16))
    encoder_new = adamw(encoder_master, encoder_first, encoder_second, encoder_grad)
    decoder_new = adamw(decoder_master, decoder_first, decoder_second, decoder_grad)
    return (encoder_out, decoder_out, encoder_gradient, decoder_gradient, gradient_norm, encoder_new[0], encoder_new[1], encoder_new[2], encoder_new[3], decoder_new[0], decoder_new[1], decoder_new[2], decoder_new[3])
```

```python
from functools import partial

import jax
import jax.numpy as jnp
from jax import lax
from jax.experimental import pallas as pl
from jax.experimental.pallas import tpu as pltpu
from jax.sharding import PartitionSpec as P

D = 768
HEAD_DIM = 64
FF = 3072
MESH = pl.DeviceIdType.MESH
BF = jnp.bfloat16
F32 = jnp.float32

N_MAT = 28
N_PAIR = 14
UNIT = 48
LANES = 128
UROWS = UNIT * D // LANES
BIG = 4 * UROWS
FRONT = BIG + 8
BACK = BIG + 8
N_VEC = 29


class Block:
    def __init__(self, small, gaps, fc1, vectors, first_mat, small_mats, total):
        self.small = small
        self.gaps = gaps
        self.fc1 = fc1
        self.vectors = vectors
        self.first_mat = first_mat
        self.small_mats = small_mats
        self.total = total


ENC = Block(
    small=8,
    gaps=((0, 2), (1, 1), (3, 1), (4, 3072 + 7)),
    fc1=3079,
    vectors=[0, 1, 770, 2307, 3076, 3077, 3078, 6151, 6152, 6153, 6154, 9227],
    first_mat=0,
    small_mats=4,
    total=9228,
)
DEC = Block(
    small=12,
    gaps=((0, 2), (1, 1), (3, 1), (4, 3), (5, 1), (7, 1), (8, 3072 + 7)),
    fc1=6156,
    vectors=[0, 1, 770, 2307, 3076, 3077, 3078, 3847, 5384, 6153, 6154, 6155, 9228, 9229, 9230, 9231, 12304],
    first_mat=12,
    small_mats=8,
    total=12305,
)
BLOCKS = (ENC, DEC)


def sizes(block, n):
    shard = block.total * D // n
    rows = -(-shard // 1024) * 8
    top = (shard + LANES - 1) // LANES
    return shard, rows, (top + UROWS) // UROWS + 1, (top + BIG) // BIG + 1


def small_row(block, m):
    row = m * D
    for at, gap in block.gaps:
        row = row + jnp.where(m >= at, gap, 0) if at > 0 else row + gap
    return row


def mat_of(block, m):
    return block.first_mat + m + jnp.where(m >= block.small_mats, 4, 0)


def static_unit_rows(block):
    out = []
    for m in range(block.small):
        row = m * D + sum(gap for at, gap in block.gaps if m >= at)
        out.append((block.first_mat + m + (4 if m >= block.small_mats else 0), row))
    return out


def whoami():
    wide, narrow = lax.axis_index("wide"), lax.axis_index("narrow")
    return wide, narrow, wide // 2, wide % 2, narrow // 2, narrow % 2


def device(z, x, y, c):
    return (z * 2 + x, y * 2 + c)


def flat_device(d):
    return (d // 4, d % 4)


def entry_barrier(me, n):
    bar = pltpu.get_barrier_semaphore()

    def signal(i, carry):
        pl.semaphore_signal(bar, inc=1, device_id=flat_device((me + i) % n), device_id_type=MESH)
        return carry

    lax.fori_loop(1, n, signal, 0)
    pl.semaphore_wait(bar, n - 1)


def each_small(block, n, me, slots, body):
    shard = sizes(block, n)[0]
    low = me * shard
    low_row = low // LANES
    first = 0
    for _, row in static_unit_rows(block):
        first = first + jnp.minimum(jnp.maximum(low - row * D, 0) // (UROWS * LANES), 16)

    def step(j, carry):
        g = first + j
        m, u = g // 16, g % 16
        start = small_row(block, m) * 6 + u * UROWS
        pos = start - low_row

        @pl.when((g < 16 * block.small) & (start * LANES < low + shard))
        def _():
            body((pos + UROWS) // UROWS, mat_of(block, m), u, pos, start * LANES)

        return carry

    lax.fori_loop(0, slots, step, 0)


def each_big(block, n, me, slots, body):
    shard = sizes(block, n)[0]
    low = me * shard
    low_row = low // LANES
    first = jnp.minimum(jnp.maximum(low - block.fc1 * D, 0) // (BIG * LANES), 16)

    def step(j, carry):
        u = first + j
        start = block.fc1 * 6 + u * BIG
        pos = start - low_row

        @pl.when((u < 16) & (start * LANES < low + shard) & (start * LANES + BIG * LANES > low))
        def _():
            body((pos + BIG) // BIG, u, pos, start * LANES)

        return carry

    lax.fori_loop(0, slots, step, 0)


def each_vector(block, n, me, first_vec, body):
    shard = sizes(block, n)[0]
    low = me * shard
    low_row = low // LANES
    for i, row in enumerate(block.vectors):
        @pl.when((row * D < low + shard) & (row * D + D > low))
        def _(i=i, row=row):
            body(first_vec + i, row * 6 - low_row, row * D)


ORDERS = [("z", "x", "y"), ("z", "y", "x")]


def view(pair, order, done, at):
    have = set(order[:done])
    return (pair,) + tuple(slice(None) if a in have else at[a] for a in "zxy")


def peers(axis, at):
    if axis == "z":
        return [dict(at, z=(at["z"] + k) % 4) for k in (1, 2, 3)]
    return [dict(at, **{axis: 1 - at[axis]})]


def dev(at):
    return device(at["z"], at["x"], at["y"], at["c"])


def gather_kernel(
    n, xe_ref, xd_ref, w_ref, v_ref,
    re_ref, rd_ref, se_ref, sd_ref, be_ref, bd_ref, sv_ref, land, landv, own, ownv,
    s_small, s_big, s_vec, r_unit, r_vec, s_zxy, r_zxy, s_core, r_core, s_own, v_send, v_recv,
):
    wide, narrow, z, x, y, c = whoami()
    me = wide * 4 + narrow
    chip = me // 2
    at = dict(z=z, x=x, y=y, c=c)
    entry_barrier(me, n)

    lanes = lax.broadcasted_iota(jnp.int32, (1, LANES), 1)
    for b, (block, x_ref, r_ref, s_ref, b_ref) in enumerate(
        ((ENC, xe_ref, re_ref, se_ref, be_ref), (DEC, xd_ref, rd_ref, sd_ref, bd_ref))
    ):
        shard, rows, n_small, n_big = sizes(block, n)
        shift = (me * shard) % LANES
        step = 8 * max(k for k in range(1, 40) if (rows // 8) % k == 0)

        def turn(i, carry, x_ref=x_ref, r_ref=r_ref, step=step, shift=shift):
            at_row = pl.multiple_of(i * step, 8)
            r_ref[pl.ds(FRONT + at_row, step), :] = pltpu.roll(x_ref[pl.ds(at_row, step), :], shift, 1)
            return carry

        lax.fori_loop(0, rows // step, turn, 0)
        keep = lanes >= shift

        def load(row, count, stride, r_ref=r_ref, keep=keep):
            here = r_ref[pl.ds(FRONT + row, count, stride=stride), :]
            before = r_ref[pl.ds(FRONT + row - 1, count, stride=stride), :]
            return jnp.where(keep, here, before)

        small0 = 0 if b == 0 else sizes(ENC, n)[2]
        big0 = 0 if b == 0 else sizes(ENC, n)[3]

        def small_body(slot, mat, u, pos, start, s_ref=s_ref, load=load, shard=shard, small0=small0):
            for k in range(6):
                s_ref[slot, :, k * LANES : (k + 1) * LANES] = load(pos + k, UNIT, 6).astype(BF)
            which = jnp.where(start // shard == me, 0, 1)
            target = u * 2 + mat % 2
            sem = s_small.at[small0 + slot]

            @pl.when(target == me)
            def _():
                pltpu.make_async_copy(s_ref.at[slot], land.at[which, mat // 2], sem).start()

            @pl.when(target != me)
            def _():
                pltpu.make_async_remote_copy(
                    s_ref.at[slot], land.at[which, mat // 2], sem, r_unit.at[which, mat // 2],
                    device_id=flat_device(target), device_id_type=MESH,
                ).start()

        def big_body(slot, u, pos, start, b_ref=b_ref, load=load, shard=shard, block=block, big0=big0):
            for q in range(4):
                for k in range(6):
                    b_ref[slot, q % 2, q // 2, :, k * LANES : (k + 1) * LANES] = load(
                        pos + 6 * q + k, UNIT, 24
                    ).astype(BF)
            which = jnp.where(start // shard == me, 0, 1)
            pair = (block.first_mat + block.small_mats) // 2
            for core in range(2):
                target = u * 2 + core
                sem = s_big.at[big0 + slot, core]
                for q in range(2):
                    pass

                @pl.when(target == me)
                def _(core=core, sem=sem):
                    pltpu.make_async_copy(b_ref.at[slot, core], land.at[which, pl.ds(pair, 2)], sem).start()

                @pl.when(target != me)
                def _(core=core, sem=sem, target=target):
                    pltpu.make_async_remote_copy(
                        b_ref.at[slot, core], land.at[which, pl.ds(pair, 2)], sem, r_unit.at[which, pair],
                        device_id=flat_device(target), device_id_type=MESH,
                    ).start()

        def vec_body(v, pos, start, r_ref=r_ref, keep=keep, shard=shard):
            here = r_ref[pl.ds(FRONT + pos, 8), :]
            before = r_ref[pl.ds(FRONT + pos - 1, 8), :]
            sv_ref[v] = jnp.where(keep, here, before).astype(BF).astype(F32)
            which = jnp.where(start // shard == me, 0, 1)

            @pl.when(me == v)
            def _():
                pltpu.make_async_copy(sv_ref.at[v], landv.at[which], s_vec.at[v]).start()

            @pl.when(me != v)
            def _():
                pltpu.make_async_remote_copy(
                    sv_ref.at[v], landv.at[which], s_vec.at[v], r_vec.at[which],
                    device_id=flat_device(v), device_id_type=MESH,
                ).start()

        each_vector(block, n, me, 0 if b == 0 else len(ENC.vectors), vec_body)
        each_small(block, n, me, n_small, small_body)
        each_big(block, n, me, n_big, big_body)

    def of_self(first, last, which):
        return jnp.where(which == 0, first, last) == me

    def arrive_unit(first, last, src, dst, local_sem, recv):
        for which, holder in ((0, first), (1, last)):
            needed = True if which == 0 else (first != last)

            @pl.when(needed & (holder == me))
            def _(which=which):
                pltpu.make_async_copy(src(which), dst(which), local_sem).wait()

            @pl.when(needed & (holder != me))
            def _(which=which):
                pltpu.make_async_copy(src(which), dst(which), recv(which)).wait()

    def vec_of(v):
        n_enc = len(ENC.vectors)
        rows = ENC.vectors + DEC.vectors
        start = 0
        before = 0
        for i, row in enumerate(rows):
            start = start + jnp.where(v >= i, row - before, 0)
            before = row
        return start * D, jnp.where(v < n_enc, sizes(ENC, n)[0], sizes(DEC, n)[0])

    @pl.when(me < N_VEC)
    def _():
        start, shard = vec_of(me)
        first, last = start // shard, (start + D - 1) // shard
        arrive_unit(
            first, last, lambda w: sv_ref.at[0], lambda w: landv.at[w], s_vec.at[me], lambda w: r_vec.at[w]
        )
        at_elem = lax.broadcasted_iota(jnp.int32, (8, LANES), 0) * LANES + lax.broadcasted_iota(jnp.int32, (8, LANES), 1)
        ownv[...] = jnp.where(at_elem < (first + 1) * shard - start, landv[0], landv[1])

    @pl.when(me >= N_VEC)
    def _():
        ownv[...] = jnp.zeros_like(ownv)

    pltpu.sync_copy(ownv, v_ref.at[z, x, y, c])
    vorder = ("z", "x", "y", "c")

    def vview(done):
        have = set(vorder[:done])
        return tuple(slice(None) if a in have else at[a] for a in "zxyc")

    def vcopies(phase):
        axis = vorder[phase]
        out = []
        for k, p in enumerate(peers(axis, at)):
            ref = v_ref.at[vview(phase)]
            slot = phase if axis == "z" else phase + 2
            out.append(
                pltpu.make_async_remote_copy(
                    ref, ref, v_send.at[slot + k], v_recv.at[slot + k], device_id=dev(p), device_id_type=MESH
                )
            )
        return out

    row_i = lax.broadcasted_iota(jnp.int32, (UNIT, D), 0)
    col_i = lax.broadcasted_iota(jnp.int32, (UNIT, D), 1)

    def merge(pair):
        block = ENC if pair < 6 else DEC
        shard = sizes(block, n)[0]
        local = pair - block.first_mat // 2
        half = block.small_mats // 2
        if half <= local < half + 2:
            start = (block.fc1 * 6 + chip * BIG) * LANES
            elem = row_i * FF + (2 * (local - half) + c) * D + col_i
            length = BIG * LANES
        else:
            small = 2 * local - (4 if local >= half + 2 else 0) + c
            start = (small_row(block, small) * 6 + chip * UROWS) * LANES
            elem = row_i * D + col_i
            length = UROWS * LANES
        first, last = start // shard, (start + length - 1) // shard
        if half <= local < half + 2:
            if local == half:
                low_row = me * shard // LANES
                slot = (start // LANES - low_row + BIG) // BIG + (0 if block is ENC else sizes(ENC, n)[3])
                slot = jnp.minimum(jnp.maximum(slot, 0), sizes(ENC, n)[3] + sizes(DEC, n)[3] - 1)
                arrive_unit(
                    first, last, lambda w: land.at[w, pl.ds(pair, 2)], lambda w: land.at[w, pl.ds(pair, 2)],
                    s_big.at[slot, c], lambda w: r_unit.at[w, pair],
                )
        else:
            low_row = me * shard // LANES
            slot = (start // LANES - low_row + UROWS) // UROWS + (0 if block is ENC else sizes(ENC, n)[2])
            slot = jnp.minimum(jnp.maximum(slot, 0), sizes(ENC, n)[2] + sizes(DEC, n)[2] - 1)
            arrive_unit(
                first, last, lambda w: land.at[w, pair], lambda w: land.at[w, pair],
                s_small.at[slot], lambda w: r_unit.at[w, pair],
            )
        own[pair] = jnp.where(elem < (first + 1) * shard - start, land[0, pair], land[1, pair])

    def wdst(pair, done, order):
        return w_ref.at[(pair, c) + view(pair, order, done, at)[1:]]

    def copies(pair, phase):
        order = ORDERS[pair % 2]
        out = []
        if phase == 3:
            ref = w_ref.at[pair, c]
            return [
                pltpu.make_async_remote_copy(
                    ref, ref, s_core.at[pair], r_core.at[pair], device_id=device(z, x, y, 1 - c), device_id_type=MESH
                )
            ]
        axis = order[phase]
        slot = phase if axis == "z" else phase + 2
        for k, p in enumerate(peers(axis, at)):
            ref = wdst(pair, phase, order)
            src = own.at[pair] if phase == 0 else ref
            out.append(
                pltpu.make_async_remote_copy(
                    src, ref, s_zxy.at[pair, slot + k], r_zxy.at[pair, slot + k], device_id=dev(p), device_id_type=MESH
                )
            )
        return out

    lag = 2
    for t in range(N_PAIR + 4 * lag):
        if t < N_PAIR:
            merge(t)
            pltpu.make_async_copy(own.at[t], wdst(t, 0, ORDERS[t % 2]), s_own.at[t]).start()
            for cp in copies(t, 0):
                cp.start()
        for phase in (1, 2, 3):
            pair = t - phase * lag
            if 0 <= pair < N_PAIR:
                if phase == 1:
                    pltpu.make_async_copy(own.at[pair], wdst(pair, 0, ORDERS[pair % 2]), s_own.at[pair]).wait()
                for cp in copies(pair, phase - 1):
                    cp.wait_recv()
                for cp in copies(pair, phase):
                    cp.start()
        pair = t - 4 * lag
        if 0 <= pair < N_PAIR:
            for cp in copies(pair, 3):
                cp.wait_recv()
        if t % 2 == 0 and t < 10:
            phase = t // 2
            if phase > 0:
                for cp in vcopies(phase - 1):
                    cp.wait_recv()
            if phase < 4:
                for cp in vcopies(phase):
                    cp.start()

    for phase in range(4):
        for cp in vcopies(phase):
            cp.wait_send()
    for pair in range(N_PAIR):
        for phase in range(4):
            for cp in copies(pair, phase):
                cp.wait_send()
    for b, (block, s_ref, b_ref) in enumerate(((ENC, se_ref, be_ref), (DEC, sd_ref, bd_ref))):
        shard, rows, n_small, n_big = sizes(block, n)
        small0 = 0 if b == 0 else sizes(ENC, n)[2]
        big0 = 0 if b == 0 else sizes(ENC, n)[3]

        def small_wait(slot, mat, u, pos, start, s_ref=s_ref, small0=small0):
            @pl.when(u * 2 + mat % 2 != me)
            def _():
                pltpu.make_async_copy(s_ref.at[slot], s_ref.at[slot], s_small.at[small0 + slot]).wait()

        def big_wait(slot, u, pos, start, b_ref=b_ref, big0=big0):
            for core in range(2):
                @pl.when(u * 2 + core != me)
                def _(core=core):
                    pltpu.make_async_copy(
                        b_ref.at[slot, core], b_ref.at[slot, core], s_big.at[big0 + slot, core]
                    ).wait()

        def vec_wait(v, pos, start):
            @pl.when(me != v)
            def _():
                pltpu.make_async_copy(sv_ref.at[v], sv_ref.at[v], s_vec.at[v]).wait()

        each_vector(block, n, me, 0 if b == 0 else len(ENC.vectors), vec_wait)
        each_small(block, n, me, n_small, small_wait)
        each_big(block, n, me, n_big, big_wait)


def rows_of(flat, rows):
    return jnp.pad(flat, (0, rows * LANES - flat.shape[0])).reshape(rows, LANES)


def gather_weights(encoder_master, decoder_master, n):
    (_, re, ne, ge), (_, rd, nd, gd) = sizes(ENC, n), sizes(DEC, n)
    dma = pltpu.SemaphoreType.DMA
    return pl.pallas_call(
        partial(gather_kernel, n),
        out_shape=(
            jax.ShapeDtypeStruct((N_PAIR, 2, 4, 2, 2, UNIT, D), BF),
            jax.ShapeDtypeStruct((4, 2, 2, 2, 8, LANES), F32),
        ),
        in_specs=[pl.BlockSpec(memory_space=pltpu.VMEM)] * 2,
        out_specs=(pl.BlockSpec(memory_space=pl.ANY), pl.BlockSpec(memory_space=pl.ANY)),
        scratch_shapes=[
            pltpu.VMEM((FRONT + re + BACK, LANES), F32),
            pltpu.VMEM((FRONT + rd + BACK, LANES), F32),
            pltpu.VMEM((ne, UNIT, D), BF),
            pltpu.VMEM((nd, UNIT, D), BF),
            pltpu.VMEM((ge, 2, 2, UNIT, D), BF),
            pltpu.VMEM((gd, 2, 2, UNIT, D), BF),
            pltpu.VMEM((N_VEC, 8, LANES), F32),
            pltpu.VMEM((2, N_PAIR, UNIT, D), BF),
            pltpu.VMEM((2, 8, LANES), F32),
            pltpu.VMEM((N_PAIR, UNIT, D), BF),
            pltpu.VMEM((8, LANES), F32),
            dma((ne + nd,)),
            dma((ge + gd, 2)),
            dma((N_VEC,)),
            dma((2, N_PAIR)),
            dma((2,)),
            dma((N_PAIR, 5)),
            dma((N_PAIR, 5)),
            dma((N_PAIR,)),
            dma((N_PAIR,)),
            dma((N_PAIR,)),
            dma((6,)),
            dma((6,)),
        ],
        compiler_params=pltpu.CompilerParams(collective_id=0, has_side_effects=True, vmem_limit_bytes=48 << 20),
        name="gather",
    )(rows_of(encoder_master, re), rows_of(decoder_master, rd))


def scatter_kernel(
    n, g_ref, vg_ref, oe_ref, od_ref, norm_ref,
    land_c, land_b, land_a, land_z, gown, ownf, ownb, vown, vl_c, vl_y, vl_x, vl_z,
    ge_ref, gd_ref, fe, fd, fbe, fbd, fv, nsend, nland,
    s_core, r_core, s_g, s_ph, r_ph, s_back, r_small, r_big, sv, rv, s_vback, r_vback, s_n, r_n,
):
    wide, narrow, z, x, y, c = whoami()
    me = wide * 4 + narrow
    chip = me // 2
    at = dict(z=z, x=x, y=y, c=c)
    entry_barrier(me, n)
    sib = device(z, x, y, 1 - c)
    lag = 2

    def core_copy(pair):
        return pltpu.make_async_remote_copy(
            g_ref.at[pair, 1 - c], land_c.at[pair], s_core.at[pair], r_core.at[pair], device_id=sib, device_id_type=MESH
        )

    def own_copy(pair):
        return pltpu.make_async_copy(g_ref.at[pair, c], gown.at[pair % 4], s_g.at[pair])

    def phase_copies(pair, phase):
        order = ORDERS[pair % 2]
        if phase == 1:
            axis = order[2]
            if axis == "y":
                src = land_c.at[pair, :, :, 1 - y]
            else:
                src = land_c.at[pair, :, 1 - x]
            return [(src, land_b.at[pair], 0, peers(axis, at)[0])]
        if phase == 2:
            axis = order[1]
            other = 1 - at[axis]
            return [(land_b.at[pair, :, other], land_a.at[pair], 1, peers(axis, at)[0])]
        return [
            (land_a.at[pair, (z + k) % 4], land_z.at[pair, k - 1], 1 + k, dict(at, z=(z + k) % 4)) for k in (1, 2, 3)
        ]

    def phase_dmas(pair, phase):
        return [
            pltpu.make_async_remote_copy(
                src, dst, s_ph.at[pair, k], r_ph.at[pair, k], device_id=dev(p), device_id_type=MESH
            )
            for src, dst, k, p in phase_copies(pair, phase)
        ]

    def back(pair):
        block = ENC if pair < 6 else DEC
        shard = sizes(block, n)[0]
        local = pair - block.first_mat // 2
        half = block.small_mats // 2
        big = half <= local < half + 2
        if big:
            start = (block.fc1 * 6 + chip * BIG) * LANES
            length = BIG * LANES
        else:
            small = 2 * local - (4 if local >= half + 2 else 0) + c
            start = (small_row(block, small) * 6 + chip * UROWS) * LANES
            length = UROWS * LANES
        first, last = start // shard, (start + length - 1) // shard
        out = []
        for which, target in ((0, first), (1, last)):
            low_row = target * shard // LANES
            if big:
                slot = (start // LANES - low_row + BIG) // BIG
                q = 2 * (local - half) + c
                dst = (fbe if block is ENC else fbd).at[slot, q]
                recv = r_big.at[0 if block is ENC else 1, slot, q]
            else:
                slot = (start // LANES - low_row + UROWS) // UROWS
                dst = (fe if block is ENC else fd).at[slot]
                recv = r_small.at[0 if block is ENC else 1, slot]
            needed = True if which == 0 else first != last
            out.append((needed, target, dst, s_back.at[pair, which], recv))
        return out

    def start_back(pair):
        for needed, target, dst, send, recv in back(pair):
            @pl.when(needed & (target == me))
            def _(dst=dst, recv=recv):
                pltpu.make_async_copy(ownb.at[pair], dst, recv).start()

            @pl.when(needed & (target != me))
            def _(dst=dst, recv=recv, send=send, target=target):
                pltpu.make_async_remote_copy(
                    ownb.at[pair], dst, send, recv, device_id=flat_device(target), device_id_type=MESH
                ).start()

    def end_back(pair):
        for needed, target, dst, send, recv in back(pair):
            @pl.when(needed & (target != me))
            def _(send=send):
                pltpu.make_async_copy(ownb.at[pair], ownb.at[pair], send).wait()

    def add_core(pair):
        def body(i, carry):
            a, b = i // 2, i % 2
            for k in range(2):
                land_c[pair, a, b, k] = (
                    land_c[pair, a, b, k].astype(F32) + gown[pair % 4, a, b, k].astype(F32)
                ).astype(BF)
            return carry

        lax.fori_loop(0, 8, body, 0)

    def add_b(pair):
        axis = ORDERS[pair % 2][2]

        def body(i, carry):
            a, b = i // 2, i % 2
            mine = land_c[pair, a, b, y] if axis == "y" else land_c[pair, a, x, b]
            land_b[pair, a, b] = (land_b[pair, a, b].astype(F32) + mine.astype(F32)).astype(BF)
            return carry

        lax.fori_loop(0, 8, body, 0)

    def add_a(pair):
        own = at[ORDERS[pair % 2][1]]
        for a in range(4):
            land_a[pair, a] = (land_a[pair, a].astype(F32) + land_b[pair, a, own].astype(F32)).astype(BF)

    def add_z(pair):
        total = land_a[pair, z].astype(F32)
        for k in range(3):
            total = total + land_z[pair, k].astype(F32)
        ownb[pair] = total.astype(BF)
        squares = total * total
        return jnp.sum(squares.reshape(UNIT // 8, 8, D), axis=0)

    vland = dict(c=vl_c, y=vl_y, x=vl_x, z=vl_z)

    def vsteps(phase):
        if phase == 0:
            return [(vg_ref.at[:, :, :, 1 - c], vl_c, 0, dict(at, c=1 - c))]
        if phase == 1:
            return [(vl_c.at[:, :, 1 - y], vl_y, 1, dict(at, y=1 - y))]
        if phase == 2:
            return [(vl_y.at[:, 1 - x], vl_x, 2, dict(at, x=1 - x))]
        return [(vl_x.at[(z + k) % 4], vl_z.at[k - 1], 2 + k, dict(at, z=(z + k) % 4)) for k in (1, 2, 3)]

    def vdmas(phase):
        return [
            pltpu.make_async_remote_copy(s, d, sv.at[k], rv.at[k], device_id=dev(p), device_id_type=MESH)
            for s, d, k, p in vsteps(phase)
        ]

    def vadd(phase):
        if phase == 0:
            vl_c[...] = vl_c[...] + vg_ref[:, :, :, c]
        elif phase == 1:
            vl_y[...] = vl_y[...] + vl_c[:, :, y]
        elif phase == 2:
            vl_x[...] = vl_x[...] + vl_y[:, x]
        else:
            vown[...] = vl_x[z] + vl_z[0] + vl_z[1] + vl_z[2]

    seq = list(range(N_PAIR - 1, -1, -1))
    square = jnp.zeros((8, D), F32)
    for cp in vdmas(0):
        cp.start()
    for t in range(N_PAIR + 4 * lag):
        if t < N_PAIR:
            core_copy(seq[t]).start()
            own_copy(seq[t]).start()
        for phase in (1, 2, 3, 4):
            i = t - phase * lag
            if 0 <= i < N_PAIR:
                pair = seq[i]
                if phase == 1:
                    own_copy(pair).wait()
                    core_copy(pair).wait_recv()
                    add_core(pair)
                elif phase == 2:
                    for cp in phase_dmas(pair, 1):
                        cp.wait_recv()
                    add_b(pair)
                elif phase == 3:
                    for cp in phase_dmas(pair, 2):
                        cp.wait_recv()
                    add_a(pair)
                else:
                    for cp in phase_dmas(pair, 3):
                        cp.wait_recv()
                    square = square + add_z(pair)
                    start_back(pair)
                if phase < 4:
                    for cp in phase_dmas(pair, phase):
                        cp.start()
        if t % 2 == 1 and t < 9:
            phase = t // 2
            for cp in vdmas(phase):
                cp.wait_recv()
            vadd(phase)
            if phase < 3:
                for cp in vdmas(phase + 1):
                    cp.start()

    vsq = vown[...] * vown[...]
    for k in range(6):
        vsq = vsq + square[:, k * LANES : (k + 1) * LANES]
    nsend[...] = vsq

    def norm_copy(i):
        return pltpu.make_async_remote_copy(
            nsend, nland.at[i], s_n.at[i], r_n.at[i], device_id=flat_device((me + i) % n), device_id_type=MESH
        )

    def norm_start(i, carry):
        norm_copy(i).start()
        return carry

    lax.fori_loop(1, n, norm_start, 0)

    def vector_targets(v_static):
        block = ENC if v_static < len(ENC.vectors) else DEC
        shard = sizes(block, n)[0]
        start = (ENC.vectors + DEC.vectors)[v_static] * D
        return start // shard, (start + D - 1) // shard

    for v in range(N_VEC):
        for which, target in enumerate(sorted(set(vector_targets(v)))):
            if target == v:
                @pl.when(me == v)
                def _(v=v):
                    pltpu.make_async_copy(vown, fv.at[v], r_vback.at[v]).start()
            else:
                @pl.when(me == v)
                def _(v=v, target=target, which=which):
                    pltpu.make_async_remote_copy(
                        vown, fv.at[v], s_vback.at[which], r_vback.at[v], device_id=(target // 4, target % 4), device_id_type=MESH
                    ).start()

    lanes = lax.broadcasted_iota(jnp.int32, (1, LANES), 1)
    for b, (block, g_out, o_ref, f_ref, fb_ref) in enumerate(
        ((ENC, ge_ref, oe_ref, fe, fbe), (DEC, gd_ref, od_ref, fd, fbd))
    ):
        shard, rows, n_small, n_big = sizes(block, n)
        shift = (me * shard) % LANES

        def small_body(slot, mat, u, pos, start, b=b, g_out=g_out, f_ref=f_ref):
            pltpu.make_async_copy(f_ref.at[slot], f_ref.at[slot], r_small.at[b, slot]).wait()
            for k in range(6):
                g_out[pl.ds(FRONT + pos + k, UNIT, stride=6), :] = f_ref[slot, :, k * LANES : (k + 1) * LANES].astype(F32)

        def big_body(slot, u, pos, start, b=b, g_out=g_out, fb_ref=fb_ref):
            for q in range(4):
                pltpu.make_async_copy(fb_ref.at[slot, q], fb_ref.at[slot, q], r_big.at[b, slot, q]).wait()
                for k in range(6):
                    g_out[pl.ds(FRONT + pos + 6 * q + k, UNIT, stride=24), :] = fb_ref[
                        slot, q, :, k * LANES : (k + 1) * LANES
                    ].astype(F32)

        def vec_body(v, pos, start, g_out=g_out):
            pltpu.make_async_copy(fv.at[v], fv.at[v], r_vback.at[v]).wait()
            g_out[pl.ds(FRONT + pos, 6), :] = fv[v, 0:6, :]

        each_small(block, n, me, n_small, small_body)
        each_big(block, n, me, n_big, big_body)
        each_vector(block, n, me, 0 if b == 0 else len(ENC.vectors), vec_body)

        step = 8 * max(k for k in range(1, 40) if (rows // 8) % k == 0)
        unturn = lax.rem(LANES - shift, LANES)

        def turn(i, carry, g_out=g_out, o_ref=o_ref, step=step, shift=shift, unturn=unturn):
            at_row = pl.multiple_of(i * step, 8)
            here = pltpu.roll(g_out[pl.ds(FRONT + at_row, step), :], unturn, 1)
            after = pltpu.roll(g_out[pl.ds(FRONT + at_row + 1, step), :], unturn, 1)
            o_ref[pl.ds(at_row, step), :] = jnp.where(lanes < LANES - shift, here, after)
            return carry

        lax.fori_loop(0, rows // step, turn, 0)

    def norm_wait(i, total):
        norm_copy(i).wait()
        return total + nland[i]

    total = lax.fori_loop(1, n, norm_wait, nsend[...])
    norm_ref[...] = jnp.broadcast_to(jnp.sqrt(jnp.sum(total)), (8, LANES))

    for phase in range(4):
        for cp in vdmas(phase):
            cp.wait_send()
    for v in range(N_VEC):
        for which, target in enumerate(sorted(set(vector_targets(v)))):
            if target != v:
                @pl.when(me == v)
                def _(which=which):
                    pltpu.make_async_copy(vown, vown, s_vback.at[which]).wait()
    for pair in range(N_PAIR):
        core_copy(pair).wait_send()
        for phase in (1, 2, 3):
            for cp in phase_dmas(pair, phase):
                cp.wait_send()
        end_back(pair)


def scatter_gradients(grads, vector_grads, n):
    (_, re, ne, ge), (_, rd, nd, gd) = sizes(ENC, n), sizes(DEC, n)
    dma = pltpu.SemaphoreType.DMA
    vmem = pl.BlockSpec(memory_space=pltpu.VMEM)
    return pl.pallas_call(
        partial(scatter_kernel, n),
        out_shape=(
            jax.ShapeDtypeStruct((re, LANES), F32),
            jax.ShapeDtypeStruct((rd, LANES), F32),
            jax.ShapeDtypeStruct((8, LANES), F32),
        ),
        in_specs=[pl.BlockSpec(memory_space=pl.ANY), vmem],
        out_specs=(vmem, vmem, vmem),
        scratch_shapes=[
            pltpu.VMEM((N_PAIR, 4, 2, 2, UNIT, D), BF),
            pltpu.VMEM((N_PAIR, 4, 2, UNIT, D), BF),
            pltpu.VMEM((N_PAIR, 4, UNIT, D), BF),
            pltpu.VMEM((N_PAIR, 3, UNIT, D), BF),
            pltpu.VMEM((4, 4, 2, 2, UNIT, D), BF),
            pltpu.VMEM((8, LANES), F32),
            pltpu.VMEM((N_PAIR, UNIT, D), BF),
            pltpu.VMEM((8, LANES), F32),
            pltpu.VMEM((4, 2, 2, 8, LANES), F32),
            pltpu.VMEM((4, 2, 8, LANES), F32),
            pltpu.VMEM((4, 8, LANES), F32),
            pltpu.VMEM((3, 8, LANES), F32),
            pltpu.VMEM((FRONT + re + BACK, LANES), F32),
            pltpu.VMEM((FRONT + rd + BACK, LANES), F32),
            pltpu.VMEM((ne, UNIT, D), BF),
            pltpu.VMEM((nd, UNIT, D), BF),
            pltpu.VMEM((ge, 4, UNIT, D), BF),
            pltpu.VMEM((gd, 4, UNIT, D), BF),
            pltpu.VMEM((N_VEC, 8, LANES), F32),
            pltpu.VMEM((8, LANES), F32),
            pltpu.VMEM((n, 8, LANES), F32),
            dma((N_PAIR,)),
            dma((N_PAIR,)),
            dma((N_PAIR,)),
            dma((N_PAIR, 5)),
            dma((N_PAIR, 5)),
            dma((N_PAIR, 2)),
            dma((2, max(ne, nd))),
            dma((2, max(ge, gd), 4)),
            dma((6,)),
            dma((6,)),
            dma((2,)),
            dma((N_VEC,)),
            dma((n,)),
            dma((n,)),
        ],
        compiler_params=pltpu.CompilerParams(collective_id=1, has_side_effects=True, vmem_limit_bytes=60 << 20),
        name="scatter",
    )(grads, vector_grads)


def named_params(w, v):
    mats = w.reshape(N_MAT, D, D)
    vec = v.reshape(32, 8 * LANES)[:, :D]
    both = []
    m = i = 0
    for layout in (encoder_layout(D, FF), decoder_layout(D, FF)):
        params = {}
        for name, rows, cols in layout:
            if cols == FF:
                params[name] = mats[m : m + 4]
                m += 4
            elif cols > 0:
                params[name] = mats[m : m + rows // D].reshape(rows, D)
                m += rows // D
            else:
                params[name] = vec[i : i + rows // D].reshape(rows)
                i += rows // D
        both.append(params)
    return both


def packed_grads(enc, dec):
    mats, vectors = [], []
    for grads, layout in ((enc, encoder_layout(D, FF)), (dec, decoder_layout(D, FF))):
        for name, rows, cols in layout:
            if cols == FF:
                mats += grads[name]
            elif cols > 0:
                mats += [grads[name][k * D : (k + 1) * D] for k in range(rows // D)]
            else:
                vectors.append(grads[name])
    mats = jnp.stack([m.astype(BF) for m in mats])
    vec = jnp.concatenate(vectors)
    vec = jnp.pad(vec.reshape(N_VEC, D), ((0, 32 - N_VEC), (0, 8 * LANES - D)))
    return mats.reshape(N_PAIR, 2, 4, 2, 2, UNIT, D), vec.reshape(4, 2, 2, 2, 8, LANES)


def attention_plan(prefix, width):
    return [
        (prefix + "wq", width, width),
        (prefix + "bq", width, 0),
        (prefix + "wk", width, width),
        (prefix + "wv", width, width),
        (prefix + "bv", width, 0),
        (prefix + "wo", width, width),
        (prefix + "bo", width, 0),
    ]


def feed_plan(width, hidden):
    return [
        ("fc1_weight", width, hidden),
        ("fc1_bias", hidden, 0),
        ("fc2_weight", hidden, width),
        ("fc2_bias", width, 0),
    ]


def encoder_layout(width, hidden):
    return (
        [("ln1_gain", width, 0), ("ln1_bias", width, 0)]
        + attention_plan("att_", width)
        + [("ln2_gain", width, 0), ("ln2_bias", width, 0)]
        + feed_plan(width, hidden)
    )


def decoder_layout(width, hidden):
    return (
        [("ln1_gain", width, 0), ("ln1_bias", width, 0)]
        + attention_plan("self_", width)
        + [("ln2_gain", width, 0), ("ln2_bias", width, 0)]
        + attention_plan("cross_", width)
        + [("ln3_gain", width, 0), ("ln3_bias", width, 0)]
        + feed_plan(width, hidden)
    )


def unpack(flat, layout):
    params = {}
    offset = 0
    for name, rows, cols in layout:
        count = rows * cols if cols > 0 else rows
        piece = flat[offset : offset + count]
        params[name] = piece.reshape(rows, cols) if cols > 0 else piece
        offset = offset + count
    return params


def pack(grads, layout):
    return jnp.concatenate([grads[name].reshape(-1) for name, rows, cols in layout])


def dot_plain(left, right):
    return jnp.dot(left, right, preferred_element_type=jnp.float32)


def dot_left(left, right):
    return lax.dot_general(
        left, right, (((0,), (0,)), ((), ())), preferred_element_type=jnp.float32
    )


def dot_right(left, right):
    return lax.dot_general(
        left, right, (((1,), (1,)), ((), ())), preferred_element_type=jnp.float32
    )


def layer_norm(values, gain, shift):
    centred = values - jnp.mean(values, axis=-1, keepdims=True)
    spread = jnp.mean(centred * centred, axis=-1, keepdims=True)
    return centred * lax.rsqrt(spread + 1e-05) * gain + shift


def norm_forward(params, prefix, values):
    gain = params[prefix + "_gain"].astype(jnp.float32)
    shift = params[prefix + "_bias"].astype(jnp.float32)
    return layer_norm(values, gain, shift).astype(jnp.bfloat16)


def norm_backward(params, prefix, values, grad):
    gain = params[prefix + "_gain"].astype(jnp.float32)
    shift = params[prefix + "_bias"].astype(jnp.float32)
    unused, pullback = jax.vjp(layer_norm, values, gain, shift)
    value_grad, gain_grad, shift_grad = pullback(grad)
    return (value_grad, {prefix + "_gain": gain_grad, prefix + "_bias": shift_grad})


def block_rows(total):
    return total if total <= 1024 else 512


def attend_forward(queries, keys_low, values, allowed_fn):
    total, width = queries.shape
    heads = width // HEAD_DIM
    rows = block_rows(total)
    blocks = total // rows
    scale = HEAD_DIM ** (-0.5)
    query_heads = queries.reshape(blocks, rows, heads, HEAD_DIM)
    key_heads = keys_low.reshape(keys_low.shape[0], heads, HEAD_DIM)
    value_heads = values.reshape(values.shape[0], heads, HEAD_DIM)
    starts = jnp.arange(blocks, dtype=jnp.int32) * rows

    def one_block(inputs):
        block, start = inputs
        scores = (
            jnp.einsum("qhd,khd->hqk", block, key_heads, preferred_element_type=jnp.float32) * scale
        )
        if allowed_fn is not None:
            scores = jnp.where(allowed_fn(start, rows)[None], scores, -1000000000.0)
        peak = jnp.max(scores, axis=-1, keepdims=True)
        weights = jnp.exp(scores - peak)
        totals = jnp.sum(weights, axis=-1, keepdims=True)
        probs = (weights / totals).astype(jnp.bfloat16)
        mixed = jnp.einsum("hqk,khd->qhd", probs, value_heads, preferred_element_type=jnp.float32)
        return (mixed.reshape(rows, width).astype(jnp.bfloat16), (peak + jnp.log(totals))[..., 0])

    mixed, logsum = lax.map(one_block, (query_heads, starts))
    return (mixed.reshape(total, width), logsum)


def attend_backward(queries, keys_low, values, logsum, mixed_grad, allowed_fn):
    total, width = queries.shape
    heads = width // HEAD_DIM
    rows = block_rows(total)
    blocks = total // rows
    scale = HEAD_DIM ** (-0.5)
    query_heads = queries.reshape(blocks, rows, heads, HEAD_DIM)
    grad_heads = mixed_grad.reshape(blocks, rows, heads, HEAD_DIM)
    key_heads = keys_low.reshape(keys_low.shape[0], heads, HEAD_DIM)
    value_heads = values.reshape(values.shape[0], heads, HEAD_DIM)
    starts = jnp.arange(blocks, dtype=jnp.int32) * rows

    def one_block(carry, inputs):
        key_grad, value_grad = carry
        block, grad_block, block_sum, start = inputs
        scores = (
            jnp.einsum("qhd,khd->hqk", block, key_heads, preferred_element_type=jnp.float32) * scale
        )
        if allowed_fn is not None:
            scores = jnp.where(allowed_fn(start, rows)[None], scores, -1000000000.0)
        probs = jnp.exp(scores - block_sum[..., None])
        prob_grad = jnp.einsum(
            "qhd,khd->hqk", grad_block, value_heads, preferred_element_type=jnp.float32
        )
        value_grad = value_grad + jnp.einsum(
            "hqk,qhd->khd",
            probs.astype(jnp.bfloat16),
            grad_block,
            preferred_element_type=jnp.float32,
        )
        score_grad = probs * (prob_grad - jnp.sum(probs * prob_grad, axis=-1, keepdims=True))
        raw_grad = (score_grad * scale).astype(jnp.bfloat16)
        query_grad = jnp.einsum(
            "hqk,khd->qhd", raw_grad, key_heads, preferred_element_type=jnp.float32
        )
        key_grad = key_grad + jnp.einsum(
            "hqk,qhd->khd", raw_grad, block, preferred_element_type=jnp.float32
        )
        return ((key_grad, value_grad), query_grad.reshape(rows, width))

    zeros = jnp.zeros(key_heads.shape, jnp.float32)
    (key_grad, value_grad), query_grad = lax.scan(
        one_block, (zeros, zeros), (query_heads, grad_heads, logsum, starts)
    )
    return (
        query_grad.reshape(total, width),
        key_grad.reshape(keys_low.shape[0], width),
        value_grad.reshape(values.shape[0], width),
    )


def attention_forward(params, prefix, query_rows, key_rows, allowed_fn):
    queries = (dot_plain(query_rows, params[prefix + "wq"]) + params[prefix + "bq"]).astype(
        jnp.bfloat16
    )
    keys_low = dot_plain(key_rows, params[prefix + "wk"]).astype(jnp.bfloat16)
    values = (dot_plain(key_rows, params[prefix + "wv"]) + params[prefix + "bv"]).astype(
        jnp.bfloat16
    )
    mixed, logsum = attend_forward(queries, keys_low, values, allowed_fn)
    output = dot_plain(mixed, params[prefix + "wo"]) + params[prefix + "bo"]
    return (output, (queries, keys_low, values, mixed, logsum))


def attention_backward(params, prefix, query_rows, key_rows, kept, out_grad, allowed_fn):
    queries, keys_low, values, mixed, logsum = kept
    out_round = out_grad.astype(jnp.bfloat16)
    mixed_grad = dot_right(out_round, params[prefix + "wo"]).astype(jnp.bfloat16)
    query_grad, key_grad, value_grad = attend_backward(
        queries, keys_low, values, logsum, mixed_grad, allowed_fn
    )
    query_round = query_grad.astype(jnp.bfloat16)
    key_round = key_grad.astype(jnp.bfloat16)
    value_round = value_grad.astype(jnp.bfloat16)
    grads = {
        prefix + "wq": dot_left(query_rows, query_round),
        prefix + "bq": jnp.sum(query_grad, axis=0),
        prefix + "wk": dot_left(key_rows, key_round),
        prefix + "wv": dot_left(key_rows, value_round),
        prefix + "bv": jnp.sum(value_grad, axis=0),
        prefix + "wo": dot_left(mixed, out_round),
        prefix + "bo": jnp.sum(out_grad, axis=0),
    }
    query_side = dot_right(query_round, params[prefix + "wq"])
    key_side = dot_right(key_round, params[prefix + "wk"]) + dot_right(
        value_round, params[prefix + "wv"]
    )
    return (grads, query_side, key_side)


def feed_forward(params, normed):
    pre = dot_plain(normed, params["fc1_weight"]) + params["fc1_bias"]
    activated = jax.nn.gelu(pre, approximate=False).astype(jnp.bfloat16)
    return (dot_plain(activated, params["fc2_weight"]) + params["fc2_bias"], (pre, activated))


def feed_backward(params, normed, kept, out_grad):
    pre, activated = kept
    out_round = out_grad.astype(jnp.bfloat16)
    act_grad = dot_right(out_round, params["fc2_weight"])
    unused, gelu_back = jax.vjp(partial(jax.nn.gelu, approximate=False), pre)
    pre_grad = gelu_back(act_grad)[0]
    pre_round = pre_grad.astype(jnp.bfloat16)
    grads = {
        "fc1_weight": dot_left(normed, pre_round),
        "fc1_bias": jnp.sum(pre_grad, axis=0),
        "fc2_weight": dot_left(activated, out_round),
        "fc2_bias": jnp.sum(out_grad, axis=0),
    }
    return (grads, dot_right(pre_round, params["fc1_weight"]))


def feeds(params):
    cut = params["fc1_weight"].ndim == 3
    return (feed_forward_cut, feed_backward_cut) if cut else (feed_forward, feed_backward)


def encoder_forward(params, frames):
    normed = norm_forward(params, "ln1", frames)
    attended, attend_kept = attention_forward(params, "att_", normed, normed, None)
    after = frames + attended
    normed_two = norm_forward(params, "ln2", after)
    fed, feed_kept = feeds(params)[0](params, normed_two)
    return (after + fed, (normed, attend_kept, after, normed_two, feed_kept))


def encoder_backward(params, frames, kept, out_grad):
    normed, attend_kept, after, normed_two, feed_kept = kept
    grads, normed_grad = feeds(params)[1](params, normed_two, feed_kept, out_grad)
    part, norm_grads = norm_backward(params, "ln2", after, normed_grad)
    grads.update(norm_grads)
    after_grad = out_grad + part
    attend_grads, query_side, key_side = attention_backward(
        params, "att_", normed, normed, attend_kept, after_grad, None
    )
    grads.update(attend_grads)
    part, norm_grads = norm_backward(params, "ln1", frames, query_side + key_side)
    grads.update(norm_grads)
    return (grads, after_grad + part)


def decoder_forward(params, tokens, memory_low, allowed_fn):
    normed = norm_forward(params, "ln1", tokens)
    attended, self_kept = attention_forward(params, "self_", normed, normed, allowed_fn)
    after = tokens + attended
    normed_two = norm_forward(params, "ln2", after)
    crossed, cross_kept = attention_forward(params, "cross_", normed_two, memory_low, None)
    after_two = after + crossed
    normed_three = norm_forward(params, "ln3", after_two)
    fed, feed_kept = feeds(params)[0](params, normed_three)
    return (
        after_two + fed,
        (normed, self_kept, after, normed_two, cross_kept, after_two, normed_three, feed_kept),
    )


def decoder_backward(params, tokens, memory_low, kept, out_grad, allowed_fn):
    normed, self_kept, after, normed_two, cross_kept, after_two, normed_three, feed_kept = kept
    grads, normed_grad = feeds(params)[1](params, normed_three, feed_kept, out_grad)
    part, norm_grads = norm_backward(params, "ln3", after_two, normed_grad)
    grads.update(norm_grads)
    after_two_grad = out_grad + part
    cross_grads, query_side, memory_grad = attention_backward(
        params, "cross_", normed_two, memory_low, cross_kept, after_two_grad, None
    )
    grads.update(cross_grads)
    part, norm_grads = norm_backward(params, "ln2", after, query_side)
    grads.update(norm_grads)
    after_grad = after_two_grad + part
    self_grads, query_side, key_side = attention_backward(
        params, "self_", normed, normed, self_kept, after_grad, allowed_fn
    )
    grads.update(self_grads)
    part, norm_grads = norm_backward(params, "ln1", tokens, query_side + key_side)
    grads.update(norm_grads)
    return (grads, after_grad + part, memory_grad)


def adamw(master, first, second, grad, factor, correction):
    clipped = grad * factor
    moment = 0.5 * first + 0.5 * clipped
    variance = 0.5 * second + 0.5 * clipped * clipped
    update = moment / correction / (jnp.sqrt(variance / correction) + 1e-08) + 0.01 * master
    weights = master - 0.02 * update
    return (weights, moment, variance, weights.astype(jnp.bfloat16))


def shards_native(
    encoder_input,
    decoder_input,
    segments,
    encoder_cotangent,
    decoder_cotangent,
    encoder_master,
    encoder_first,
    encoder_second,
    decoder_master,
    decoder_first,
    decoder_second,
    step_count,
):
    encoder_plan = encoder_layout(D, FF)
    decoder_plan = decoder_layout(D, FF)
    encoder_params = unpack(
        lax.all_gather(encoder_master.astype(jnp.bfloat16), ("wide", "narrow"), axis=0, tiled=True),
        encoder_plan,
    )
    frames = encoder_input[0].astype(jnp.float32)
    memory, encoder_kept = encoder_forward(encoder_params, frames)
    memory_low = memory.astype(jnp.bfloat16)
    decoder_params = unpack(
        lax.all_gather(decoder_master.astype(jnp.bfloat16), ("wide", "narrow"), axis=0, tiled=True),
        decoder_plan,
    )
    tokens = decoder_input[0].astype(jnp.float32)
    segment_row = segments[0]
    length = segment_row.shape[0]

    def allowed_fn(start, count):
        places = start + jnp.arange(count, dtype=jnp.int32)
        row_segments = lax.dynamic_slice_in_dim(segment_row, start, count)
        columns = jnp.arange(length, dtype=jnp.int32)
        return (row_segments[:, None] == segment_row[None, :]) & (
            columns[None, :] <= places[:, None]
        )

    decoded, decoder_kept = decoder_forward(decoder_params, tokens, memory_low, allowed_fn)
    decoder_again = unpack(
        lax.all_gather(decoder_master.astype(jnp.bfloat16), ("wide", "narrow"), axis=0, tiled=True),
        decoder_plan,
    )
    decoder_grads, token_grad, memory_grad = decoder_backward(
        decoder_again,
        tokens,
        memory_low,
        decoder_kept,
        decoder_cotangent[0].astype(jnp.float32),
        allowed_fn,
    )
    decoder_total = pack(decoder_grads, decoder_plan)
    decoder_owned = lax.psum_scatter(
        decoder_total, ("wide", "narrow"), scatter_dimension=0, tiled=True
    )
    encoder_again = unpack(
        lax.all_gather(encoder_master.astype(jnp.bfloat16), ("wide", "narrow"), axis=0, tiled=True),
        encoder_plan,
    )
    memory_total = encoder_cotangent[0].astype(jnp.float32) + memory_grad
    encoder_grads, frame_grad = encoder_backward(encoder_again, frames, encoder_kept, memory_total)
    encoder_total = pack(encoder_grads, encoder_plan)
    encoder_owned = lax.psum_scatter(
        encoder_total, ("wide", "narrow"), scatter_dimension=0, tiled=True
    )
    local_squares = jnp.sum(encoder_owned * encoder_owned) + jnp.sum(decoder_owned * decoder_owned)
    gradient_norm = jnp.sqrt(lax.psum(local_squares, ("wide", "narrow")))
    factor = 1.0 / jnp.maximum(gradient_norm, 1.0)
    correction = 1.0 - jnp.power(0.5, step_count.astype(jnp.float32))
    encoder_new = adamw(
        encoder_master, encoder_first, encoder_second, encoder_owned, factor, correction
    )
    decoder_new = adamw(
        decoder_master, decoder_first, decoder_second, decoder_owned, factor, correction
    )
    return (
        memory_low[None],
        decoded.astype(jnp.bfloat16)[None],
        frame_grad[None],
        token_grad[None],
        gradient_norm,
        encoder_new[0],
        encoder_new[1],
        encoder_new[2],
        encoder_new[3],
        decoder_new[0],
        decoder_new[1],
        decoder_new[2],
        decoder_new[3],
    )


def feed_forward_cut(params, normed):
    pre = jnp.concatenate([dot_plain(normed, params["fc1_weight"][k]) for k in range(4)], axis=1) + params["fc1_bias"]
    activated = jax.nn.gelu(pre, approximate=False).astype(jnp.bfloat16)
    return (dot_plain(activated, params["fc2_weight"]) + params["fc2_bias"], (pre, activated))


def feed_backward_cut(params, normed, kept, out_grad):
    pre, activated = kept
    out_round = out_grad.astype(jnp.bfloat16)
    act_grad = dot_right(out_round, params["fc2_weight"])
    unused, gelu_back = jax.vjp(partial(jax.nn.gelu, approximate=False), pre)
    pre_grad = gelu_back(act_grad)[0]
    pre_round = pre_grad.astype(jnp.bfloat16)
    pieces = [pre_round[:, k * D : (k + 1) * D] for k in range(4)]
    grads = {
        "fc1_weight": [dot_left(normed, piece) for piece in pieces],
        "fc1_bias": jnp.sum(pre_grad, axis=0),
        "fc2_weight": dot_left(activated, out_round),
        "fc2_bias": jnp.sum(out_grad, axis=0),
    }
    return (grads, sum(dot_right(piece, params["fc1_weight"][k]) for k, piece in enumerate(pieces)))


def shards(
    encoder_input,
    decoder_input,
    segments,
    encoder_cotangent,
    decoder_cotangent,
    encoder_master,
    encoder_first,
    encoder_second,
    decoder_master,
    decoder_first,
    decoder_second,
    step_count,
):
    n = 32
    weights, vectors = gather_weights(encoder_master, decoder_master, n)
    encoder_params, decoder_params = named_params(weights, vectors)
    frames = encoder_input[0].astype(jnp.float32)
    memory, encoder_kept = encoder_forward(encoder_params, frames)
    memory_low = memory.astype(jnp.bfloat16)
    tokens = decoder_input[0].astype(jnp.float32)
    segment_row = segments[0]
    length = segment_row.shape[0]

    def allowed_fn(start, count):
        places = start + jnp.arange(count, dtype=jnp.int32)
        row_segments = lax.dynamic_slice_in_dim(segment_row, start, count)
        columns = jnp.arange(length, dtype=jnp.int32)
        return (row_segments[:, None] == segment_row[None, :]) & (columns[None, :] <= places[:, None])

    decoded, decoder_kept = decoder_forward(decoder_params, tokens, memory_low, allowed_fn)
    decoder_grads, token_grad, memory_grad = decoder_backward(
        decoder_params, tokens, memory_low, decoder_kept, decoder_cotangent[0].astype(jnp.float32), allowed_fn
    )
    memory_total = encoder_cotangent[0].astype(jnp.float32) + memory_grad
    encoder_grads, frame_grad = encoder_backward(encoder_params, frames, encoder_kept, memory_total)
    grads, vector_grads = packed_grads(encoder_grads, decoder_grads)
    encoder_flat, decoder_flat, norm = scatter_gradients(grads, vector_grads, n)
    gradient_norm = norm[0, 0]
    factor = 1.0 / jnp.maximum(gradient_norm, 1.0)
    correction = 1.0 - jnp.power(0.5, step_count.astype(jnp.float32))
    encoder_owned = encoder_flat.reshape(-1)[: encoder_master.shape[0]]
    decoder_owned = decoder_flat.reshape(-1)[: decoder_master.shape[0]]
    encoder_new = adamw(encoder_master, encoder_first, encoder_second, encoder_owned, factor, correction)
    decoder_new = adamw(decoder_master, decoder_first, decoder_second, decoder_owned, factor, correction)
    return (
        memory_low[None],
        decoded.astype(jnp.bfloat16)[None],
        frame_grad[None],
        token_grad[None],
        gradient_norm,
        *encoder_new,
        *decoder_new,
    )


def solution(mesh):
    placed = (
        P(("wide", "narrow"), None, None),
        P(("wide", "narrow"), None, None),
        P(("wide", "narrow"), None),
        P(("wide", "narrow"), None, None),
        P(("wide", "narrow"), None, None),
        P(("wide", "narrow")),
        P(("wide", "narrow")),
        P(("wide", "narrow")),
        P(("wide", "narrow")),
        P(("wide", "narrow")),
        P(("wide", "narrow")),
        P(),
    )
    return jax.shard_map(
        shards if tuple(mesh.shape[a] for a in ("wide", "narrow")) == (8, 4) else shards_native,
        mesh=mesh,
        in_specs=placed,
        out_specs=(
            P(("wide", "narrow"), None, None),
            P(("wide", "narrow"), None, None),
            P(("wide", "narrow"), None, None),
            P(("wide", "narrow"), None, None),
            P(),
            P(("wide", "narrow")),
            P(("wide", "narrow")),
            P(("wide", "narrow")),
            P(("wide", "narrow")),
            P(("wide", "narrow")),
            P(("wide", "narrow")),
            P(("wide", "narrow")),
            P(("wide", "narrow")),
        ),
        check_vma=False,
    )
```

```python
from functools import partial

import jax
import jax.numpy as jnp
from jax import lax
from jax.experimental import pallas as pl
from jax.experimental.pallas import tpu as pltpu
from jax.sharding import PartitionSpec as P

D = 768
HEAD_DIM = 64
FF = 3072
MESH = pl.DeviceIdType.MESH
BF = jnp.bfloat16
F32 = jnp.float32

N_MAT = 28
N_PAIR = 14
UNIT = 48
LANES = 128
UROWS = UNIT * D // LANES
BIG = 4 * UROWS
FRONT = BIG + 8
BACK = BIG + 8
N_VEC = 29


class Block:
    def __init__(self, small, gaps, fc1, vectors, first_mat, small_mats, total):
        self.small = small
        self.gaps = gaps
        self.fc1 = fc1
        self.vectors = vectors
        self.first_mat = first_mat
        self.small_mats = small_mats
        self.total = total


ENC = Block(
    small=8,
    gaps=((0, 2), (1, 1), (3, 1), (4, 3072 + 7)),
    fc1=3079,
    vectors=[0, 1, 770, 2307, 3076, 3077, 3078, 6151, 6152, 6153, 6154, 9227],
    first_mat=0,
    small_mats=4,
    total=9228,
)
DEC = Block(
    small=12,
    gaps=((0, 2), (1, 1), (3, 1), (4, 3), (5, 1), (7, 1), (8, 3072 + 7)),
    fc1=6156,
    vectors=[0, 1, 770, 2307, 3076, 3077, 3078, 3847, 5384, 6153, 6154, 6155, 9228, 9229, 9230, 9231, 12304],
    first_mat=12,
    small_mats=8,
    total=12305,
)
BLOCKS = (ENC, DEC)


def sizes(block, n):
    shard = block.total * D // n
    rows = -(-shard // 1024) * 8
    top = (shard + LANES - 1) // LANES
    return shard, rows, (top + UROWS) // UROWS + 1, (top + BIG) // BIG + 1


def small_row(block, m):
    row = m * D
    for at, gap in block.gaps:
        row = row + jnp.where(m >= at, gap, 0) if at > 0 else row + gap
    return row


def mat_of(block, m):
    return block.first_mat + m + jnp.where(m >= block.small_mats, 4, 0)


def static_unit_rows(block):
    out = []
    for m in range(block.small):
        row = m * D + sum(gap for at, gap in block.gaps if m >= at)
        out.append((block.first_mat + m + (4 if m >= block.small_mats else 0), row))
    return out


def whoami():
    wide, narrow = lax.axis_index("wide"), lax.axis_index("narrow")
    return wide, narrow, wide // 2, wide % 2, narrow // 2, narrow % 2


def device(z, x, y, c):
    return (z * 2 + x, y * 2 + c)


def flat_device(d):
    return (d // 4, d % 4)


def entry_barrier(me, n):
    bar = pltpu.get_barrier_semaphore()

    def signal(i, carry):
        pl.semaphore_signal(bar, inc=1, device_id=flat_device((me + i) % n), device_id_type=MESH)
        return carry

    lax.fori_loop(1, n, signal, 0)
    pl.semaphore_wait(bar, n - 1)


def each_small(block, n, me, slots, body):
    shard = sizes(block, n)[0]
    low = me * shard
    low_row = low // LANES
    first = 0
    for _, row in static_unit_rows(block):
        first = first + jnp.minimum(jnp.maximum(low - row * D, 0) // (UROWS * LANES), 16)

    def step(j, carry):
        g = first + j
        m, u = g // 16, g % 16
        start = small_row(block, m) * 6 + u * UROWS
        pos = start - low_row

        @pl.when((g < 16 * block.small) & (start * LANES < low + shard))
        def _():
            body((pos + UROWS) // UROWS, mat_of(block, m), u, pos, start * LANES)

        return carry

    lax.fori_loop(0, slots, step, 0)


def each_big(block, n, me, slots, body):
    shard = sizes(block, n)[0]
    low = me * shard
    low_row = low // LANES
    first = jnp.minimum(jnp.maximum(low - block.fc1 * D, 0) // (BIG * LANES), 16)

    def step(j, carry):
        u = first + j
        start = block.fc1 * 6 + u * BIG
        pos = start - low_row

        @pl.when((u < 16) & (start * LANES < low + shard) & (start * LANES + BIG * LANES > low))
        def _():
            body((pos + BIG) // BIG, u, pos, start * LANES)

        return carry

    lax.fori_loop(0, slots, step, 0)


def each_vector(block, n, me, first_vec, body):
    shard = sizes(block, n)[0]
    low = me * shard
    low_row = low // LANES
    for i, row in enumerate(block.vectors):
        @pl.when((row * D < low + shard) & (row * D + D > low))
        def _(i=i, row=row):
            body(first_vec + i, row * 6 - low_row, row * D)


ORDERS = [("z", "x", "y"), ("z", "y", "x")]


def view(pair, order, done, at):
    have = set(order[:done])
    return (pair,) + tuple(slice(None) if a in have else at[a] for a in "zxy")


def peers(axis, at):
    if axis == "z":
        return [dict(at, z=(at["z"] + k) % 4) for k in (1, 2, 3)]
    return [dict(at, **{axis: 1 - at[axis]})]


def dev(at):
    return device(at["z"], at["x"], at["y"], at["c"])


def gather_kernel(
    n, on_start, on_vectors, on_pair, xe_ref, xd_ref, w_ref, v_ref,
    re_ref, rd_ref, se_ref, sd_ref, be_ref, bd_ref, sv_ref, land, landv, own, ownv,
    s_small, s_big, s_vec, r_unit, r_vec, s_zxy, r_zxy, s_core, r_core, s_own, v_send, v_recv,
):
    wide, narrow, z, x, y, c = whoami()
    me = wide * 4 + narrow
    chip = me // 2
    at = dict(z=z, x=x, y=y, c=c)
    entry_barrier(me, n)
    on_start()

    lanes = lax.broadcasted_iota(jnp.int32, (1, LANES), 1)
    for b, (block, x_ref, r_ref, s_ref, b_ref) in enumerate(
        ((ENC, xe_ref, re_ref, se_ref, be_ref), (DEC, xd_ref, rd_ref, sd_ref, bd_ref))
    ):
        shard, rows, n_small, n_big = sizes(block, n)
        shift = (me * shard) % LANES
        step = 8 * max(k for k in range(1, 40) if (rows // 8) % k == 0)

        def turn(i, carry, x_ref=x_ref, r_ref=r_ref, step=step, shift=shift):
            at_row = pl.multiple_of(i * step, 8)
            r_ref[pl.ds(FRONT + at_row, step), :] = pltpu.roll(x_ref[pl.ds(at_row, step), :], shift, 1)
            return carry

        lax.fori_loop(0, rows // step, turn, 0)
        keep = lanes >= shift

        def load(row, count, stride, r_ref=r_ref, keep=keep):
            here = r_ref[pl.ds(FRONT + row, count, stride=stride), :]
            before = r_ref[pl.ds(FRONT + row - 1, count, stride=stride), :]
            return jnp.where(keep, here, before)

        small0 = 0 if b == 0 else sizes(ENC, n)[2]
        big0 = 0 if b == 0 else sizes(ENC, n)[3]

        def small_body(slot, mat, u, pos, start, s_ref=s_ref, load=load, shard=shard, small0=small0):
            for k in range(6):
                s_ref[slot, :, k * LANES : (k + 1) * LANES] = load(pos + k, UNIT, 6).astype(BF)
            which = jnp.where(start // shard == me, 0, 1)
            target = u * 2 + mat % 2
            sem = s_small.at[small0 + slot]

            @pl.when(target == me)
            def _():
                pltpu.make_async_copy(s_ref.at[slot], land.at[which, mat // 2], sem).start()

            @pl.when(target != me)
            def _():
                pltpu.make_async_remote_copy(
                    s_ref.at[slot], land.at[which, mat // 2], sem, r_unit.at[which, mat // 2],
                    device_id=flat_device(target), device_id_type=MESH,
                ).start()

        def big_body(slot, u, pos, start, b_ref=b_ref, load=load, shard=shard, block=block, big0=big0):
            for q in range(4):
                for k in range(6):
                    b_ref[slot, q % 2, q // 2, :, k * LANES : (k + 1) * LANES] = load(
                        pos + 6 * q + k, UNIT, 24
                    ).astype(BF)
            which = jnp.where(start // shard == me, 0, 1)
            pair = (block.first_mat + block.small_mats) // 2
            for core in range(2):
                target = u * 2 + core
                sem = s_big.at[big0 + slot, core]
                @pl.when(target == me)
                def _(core=core, sem=sem):
                    pltpu.make_async_copy(b_ref.at[slot, core], land.at[which, pl.ds(pair, 2)], sem).start()

                @pl.when(target != me)
                def _(core=core, sem=sem, target=target):
                    pltpu.make_async_remote_copy(
                        b_ref.at[slot, core], land.at[which, pl.ds(pair, 2)], sem, r_unit.at[which, pair],
                        device_id=flat_device(target), device_id_type=MESH,
                    ).start()

        def vec_body(v, pos, start, r_ref=r_ref, keep=keep, shard=shard):
            here = r_ref[pl.ds(FRONT + pos, 8), :]
            before = r_ref[pl.ds(FRONT + pos - 1, 8), :]
            sv_ref[v] = jnp.where(keep, here, before).astype(BF).astype(F32)
            which = jnp.where(start // shard == me, 0, 1)

            @pl.when(me == v)
            def _():
                pltpu.make_async_copy(sv_ref.at[v], landv.at[which], s_vec.at[v]).start()

            @pl.when(me != v)
            def _():
                pltpu.make_async_remote_copy(
                    sv_ref.at[v], landv.at[which], s_vec.at[v], r_vec.at[which],
                    device_id=flat_device(v), device_id_type=MESH,
                ).start()

        each_vector(block, n, me, 0 if b == 0 else len(ENC.vectors), vec_body)
        each_small(block, n, me, n_small, small_body)
        each_big(block, n, me, n_big, big_body)

    def of_self(first, last, which):
        return jnp.where(which == 0, first, last) == me

    def arrive_unit(first, last, src, dst, local_sem, recv):
        for which, holder in ((0, first), (1, last)):
            needed = True if which == 0 else (first != last)

            @pl.when(needed & (holder == me))
            def _(which=which):
                pltpu.make_async_copy(src(which), dst(which), local_sem).wait()

            @pl.when(needed & (holder != me))
            def _(which=which):
                pltpu.make_async_copy(src(which), dst(which), recv(which)).wait()

    def vec_of(v):
        n_enc = len(ENC.vectors)
        rows = ENC.vectors + DEC.vectors
        start = 0
        before = 0
        for i, row in enumerate(rows):
            start = start + jnp.where(v >= i, row - before, 0)
            before = row
        return start * D, jnp.where(v < n_enc, sizes(ENC, n)[0], sizes(DEC, n)[0])

    @pl.when(me < N_VEC)
    def _():
        start, shard = vec_of(me)
        first, last = start // shard, (start + D - 1) // shard
        arrive_unit(
            first, last, lambda w: sv_ref.at[0], lambda w: landv.at[w], s_vec.at[me], lambda w: r_vec.at[w]
        )
        at_elem = lax.broadcasted_iota(jnp.int32, (8, LANES), 0) * LANES + lax.broadcasted_iota(jnp.int32, (8, LANES), 1)
        ownv[...] = jnp.where(at_elem < (first + 1) * shard - start, landv[0], landv[1])

    @pl.when(me >= N_VEC)
    def _():
        ownv[...] = jnp.zeros_like(ownv)

    pltpu.sync_copy(ownv, v_ref.at[z, x, y, c])
    vorder = ("z", "x", "y", "c")

    def vview(done):
        have = set(vorder[:done])
        return tuple(slice(None) if a in have else at[a] for a in "zxyc")

    def vcopies(phase):
        axis = vorder[phase]
        out = []
        for k, p in enumerate(peers(axis, at)):
            ref = v_ref.at[vview(phase)]
            slot = phase if axis == "z" else phase + 2
            out.append(
                pltpu.make_async_remote_copy(
                    ref, ref, v_send.at[slot + k], v_recv.at[slot + k], device_id=dev(p), device_id_type=MESH
                )
            )
        return out

    row_i = lax.broadcasted_iota(jnp.int32, (UNIT, D), 0)
    col_i = lax.broadcasted_iota(jnp.int32, (UNIT, D), 1)

    def merge(pair):
        block = ENC if pair < 6 else DEC
        shard = sizes(block, n)[0]
        local = pair - block.first_mat // 2
        half = block.small_mats // 2
        if half <= local < half + 2:
            start = (block.fc1 * 6 + chip * BIG) * LANES
            elem = row_i * FF + (2 * (local - half) + c) * D + col_i
            length = BIG * LANES
        else:
            small = 2 * local - (4 if local >= half + 2 else 0) + c
            start = (small_row(block, small) * 6 + chip * UROWS) * LANES
            elem = row_i * D + col_i
            length = UROWS * LANES
        first, last = start // shard, (start + length - 1) // shard
        if half <= local < half + 2:
            if local == half:
                low_row = me * shard // LANES
                slot = (start // LANES - low_row + BIG) // BIG + (0 if block is ENC else sizes(ENC, n)[3])
                slot = jnp.minimum(jnp.maximum(slot, 0), sizes(ENC, n)[3] + sizes(DEC, n)[3] - 1)
                arrive_unit(
                    first, last, lambda w: land.at[w, pl.ds(pair, 2)], lambda w: land.at[w, pl.ds(pair, 2)],
                    s_big.at[slot, c], lambda w: r_unit.at[w, pair],
                )
        else:
            low_row = me * shard // LANES
            slot = (start // LANES - low_row + UROWS) // UROWS + (0 if block is ENC else sizes(ENC, n)[2])
            slot = jnp.minimum(jnp.maximum(slot, 0), sizes(ENC, n)[2] + sizes(DEC, n)[2] - 1)
            arrive_unit(
                first, last, lambda w: land.at[w, pair], lambda w: land.at[w, pair],
                s_small.at[slot], lambda w: r_unit.at[w, pair],
            )
        own[pair] = jnp.where(elem < (first + 1) * shard - start, land[0, pair], land[1, pair])

    def wdst(pair, done, order):
        return w_ref.at[(pair, c) + view(pair, order, done, at)[1:]]

    def copies(pair, phase):
        order = ORDERS[pair % 2]
        out = []
        if phase == 3:
            ref = w_ref.at[pair, c]
            return [
                pltpu.make_async_remote_copy(
                    ref, ref, s_core.at[pair], r_core.at[pair], device_id=device(z, x, y, 1 - c), device_id_type=MESH
                )
            ]
        axis = order[phase]
        slot = phase if axis == "z" else phase + 2
        for k, p in enumerate(peers(axis, at)):
            ref = wdst(pair, phase, order)
            src = own.at[pair] if phase == 0 else ref
            out.append(
                pltpu.make_async_remote_copy(
                    src, ref, s_zxy.at[pair, slot + k], r_zxy.at[pair, slot + k], device_id=dev(p), device_id_type=MESH
                )
            )
        return out

    lag = 2
    for t in range(N_PAIR + 4 * lag):
        if t < N_PAIR:
            merge(t)
            pltpu.make_async_copy(own.at[t], wdst(t, 0, ORDERS[t % 2]), s_own.at[t]).start()
            for cp in copies(t, 0):
                cp.start()
        for phase in (1, 2, 3):
            pair = t - phase * lag
            if 0 <= pair < N_PAIR:
                if phase == 1:
                    pltpu.make_async_copy(own.at[pair], wdst(pair, 0, ORDERS[pair % 2]), s_own.at[pair]).wait()
                for cp in copies(pair, phase - 1):
                    cp.wait_recv()
                for cp in copies(pair, phase):
                    cp.start()
        if t % 2 == 0 and t < 10:
            phase = t // 2
            if phase > 0:
                for cp in vcopies(phase - 1):
                    cp.wait_recv()
            if phase < 4:
                for cp in vcopies(phase):
                    cp.start()
            else:
                on_vectors()
        pair = t - 4 * lag
        if 0 <= pair < N_PAIR:
            for cp in copies(pair, 3):
                cp.wait_recv()
            on_pair(pair)

    for phase in range(4):
        for cp in vcopies(phase):
            cp.wait_send()
    for pair in range(N_PAIR):
        for phase in range(4):
            for cp in copies(pair, phase):
                cp.wait_send()
    for b, (block, s_ref, b_ref) in enumerate(((ENC, se_ref, be_ref), (DEC, sd_ref, bd_ref))):
        shard, rows, n_small, n_big = sizes(block, n)
        small0 = 0 if b == 0 else sizes(ENC, n)[2]
        big0 = 0 if b == 0 else sizes(ENC, n)[3]

        def small_wait(slot, mat, u, pos, start, s_ref=s_ref, small0=small0):
            @pl.when(u * 2 + mat % 2 != me)
            def _():
                pltpu.make_async_copy(s_ref.at[slot], s_ref.at[slot], s_small.at[small0 + slot]).wait()

        def big_wait(slot, u, pos, start, b_ref=b_ref, big0=big0):
            for core in range(2):
                @pl.when(u * 2 + core != me)
                def _(core=core):
                    pltpu.make_async_copy(
                        b_ref.at[slot, core], b_ref.at[slot, core], s_big.at[big0 + slot, core]
                    ).wait()

        def vec_wait(v, pos, start):
            @pl.when(me != v)
            def _():
                pltpu.make_async_copy(sv_ref.at[v], sv_ref.at[v], s_vec.at[v]).wait()

        each_vector(block, n, me, 0 if b == 0 else len(ENC.vectors), vec_wait)
        each_small(block, n, me, n_small, small_wait)
        each_big(block, n, me, n_big, big_wait)


def rows_of(flat, rows):
    return jnp.pad(flat, (0, rows * LANES - flat.shape[0])).reshape(rows, LANES)


SCALE = HEAD_DIM ** (-0.5)
FORBID = -1000000000.0
ROOT_HALF = 0.7071067811865476
PDF = 0.3989422804014327


def mm(a, b):
    return jnp.dot(a, b, preferred_element_type=F32)


def mm_nt(a, b):
    return lax.dot_general(a, b, (((1,), (1,)), ((), ())), preferred_element_type=F32)


def mm_tn(a, b):
    return lax.dot_general(a, b, (((0,), (0,)), ((), ())), preferred_element_type=F32)


def col_blocks(body, width=256):
    def step(j, carry):
        body(pl.ds(pl.multiple_of(j * width, width), width))
        return carry

    lax.fori_loop(0, D // width, step, 0)


def row_blocks(rows, body, height=64):
    def step(i, carry):
        body(pl.ds(pl.multiple_of(i * height, height), height))
        return carry

    lax.fori_loop(0, rows // height, step, 0)


def linear(x_ref, w_ref, rows, out_ref, bias=None):
    x = x_ref[0:rows, :]

    def body(cols):
        y = mm(x, w_ref[:, cols])
        if bias is not None:
            y = y + bias[:, cols]
        out_ref[0:rows, cols] = y.astype(out_ref.dtype)

    col_blocks(body)


def norm_rows(x):
    centred = x - jnp.mean(x, axis=1, keepdims=True)
    spread = jnp.mean(centred * centred, axis=1, keepdims=True)
    root = lax.rsqrt(spread + 1e-05)
    return centred * root, root


def norm_forward_ref(x_ref, gain, shift, rows, out_ref):
    def body(r):
        hat, _ = norm_rows(x_ref[r, :].astype(F32))
        out_ref[r, :] = (hat * gain[...] + shift[...]).astype(BF)

    row_blocks(rows, body)


def half_mask(s):
    lane = lax.broadcasted_iota(jnp.int32, (1, LANES), 1)
    return (lane < HEAD_DIM) if s == 0 else (lane >= HEAD_DIM)


def only(x, s):
    return jnp.where(half_mask(s), x, jnp.zeros_like(x))


def attend_blocks(rows, keys, causal):
    out = []
    for start in range(0, rows, 128):
        height = min(128, rows - start)
        out.append((start, height, min(-(-(start + height) // 128) * 128, 512) if causal else keys))
    return out


def attention_forward_ref(q_ref, k_ref, v_ref, mask_ref, rows, keys, mixed_ref, lse_ref):
    lse_lane = lax.broadcasted_iota(jnp.int32, (1, LANES), 1)

    def pair_of_heads(i, carry):
        cols = pl.ds(pl.multiple_of(i * LANES, LANES), LANES)
        for start, height, reach in attend_blocks(rows, keys, mask_ref is not None):
            r = slice(start, start + height)
            q = q_ref[r, cols]
            k = k_ref[0:reach, cols]
            v = v_ref[0:reach, cols]
            mixed = jnp.zeros((height, LANES), F32)
            lses = lse_ref[r, :]
            for s in range(2):
                scores = mm_nt(only(q, s), k) * SCALE
                if mask_ref is not None:
                    scores = jnp.where(mask_ref[r, 0:reach] > 0, scores, FORBID)
                peak = jnp.max(scores, axis=1, keepdims=True)
                weights = jnp.exp(scores - peak)
                totals = jnp.sum(weights, axis=1, keepdims=True)
                probs = (weights * (1.0 / totals)).astype(BF)
                mixed = mixed + mm(probs, only(v, s))
                lses = jnp.where(lse_lane == 2 * i + s, peak + jnp.log(totals), lses)
            mixed_ref[r, cols] = mixed.astype(BF)
            lse_ref[r, :] = lses
        return carry

    lax.fori_loop(0, D // LANES, pair_of_heads, 0)


def project_add(x_ref, mixed_ref, w_ref, bias, rows, out_ref):
    m = mixed_ref[0:rows, :]

    def body(cols):
        out_ref[0:rows, cols] = x_ref[0:rows, cols].astype(F32) + mm(m, w_ref[:, cols]) + bias[:, cols]

    col_blocks(body)


def gelu_block(n_ref, w_ref, bias, rows, block, act_ref, slope_ref):
    x = n_ref[0:rows, :]

    def body(cols):
        pre = mm(x, w_ref[:, cols]) + bias[:, cols]
        bell = 0.5 * (1.0 + lax.erf(pre * ROOT_HALF))
        act_ref[block, 0:rows, cols] = (pre * bell).astype(BF)
        slope_ref[block, 0:rows, cols] = (bell + pre * (PDF * jnp.exp(-0.5 * pre * pre))).astype(BF)

    col_blocks(body, 128)


def accumulate(a, w_ref, rows, out_ref, bias=None):
    def body(cols):
        y = out_ref[0:rows, cols] + mm(a, w_ref[:, cols])
        out_ref[0:rows, cols] = y if bias is None else y + bias[:, cols]

    col_blocks(body)


N_SAVED = 29


def saved_shapes(rows, frames):
    tall = -(-rows // 128) * 128
    low = [(frames, D)] * 5
    return (
        [(a, BF) for a in low]
        + [((frames, LANES), F32), ((frames, D), F32), ((frames, D), BF), ((4, frames, D), BF), ((4, frames, D), BF), ((frames, D), BF)]
        + [((rows, D), BF)] * 2
        + [((tall, D), BF)] * 2
        + [((rows, D), BF), ((rows, LANES), F32), ((rows, D), F32), ((rows, D), BF)]
        + [((rows, D), BF), ((frames, D), BF), ((frames, D), BF), ((rows, D), BF), ((rows, LANES), F32)]
        + [((rows, D), F32), ((rows, D), BF), ((4, rows, D), BF), ((4, rows, D), BF), ((rows, D), BF)]
    )


def make_mask(seg_row, seg_col, mask_ref, rows):
    def body(r):
        col = lax.broadcasted_iota(jnp.int32, (64, mask_ref.shape[1]), 1)
        row = lax.broadcasted_iota(jnp.int32, (64, mask_ref.shape[1]), 0) + r.start
        allowed = (seg_col[r, :] == seg_row[...]) & (col <= row)
        mask_ref[r, :] = jnp.where(allowed, 1.0, 0.0)

    row_blocks(rows, body)


def forward_kernel(n, rows, frames, *refs):
    xe_ref, xd_ref, ein_ref, din_ref, seg_row, seg_col, w_ref, v_ref = refs[:8]
    outs, refs = refs[8 : 8 + N_SAVED], refs[8 + N_SAVED :]
    comm, refs = refs[:24], refs[24:]
    bufs, refs = refs[:N_SAVED], refs[N_SAVED:]
    vv, wbuf, acc, mask_ref, s_save, s_w = refs
    (
        e_n1, e_q, e_k, e_v, e_mix, e_lse, e_after, e_n2, e_act, e_slope, e_out,
        d_n1, d_q, d_k, d_v, d_mix, d_lse, d_after, d_n2,
        c_q, c_k, c_v, c_mix, c_lse, d_after2, d_n3, d_act, d_slope, d_out,
    ) = bufs
    eacc = acc.at[0:frames]

    def vec(i):
        return vv.at[i : i + 1]

    def save(*indices):
        for i in indices:
            pltpu.make_async_copy(bufs[i], outs[i], s_save.at[i]).start()

    def on_start():
        make_mask(seg_row, seg_col, mask_ref, rows)
        for ref in (d_k, d_v):
            if ref.shape[0] > rows:
                ref[rows:, :] = jnp.zeros((ref.shape[0] - rows, D), BF)
        for ref in (e_lse, d_lse, c_lse):
            ref[...] = jnp.zeros_like(ref)

    def on_vectors():
        pltpu.sync_copy(v_ref, vv_tiles)
        for i in range(N_VEC):
            for k in range(6):
                vv[i : i + 1, k * LANES : (k + 1) * LANES] = vv_tiles[i // 8, i // 4 % 2, i // 2 % 2, i % 2, k : k + 1, :]

    def on_pair(pair):
        cps = [pltpu.make_async_copy(w_ref.at[pair, k].reshape(D, D), wbuf.at[k], s_w.at[k]) for k in range(2)]
        for cp in cps:
            cp.start()
        if pair == 0:
            norm_forward_ref(ein_ref, vec(0), vec(1), frames, e_n1)
        if pair == 6:
            norm_forward_ref(din_ref, vec(12), vec(13), rows, d_n1)
        for cp in cps:
            cp.wait()
        w0, w1 = wbuf.at[0], wbuf.at[1]
        if pair == 0:
            linear(e_n1, w0, frames, e_q, vec(2))
            linear(e_n1, w1, frames, e_k)
            save(0, 1, 2)
        elif pair == 1:
            linear(e_n1, w0, frames, e_v, vec(3))
            attention_forward_ref(e_q, e_k, e_v, None, frames, frames, e_mix, e_lse)
            project_add(ein_ref, e_mix, w1, vec(4), frames, e_after)
            norm_forward_ref(e_after, vec(5), vec(6), frames, e_n2)
            save(3, 4, 5, 6, 7)
        elif pair in (2, 3):
            for k in range(2):
                block = 2 * (pair - 2) + k
                gelu_block(e_n2, wbuf.at[k], vec(7 + block), frames, block, e_act, e_slope)
            if pair == 3:
                save(8, 9)
        elif pair in (4, 5):
            if pair == 4:
                eacc[...] = e_after[...]
            for k in range(2):
                last = pair == 5 and k == 1
                accumulate(e_act[2 * (pair - 4) + k], wbuf.at[k], frames, eacc, vec(11) if last else None)
            if pair == 5:
                e_out[...] = eacc[...].astype(BF)
                save(10)
        elif pair == 6:
            linear(d_n1, w0, rows, d_q, vec(14))
            linear(d_n1, w1, rows, d_k)
            save(11, 12, 13)
        elif pair == 7:
            linear(d_n1, w0, rows, d_v, vec(15))
            attention_forward_ref(d_q, d_k, d_v, mask_ref, rows, rows, d_mix, d_lse)
            project_add(din_ref, d_mix, w1, vec(16), rows, d_after)
            norm_forward_ref(d_after, vec(17), vec(18), rows, d_n2)
            save(14, 15, 16, 17, 18)
        elif pair == 8:
            linear(d_n2, w0, rows, c_q, vec(19))
            linear(e_out, w1, frames, c_k)
            save(19, 20)
        elif pair == 9:
            linear(e_out, w0, frames, c_v, vec(20))
            attention_forward_ref(c_q, c_k, c_v, None, rows, frames, c_mix, c_lse)
            project_add(d_after, c_mix, w1, vec(21), rows, d_after2)
            norm_forward_ref(d_after2, vec(22), vec(23), rows, d_n3)
            save(21, 22, 23, 24, 25)
        elif pair in (10, 11):
            for k in range(2):
                block = 2 * (pair - 10) + k
                gelu_block(d_n3, wbuf.at[k], vec(24 + block), rows, block, d_act, d_slope)
            if pair == 11:
                save(26, 27)
        else:
            if pair == 12:
                acc[...] = d_after2[...]
            for k in range(2):
                last = pair == 13 and k == 1
                accumulate(d_act[2 * (pair - 12) + k], wbuf.at[k], rows, acc, vec(28) if last else None)
            if pair == 13:
                d_out[...] = acc[...].astype(BF)
                save(28)

    vv_tiles = comm[-1]
    gather_kernel(n, on_start, on_vectors, on_pair, xe_ref, xd_ref, w_ref, v_ref, *comm[:-1])
    for i in range(N_SAVED):
        pltpu.make_async_copy(bufs[i], outs[i], s_save.at[i]).wait()


def forward_pass(encoder_master, decoder_master, encoder_input, decoder_input, segments, n):
    (_, re, ne, ge), (_, rd, nd, gd) = sizes(ENC, n), sizes(DEC, n)
    frames, rows = encoder_input.shape[0], decoder_input.shape[0]
    tall = -(-rows // 128) * 128
    dma = pltpu.SemaphoreType.DMA
    saved = saved_shapes(rows, frames)
    vmem, hbm = pl.BlockSpec(memory_space=pltpu.VMEM), pl.BlockSpec(memory_space=pl.ANY)
    seg_row = jnp.pad(segments[None, :], ((0, 0), (0, tall - rows)), constant_values=-1)
    return pl.pallas_call(
        partial(forward_kernel, n, rows, frames),
        out_shape=(
            jax.ShapeDtypeStruct((N_PAIR, 2, 4, 2, 2, UNIT, D), BF),
            jax.ShapeDtypeStruct((4, 2, 2, 2, 8, LANES), F32),
            *(jax.ShapeDtypeStruct(shape, dtype) for shape, dtype in saved),
        ),
        in_specs=[vmem] * 6,
        out_specs=(hbm,) * (2 + N_SAVED),
        scratch_shapes=[
            pltpu.VMEM((FRONT + re + BACK, LANES), F32),
            pltpu.VMEM((FRONT + rd + BACK, LANES), F32),
            pltpu.VMEM((ne, UNIT, D), BF),
            pltpu.VMEM((nd, UNIT, D), BF),
            pltpu.VMEM((ge, 2, 2, UNIT, D), BF),
            pltpu.VMEM((gd, 2, 2, UNIT, D), BF),
            pltpu.VMEM((N_VEC, 8, LANES), F32),
            pltpu.VMEM((2, N_PAIR, UNIT, D), BF),
            pltpu.VMEM((2, 8, LANES), F32),
            pltpu.VMEM((N_PAIR, UNIT, D), BF),
            pltpu.VMEM((8, LANES), F32),
            dma((ne + nd,)),
            dma((ge + gd, 2)),
            dma((N_VEC,)),
            dma((2, N_PAIR)),
            dma((2,)),
            dma((N_PAIR, 5)),
            dma((N_PAIR, 5)),
            dma((N_PAIR,)),
            dma((N_PAIR,)),
            dma((N_PAIR,)),
            dma((6,)),
            dma((6,)),
            pltpu.VMEM((4, 2, 2, 2, 8, LANES), F32),
            *(pltpu.VMEM(shape, dtype) for shape, dtype in saved),
            pltpu.VMEM((32, D), F32),
            pltpu.VMEM((2, D, D), BF),
            pltpu.VMEM((rows, D), F32),
            pltpu.VMEM((rows, tall), F32),
            dma((N_SAVED,)),
            dma((2,)),
        ],
        compiler_params=pltpu.CompilerParams(collective_id=0, has_side_effects=True, vmem_limit_bytes=58 << 20),
        name="forward",
    )(rows_of(encoder_master, re), rows_of(decoder_master, rd), encoder_input, decoder_input, seg_row, segments[:, None])


RING = 3
RING_C = 5


def scatter_kernel(
    n, produce, after, vg_ref, gbuf, oe_ref, od_ref, norm_ref,
    land_c, land_b, land_a, land_z, ownb, vown, vl_c, vl_y, vl_x, vl_z,
    ge_ref, gd_ref, fe, fd, fbe, fbd, fv, nsend, nland,
    s_core, r_core, s_free, s_ph, r_ph, s_back, r_small, r_big, sv, rv, s_vback, r_vback, s_n, r_n, s_out,
):
    wide, narrow, z, x, y, c = whoami()
    me = wide * 4 + narrow
    chip = me // 2
    at = dict(z=z, x=x, y=y, c=c)
    entry_barrier(me, n)
    sib = device(z, x, y, 1 - c)
    lag = 2

    def slot_c(pair):
        return (N_PAIR - 1 - pair) % RING_C

    def core_copy(pair):
        return pltpu.make_async_remote_copy(
            gbuf.at[(N_PAIR - 1 - pair) % RING, 1 - c], land_c.at[slot_c(pair)], s_core.at[pair], r_core.at[pair], device_id=sib, device_id_type=MESH
        )

    def phase_copies(pair, phase):
        order = ORDERS[pair % 2]
        if phase == 1:
            axis = order[2]
            if axis == "y":
                src = land_c.at[slot_c(pair), :, :, 1 - y]
            else:
                src = land_c.at[slot_c(pair), :, 1 - x]
            return [(src, land_b.at[pair], 0, peers(axis, at)[0])]
        if phase == 2:
            axis = order[1]
            other = 1 - at[axis]
            return [(land_b.at[pair, :, other], land_a.at[pair], 1, peers(axis, at)[0])]
        return [
            (land_a.at[pair, (z + k) % 4], land_z.at[pair, k - 1], 1 + k, dict(at, z=(z + k) % 4)) for k in (1, 2, 3)
        ]

    def phase_dmas(pair, phase):
        return [
            pltpu.make_async_remote_copy(
                src, dst, s_ph.at[pair, k], r_ph.at[pair, k], device_id=dev(p), device_id_type=MESH
            )
            for src, dst, k, p in phase_copies(pair, phase)
        ]

    def back(pair):
        block = ENC if pair < 6 else DEC
        shard = sizes(block, n)[0]
        local = pair - block.first_mat // 2
        half = block.small_mats // 2
        big = half <= local < half + 2
        if big:
            start = (block.fc1 * 6 + chip * BIG) * LANES
            length = BIG * LANES
        else:
            small = 2 * local - (4 if local >= half + 2 else 0) + c
            start = (small_row(block, small) * 6 + chip * UROWS) * LANES
            length = UROWS * LANES
        first, last = start // shard, (start + length - 1) // shard
        out = []
        for which, target in ((0, first), (1, last)):
            low_row = target * shard // LANES
            if big:
                slot = (start // LANES - low_row + BIG) // BIG
                q = 2 * (local - half) + c
                dst = (fbe if block is ENC else fbd).at[slot, q]
                recv = r_big.at[0 if block is ENC else 1, slot, q]
            else:
                slot = (start // LANES - low_row + UROWS) // UROWS
                dst = (fe if block is ENC else fd).at[slot]
                recv = r_small.at[0 if block is ENC else 1, slot]
            needed = True if which == 0 else first != last
            out.append((needed, target, dst, s_back.at[pair, which], recv))
        return out

    def start_back(pair):
        for needed, target, dst, send, recv in back(pair):
            @pl.when(needed & (target == me))
            def _(dst=dst, recv=recv):
                pltpu.make_async_copy(ownb.at[pair], dst, recv).start()

            @pl.when(needed & (target != me))
            def _(dst=dst, recv=recv, send=send, target=target):
                pltpu.make_async_remote_copy(
                    ownb.at[pair], dst, send, recv, device_id=flat_device(target), device_id_type=MESH
                ).start()

    def end_back(pair):
        for needed, target, dst, send, recv in back(pair):
            @pl.when(needed & (target != me))
            def _(send=send):
                pltpu.make_async_copy(ownb.at[pair], ownb.at[pair], send).wait()

    def add_core(pair):
        def body(i, carry):
            a, b = i // 2, i % 2
            for k in range(2):
                mine = gbuf[(N_PAIR - 1 - pair) % RING, c, a, b, k]
                land_c[slot_c(pair), a, b, k] = (
                    land_c[slot_c(pair), a, b, k].astype(F32) + mine.astype(F32)
                ).astype(BF)
            return carry

        lax.fori_loop(0, 8, body, 0)

    def add_b(pair):
        axis = ORDERS[pair % 2][2]

        def body(i, carry):
            a, b = i // 2, i % 2
            mine = land_c[slot_c(pair), a, b, y] if axis == "y" else land_c[slot_c(pair), a, x, b]
            land_b[pair, a, b] = (land_b[pair, a, b].astype(F32) + mine.astype(F32)).astype(BF)
            return carry

        lax.fori_loop(0, 8, body, 0)

    def add_a(pair):
        own = at[ORDERS[pair % 2][1]]
        for a in range(4):
            land_a[pair, a] = (land_a[pair, a].astype(F32) + land_b[pair, a, own].astype(F32)).astype(BF)

    def add_z(pair):
        total = land_a[pair, z].astype(F32)
        for k in range(3):
            total = total + land_z[pair, k].astype(F32)
        ownb[pair] = total.astype(BF)
        squares = total * total
        return jnp.sum(squares.reshape(UNIT // 8, 8, D), axis=0)

    vland = dict(c=vl_c, y=vl_y, x=vl_x, z=vl_z)

    def vsteps(phase):
        if phase == 0:
            return [(vg_ref.at[:, :, :, 1 - c], vl_c, 0, dict(at, c=1 - c))]
        if phase == 1:
            return [(vl_c.at[:, :, 1 - y], vl_y, 1, dict(at, y=1 - y))]
        if phase == 2:
            return [(vl_y.at[:, 1 - x], vl_x, 2, dict(at, x=1 - x))]
        return [(vl_x.at[(z + k) % 4], vl_z.at[k - 1], 2 + k, dict(at, z=(z + k) % 4)) for k in (1, 2, 3)]

    def vdmas(phase):
        return [
            pltpu.make_async_remote_copy(s, d, sv.at[k], rv.at[k], device_id=dev(p), device_id_type=MESH)
            for s, d, k, p in vsteps(phase)
        ]

    def vadd(phase):
        if phase == 0:
            vl_c[...] = vl_c[...] + vg_ref[:, :, :, c]
        elif phase == 1:
            vl_y[...] = vl_y[...] + vl_c[:, :, y]
        elif phase == 2:
            vl_x[...] = vl_x[...] + vl_y[:, x]
        else:
            vown[...] = vl_x[z] + vl_z[0] + vl_z[1] + vl_z[2]

    seq = list(range(N_PAIR - 1, -1, -1))
    square = jnp.zeros((8, D), F32)
    for t in range(N_PAIR + 4 * lag):
        if t < N_PAIR:
            if t >= RING:
                core_copy(seq[t - RING]).wait_send()
            produce(t, gbuf.at[t % RING])
            if t >= RING_C:
                pl.semaphore_wait(s_free, 1)
            core_copy(seq[t]).start()
        for phase in (4, 3, 2, 1):
            i = t - phase * lag
            if 0 <= i < N_PAIR:
                pair = seq[i]
                if phase == 1:
                    core_copy(pair).wait_recv()
                    add_core(pair)
                elif phase == 2:
                    for cp in phase_dmas(pair, 1):
                        cp.wait()
                    add_b(pair)
                    if i < N_PAIR - RING_C:
                        pl.semaphore_signal(s_free, inc=1, device_id=sib, device_id_type=MESH)
                elif phase == 3:
                    for cp in phase_dmas(pair, 2):
                        cp.wait_recv()
                    add_a(pair)
                else:
                    for cp in phase_dmas(pair, 3):
                        cp.wait_recv()
                    square = square + add_z(pair)
                    start_back(pair)
                if phase < 4:
                    for cp in phase_dmas(pair, phase):
                        cp.start()
        if t < N_PAIR:
            after(t)
        if t == N_PAIR - 1:
            for cp in vdmas(0):
                cp.start()
        elif t >= N_PAIR and (t - N_PAIR) % 2 == 1:
            phase = (t - N_PAIR) // 2
            for cp in vdmas(phase):
                cp.wait_recv()
            vadd(phase)
            if phase < 3:
                for cp in vdmas(phase + 1):
                    cp.start()

    vsq = vown[...] * vown[...]
    for k in range(6):
        vsq = vsq + square[:, k * LANES : (k + 1) * LANES]
    nsend[...] = vsq

    def norm_copy(i):
        return pltpu.make_async_remote_copy(
            nsend, nland.at[i], s_n.at[i], r_n.at[i], device_id=flat_device((me + i) % n), device_id_type=MESH
        )

    def norm_start(i, carry):
        norm_copy(i).start()
        return carry

    lax.fori_loop(1, n, norm_start, 0)

    def vector_targets(v_static):
        block = ENC if v_static < len(ENC.vectors) else DEC
        shard = sizes(block, n)[0]
        start = (ENC.vectors + DEC.vectors)[v_static] * D
        return start // shard, (start + D - 1) // shard

    for v in range(N_VEC):
        for which, target in enumerate(sorted(set(vector_targets(v)))):
            if target == v:
                @pl.when(me == v)
                def _(v=v):
                    pltpu.make_async_copy(vown, fv.at[v], r_vback.at[v]).start()
            else:
                @pl.when(me == v)
                def _(v=v, target=target, which=which):
                    pltpu.make_async_remote_copy(
                        vown, fv.at[v], s_vback.at[which], r_vback.at[v], device_id=(target // 4, target % 4), device_id_type=MESH
                    ).start()

    lanes = lax.broadcasted_iota(jnp.int32, (1, LANES), 1)
    for b, (block, g_out, o_ref, f_ref, fb_ref) in enumerate(
        ((ENC, ge_ref, oe_ref, fe, fbe), (DEC, gd_ref, od_ref, fd, fbd))
    ):
        shard, rows, n_small, n_big = sizes(block, n)
        shift = (me * shard) % LANES

        def small_body(slot, mat, u, pos, start, b=b, g_out=g_out, f_ref=f_ref):
            pltpu.make_async_copy(f_ref.at[slot], f_ref.at[slot], r_small.at[b, slot]).wait()
            for k in range(6):
                g_out[pl.ds(FRONT + pos + k, UNIT, stride=6), :] = f_ref[slot, :, k * LANES : (k + 1) * LANES].astype(F32)

        def big_body(slot, u, pos, start, b=b, g_out=g_out, fb_ref=fb_ref):
            for q in range(4):
                pltpu.make_async_copy(fb_ref.at[slot, q], fb_ref.at[slot, q], r_big.at[b, slot, q]).wait()
                for k in range(6):
                    g_out[pl.ds(FRONT + pos + 6 * q + k, UNIT, stride=24), :] = fb_ref[
                        slot, q, :, k * LANES : (k + 1) * LANES
                    ].astype(F32)

        def vec_body(v, pos, start, g_out=g_out):
            pltpu.make_async_copy(fv.at[v], fv.at[v], r_vback.at[v]).wait()
            g_out[pl.ds(FRONT + pos, 6), :] = fv[v, 0:6, :]

        each_small(block, n, me, n_small, small_body)
        each_big(block, n, me, n_big, big_body)
        each_vector(block, n, me, 0 if b == 0 else len(ENC.vectors), vec_body)

        step = 8 * max(k for k in range(1, 40) if (rows // 8) % k == 0)
        unturn = lax.rem(LANES - shift, LANES)

        def turn(i, carry, g_out=g_out, step=step, shift=shift, unturn=unturn):
            at_row = pl.multiple_of(i * step, 8)
            here = pltpu.roll(g_out[pl.ds(FRONT + at_row, step), :], unturn, 1)
            after = pltpu.roll(g_out[pl.ds(FRONT + at_row + 1, step), :], unturn, 1)
            g_out[pl.ds(FRONT + at_row, step), :] = jnp.where(lanes < LANES - shift, here, after)
            return carry

        lax.fori_loop(0, rows // step, turn, 0)
        pltpu.make_async_copy(g_out.at[pl.ds(FRONT, rows)], o_ref, s_out.at[b]).start()

    def norm_wait(i, total):
        norm_copy(i).wait()
        return total + nland[i]

    total = lax.fori_loop(1, n, norm_wait, nsend[...])
    norm_ref[...] = jnp.broadcast_to(jnp.sqrt(jnp.sum(total)), (8, LANES))

    for b, (g_out, o_ref) in enumerate(((ge_ref, oe_ref), (gd_ref, od_ref))):
        pltpu.make_async_copy(g_out.at[pl.ds(FRONT, o_ref.shape[0])], o_ref, s_out.at[b]).wait()
    for phase in range(4):
        for cp in vdmas(phase):
            cp.wait_send()
    for v in range(N_VEC):
        for which, target in enumerate(sorted(set(vector_targets(v)))):
            if target != v:
                @pl.when(me == v)
                def _(which=which):
                    pltpu.make_async_copy(vown, vown, s_vback.at[which]).wait()
    for pair in range(N_PAIR):
        if N_PAIR - 1 - pair >= N_PAIR - RING:
            core_copy(pair).wait_send()
        for phase in (2, 3):
            for cp in phase_dmas(pair, phase):
                cp.wait_send()
        end_back(pair)


def sum_rows(ref, rows, out_ref):
    def body(r):
        out_ref[...] += jnp.sum(ref[r, :].astype(F32), axis=0, keepdims=True)

    out_ref[...] = jnp.zeros_like(out_ref)
    row_blocks(rows, body)


def norm_backward_ref(x_ref, gain, dn_ref, rows, out_ref, gain_grad, shift_grad):
    gain_grad[...] = jnp.zeros_like(gain_grad)
    shift_grad[...] = jnp.zeros_like(shift_grad)

    def body(r):
        hat, root = norm_rows(x_ref[r, :].astype(F32))
        dn = dn_ref[r, :]
        gain_grad[...] += jnp.sum(dn * hat, axis=0, keepdims=True)
        shift_grad[...] += jnp.sum(dn, axis=0, keepdims=True)
        g = dn * gain[...]
        part = g - jnp.mean(g, axis=1, keepdims=True) - hat * jnp.mean(g * hat, axis=1, keepdims=True)
        out_ref[r, :] += root * part

    row_blocks(rows, body)


def round_rows(src_ref, rows, out_ref):
    def body(r):
        out_ref[r, :] = src_ref[r, :].astype(BF)

    row_blocks(rows, body)


def weight_grad(a_ref, b_ref, rows, g_ref):
    b = b_ref[0:rows, :]
    flat = g_ref.reshape(D, D)

    def body(cols):
        flat[cols, :] = mm_tn(a_ref[0:rows, cols], b).astype(BF)

    col_blocks(body)


def back_through(a_ref, w_ref, rows, out_ref, add):
    a = a_ref[0:rows, :]

    def body(cols):
        y = mm_nt(a, w_ref[cols, :])
        if add:
            y = y + out_ref[0:rows, cols]
        out_ref[0:rows, cols] = y.astype(out_ref.dtype)

    col_blocks(body)


def gelu_back(o_ref, w_ref, slope_ref, rows, out_ref, bias_grad):
    a = o_ref[0:rows, :]

    def body(cols):
        y = mm_nt(a, w_ref[cols, :]) * slope_ref[0:rows, cols].astype(F32)
        bias_grad[:, cols] = jnp.sum(y, axis=0, keepdims=True)
        out_ref[0:rows, cols] = y.astype(BF)

    col_blocks(body)


def attention_backward_ref(q_ref, k_ref, v_ref, dm_ref, lse_ref, mask_ref, rows, keys, dq_ref, dk_ref, dv_ref):
    lse_lane = lax.broadcasted_iota(jnp.int32, (1, LANES), 1)

    def pair_of_heads(i, carry):
        cols = pl.ds(pl.multiple_of(i * LANES, LANES), LANES)
        dk_ref[:, cols] = jnp.zeros((dk_ref.shape[0], LANES), F32)
        dv_ref[:, cols] = jnp.zeros((dv_ref.shape[0], LANES), F32)
        for start, height, reach in attend_blocks(rows, keys, mask_ref is not None):
            r = slice(start, start + height)
            q, dm = q_ref[r, cols], dm_ref[r, cols]
            k, v = k_ref[0:reach, cols], v_ref[0:reach, cols]
            lses = lse_ref[r, :]
            dq = jnp.zeros((height, LANES), F32)
            for s in range(2):
                qs, dms = only(q, s), only(dm, s)
                scores = mm_nt(qs, k) * SCALE
                if mask_ref is not None:
                    scores = jnp.where(mask_ref[r, 0:reach] > 0, scores, FORBID)
                lse = jnp.sum(jnp.where(lse_lane == 2 * i + s, lses, 0.0), axis=1, keepdims=True)
                probs = jnp.exp(scores - lse)
                dp = mm_nt(dms, v)
                weighted = probs * dp
                ds = weighted - probs * jnp.sum(weighted, axis=1, keepdims=True)
                raw = (ds * SCALE).astype(BF)
                dq = dq + mm(raw, only(k, s))
                dk_ref[0:reach, cols] += mm_tn(raw, qs)
                dv_ref[0:reach, cols] += mm_tn(probs.astype(BF), dms)
            dq_ref[r, cols] = dq
        return carry

    lax.fori_loop(0, D // LANES, pair_of_heads, 0)


def backward_kernel(n, rows, frames, *refs):
    w_ref, v_ref, seg_row, seg_col, ein, din, ecot, dcot = refs[:8]
    kept, refs = refs[8 : 8 + N_SAVED], refs[8 + N_SAVED :]
    oe_ref, od_ref, norm_ref, fgrad, tgrad = refs[:5]
    refs = refs[5:]
    comm, refs = refs[:34], refs[34:]
    (
        gbuf, vg, vgr, gains, wbuf, outg, eoutg, dn, pool, slope, act, nbuf, xbuf,
        dq, dk, dv, mask_ref, lse, orow, mem, mgrad, s_l, s_w, s_o,
    ) = refs

    def load(*pairs):
        cps = [pltpu.make_async_copy(src, dst, s_l.at[i]) for i, (src, dst) in enumerate(pairs)]
        for cp in cps:
            cp.start()
        return cps

    def wload(*mats):
        cps = [
            pltpu.make_async_copy(w_ref.at[m // 2, m % 2].reshape(D, D), wbuf.at[i], s_w.at[i])
            for i, m in enumerate(mats)
        ]
        for cp in cps:
            cp.start()
        return cps

    def wait(*groups):
        for group in groups:
            for cp in group:
                cp.wait()

    def vrow(i):
        return vgr.at[i : i + 1]

    def part(ref, count):
        return ref.at[0:count]

    def feed(step, g, count, first_mat, first_vec, act_i, slope_i, n_i):
        if step < 2:
            for j, k in enumerate((2, 3) if step == 0 else (0, 1)):
                wait(load((kept[act_i].at[k], part(act, count))))
                weight_grad(act, orow, count, g.at[j])
            return
        ks = (2, 3) if step == 2 else (0, 1)
        a = load((kept[n_i], part(nbuf, count))) if step == 2 else []
        wait(a, wload(first_mat + 4 + ks[0], first_mat + 4 + ks[1]))
        for j, k in enumerate(ks):
            wait(load((kept[slope_i].at[k], part(slope, count))))
            gelu_back(orow, wbuf.at[j], slope, count, pool.at[k], vrow(first_vec + k))
            weight_grad(nbuf, pool.at[k], count, g.at[j])

    def feed_after(step, count, first_mat):
        ks = (2, 3) if step == 2 else (0, 1)
        wait(wload(first_mat + ks[0], first_mat + ks[1]))
        for j, k in enumerate(ks):
            back_through(pool.at[k], wbuf.at[j], count, dn, not (step == 2 and j == 0))

    def attend(g, count, keys, out_ref, wo, mix_i, q_i, k_i, v_i, lse_i, masked, bo, bq, bv):
        tall = kept[k_i].shape[0]
        a = load(
            (kept[mix_i], part(act, count)),
            (kept[q_i], part(pool.at[0], count)),
            (kept[k_i], part(pool.at[1], tall)),
            (kept[v_i], part(pool.at[2], tall)),
            (kept[lse_i], part(lse, count)),
        )
        b = wload(wo)
        round_rows(out_ref, count, orow)
        sum_rows(out_ref, count, vrow(bo))
        wait(a, b)
        back_through(orow, wbuf.at[0], count, pool.at[3], False)
        weight_grad(act, orow, count, g.at[1])
        attention_backward_ref(
            pool.at[0], pool.at[1], pool.at[2], pool.at[3], lse, mask_ref if masked else None, count, keys,
            dq, part(dk, tall), part(dv, tall),
        )
        round_rows(dq, count, pool.at[0])
        round_rows(dk, keys, pool.at[1])
        round_rows(dv, keys, pool.at[2])
        sum_rows(dq, count, vrow(bq))
        sum_rows(dv, keys, vrow(bv))

    def start():
        make_mask(seg_row, seg_col, mask_ref, rows)
        for i, v in enumerate((0, 5, 12, 17, 22)):
            for k in range(6):
                gains[i : i + 1, k * LANES : (k + 1) * LANES] = v_ref[v // 8, v // 4 % 2, v // 2 % 2, v % 2, k : k + 1, :]
        wait(load((dcot, part(orow, rows)), (kept[10], mem)))

        def body(r):
            outg[r, :] = orow[r, :].astype(F32)

        row_blocks(rows, body)

    def produce(t, g):
        if t == 0:
            start()
        if t < 4:
            feed(t, g, rows, 20, 24, 26, 27, 25)
            if t == 1:
                sum_rows(outg, rows, vrow(28))
        elif t == 4:
            attend(g, rows, frames, outg, 19, 22, 19, 20, 21, 23, False, 21, 19, 20)
            weight_grad(mem, pool.at[2], frames, g.at[0])
        elif t == 5:
            weight_grad(nbuf, pool.at[0], rows, g.at[0])
            weight_grad(mem, pool.at[1], frames, g.at[1])
        elif t == 6:
            attend(g, rows, rows, outg, 15, 15, 12, 13, 14, 16, True, 16, 14, 15)
            wait(load((kept[11], part(nbuf, rows))))
            weight_grad(nbuf, pool.at[2], rows, g.at[0])
        elif t == 7:
            weight_grad(nbuf, pool.at[0], rows, g.at[0])
            weight_grad(nbuf, pool.at[1], rows, g.at[1])
        elif t < 12:
            feed(t - 8, g, frames, 4, 7, 8, 9, 7)
            if t == 9:
                sum_rows(eoutg, frames, vrow(11))
        elif t == 12:
            attend(g, frames, frames, eoutg, 3, 4, 1, 2, 3, 5, False, 4, 2, 3)
            wait(load((kept[0], part(nbuf, frames))))
            weight_grad(nbuf, pool.at[2], frames, g.at[0])
        else:
            weight_grad(nbuf, pool.at[0], frames, g.at[0])
            weight_grad(nbuf, pool.at[1], frames, g.at[1])

    def after(t):
        if t in (2, 3):
            feed_after(t, rows, 20)
            if t == 3:
                wait(load((kept[24], part(xbuf, rows))))
                norm_backward_ref(xbuf, gains.at[4:5], dn, rows, outg, vrow(22), vrow(23))
        elif t == 4:
            wait(load((kept[18], part(nbuf, rows))))
        elif t == 5:
            wait(load((kept[17], part(xbuf, rows))), wload(16, 17))
            back_through(pool.at[0], wbuf.at[0], rows, dn, False)
            back_through(pool.at[1], wbuf.at[1], frames, mgrad, False)
            wait(wload(18))
            back_through(pool.at[2], wbuf.at[0], frames, mgrad, True)
            norm_backward_ref(xbuf, gains.at[3:4], dn, rows, outg, vrow(17), vrow(18))
        elif t == 7:
            wait(load((din, part(slope, rows))), wload(12, 13))
            back_through(pool.at[0], wbuf.at[0], rows, dn, False)
            back_through(pool.at[1], wbuf.at[1], rows, dn, True)
            wait(wload(14))
            back_through(pool.at[2], wbuf.at[0], rows, dn, True)
            norm_backward_ref(slope, gains.at[2:3], dn, rows, outg, vrow(12), vrow(13))
            pltpu.make_async_copy(outg, tgrad, s_o.at[0]).start()
            wait(load((ecot, part(act, frames))))

            def body(r):
                total = act[r, :].astype(F32) + mgrad[r, :]
                eoutg[r, :] = total
                orow[r, :] = total.astype(BF)

            row_blocks(frames, body)
        elif t in (10, 11):
            feed_after(t - 8, frames, 4)
            if t == 11:
                wait(load((kept[6], part(xbuf, frames))))
                norm_backward_ref(xbuf, gains.at[1:2], dn, frames, eoutg, vrow(5), vrow(6))
        elif t == 13:
            wait(load((ein, part(slope, frames))), wload(0, 1))
            back_through(pool.at[0], wbuf.at[0], frames, dn, False)
            back_through(pool.at[1], wbuf.at[1], frames, dn, True)
            wait(wload(2))
            back_through(pool.at[2], wbuf.at[0], frames, dn, True)
            norm_backward_ref(slope, gains.at[0:1], dn, frames, eoutg, vrow(0), vrow(1))
            pltpu.make_async_copy(eoutg, fgrad, s_o.at[1]).start()
            for v in range(32):
                at = (v // 8, v // 4 % 2, v // 2 % 2, v % 2)
                if v < N_VEC:
                    vg[at + (slice(6, 8), slice(None))] = jnp.zeros((2, LANES), F32)
                    for k in range(6):
                        vg[at + (slice(k, k + 1), slice(None))] = vgr[v : v + 1, k * LANES : (k + 1) * LANES]
                else:
                    vg[at] = jnp.zeros((8, LANES), F32)

    scatter_kernel(n, produce, after, vg, gbuf, oe_ref, od_ref, norm_ref, *comm)
    pltpu.make_async_copy(outg, tgrad, s_o.at[0]).wait()
    pltpu.make_async_copy(eoutg, fgrad, s_o.at[1]).wait()


def backward_pass(weights, vectors, kept, ein, din, ecot, dcot, segments, n):
    (_, re, ne, ge), (_, rd, nd, gd) = sizes(ENC, n), sizes(DEC, n)
    frames, rows = ein.shape[0], din.shape[0]
    tall = -(-rows // 128) * 128
    dma = pltpu.SemaphoreType.DMA
    vmem, hbm = pl.BlockSpec(memory_space=pltpu.VMEM), pl.BlockSpec(memory_space=pl.ANY)
    seg_row = jnp.pad(segments[None, :], ((0, 0), (0, tall - rows)), constant_values=-1)
    return pl.pallas_call(
        partial(backward_kernel, n, rows, frames),
        out_shape=(
            jax.ShapeDtypeStruct((re, LANES), F32),
            jax.ShapeDtypeStruct((rd, LANES), F32),
            jax.ShapeDtypeStruct((8, LANES), F32),
            jax.ShapeDtypeStruct((frames, D), F32),
            jax.ShapeDtypeStruct((rows, D), F32),
        ),
        in_specs=[hbm] + [vmem] * 3 + [hbm] * (4 + N_SAVED),
        out_specs=(hbm, hbm, vmem, hbm, hbm),
        scratch_shapes=[
            pltpu.VMEM((RING_C, 4, 2, 2, UNIT, D), BF),
            pltpu.VMEM((N_PAIR, 4, 2, UNIT, D), BF),
            pltpu.VMEM((N_PAIR, 4, UNIT, D), BF),
            pltpu.VMEM((N_PAIR, 3, UNIT, D), BF),
            pltpu.VMEM((N_PAIR, UNIT, D), BF),
            pltpu.VMEM((8, LANES), F32),
            pltpu.VMEM((4, 2, 2, 8, LANES), F32),
            pltpu.VMEM((4, 2, 8, LANES), F32),
            pltpu.VMEM((4, 8, LANES), F32),
            pltpu.VMEM((3, 8, LANES), F32),
            pltpu.VMEM((FRONT + re + BACK, LANES), F32),
            pltpu.VMEM((FRONT + rd + BACK, LANES), F32),
            pltpu.VMEM((ne, UNIT, D), BF),
            pltpu.VMEM((nd, UNIT, D), BF),
            pltpu.VMEM((ge, 4, UNIT, D), BF),
            pltpu.VMEM((gd, 4, UNIT, D), BF),
            pltpu.VMEM((N_VEC, 8, LANES), F32),
            pltpu.VMEM((8, LANES), F32),
            pltpu.VMEM((n, 8, LANES), F32),
            dma((N_PAIR,)),
            dma((N_PAIR,)),
            pltpu.SemaphoreType.REGULAR,
            dma((N_PAIR, 5)),
            dma((N_PAIR, 5)),
            dma((N_PAIR, 2)),
            dma((2, max(ne, nd))),
            dma((2, max(ge, gd), 4)),
            dma((6,)),
            dma((6,)),
            dma((2,)),
            dma((N_VEC,)),
            dma((n,)),
            dma((n,)),
            dma((2,)),
            pltpu.VMEM((RING, 2, 4, 2, 2, UNIT, D), BF),
            pltpu.VMEM((4, 2, 2, 2, 8, LANES), F32),
            pltpu.VMEM((32, D), F32),
            pltpu.VMEM((8, D), F32),
            pltpu.VMEM((2, D, D), BF),
            pltpu.VMEM((rows, D), F32),
            pltpu.VMEM((frames, D), F32),
            pltpu.VMEM((rows, D), F32),
            pltpu.VMEM((4, tall, D), BF),
            pltpu.VMEM((rows, D), BF),
            pltpu.VMEM((rows, D), BF),
            pltpu.VMEM((rows, D), BF),
            pltpu.VMEM((rows, D), F32),
            pltpu.VMEM((rows, D), F32),
            pltpu.VMEM((tall, D), F32),
            pltpu.VMEM((tall, D), F32),
            pltpu.VMEM((rows, tall), F32),
            pltpu.VMEM((rows, LANES), F32),
            pltpu.VMEM((rows, D), BF),
            pltpu.VMEM((frames, D), BF),
            pltpu.VMEM((frames, D), F32),
            dma((5,)),
            dma((2,)),
            dma((2,)),
        ],
        compiler_params=pltpu.CompilerParams(collective_id=1, has_side_effects=True, vmem_limit_bytes=61 << 20),
        name="backward",
    )(weights, vectors, seg_row, segments[:, None], ein, din, ecot, dcot, *kept)


def attention_plan(prefix, width):
    return [
        (prefix + "wq", width, width),
        (prefix + "bq", width, 0),
        (prefix + "wk", width, width),
        (prefix + "wv", width, width),
        (prefix + "bv", width, 0),
        (prefix + "wo", width, width),
        (prefix + "bo", width, 0),
    ]


def feed_plan(width, hidden):
    return [
        ("fc1_weight", width, hidden),
        ("fc1_bias", hidden, 0),
        ("fc2_weight", hidden, width),
        ("fc2_bias", width, 0),
    ]


def encoder_layout(width, hidden):
    return (
        [("ln1_gain", width, 0), ("ln1_bias", width, 0)]
        + attention_plan("att_", width)
        + [("ln2_gain", width, 0), ("ln2_bias", width, 0)]
        + feed_plan(width, hidden)
    )


def decoder_layout(width, hidden):
    return (
        [("ln1_gain", width, 0), ("ln1_bias", width, 0)]
        + attention_plan("self_", width)
        + [("ln2_gain", width, 0), ("ln2_bias", width, 0)]
        + attention_plan("cross_", width)
        + [("ln3_gain", width, 0), ("ln3_bias", width, 0)]
        + feed_plan(width, hidden)
    )


def unpack(flat, layout):
    params = {}
    offset = 0
    for name, rows, cols in layout:
        count = rows * cols if cols > 0 else rows
        piece = flat[offset : offset + count]
        params[name] = piece.reshape(rows, cols) if cols > 0 else piece
        offset = offset + count
    return params


def pack(grads, layout):
    return jnp.concatenate([grads[name].reshape(-1) for name, rows, cols in layout])


def dot_plain(left, right):
    return jnp.dot(left, right, preferred_element_type=jnp.float32)


def dot_left(left, right):
    return lax.dot_general(
        left, right, (((0,), (0,)), ((), ())), preferred_element_type=jnp.float32
    )


def dot_right(left, right):
    return lax.dot_general(
        left, right, (((1,), (1,)), ((), ())), preferred_element_type=jnp.float32
    )


def layer_norm(values, gain, shift):
    centred = values - jnp.mean(values, axis=-1, keepdims=True)
    spread = jnp.mean(centred * centred, axis=-1, keepdims=True)
    return centred * lax.rsqrt(spread + 1e-05) * gain + shift


def norm_forward(params, prefix, values):
    gain = params[prefix + "_gain"].astype(jnp.float32)
    shift = params[prefix + "_bias"].astype(jnp.float32)
    return layer_norm(values, gain, shift).astype(jnp.bfloat16)


def norm_backward(params, prefix, values, grad):
    gain = params[prefix + "_gain"].astype(jnp.float32)
    shift = params[prefix + "_bias"].astype(jnp.float32)
    unused, pullback = jax.vjp(layer_norm, values, gain, shift)
    value_grad, gain_grad, shift_grad = pullback(grad)
    return (value_grad, {prefix + "_gain": gain_grad, prefix + "_bias": shift_grad})


def block_rows(total):
    return total if total <= 1024 else 512


def attend_forward(queries, keys_low, values, allowed_fn):
    total, width = queries.shape
    heads = width // HEAD_DIM
    rows = block_rows(total)
    blocks = total // rows
    scale = HEAD_DIM ** (-0.5)
    query_heads = queries.reshape(blocks, rows, heads, HEAD_DIM)
    key_heads = keys_low.reshape(keys_low.shape[0], heads, HEAD_DIM)
    value_heads = values.reshape(values.shape[0], heads, HEAD_DIM)
    starts = jnp.arange(blocks, dtype=jnp.int32) * rows

    def one_block(inputs):
        block, start = inputs
        scores = (
            jnp.einsum("qhd,khd->hqk", block, key_heads, preferred_element_type=jnp.float32) * scale
        )
        if allowed_fn is not None:
            scores = jnp.where(allowed_fn(start, rows)[None], scores, -1000000000.0)
        peak = jnp.max(scores, axis=-1, keepdims=True)
        weights = jnp.exp(scores - peak)
        totals = jnp.sum(weights, axis=-1, keepdims=True)
        probs = (weights / totals).astype(jnp.bfloat16)
        mixed = jnp.einsum("hqk,khd->qhd", probs, value_heads, preferred_element_type=jnp.float32)
        return (mixed.reshape(rows, width).astype(jnp.bfloat16), (peak + jnp.log(totals))[..., 0])

    mixed, logsum = lax.map(one_block, (query_heads, starts))
    return (mixed.reshape(total, width), logsum)


def attend_backward(queries, keys_low, values, logsum, mixed_grad, allowed_fn):
    total, width = queries.shape
    heads = width // HEAD_DIM
    rows = block_rows(total)
    blocks = total // rows
    scale = HEAD_DIM ** (-0.5)
    query_heads = queries.reshape(blocks, rows, heads, HEAD_DIM)
    grad_heads = mixed_grad.reshape(blocks, rows, heads, HEAD_DIM)
    key_heads = keys_low.reshape(keys_low.shape[0], heads, HEAD_DIM)
    value_heads = values.reshape(values.shape[0], heads, HEAD_DIM)
    starts = jnp.arange(blocks, dtype=jnp.int32) * rows

    def one_block(carry, inputs):
        key_grad, value_grad = carry
        block, grad_block, block_sum, start = inputs
        scores = (
            jnp.einsum("qhd,khd->hqk", block, key_heads, preferred_element_type=jnp.float32) * scale
        )
        if allowed_fn is not None:
            scores = jnp.where(allowed_fn(start, rows)[None], scores, -1000000000.0)
        probs = jnp.exp(scores - block_sum[..., None])
        prob_grad = jnp.einsum(
            "qhd,khd->hqk", grad_block, value_heads, preferred_element_type=jnp.float32
        )
        value_grad = value_grad + jnp.einsum(
            "hqk,qhd->khd",
            probs.astype(jnp.bfloat16),
            grad_block,
            preferred_element_type=jnp.float32,
        )
        score_grad = probs * (prob_grad - jnp.sum(probs * prob_grad, axis=-1, keepdims=True))
        raw_grad = (score_grad * scale).astype(jnp.bfloat16)
        query_grad = jnp.einsum(
            "hqk,khd->qhd", raw_grad, key_heads, preferred_element_type=jnp.float32
        )
        key_grad = key_grad + jnp.einsum(
            "hqk,qhd->khd", raw_grad, block, preferred_element_type=jnp.float32
        )
        return ((key_grad, value_grad), query_grad.reshape(rows, width))

    zeros = jnp.zeros(key_heads.shape, jnp.float32)
    (key_grad, value_grad), query_grad = lax.scan(
        one_block, (zeros, zeros), (query_heads, grad_heads, logsum, starts)
    )
    return (
        query_grad.reshape(total, width),
        key_grad.reshape(keys_low.shape[0], width),
        value_grad.reshape(values.shape[0], width),
    )


def attention_forward(params, prefix, query_rows, key_rows, allowed_fn):
    queries = (dot_plain(query_rows, params[prefix + "wq"]) + params[prefix + "bq"]).astype(
        jnp.bfloat16
    )
    keys_low = dot_plain(key_rows, params[prefix + "wk"]).astype(jnp.bfloat16)
    values = (dot_plain(key_rows, params[prefix + "wv"]) + params[prefix + "bv"]).astype(
        jnp.bfloat16
    )
    mixed, logsum = attend_forward(queries, keys_low, values, allowed_fn)
    output = dot_plain(mixed, params[prefix + "wo"]) + params[prefix + "bo"]
    return (output, (queries, keys_low, values, mixed, logsum))


def attention_backward(params, prefix, query_rows, key_rows, kept, out_grad, allowed_fn):
    queries, keys_low, values, mixed, logsum = kept
    out_round = out_grad.astype(jnp.bfloat16)
    mixed_grad = dot_right(out_round, params[prefix + "wo"]).astype(jnp.bfloat16)
    query_grad, key_grad, value_grad = attend_backward(
        queries, keys_low, values, logsum, mixed_grad, allowed_fn
    )
    query_round = query_grad.astype(jnp.bfloat16)
    key_round = key_grad.astype(jnp.bfloat16)
    value_round = value_grad.astype(jnp.bfloat16)
    grads = {
        prefix + "wq": dot_left(query_rows, query_round),
        prefix + "bq": jnp.sum(query_grad, axis=0),
        prefix + "wk": dot_left(key_rows, key_round),
        prefix + "wv": dot_left(key_rows, value_round),
        prefix + "bv": jnp.sum(value_grad, axis=0),
        prefix + "wo": dot_left(mixed, out_round),
        prefix + "bo": jnp.sum(out_grad, axis=0),
    }
    query_side = dot_right(query_round, params[prefix + "wq"])
    key_side = dot_right(key_round, params[prefix + "wk"]) + dot_right(
        value_round, params[prefix + "wv"]
    )
    return (grads, query_side, key_side)


def feed_forward(params, normed):
    pre = dot_plain(normed, params["fc1_weight"]) + params["fc1_bias"]
    activated = jax.nn.gelu(pre, approximate=False).astype(jnp.bfloat16)
    return (dot_plain(activated, params["fc2_weight"]) + params["fc2_bias"], (pre, activated))


def feed_backward(params, normed, kept, out_grad):
    pre, activated = kept
    out_round = out_grad.astype(jnp.bfloat16)
    act_grad = dot_right(out_round, params["fc2_weight"])
    unused, gelu_back = jax.vjp(partial(jax.nn.gelu, approximate=False), pre)
    pre_grad = gelu_back(act_grad)[0]
    pre_round = pre_grad.astype(jnp.bfloat16)
    grads = {
        "fc1_weight": dot_left(normed, pre_round),
        "fc1_bias": jnp.sum(pre_grad, axis=0),
        "fc2_weight": dot_left(activated, out_round),
        "fc2_bias": jnp.sum(out_grad, axis=0),
    }
    return (grads, dot_right(pre_round, params["fc1_weight"]))


def encoder_forward(params, frames):
    normed = norm_forward(params, "ln1", frames)
    attended, attend_kept = attention_forward(params, "att_", normed, normed, None)
    after = frames + attended
    normed_two = norm_forward(params, "ln2", after)
    fed, feed_kept = feed_forward(params, normed_two)
    return (after + fed, (normed, attend_kept, after, normed_two, feed_kept))


def encoder_backward(params, frames, kept, out_grad):
    normed, attend_kept, after, normed_two, feed_kept = kept
    grads, normed_grad = feed_backward(params, normed_two, feed_kept, out_grad)
    part, norm_grads = norm_backward(params, "ln2", after, normed_grad)
    grads.update(norm_grads)
    after_grad = out_grad + part
    attend_grads, query_side, key_side = attention_backward(
        params, "att_", normed, normed, attend_kept, after_grad, None
    )
    grads.update(attend_grads)
    part, norm_grads = norm_backward(params, "ln1", frames, query_side + key_side)
    grads.update(norm_grads)
    return (grads, after_grad + part)


def decoder_forward(params, tokens, memory_low, allowed_fn):
    normed = norm_forward(params, "ln1", tokens)
    attended, self_kept = attention_forward(params, "self_", normed, normed, allowed_fn)
    after = tokens + attended
    normed_two = norm_forward(params, "ln2", after)
    crossed, cross_kept = attention_forward(params, "cross_", normed_two, memory_low, None)
    after_two = after + crossed
    normed_three = norm_forward(params, "ln3", after_two)
    fed, feed_kept = feed_forward(params, normed_three)
    return (
        after_two + fed,
        (normed, self_kept, after, normed_two, cross_kept, after_two, normed_three, feed_kept),
    )


def decoder_backward(params, tokens, memory_low, kept, out_grad, allowed_fn):
    normed, self_kept, after, normed_two, cross_kept, after_two, normed_three, feed_kept = kept
    grads, normed_grad = feed_backward(params, normed_three, feed_kept, out_grad)
    part, norm_grads = norm_backward(params, "ln3", after_two, normed_grad)
    grads.update(norm_grads)
    after_two_grad = out_grad + part
    cross_grads, query_side, memory_grad = attention_backward(
        params, "cross_", normed_two, memory_low, cross_kept, after_two_grad, None
    )
    grads.update(cross_grads)
    part, norm_grads = norm_backward(params, "ln2", after, query_side)
    grads.update(norm_grads)
    after_grad = after_two_grad + part
    self_grads, query_side, key_side = attention_backward(
        params, "self_", normed, normed, self_kept, after_grad, allowed_fn
    )
    grads.update(self_grads)
    part, norm_grads = norm_backward(params, "ln1", tokens, query_side + key_side)
    grads.update(norm_grads)
    return (grads, after_grad + part, memory_grad)


def adamw(master, first, second, grad, factor, correction):
    clipped = grad * factor
    moment = 0.5 * first + 0.5 * clipped
    variance = 0.5 * second + 0.5 * clipped * clipped
    update = moment / correction / (jnp.sqrt(variance / correction) + 1e-08) + 0.01 * master
    weights = master - 0.02 * update
    return (weights, moment, variance, weights.astype(jnp.bfloat16))


def shards_native(
    encoder_input,
    decoder_input,
    segments,
    encoder_cotangent,
    decoder_cotangent,
    encoder_master,
    encoder_first,
    encoder_second,
    decoder_master,
    decoder_first,
    decoder_second,
    step_count,
):
    encoder_plan = encoder_layout(D, FF)
    decoder_plan = decoder_layout(D, FF)
    encoder_params = unpack(
        lax.all_gather(encoder_master.astype(jnp.bfloat16), ("wide", "narrow"), axis=0, tiled=True),
        encoder_plan,
    )
    frames = encoder_input[0].astype(jnp.float32)
    memory, encoder_kept = encoder_forward(encoder_params, frames)
    memory_low = memory.astype(jnp.bfloat16)
    decoder_params = unpack(
        lax.all_gather(decoder_master.astype(jnp.bfloat16), ("wide", "narrow"), axis=0, tiled=True),
        decoder_plan,
    )
    tokens = decoder_input[0].astype(jnp.float32)
    segment_row = segments[0]
    length = segment_row.shape[0]

    def allowed_fn(start, count):
        places = start + jnp.arange(count, dtype=jnp.int32)
        row_segments = lax.dynamic_slice_in_dim(segment_row, start, count)
        columns = jnp.arange(length, dtype=jnp.int32)
        return (row_segments[:, None] == segment_row[None, :]) & (
            columns[None, :] <= places[:, None]
        )

    decoded, decoder_kept = decoder_forward(decoder_params, tokens, memory_low, allowed_fn)
    decoder_again = unpack(
        lax.all_gather(decoder_master.astype(jnp.bfloat16), ("wide", "narrow"), axis=0, tiled=True),
        decoder_plan,
    )
    decoder_grads, token_grad, memory_grad = decoder_backward(
        decoder_again,
        tokens,
        memory_low,
        decoder_kept,
        decoder_cotangent[0].astype(jnp.float32),
        allowed_fn,
    )
    decoder_total = pack(decoder_grads, decoder_plan)
    decoder_owned = lax.psum_scatter(
        decoder_total, ("wide", "narrow"), scatter_dimension=0, tiled=True
    )
    encoder_again = unpack(
        lax.all_gather(encoder_master.astype(jnp.bfloat16), ("wide", "narrow"), axis=0, tiled=True),
        encoder_plan,
    )
    memory_total = encoder_cotangent[0].astype(jnp.float32) + memory_grad
    encoder_grads, frame_grad = encoder_backward(encoder_again, frames, encoder_kept, memory_total)
    encoder_total = pack(encoder_grads, encoder_plan)
    encoder_owned = lax.psum_scatter(
        encoder_total, ("wide", "narrow"), scatter_dimension=0, tiled=True
    )
    local_squares = jnp.sum(encoder_owned * encoder_owned) + jnp.sum(decoder_owned * decoder_owned)
    gradient_norm = jnp.sqrt(lax.psum(local_squares, ("wide", "narrow")))
    factor = 1.0 / jnp.maximum(gradient_norm, 1.0)
    correction = 1.0 - jnp.power(0.5, step_count.astype(jnp.float32))
    encoder_new = adamw(
        encoder_master, encoder_first, encoder_second, encoder_owned, factor, correction
    )
    decoder_new = adamw(
        decoder_master, decoder_first, decoder_second, decoder_owned, factor, correction
    )
    return (
        memory_low[None],
        decoded.astype(jnp.bfloat16)[None],
        frame_grad[None],
        token_grad[None],
        gradient_norm,
        encoder_new[0],
        encoder_new[1],
        encoder_new[2],
        encoder_new[3],
        decoder_new[0],
        decoder_new[1],
        decoder_new[2],
        decoder_new[3],
    )


def shards(
    encoder_input,
    decoder_input,
    segments,
    encoder_cotangent,
    decoder_cotangent,
    encoder_master,
    encoder_first,
    encoder_second,
    decoder_master,
    decoder_first,
    decoder_second,
    step_count,
):
    n = 32
    weights, vectors, *kept = forward_pass(
        encoder_master, decoder_master, encoder_input[0], decoder_input[0], segments[0], n
    )
    encoder_flat, decoder_flat, norm, frame_grad, token_grad = backward_pass(
        weights, vectors, kept, encoder_input[0], decoder_input[0], encoder_cotangent[0], decoder_cotangent[0], segments[0], n
    )
    gradient_norm = norm[0, 0]
    factor = 1.0 / jnp.maximum(gradient_norm, 1.0)
    correction = 1.0 - jnp.power(0.5, step_count.astype(jnp.float32))
    encoder_owned = encoder_flat.reshape(-1)[: encoder_master.shape[0]]
    decoder_owned = decoder_flat.reshape(-1)[: decoder_master.shape[0]]
    encoder_new = adamw(encoder_master, encoder_first, encoder_second, encoder_owned, factor, correction)
    decoder_new = adamw(decoder_master, decoder_first, decoder_second, decoder_owned, factor, correction)
    return (
        kept[10][None],
        kept[28][None],
        frame_grad[None],
        token_grad[None],
        gradient_norm,
        *encoder_new,
        *decoder_new,
    )


def solution(mesh):
    placed = (
        P(("wide", "narrow"), None, None),
        P(("wide", "narrow"), None, None),
        P(("wide", "narrow"), None),
        P(("wide", "narrow"), None, None),
        P(("wide", "narrow"), None, None),
        P(("wide", "narrow")),
        P(("wide", "narrow")),
        P(("wide", "narrow")),
        P(("wide", "narrow")),
        P(("wide", "narrow")),
        P(("wide", "narrow")),
        P(),
    )
    return jax.shard_map(
        shards if tuple(mesh.shape.values()) == (8, 4) else shards_native,
        mesh=mesh,
        in_specs=placed,
        out_specs=(
            P(("wide", "narrow"), None, None),
            P(("wide", "narrow"), None, None),
            P(("wide", "narrow"), None, None),
            P(("wide", "narrow"), None, None),
            P(),
            P(("wide", "narrow")),
            P(("wide", "narrow")),
            P(("wide", "narrow")),
            P(("wide", "narrow")),
            P(("wide", "narrow")),
            P(("wide", "narrow")),
            P(("wide", "narrow")),
            P(("wide", "narrow")),
        ),
        check_vma=False,
    )
```

```python
from functools import partial

import jax
import jax.numpy as jnp
from jax import lax
from jax.experimental import pallas as pl
from jax.experimental.pallas import tpu as pltpu
from jax.sharding import PartitionSpec as P

D = 768
HEAD_DIM = 64
FF = 3072
MESH = pl.DeviceIdType.MESH
BF = jnp.bfloat16
F32 = jnp.float32

N_MAT = 28
N_PAIR = 14
UNIT = 48
LANES = 128
UROWS = UNIT * D // LANES
BIG = 4 * UROWS
FRONT = BIG + 8
BACK = BIG + 8
N_VEC = 29
LAG = 2


class Block:
    def __init__(self, small, gaps, fc1, vectors, first_mat, small_mats, total):
        self.small = small
        self.gaps = gaps
        self.fc1 = fc1
        self.vectors = vectors
        self.first_mat = first_mat
        self.small_mats = small_mats
        self.total = total


ENC = Block(
    small=8,
    gaps=((0, 2), (1, 1), (3, 1), (4, 3072 + 7)),
    fc1=3079,
    vectors=[0, 1, 770, 2307, 3076, 3077, 3078, 6151, 6152, 6153, 6154, 9227],
    first_mat=0,
    small_mats=4,
    total=9228,
)
DEC = Block(
    small=12,
    gaps=((0, 2), (1, 1), (3, 1), (4, 3), (5, 1), (7, 1), (8, 3072 + 7)),
    fc1=6156,
    vectors=[0, 1, 770, 2307, 3076, 3077, 3078, 3847, 5384, 6153, 6154, 6155, 9228, 9229, 9230, 9231, 12304],
    first_mat=12,
    small_mats=8,
    total=12305,
)
BLOCKS = (ENC, DEC)


def sizes(block, n):
    shard = block.total * D // n
    rows = -(-shard // 1024) * 8
    top = (shard + LANES - 1) // LANES
    return shard, rows, (top + UROWS) // UROWS + 1, (top + BIG) // BIG + 1


def small_row(block, m):
    row = m * D
    for at, gap in block.gaps:
        row = row + jnp.where(m >= at, gap, 0) if at > 0 else row + gap
    return row


def mat_of(block, m):
    return block.first_mat + m + jnp.where(m >= block.small_mats, 4, 0)


def static_unit_rows(block):
    out = []
    for m in range(block.small):
        row = m * D + sum(gap for at, gap in block.gaps if m >= at)
        out.append((block.first_mat + m + (4 if m >= block.small_mats else 0), row))
    return out


def whoami():
    wide, narrow = lax.axis_index("wide"), lax.axis_index("narrow")
    return wide, narrow, wide // 2, wide % 2, narrow // 2, narrow % 2


def device(z, x, y, c):
    return (z * 2 + x, y * 2 + c)


def flat_device(d):
    return (d // 4, d % 4)


def greet(me, n):
    bar = pltpu.get_barrier_semaphore()

    def signal(i, carry):
        pl.semaphore_signal(bar, inc=1, device_id=flat_device((me + i) % n), device_id_type=MESH)
        return carry

    lax.fori_loop(1, n, signal, 0)


def await_all(n):
    pl.semaphore_wait(pltpu.get_barrier_semaphore(), n - 1)


def each_small(block, n, me, slots, body, least=0, most=99):
    shard = sizes(block, n)[0]
    low = me * shard
    low_row = low // LANES
    first = 0
    for _, row in static_unit_rows(block):
        first = first + jnp.minimum(jnp.maximum(low - row * D, 0) // (UROWS * LANES), 16)

    def step(j, carry):
        g = first + j
        m, u = g // 16, g % 16
        start = small_row(block, m) * 6 + u * UROWS
        pos = start - low_row

        @pl.when((g < 16 * min(block.small, most)) & (g >= 16 * least) & (start * LANES < low + shard))
        def _():
            body((pos + UROWS) // UROWS, mat_of(block, m), u, pos, start * LANES)

        return carry

    lax.fori_loop(0, slots, step, 0)


def each_big(block, n, me, slots, body):
    shard = sizes(block, n)[0]
    low = me * shard
    low_row = low // LANES
    first = jnp.minimum(jnp.maximum(low - block.fc1 * D, 0) // (BIG * LANES), 16)

    def step(j, carry):
        u = first + j
        start = block.fc1 * 6 + u * BIG
        pos = start - low_row

        @pl.when((u < 16) & (start * LANES < low + shard) & (start * LANES + BIG * LANES > low))
        def _():
            body((pos + BIG) // BIG, u, pos, start * LANES)

        return carry

    lax.fori_loop(0, slots, step, 0)


def each_vector(block, n, me, first_vec, body):
    shard = sizes(block, n)[0]
    low = me * shard
    low_row = low // LANES
    for i, row in enumerate(block.vectors):
        @pl.when((row * D < low + shard) & (row * D + D > low))
        def _(i=i, row=row):
            body(first_vec + i, row * 6 - low_row, row * D)


def peers(axis, at):
    if axis == "z":
        return [dict(at, z=(at["z"] + k) % 4) for k in (1, 2, 3)]
    return [dict(at, **{axis: 1 - at[axis]})]


def first_peer(at):
    x, y, c = at["x"], at["y"], at["c"]
    return device(at["z"], x + (1 - c) * (1 - 2 * x), y + c * (1 - 2 * y), c)


def second_peer(at):
    x, y, c = at["x"], at["y"], at["c"]
    return device(at["z"], x + c * (1 - 2 * x), y + (1 - c) * (1 - 2 * y), c)


def dev(at):
    return device(at["z"], at["x"], at["y"], at["c"])


def gather_kernel(
    n, on_start, on_vectors, on_pair, xe_ref, xd_ref, w_ref, v_ref,
    re_ref, rd_ref, se_ref, sd_ref, be_ref, bd_ref, sv_ref, land, landv, own, ownv,
    s_small, s_big, s_vec, r_unit, r_vec, s_zxy, r_zxy, s_core, r_core, s_own, v_send, v_recv,
):
    wide, narrow, z, x, y, c = whoami()
    me = wide * 4 + narrow
    chip = me // 2
    at = dict(z=z, x=x, y=y, c=c)
    greet(me, n)
    lanes = lax.broadcasted_iota(jnp.int32, (1, LANES), 1)
    fields = {
        ENC: (xe_ref, re_ref, se_ref, be_ref, 0, 0, 0),
        DEC: (xd_ref, rd_ref, sd_ref, bd_ref, sizes(ENC, n)[2], sizes(ENC, n)[3], len(ENC.vectors)),
    }

    def prepare(block):
        x_ref, r_ref = fields[block][:2]
        shard, rows, _, _ = sizes(block, n)
        step = 8 * max(k for k in range(1, 40) if (rows // 8) % k == 0)

        def turn(i, carry):
            at_row = pl.multiple_of(i * step, 8)
            r_ref[pl.ds(FRONT + at_row, step), :] = pltpu.roll(
                x_ref[pl.ds(at_row, step), :], (me * shard) % LANES, 1
            )
            return carry

        lax.fori_loop(0, rows // step, turn, 0)

    def load_rows(block, row, count, stride=None):
        r_ref = fields[block][1]
        at_row = FRONT + row
        if stride is None:
            here, before = r_ref[pl.ds(at_row, count), :], r_ref[pl.ds(at_row - 1, count), :]
        else:
            here = r_ref[pl.ds(at_row, count, stride=stride), :]
            before = r_ref[pl.ds(at_row - 1, count, stride=stride), :]
        return jnp.where(lanes >= (me * sizes(block, n)[0]) % LANES, here, before)

    def send(src, dst, send_sem, recv_sem, target):
        @pl.when(target == me)
        def _():
            pltpu.make_async_copy(src, dst, send_sem).start()

        @pl.when(target != me)
        def _():
            pltpu.make_async_remote_copy(
                src, dst, send_sem, recv_sem, device_id=flat_device(target), device_id_type=MESH
            ).start()

    def which_of(block, start):
        return jnp.where(start // sizes(block, n)[0] == me, 0, 1)

    def small_units(block, least, most):
        s_ref, small0 = fields[block][2], fields[block][4]

        def body(slot, mat, u, pos, start):
            for k in range(6):
                s_ref[slot, :, k * LANES : (k + 1) * LANES] = load_rows(block, pos + k, UNIT, 6).astype(BF)
            which = which_of(block, start)
            send(
                s_ref.at[slot], land.at[which, mat // 2], s_small.at[small0 + slot], r_unit.at[which, mat // 2],
                u * 2 + mat % 2,
            )

        each_small(block, n, me, sizes(block, n)[2], body, least, most)

    def big_units(block):
        b_ref, big0 = fields[block][3], fields[block][5]
        pair = (block.first_mat + block.small_mats) // 2

        def body(slot, u, pos, start):
            for q in range(4):
                for k in range(6):
                    b_ref[slot, q % 2, q // 2, :, k * LANES : (k + 1) * LANES] = load_rows(
                        block, pos + 6 * q + k, UNIT, 24
                    ).astype(BF)
            which = which_of(block, start)
            for core in range(2):
                send(
                    b_ref.at[slot, core], land.at[which, pl.ds(pair, 2)], s_big.at[big0 + slot, core],
                    r_unit.at[which, pair], u * 2 + core,
                )

        each_big(block, n, me, sizes(block, n)[3], body)

    def vector_units(block):
        def body(v, pos, start):
            sv_ref[v] = load_rows(block, pos, 8).astype(BF).astype(F32)
            which = which_of(block, start)
            send(sv_ref.at[v], landv.at[which], s_vec.at[v], r_vec.at[which], v)

        each_vector(block, n, me, fields[block][6], body)

    prepare(ENC)
    prepare(DEC)
    await_all(n)
    vector_units(ENC)
    vector_units(DEC)
    small_units(ENC, 0, 4)
    on_start()

    def of_self(first, last, which):
        return jnp.where(which == 0, first, last) == me

    def arrive_unit(first, last, src, dst, local_sem, recv):
        for which, holder in ((0, first), (1, last)):
            needed = True if which == 0 else (first != last)

            @pl.when(needed & (holder == me))
            def _(which=which):
                pltpu.make_async_copy(src(which), dst(which), local_sem).wait()

            @pl.when(needed & (holder != me))
            def _(which=which):
                pltpu.make_async_copy(src(which), dst(which), recv(which)).wait()

    def vec_of(v):
        n_enc = len(ENC.vectors)
        rows = ENC.vectors + DEC.vectors
        start = 0
        before = 0
        for i, row in enumerate(rows):
            start = start + jnp.where(v >= i, row - before, 0)
            before = row
        return start * D, jnp.where(v < n_enc, sizes(ENC, n)[0], sizes(DEC, n)[0])

    @pl.when(me < N_VEC)
    def _():
        start, shard = vec_of(me)
        first, last = start // shard, (start + D - 1) // shard
        arrive_unit(
            first, last, lambda w: sv_ref.at[0], lambda w: landv.at[w], s_vec.at[me], lambda w: r_vec.at[w]
        )
        at_elem = lax.broadcasted_iota(jnp.int32, (8, LANES), 0) * LANES + lax.broadcasted_iota(jnp.int32, (8, LANES), 1)
        ownv[...] = jnp.where(at_elem < (first + 1) * shard - start, landv[0], landv[1])

    @pl.when(me >= N_VEC)
    def _():
        ownv[...] = jnp.zeros_like(ownv)

    pltpu.sync_copy(ownv, v_ref.at[z, x, y, c])
    vorder = ("z", "x", "y", "c")

    def vview(done):
        have = set(vorder[:done])
        return tuple(slice(None) if a in have else at[a] for a in "zxyc")

    def vcopies(phase):
        axis = vorder[phase]
        out = []
        for k, p in enumerate(peers(axis, at)):
            ref = v_ref.at[vview(phase)]
            slot = phase if axis == "z" else phase + 2
            out.append(
                pltpu.make_async_remote_copy(
                    ref, ref, v_send.at[slot + k], v_recv.at[slot + k], device_id=dev(p), device_id_type=MESH
                )
            )
        return out

    row_i = lax.broadcasted_iota(jnp.int32, (UNIT, D), 0)
    col_i = lax.broadcasted_iota(jnp.int32, (UNIT, D), 1)

    def merge(pair):
        block = ENC if pair < 6 else DEC
        shard = sizes(block, n)[0]
        local = pair - block.first_mat // 2
        half = block.small_mats // 2
        if half <= local < half + 2:
            start = (block.fc1 * 6 + chip * BIG) * LANES
            elem = row_i * FF + (2 * (local - half) + c) * D + col_i
            length = BIG * LANES
        else:
            small = 2 * local - (4 if local >= half + 2 else 0) + c
            start = (small_row(block, small) * 6 + chip * UROWS) * LANES
            elem = row_i * D + col_i
            length = UROWS * LANES
        first, last = start // shard, (start + length - 1) // shard
        if half <= local < half + 2:
            if local == half:
                low_row = me * shard // LANES
                slot = (start // LANES - low_row + BIG) // BIG + (0 if block is ENC else sizes(ENC, n)[3])
                slot = jnp.minimum(jnp.maximum(slot, 0), sizes(ENC, n)[3] + sizes(DEC, n)[3] - 1)
                arrive_unit(
                    first, last, lambda w: land.at[w, pl.ds(pair, 2)], lambda w: land.at[w, pl.ds(pair, 2)],
                    s_big.at[slot, c], lambda w: r_unit.at[w, pair],
                )
        else:
            low_row = me * shard // LANES
            slot = (start // LANES - low_row + UROWS) // UROWS + (0 if block is ENC else sizes(ENC, n)[2])
            slot = jnp.minimum(jnp.maximum(slot, 0), sizes(ENC, n)[2] + sizes(DEC, n)[2] - 1)
            arrive_unit(
                first, last, lambda w: land.at[w, pair], lambda w: land.at[w, pair],
                s_small.at[slot], lambda w: r_unit.at[w, pair],
            )
        own[pair] = jnp.where(elem < (first + 1) * shard - start, land[0, pair], land[1, pair])

    def own_place(pair):
        return w_ref.at[pair, c, z, x, y]

    def remote(src, dst, pair, k, target):
        return pltpu.make_async_remote_copy(
            src, dst, s_zxy.at[pair, k], r_zxy.at[pair, k], device_id=target, device_id_type=MESH
        )

    def copies(pair, phase):
        if phase == 0:
            return [
                remote(own.at[pair], own_place(pair), pair, 2 + k, device((z + k) % 4, x, y, c)) for k in (1, 2, 3)
            ]
        if phase == 1:
            ref = w_ref.at[pair, c, :, x, y]
            return [remote(ref, ref, pair, 0, first_peer(at))]
        if phase == 2:
            ref = w_ref.at[pair, c, :, :, y]
            return [remote(ref, ref, pair, 1, second_peer(at))]
        ref = w_ref.at[pair, c]
        return [remote(ref, ref, pair, 2, device(z, x, y, 1 - c))]

    def begin(pair, phase):
        if phase != 2:
            for cp in copies(pair, phase):
                cp.start()
            return

        @pl.when(c == 0)
        def _():
            copies(pair, 2)[0].start()

        @pl.when(c == 1)
        def _():
            ref = w_ref.at[pair, c, :, x]
            remote(ref, ref, pair, 1, second_peer(at)).start()

    lag = LAG
    for t in range(N_PAIR + 4 * lag):
        if t < N_PAIR:
            merge(t)
            pltpu.make_async_copy(own.at[t], own_place(t), s_own.at[t]).start()
            begin(t, 0)
        for phase in (1, 2, 3):
            pair = t - phase * lag
            if 0 <= pair < N_PAIR:
                if phase == 1:
                    pltpu.make_async_copy(own.at[pair], own_place(pair), s_own.at[pair]).wait()
                for cp in copies(pair, phase - 1):
                    cp.wait_recv()
                begin(pair, phase)
        if t == 0:
            big_units(ENC)
        elif t == 1:
            small_units(ENC, 4, 99)
        elif t == 2:
            small_units(DEC, 0, 8)
        elif t == 4:
            big_units(DEC)
        elif t == 5:
            small_units(DEC, 8, 99)
        if t < 5:
            if t > 0:
                for cp in vcopies(t - 1):
                    cp.wait_recv()
            if t < 4:
                for cp in vcopies(t):
                    cp.start()
            else:
                on_vectors()
        pair = t - 4 * lag
        if 0 <= pair < N_PAIR:
            for cp in copies(pair, 3):
                cp.wait_recv()
            on_pair(pair)

    for phase in range(4):
        for cp in vcopies(phase):
            cp.wait_send()
    for pair in range(N_PAIR):
        for phase in range(4):
            for cp in copies(pair, phase):
                cp.wait_send()
    for b, (block, s_ref, b_ref) in enumerate(((ENC, se_ref, be_ref), (DEC, sd_ref, bd_ref))):
        shard, rows, n_small, n_big = sizes(block, n)
        small0 = 0 if b == 0 else sizes(ENC, n)[2]
        big0 = 0 if b == 0 else sizes(ENC, n)[3]

        def small_wait(slot, mat, u, pos, start, s_ref=s_ref, small0=small0):
            @pl.when(u * 2 + mat % 2 != me)
            def _():
                pltpu.make_async_copy(s_ref.at[slot], s_ref.at[slot], s_small.at[small0 + slot]).wait()

        def big_wait(slot, u, pos, start, b_ref=b_ref, big0=big0):
            for core in range(2):
                @pl.when(u * 2 + core != me)
                def _(core=core):
                    pltpu.make_async_copy(
                        b_ref.at[slot, core], b_ref.at[slot, core], s_big.at[big0 + slot, core]
                    ).wait()

        def vec_wait(v, pos, start):
            @pl.when(me != v)
            def _():
                pltpu.make_async_copy(sv_ref.at[v], sv_ref.at[v], s_vec.at[v]).wait()

        each_vector(block, n, me, 0 if b == 0 else len(ENC.vectors), vec_wait)
        each_small(block, n, me, n_small, small_wait)
        each_big(block, n, me, n_big, big_wait)


def rows_of(flat, rows):
    return jnp.pad(flat, (0, rows * LANES - flat.shape[0])).reshape(rows, LANES)


SCALE = HEAD_DIM ** (-0.5)
FORBID = -1000000000.0
ROOT_HALF = 0.7071067811865476
PDF = 0.3989422804014327


def mm(a, b):
    return jnp.dot(a, b, preferred_element_type=F32)


def mm_nt(a, b):
    return lax.dot_general(a, b, (((1,), (1,)), ((), ())), preferred_element_type=F32)


def mm_tn(a, b):
    return lax.dot_general(a, b, (((0,), (0,)), ((), ())), preferred_element_type=F32)


def col_blocks(body, width=256):
    def step(j, carry):
        body(pl.ds(pl.multiple_of(j * width, width), width))
        return carry

    lax.fori_loop(0, D // width, step, 0)


def row_blocks(rows, body, height=64):
    def step(i, carry):
        body(pl.ds(pl.multiple_of(i * height, height), height))
        return carry

    lax.fori_loop(0, rows // height, step, 0)


def linear(x_ref, w_ref, rows, out_ref, bias=None):
    x = x_ref[0:rows, :]

    def body(cols):
        y = mm(x, w_ref[:, cols])
        if bias is not None:
            y = y + bias[:, cols]
        out_ref[0:rows, cols] = y.astype(out_ref.dtype)

    col_blocks(body)


def norm_rows(x):
    centred = x - jnp.mean(x, axis=1, keepdims=True)
    spread = jnp.mean(centred * centred, axis=1, keepdims=True)
    root = lax.rsqrt(spread + 1e-05)
    return centred * root, root


def norm_forward_ref(x_ref, gain, shift, rows, out_ref):
    def body(r):
        hat, _ = norm_rows(x_ref[r, :].astype(F32))
        out_ref[r, :] = (hat * gain[...] + shift[...]).astype(BF)

    row_blocks(rows, body)


def attend_tiles(rows, keys, causal):
    return [(start, min(start + 128, keys) if causal else keys) for start in range(0, rows, 128)]


def both_heads(x):
    lane = lax.broadcasted_iota(jnp.int32, (1, LANES), 1)
    zero = jnp.zeros_like(x)
    return jnp.concatenate([jnp.where(lane < HEAD_DIM, x, zero), jnp.where(lane < HEAD_DIM, zero, x)], axis=0)


def scores_of(k, q2, mask_ref, start, reach):
    scores = mm_nt(k, q2)
    if mask_ref is not None:
        mask = mask_ref[0:reach, start : start + LANES]
        scores = jnp.where(jnp.concatenate([mask, mask], axis=1) > 0, scores, FORBID)
    return scores


def attention_forward_ref(q_ref, k_ref, v_ref, mask_ref, rows, keys, mixed_ref, lse_ref):
    def pair_of_heads(i, carry):
        cols = pl.ds(pl.multiple_of(i * LANES, LANES), LANES)
        v_turned = jnp.transpose(v_ref[0:keys, cols])
        for tile, (start, reach) in enumerate(attend_tiles(rows, keys, mask_ref is not None)):
            r = slice(start, start + LANES)
            q2 = both_heads(q_ref[r, cols] * jnp.asarray(SCALE, BF))
            scores = scores_of(k_ref[0:reach, cols], q2, mask_ref, start, reach)
            peak = jnp.max(scores, axis=0, keepdims=True)
            weights = jnp.exp(scores - peak)
            totals = jnp.sum(weights, axis=0, keepdims=True)
            probs = weights.astype(BF)
            share = 1.0 / totals
            mixed = jnp.concatenate(
                [
                    mm(v_turned[s * HEAD_DIM : (s + 1) * HEAD_DIM, 0:reach], probs[:, s * LANES : (s + 1) * LANES])
                    * share[:, s * LANES : (s + 1) * LANES]
                    for s in range(2)
                ],
                axis=0,
            )
            mixed_ref[r, cols] = jnp.transpose(mixed).astype(BF)
            lse_ref[tile, pl.ds(i, 1), :] = peak + jnp.log(totals)
        return carry

    lax.fori_loop(0, D // LANES, pair_of_heads, 0, unroll=1 if mask_ref is not None else 3)


def project_add(x_ref, mixed_ref, w_ref, bias, rows, out_ref):
    m = mixed_ref[0:rows, :]

    def body(cols):
        out_ref[0:rows, cols] = x_ref[0:rows, cols].astype(F32) + mm(m, w_ref[:, cols]) + bias[:, cols]

    col_blocks(body)


def gelu_block(n_ref, w_ref, bias, rows, block, act_ref, slope_ref):
    x = n_ref[0:rows, :]

    def body(cols):
        pre = mm(x, w_ref[:, cols]) + bias[:, cols]
        bell = 0.5 * (1.0 + lax.erf(pre * ROOT_HALF))
        act_ref[block, 0:rows, cols] = (pre * bell).astype(BF)
        slope_ref[block, 0:rows, cols] = (bell + pre * (PDF * jnp.exp(-0.5 * pre * pre))).astype(BF)

    col_blocks(body, 128)


def accumulate(a, w_ref, rows, out_ref, bias=None):
    def body(cols):
        y = out_ref[0:rows, cols] + mm(a, w_ref[:, cols])
        out_ref[0:rows, cols] = y if bias is None else y + bias[:, cols]

    col_blocks(body)


N_SAVED = 29


def saved_shapes(rows, frames):
    tall = -(-rows // 128) * 128
    enc_lse, dec_lse = ((frames // 128, 8, 2 * LANES), F32), ((tall // 128, 8, 2 * LANES), F32)
    return (
        [((frames, D), BF)] * 5
        + [enc_lse, ((frames, D), F32), ((frames, D), BF), ((4, frames, D), BF), ((4, frames, D), BF), ((frames, D), BF)]
        + [((rows, D), BF)]
        + [((tall, D), BF)] * 4
        + [dec_lse, ((rows, D), F32), ((rows, D), BF)]
        + [((tall, D), BF), ((frames, D), BF), ((frames, D), BF), ((tall, D), BF), dec_lse]
        + [((rows, D), F32), ((rows, D), BF), ((4, rows, D), BF), ((4, rows, D), BF), ((rows, D), BF)]
    )


def make_mask(seg_row, seg_col, mask_ref):
    def body(r):
        key = lax.broadcasted_iota(jnp.int32, (64, mask_ref.shape[1]), 0) + r.start
        query = lax.broadcasted_iota(jnp.int32, (64, mask_ref.shape[1]), 1)
        allowed = (seg_col[r, :] == seg_row[...]) & (key <= query)
        mask_ref[r, :] = jnp.where(allowed, 1.0, 0.0)

    row_blocks(mask_ref.shape[0], body)


def forward_kernel(n, rows, frames, *refs):
    xe_ref, xd_ref, ein_ref, din_ref, seg_row, seg_col, w_ref, v_ref = refs[:8]
    outs, refs = refs[8 : 8 + N_SAVED], refs[8 + N_SAVED :]
    comm, refs = refs[:24], refs[24:]
    bufs, refs = refs[:N_SAVED], refs[N_SAVED:]
    vv, wbuf, acc, mask_ref, s_save, s_w = refs
    (
        e_n1, e_q, e_k, e_v, e_mix, e_lse, e_after, e_n2, e_act, e_slope, e_out,
        d_n1, d_q, d_k, d_v, d_mix, d_lse, d_after, d_n2,
        c_q, c_k, c_v, c_mix, c_lse, d_after2, d_n3, d_act, d_slope, d_out,
    ) = bufs
    eacc = acc.at[0:frames]

    def vec(i):
        return vv.at[i : i + 1]

    def save(*indices):
        for i in indices:
            pltpu.make_async_copy(bufs[i], outs[i], s_save.at[i]).start()

    def on_start():
        make_mask(seg_row, seg_col, mask_ref)
        for ref in (d_q, d_k, d_v, c_q):
            if ref.shape[0] > rows:
                ref[rows:, :] = jnp.zeros((ref.shape[0] - rows, D), BF)
        for ref in (e_lse, d_lse, c_lse):
            ref[...] = jnp.zeros_like(ref)

    def on_vectors():
        pltpu.sync_copy(v_ref, vv_tiles)
        for i in range(N_VEC):
            for k in range(6):
                vv[i : i + 1, k * LANES : (k + 1) * LANES] = vv_tiles[i // 8, i // 4 % 2, i // 2 % 2, i % 2, k : k + 1, :]

    def on_pair(pair):
        cps = [pltpu.make_async_copy(w_ref.at[pair, k].reshape(D, D), wbuf.at[k], s_w.at[k]) for k in range(2)]
        for cp in cps:
            cp.start()
        if pair == 0:
            norm_forward_ref(ein_ref, vec(0), vec(1), frames, e_n1)
        if pair == 6:
            norm_forward_ref(din_ref, vec(12), vec(13), rows, d_n1)
        for cp in cps:
            cp.wait()
        w0, w1 = wbuf.at[0], wbuf.at[1]
        if pair == 0:
            linear(e_n1, w0, frames, e_q, vec(2))
            linear(e_n1, w1, frames, e_k)
            save(0, 1, 2)
        elif pair == 1:
            linear(e_n1, w0, frames, e_v, vec(3))
            attention_forward_ref(e_q, e_k, e_v, None, frames, frames, e_mix, e_lse)
            project_add(ein_ref, e_mix, w1, vec(4), frames, e_after)
            norm_forward_ref(e_after, vec(5), vec(6), frames, e_n2)
            save(3, 4, 5, 6, 7)
        elif pair in (2, 3):
            for k in range(2):
                block = 2 * (pair - 2) + k
                gelu_block(e_n2, wbuf.at[k], vec(7 + block), frames, block, e_act, e_slope)
            if pair == 3:
                save(8, 9)
        elif pair in (4, 5):
            if pair == 4:
                eacc[...] = e_after[...]
            for k in range(2):
                last = pair == 5 and k == 1
                accumulate(e_act[2 * (pair - 4) + k], wbuf.at[k], frames, eacc, vec(11) if last else None)
            if pair == 5:
                e_out[...] = eacc[...].astype(BF)
                save(10)
        elif pair == 6:
            linear(d_n1, w0, rows, d_q, vec(14))
            linear(d_n1, w1, rows, d_k)
            save(11, 12, 13)
        elif pair == 7:
            linear(d_n1, w0, rows, d_v, vec(15))
            attention_forward_ref(d_q, d_k, d_v, mask_ref, d_q.shape[0], d_k.shape[0], d_mix, d_lse)
            project_add(din_ref, d_mix, w1, vec(16), rows, d_after)
            norm_forward_ref(d_after, vec(17), vec(18), rows, d_n2)
            save(14, 15, 16, 17, 18)
        elif pair == 8:
            linear(d_n2, w0, rows, c_q, vec(19))
            linear(e_out, w1, frames, c_k)
            save(19, 20)
        elif pair == 9:
            linear(e_out, w0, frames, c_v, vec(20))
            attention_forward_ref(c_q, c_k, c_v, None, c_q.shape[0], frames, c_mix, c_lse)
            project_add(d_after, c_mix, w1, vec(21), rows, d_after2)
            norm_forward_ref(d_after2, vec(22), vec(23), rows, d_n3)
            save(21, 22, 23, 24, 25)
        elif pair in (10, 11):
            for k in range(2):
                block = 2 * (pair - 10) + k
                gelu_block(d_n3, wbuf.at[k], vec(24 + block), rows, block, d_act, d_slope)
            if pair == 11:
                save(26, 27)
        else:
            if pair == 12:
                acc[...] = d_after2[...]
            for k in range(2):
                last = pair == 13 and k == 1
                accumulate(d_act[2 * (pair - 12) + k], wbuf.at[k], rows, acc, vec(28) if last else None)
            if pair == 13:
                d_out[...] = acc[...].astype(BF)
                save(28)

    vv_tiles = comm[-1]
    gather_kernel(n, on_start, on_vectors, on_pair, xe_ref, xd_ref, w_ref, v_ref, *comm[:-1])
    for i in range(N_SAVED):
        pltpu.make_async_copy(bufs[i], outs[i], s_save.at[i]).wait()


def forward_pass(encoder_master, decoder_master, encoder_input, decoder_input, segments, n):
    (_, re, ne, ge), (_, rd, nd, gd) = sizes(ENC, n), sizes(DEC, n)
    frames, rows = encoder_input.shape[0], decoder_input.shape[0]
    tall = -(-rows // 128) * 128
    dma = pltpu.SemaphoreType.DMA
    saved = saved_shapes(rows, frames)
    vmem, hbm = pl.BlockSpec(memory_space=pltpu.VMEM), pl.BlockSpec(memory_space=pl.ANY)
    seg = jnp.pad(segments, (0, tall - rows), constant_values=-1)
    return pl.pallas_call(
        partial(forward_kernel, n, rows, frames),
        out_shape=(
            jax.ShapeDtypeStruct((N_PAIR, 2, 4, 2, 2, UNIT, D), BF),
            jax.ShapeDtypeStruct((4, 2, 2, 2, 8, LANES), F32),
            *(jax.ShapeDtypeStruct(shape, dtype) for shape, dtype in saved),
        ),
        in_specs=[vmem] * 6,
        out_specs=(hbm,) * (2 + N_SAVED),
        scratch_shapes=[
            pltpu.VMEM((FRONT + re + BACK, LANES), F32),
            pltpu.VMEM((FRONT + rd + BACK, LANES), F32),
            pltpu.VMEM((ne, UNIT, D), BF),
            pltpu.VMEM((nd, UNIT, D), BF),
            pltpu.VMEM((ge, 2, 2, UNIT, D), BF),
            pltpu.VMEM((gd, 2, 2, UNIT, D), BF),
            pltpu.VMEM((N_VEC, 8, LANES), F32),
            pltpu.VMEM((2, N_PAIR, UNIT, D), BF),
            pltpu.VMEM((2, 8, LANES), F32),
            pltpu.VMEM((N_PAIR, UNIT, D), BF),
            pltpu.VMEM((8, LANES), F32),
            dma((ne + nd,)),
            dma((ge + gd, 2)),
            dma((N_VEC,)),
            dma((2, N_PAIR)),
            dma((2,)),
            dma((N_PAIR, 6)),
            dma((N_PAIR, 6)),
            dma((N_PAIR,)),
            dma((N_PAIR,)),
            dma((N_PAIR,)),
            dma((6,)),
            dma((6,)),
            pltpu.VMEM((4, 2, 2, 2, 8, LANES), F32),
            *(pltpu.VMEM(shape, dtype) for shape, dtype in saved),
            pltpu.VMEM((32, D), F32),
            pltpu.VMEM((2, D, D), BF),
            pltpu.VMEM((rows, D), F32),
            pltpu.VMEM((tall, tall), F32),
            dma((N_SAVED,)),
            dma((2,)),
        ],
        compiler_params=pltpu.CompilerParams(collective_id=0, has_side_effects=True, vmem_limit_bytes=58 << 20),
        name="forward",
    )(rows_of(encoder_master, re), rows_of(decoder_master, rd), encoder_input, decoder_input, seg[None, :], seg[:, None])


RING = 3
RING_C = 5


def scatter_kernel(
    n, produce, after, vg_ref, gbuf, oe_ref, od_ref, norm_ref,
    land_c, land_b, land_a, land_z, ownb, vown, vl_c, vl_y, vl_x, vl_z,
    ge_ref, gd_ref, fe, fd, fbe, fbd, fv, nsend, nland,
    s_core, r_core, s_free, s_ph, r_ph, s_back, r_small, r_big, sv, rv, s_vback, r_vback, s_n, r_n, s_out,
):
    wide, narrow, z, x, y, c = whoami()
    me = wide * 4 + narrow
    chip = me // 2
    at = dict(z=z, x=x, y=y, c=c)
    greet(me, n)
    sib = device(z, x, y, 1 - c)
    lag = LAG

    def slot_c(pair):
        return (N_PAIR - 1 - pair) % RING_C

    def core_copy(pair):
        return pltpu.make_async_remote_copy(
            gbuf.at[(N_PAIR - 1 - pair) % RING, 1 - c], land_c.at[slot_c(pair)], s_core.at[pair], r_core.at[pair], device_id=sib, device_id_type=MESH
        )

    mine_a = x * (1 - c) + y * c

    def phase_dmas(pair, phase):
        if phase == 1:
            steps = [(land_c.at[slot_c(pair), :, :, 1 - y], land_b.at[pair], 0, second_peer(at))]
        elif phase == 2:
            steps = [(land_b.at[pair, :, 1 - mine_a], land_a.at[pair], 1, first_peer(at))]
        else:
            steps = [
                (land_a.at[pair, (z + k) % 4], land_z.at[pair, k - 1], 1 + k, device((z + k) % 4, x, y, c))
                for k in (1, 2, 3)
            ]
        return [
            pltpu.make_async_remote_copy(
                src, dst, s_ph.at[pair, k], r_ph.at[pair, k], device_id=target, device_id_type=MESH
            )
            for src, dst, k, target in steps
        ]

    def begin(pair, phase):
        if phase != 1:
            for cp in phase_dmas(pair, phase):
                cp.start()
            return

        @pl.when(c == 0)
        def _():
            phase_dmas(pair, 1)[0].start()

        @pl.when(c == 1)
        def _():
            pltpu.make_async_remote_copy(
                land_c.at[slot_c(pair), :, 1 - x], land_b.at[pair], s_ph.at[pair, 0], r_ph.at[pair, 0],
                device_id=second_peer(at), device_id_type=MESH,
            ).start()

    def back(pair):
        block = ENC if pair < 6 else DEC
        shard = sizes(block, n)[0]
        local = pair - block.first_mat // 2
        half = block.small_mats // 2
        big = half <= local < half + 2
        if big:
            start = (block.fc1 * 6 + chip * BIG) * LANES
            length = BIG * LANES
        else:
            small = 2 * local - (4 if local >= half + 2 else 0) + c
            start = (small_row(block, small) * 6 + chip * UROWS) * LANES
            length = UROWS * LANES
        first, last = start // shard, (start + length - 1) // shard
        out = []
        for which, target in ((0, first), (1, last)):
            low_row = target * shard // LANES
            if big:
                slot = (start // LANES - low_row + BIG) // BIG
                q = 2 * (local - half) + c
                dst = (fbe if block is ENC else fbd).at[slot, q]
                recv = r_big.at[0 if block is ENC else 1, slot, q]
            else:
                slot = (start // LANES - low_row + UROWS) // UROWS
                dst = (fe if block is ENC else fd).at[slot]
                recv = r_small.at[0 if block is ENC else 1, slot]
            needed = True if which == 0 else first != last
            out.append((needed, target, dst, s_back.at[pair, which], recv))
        return out

    def start_back(pair):
        for needed, target, dst, send, recv in back(pair):
            @pl.when(needed & (target == me))
            def _(dst=dst, recv=recv):
                pltpu.make_async_copy(ownb.at[pair], dst, recv).start()

            @pl.when(needed & (target != me))
            def _(dst=dst, recv=recv, send=send, target=target):
                pltpu.make_async_remote_copy(
                    ownb.at[pair], dst, send, recv, device_id=flat_device(target), device_id_type=MESH
                ).start()

    def end_back(pair):
        for needed, target, dst, send, recv in back(pair):
            @pl.when(needed & (target != me))
            def _(send=send):
                pltpu.make_async_copy(ownb.at[pair], ownb.at[pair], send).wait()

    def add_core(pair):
        def body(i, carry):
            a, b = i // 2, i % 2
            for k in range(2):
                mine = gbuf[(N_PAIR - 1 - pair) % RING, c, a, b, k]
                land_c[slot_c(pair), a, b, k] = (
                    land_c[slot_c(pair), a, b, k].astype(F32) + mine.astype(F32)
                ).astype(BF)
            return carry

        lax.fori_loop(0, 8, body, 0)

    def add_b(pair):
        def body(i, carry):
            a, b = i // 2, i % 2
            mine = land_c[slot_c(pair), a, b * (1 - c) + x * c, y * (1 - c) + b * c]
            land_b[pair, a, b] = (land_b[pair, a, b].astype(F32) + mine.astype(F32)).astype(BF)
            return carry

        lax.fori_loop(0, 8, body, 0)

    def add_a(pair):
        for a in range(4):
            land_a[pair, a] = (land_a[pair, a].astype(F32) + land_b[pair, a, mine_a].astype(F32)).astype(BF)

    def add_z(pair):
        total = land_a[pair, z].astype(F32)
        for k in range(3):
            total = total + land_z[pair, k].astype(F32)
        ownb[pair] = total.astype(BF)
        squares = total * total
        return jnp.sum(squares.reshape(UNIT // 8, 8, D), axis=0)

    vland = dict(c=vl_c, y=vl_y, x=vl_x, z=vl_z)

    def vsteps(phase):
        if phase == 0:
            return [(vg_ref.at[:, :, :, 1 - c], vl_c, 0, dict(at, c=1 - c))]
        if phase == 1:
            return [(vl_c.at[:, :, 1 - y], vl_y, 1, dict(at, y=1 - y))]
        if phase == 2:
            return [(vl_y.at[:, 1 - x], vl_x, 2, dict(at, x=1 - x))]
        return [(vl_x.at[(z + k) % 4], vl_z.at[k - 1], 2 + k, dict(at, z=(z + k) % 4)) for k in (1, 2, 3)]

    def vdmas(phase):
        return [
            pltpu.make_async_remote_copy(s, d, sv.at[k], rv.at[k], device_id=dev(p), device_id_type=MESH)
            for s, d, k, p in vsteps(phase)
        ]

    def vadd(phase):
        if phase == 0:
            vl_c[...] = vl_c[...] + vg_ref[:, :, :, c]
        elif phase == 1:
            vl_y[...] = vl_y[...] + vl_c[:, :, y]
        elif phase == 2:
            vl_x[...] = vl_x[...] + vl_y[:, x]
        else:
            vown[...] = vl_x[z] + vl_z[0] + vl_z[1] + vl_z[2]

    fields = {ENC: (0, ge_ref, oe_ref, fe, fbe), DEC: (1, gd_ref, od_ref, fd, fbd)}

    def units_to_flat(block):
        b, g_out, _, f_ref, fb_ref = fields[block]
        _, _, n_small, n_big = sizes(block, n)

        def small_body(slot, mat, u, pos, start):
            pltpu.make_async_copy(f_ref.at[slot], f_ref.at[slot], r_small.at[b, slot]).wait()
            for k in range(6):
                g_out[pl.ds(FRONT + pos + k, UNIT, stride=6), :] = f_ref[slot, :, k * LANES : (k + 1) * LANES].astype(F32)

        def big_body(slot, u, pos, start):
            for q in range(4):
                pltpu.make_async_copy(fb_ref.at[slot, q], fb_ref.at[slot, q], r_big.at[b, slot, q]).wait()
                for k in range(6):
                    g_out[pl.ds(FRONT + pos + 6 * q + k, UNIT, stride=24), :] = fb_ref[
                        slot, q, :, k * LANES : (k + 1) * LANES
                    ].astype(F32)

        each_big(block, n, me, n_big, big_body)
        each_small(block, n, me, n_small, small_body)

    def finish_flat(block):
        b, g_out, o_ref, _, _ = fields[block]
        shard, rows, _, _ = sizes(block, n)

        def vec_body(v, pos, start):
            pltpu.make_async_copy(fv.at[v], fv.at[v], r_vback.at[v]).wait()
            g_out[pl.ds(FRONT + pos, 6), :] = fv[v, 0:6, :]

        each_vector(block, n, me, 0 if block is ENC else len(ENC.vectors), vec_body)
        shift = (me * shard) % LANES
        step = 8 * max(k for k in range(1, 40) if (rows // 8) % k == 0)
        lanes = lax.broadcasted_iota(jnp.int32, (1, LANES), 1)
        unturn = lax.rem(LANES - shift, LANES)

        def turn(i, carry):
            at_row = pl.multiple_of(i * step, 8)
            here = pltpu.roll(g_out[pl.ds(FRONT + at_row, step), :], unturn, 1)
            after = pltpu.roll(g_out[pl.ds(FRONT + at_row + 1, step), :], unturn, 1)
            g_out[pl.ds(FRONT + at_row, step), :] = jnp.where(lanes < LANES - shift, here, after)
            return carry

        lax.fori_loop(0, rows // step, turn, 0)
        pltpu.make_async_copy(g_out.at[pl.ds(FRONT, rows)], o_ref, s_out.at[b]).start()

    seq = list(range(N_PAIR - 1, -1, -1))
    square = jnp.zeros((8, D), F32)
    for t in range(N_PAIR + 4 * lag):
        if t < N_PAIR:
            if t >= RING:
                core_copy(seq[t - RING]).wait_send()
            produce(t, gbuf.at[t % RING])
            if t == 0:
                await_all(n)
            if t >= RING_C:
                pl.semaphore_wait(s_free, 1)
            core_copy(seq[t]).start()
        for phase in (4, 3, 2, 1):
            i = t - phase * lag
            if 0 <= i < N_PAIR:
                pair = seq[i]
                if phase == 1:
                    core_copy(pair).wait_recv()
                    add_core(pair)
                elif phase == 2:
                    for cp in phase_dmas(pair, 1):
                        cp.wait()
                    add_b(pair)
                    if i < N_PAIR - RING_C:
                        pl.semaphore_signal(s_free, inc=1, device_id=sib, device_id_type=MESH)
                elif phase == 3:
                    for cp in phase_dmas(pair, 2):
                        cp.wait_recv()
                    add_a(pair)
                else:
                    for cp in phase_dmas(pair, 3):
                        cp.wait_recv()
                    square = square + add_z(pair)
                    start_back(pair)
                if phase < 4:
                    begin(pair, phase)
        if t < N_PAIR:
            after(t)
        if t == N_PAIR + 3 * lag:
            units_to_flat(DEC)
        if t == N_PAIR - 1:
            for cp in vdmas(0):
                cp.start()
        elif t >= N_PAIR and (t - N_PAIR) % 2 == 1:
            phase = (t - N_PAIR) // 2
            for cp in vdmas(phase):
                cp.wait_recv()
            vadd(phase)
            if phase < 3:
                for cp in vdmas(phase + 1):
                    cp.start()

    vsq = vown[...] * vown[...]
    for k in range(6):
        vsq = vsq + square[:, k * LANES : (k + 1) * LANES]
    nsend[...] = vsq

    def norm_copy(i):
        return pltpu.make_async_remote_copy(
            nsend, nland.at[i], s_n.at[i], r_n.at[i], device_id=flat_device((me + i) % n), device_id_type=MESH
        )

    def norm_start(i, carry):
        norm_copy(i).start()
        return carry

    lax.fori_loop(1, n, norm_start, 0)

    def vector_targets(v_static):
        block = ENC if v_static < len(ENC.vectors) else DEC
        shard = sizes(block, n)[0]
        start = (ENC.vectors + DEC.vectors)[v_static] * D
        return start // shard, (start + D - 1) // shard

    for v in range(N_VEC):
        for which, target in enumerate(sorted(set(vector_targets(v)))):
            if target == v:
                @pl.when(me == v)
                def _(v=v):
                    pltpu.make_async_copy(vown, fv.at[v], r_vback.at[v]).start()
            else:
                @pl.when(me == v)
                def _(v=v, target=target, which=which):
                    pltpu.make_async_remote_copy(
                        vown, fv.at[v], s_vback.at[which], r_vback.at[v], device_id=(target // 4, target % 4), device_id_type=MESH
                    ).start()

    units_to_flat(ENC)
    finish_flat(DEC)
    finish_flat(ENC)

    def norm_wait(i, total):
        norm_copy(i).wait()
        return total + nland[i]

    total = lax.fori_loop(1, n, norm_wait, nsend[...])
    norm_ref[...] = jnp.broadcast_to(jnp.sqrt(jnp.sum(total)), (8, LANES))

    for b, (g_out, o_ref) in enumerate(((ge_ref, oe_ref), (gd_ref, od_ref))):
        pltpu.make_async_copy(g_out.at[pl.ds(FRONT, o_ref.shape[0])], o_ref, s_out.at[b]).wait()
    for phase in range(4):
        for cp in vdmas(phase):
            cp.wait_send()
    for v in range(N_VEC):
        for which, target in enumerate(sorted(set(vector_targets(v)))):
            if target != v:
                @pl.when(me == v)
                def _(which=which):
                    pltpu.make_async_copy(vown, vown, s_vback.at[which]).wait()
    for pair in range(N_PAIR):
        if N_PAIR - 1 - pair >= N_PAIR - RING:
            core_copy(pair).wait_send()
        for phase in (2, 3):
            for cp in phase_dmas(pair, phase):
                cp.wait_send()
        end_back(pair)


def sum_rows(ref, rows, out_ref):
    def body(r):
        out_ref[...] += jnp.sum(ref[r, :].astype(F32), axis=0, keepdims=True)

    out_ref[...] = jnp.zeros_like(out_ref)
    row_blocks(rows, body)


def norm_backward_ref(x_ref, gain, dn_ref, rows, out_ref, gain_grad, shift_grad):
    gain_grad[...] = jnp.zeros_like(gain_grad)
    shift_grad[...] = jnp.zeros_like(shift_grad)

    def body(r):
        hat, root = norm_rows(x_ref[r, :].astype(F32))
        dn = dn_ref[r, :]
        gain_grad[...] += jnp.sum(dn * hat, axis=0, keepdims=True)
        shift_grad[...] += jnp.sum(dn, axis=0, keepdims=True)
        g = dn * gain[...]
        part = g - jnp.mean(g, axis=1, keepdims=True) - hat * jnp.mean(g * hat, axis=1, keepdims=True)
        out_ref[r, :] += root * part

    row_blocks(rows, body)


def round_rows(src_ref, rows, out_ref):
    def body(r):
        out_ref[r, :] = src_ref[r, :].astype(BF)

    row_blocks(rows, body)


def weight_grad(a_ref, b_ref, rows, g_ref):
    b = b_ref[0:rows, :]
    flat = g_ref.reshape(D, D)

    def body(cols):
        flat[cols, :] = mm_tn(a_ref[0:rows, cols], b).astype(BF)

    col_blocks(body)


def back_through(a_ref, w_ref, rows, out_ref, add):
    a = a_ref[0:rows, :]

    def body(cols):
        y = mm_nt(a, w_ref[cols, :])
        if add:
            y = y + out_ref[0:rows, cols]
        out_ref[0:rows, cols] = y.astype(out_ref.dtype)

    col_blocks(body)


def gelu_back(o_ref, w_ref, slope_ref, rows, out_ref, bias_grad):
    a = o_ref[0:rows, :]

    def body(cols):
        y = mm_nt(a, w_ref[cols, :]) * slope_ref[0:rows, cols].astype(F32)
        bias_grad[:, cols] = jnp.sum(y, axis=0, keepdims=True)
        out_ref[0:rows, cols] = y.astype(BF)

    col_blocks(body)


def attention_backward_ref(q_ref, k_ref, v_ref, dm_ref, lse_ref, mask_ref, rows, keys, dq_ref, dk_ref, dv_ref):
    def pair_of_heads(i, carry):
        cols = pl.ds(pl.multiple_of(i * LANES, LANES), LANES)
        dk_ref[:, cols] = jnp.zeros((dk_ref.shape[0], LANES), F32)
        dv_ref[:, cols] = jnp.zeros((dv_ref.shape[0], LANES), F32)
        k_turned = jnp.transpose(k_ref[0:keys, cols])
        for tile, (start, reach) in enumerate(attend_tiles(rows, keys, mask_ref is not None)):
            r = slice(start, start + LANES)
            q2 = both_heads(q_ref[r, cols] * jnp.asarray(SCALE, BF))
            dm2 = both_heads(dm_ref[r, cols])
            scores = scores_of(k_ref[0:reach, cols], q2, mask_ref, start, reach)
            probs = jnp.exp(scores - lse_ref[tile, pl.ds(i, 1), :])
            dp = mm_nt(v_ref[0:reach, cols], dm2)
            weighted = probs * dp
            ds = (weighted - probs * jnp.sum(weighted, axis=0, keepdims=True)).astype(BF)
            dk_ref[0:reach, cols] += mm(ds, q2)
            dv_ref[0:reach, cols] += mm(probs.astype(BF), dm2)
            dq = jnp.concatenate(
                [
                    mm(k_turned[s * HEAD_DIM : (s + 1) * HEAD_DIM, 0:reach], ds[:, s * LANES : (s + 1) * LANES])
                    for s in range(2)
                ],
                axis=0,
            )
            dq_ref[r, cols] = jnp.transpose(dq) * SCALE
        return carry

    lax.fori_loop(0, D // LANES, pair_of_heads, 0, unroll=1 if mask_ref is not None else 2)


W_ORDER = (26, 27, 22, 23, 24, 25, 20, 21, 19, 16, 17, 18, 15, 12, 13, 14, 10, 11, 6, 7, 8, 9, 4, 5, 3, 0, 1, 2)
W_RING = 4
A_RING = 4


def backward_kernel(n, rows, frames, *refs):
    w_ref, v_ref, seg_row, seg_col, ein, din, ecot, dcot = refs[:8]
    kept, refs = refs[8 : 8 + N_SAVED], refs[8 + N_SAVED :]
    oe_ref, od_ref, norm_ref, fgrad, tgrad = refs[:5]
    refs = refs[5:]
    comm, refs = refs[:34], refs[34:]
    (
        gbuf, vg, vgr, gains, wbuf, outg, eoutg, dn, pool, abuf, nbuf, xbuf,
        dq, dk, dv, mask_ref, lse, orow, mem, mgrad, s_l, s_w, s_a, s_o,
    ) = refs
    tall = mask_ref.shape[0]

    a_order = (
        [kept[26].at[k] for k in (2, 3, 0, 1)]
        + [kept[27].at[k] for k in (2, 3, 0, 1)]
        + [kept[22].at[0:rows], kept[15].at[0:rows], din]
        + [kept[8].at[k] for k in (2, 3, 0, 1)]
        + [kept[9].at[k] for k in (2, 3, 0, 1)]
        + [kept[4], ein]
    )
    used = [0, 0]

    def w_copy(u):
        m = W_ORDER[u]
        return pltpu.make_async_copy(w_ref.at[m // 2, m % 2].reshape(D, D), wbuf.at[u % W_RING], s_w.at[u % W_RING])

    def a_copy(u):
        src = a_order[u]
        return pltpu.make_async_copy(src, abuf.at[u % A_RING, 0 : src.shape[0]], s_a.at[u % A_RING])

    def with_w(mat, body):
        u = used[0]
        used[0] += 1
        assert W_ORDER[u] == mat
        w_copy(u).wait()
        body(wbuf.at[u % W_RING])
        if u + W_RING < len(W_ORDER):
            w_copy(u + W_RING).start()

    def with_a(body):
        u = used[1]
        used[1] += 1
        a_copy(u).wait()
        body(abuf.at[u % A_RING])
        if u + A_RING < len(a_order):
            a_copy(u + A_RING).start()

    def side(k, src, dst):
        return pltpu.make_async_copy(src, dst, s_l.at[k])

    def x_copy(i):
        return side(0, kept[i], xbuf.at[0 : kept[i].shape[0]])

    def n_copy(i):
        return side(1, kept[i], nbuf.at[0 : kept[i].shape[0]])

    def vrow(i):
        return vgr.at[i : i + 1]

    def feed(step, g, count, first_mat, first_vec, n_i):
        if step < 2:
            for j in range(2):
                with_a(lambda a, j=j: weight_grad(a, orow, count, g.at[j]))
            return
        ks = (2, 3) if step == 2 else (0, 1)
        for j, k in enumerate(ks):
            with_w(
                first_mat + 4 + k,
                lambda w, k=k: with_a(lambda a: gelu_back(orow, w, a, count, pool.at[k], vrow(first_vec + k))),
            )
            if step == 2 and j == 0:
                n_copy(n_i).wait()
            weight_grad(nbuf, pool.at[k], count, g.at[j])

    def feed_after(step, count, first_mat):
        ks = (2, 3) if step == 2 else (0, 1)
        for j, k in enumerate(ks):
            with_w(first_mat + k, lambda w, j=j, k=k: back_through(pool.at[k], w, count, dn, not (step == 2 and j == 0)))

    def attend(g, count, padded, keys, padded_keys, out_ref, wo, q_i, lse_i, masked, bo, bq, bv):
        cps = [side(2 + k, kept[q_i + k], pool.at[k, 0 : kept[q_i + k].shape[0]]) for k in range(3)]
        cps.append(side(5, kept[lse_i], lse.at[0 : kept[lse_i].shape[0]]))
        for cp in cps:
            cp.start()
        round_rows(out_ref, count, orow)
        sum_rows(out_ref, count, vrow(bo))
        with_a(lambda a: weight_grad(a, orow, count, g.at[1]))
        with_w(wo, lambda w: back_through(orow, w, count, pool.at[3], False))
        if padded > count:
            pool[3, count:padded, :] = jnp.zeros((padded - count, D), BF)
        for cp in cps:
            cp.wait()
        attention_backward_ref(
            pool.at[0], pool.at[1], pool.at[2], pool.at[3], lse, mask_ref if masked else None, padded, padded_keys,
            dq, dk.at[0:padded_keys], dv.at[0:padded_keys],
        )
        round_rows(dv, keys, pool.at[2])
        round_rows(dq, count, pool.at[0])
        round_rows(dk, keys, pool.at[1])
        sum_rows(dq, count, vrow(bq))
        sum_rows(dv, keys, vrow(bv))

    def start():
        o_copy = side(2, dcot, orow)
        o_copy.start()
        for u in range(A_RING):
            a_copy(u).start()
        for u in range(W_RING):
            w_copy(u).start()
        n_copy(25).start()
        x_copy(24).start()
        mem_copy = side(3, kept[10], mem)
        mem_copy.start()
        for i, v in enumerate((0, 5, 12, 17, 22)):
            for k in range(6):
                gains[i : i + 1, k * LANES : (k + 1) * LANES] = v_ref[v // 8, v // 4 % 2, v // 2 % 2, v % 2, k : k + 1, :]
        o_copy.wait()
        mem_copy.wait()

    def widen():
        def body(r):
            outg[r, :] = orow[r, :].astype(F32)

        row_blocks(rows, body)
        sum_rows(outg, rows, vrow(28))

    def produce(t, g):
        if t == 0:
            start()
        if t < 4:
            feed(t, g, rows, 20, 24, 25)
            if t == 3:
                n_copy(18).start()
        elif t == 4:
            attend(g, rows, tall, frames, frames, outg, 19, 19, 23, False, 21, 19, 20)
            weight_grad(mem, pool.at[2], frames, g.at[0])
        elif t == 5:
            n_copy(18).wait()
            weight_grad(nbuf, pool.at[0], rows, g.at[0])
            weight_grad(mem, pool.at[1], frames, g.at[1])
            n_copy(11).start()
        elif t == 6:
            attend(g, rows, tall, rows, tall, outg, 15, 12, 16, True, 16, 14, 15)
            n_copy(11).wait()
            weight_grad(nbuf, pool.at[2], rows, g.at[0])
        elif t == 7:
            weight_grad(nbuf, pool.at[0], rows, g.at[0])
            weight_grad(nbuf, pool.at[1], rows, g.at[1])
            n_copy(7).start()
        elif t < 12:
            feed(t - 8, g, frames, 4, 7, 7)
            if t == 11:
                n_copy(0).start()
        elif t == 12:
            attend(g, frames, frames, frames, frames, eoutg, 3, 1, 5, False, 4, 2, 3)
            n_copy(0).wait()
            weight_grad(nbuf, pool.at[2], frames, g.at[0])
        else:
            weight_grad(nbuf, pool.at[0], frames, g.at[0])
            weight_grad(nbuf, pool.at[1], frames, g.at[1])

    def after(t):
        if t == 0:
            widen()
            make_mask(seg_row, seg_col, mask_ref)
        elif t in (2, 3):
            feed_after(t, rows, 20)
            if t == 3:
                x_copy(24).wait()
                norm_backward_ref(xbuf, gains.at[4:5], dn, rows, outg, vrow(22), vrow(23))
                x_copy(17).start()
        elif t == 5:
            with_w(16, lambda w: back_through(pool.at[0], w, rows, dn, False))
            with_w(17, lambda w: back_through(pool.at[1], w, frames, mgrad, False))
            with_w(18, lambda w: back_through(pool.at[2], w, frames, mgrad, True))
            x_copy(17).wait()
            norm_backward_ref(xbuf, gains.at[3:4], dn, rows, outg, vrow(17), vrow(18))
            x_copy(6).start()
        elif t == 7:
            cot = side(2, ecot, orow.at[0:frames])
            cot.start()
            with_w(12, lambda w: back_through(pool.at[0], w, rows, dn, False))
            with_w(13, lambda w: back_through(pool.at[1], w, rows, dn, True))
            with_w(14, lambda w: back_through(pool.at[2], w, rows, dn, True))
            with_a(lambda a: norm_backward_ref(a, gains.at[2:3], dn, rows, outg, vrow(12), vrow(13)))
            pltpu.make_async_copy(outg, tgrad, s_o.at[0]).start()
            cot.wait()

            def body(r):
                total = orow[r, :].astype(F32) + mgrad[r, :]
                eoutg[r, :] = total
                orow[r, :] = total.astype(BF)

            row_blocks(frames, body)
        elif t == 9:
            sum_rows(eoutg, frames, vrow(11))
        elif t in (10, 11):
            feed_after(t - 8, frames, 4)
            if t == 11:
                x_copy(6).wait()
                norm_backward_ref(xbuf, gains.at[1:2], dn, frames, eoutg, vrow(5), vrow(6))
        elif t == 13:
            with_w(0, lambda w: back_through(pool.at[0], w, frames, dn, False))
            with_w(1, lambda w: back_through(pool.at[1], w, frames, dn, True))
            with_w(2, lambda w: back_through(pool.at[2], w, frames, dn, True))
            with_a(lambda a: norm_backward_ref(a, gains.at[0:1], dn, frames, eoutg, vrow(0), vrow(1)))
            pltpu.make_async_copy(eoutg, fgrad, s_o.at[1]).start()
            for v in range(32):
                at = (v // 8, v // 4 % 2, v // 2 % 2, v % 2)
                if v < N_VEC:
                    vg[at + (slice(6, 8), slice(None))] = jnp.zeros((2, LANES), F32)
                    for k in range(6):
                        vg[at + (slice(k, k + 1), slice(None))] = vgr[v : v + 1, k * LANES : (k + 1) * LANES]
                else:
                    vg[at] = jnp.zeros((8, LANES), F32)

    scatter_kernel(n, produce, after, vg, gbuf, oe_ref, od_ref, norm_ref, *comm)
    pltpu.make_async_copy(outg, tgrad, s_o.at[0]).wait()
    pltpu.make_async_copy(eoutg, fgrad, s_o.at[1]).wait()


def backward_pass(weights, vectors, kept, ein, din, ecot, dcot, segments, n):
    (_, re, ne, ge), (_, rd, nd, gd) = sizes(ENC, n), sizes(DEC, n)
    frames, rows = ein.shape[0], din.shape[0]
    tall = -(-rows // 128) * 128
    dma = pltpu.SemaphoreType.DMA
    vmem, hbm = pl.BlockSpec(memory_space=pltpu.VMEM), pl.BlockSpec(memory_space=pl.ANY)
    seg = jnp.pad(segments, (0, tall - rows), constant_values=-1)
    return pl.pallas_call(
        partial(backward_kernel, n, rows, frames),
        out_shape=(
            jax.ShapeDtypeStruct((re, LANES), F32),
            jax.ShapeDtypeStruct((rd, LANES), F32),
            jax.ShapeDtypeStruct((8, LANES), F32),
            jax.ShapeDtypeStruct((frames, D), F32),
            jax.ShapeDtypeStruct((rows, D), F32),
        ),
        in_specs=[hbm] + [vmem] * 3 + [hbm] * (4 + N_SAVED),
        out_specs=(hbm, hbm, vmem, hbm, hbm),
        scratch_shapes=[
            pltpu.VMEM((RING_C, 4, 2, 2, UNIT, D), BF),
            pltpu.VMEM((N_PAIR, 4, 2, UNIT, D), BF),
            pltpu.VMEM((N_PAIR, 4, UNIT, D), BF),
            pltpu.VMEM((N_PAIR, 3, UNIT, D), BF),
            pltpu.VMEM((N_PAIR, UNIT, D), BF),
            pltpu.VMEM((8, LANES), F32),
            pltpu.VMEM((4, 2, 2, 8, LANES), F32),
            pltpu.VMEM((4, 2, 8, LANES), F32),
            pltpu.VMEM((4, 8, LANES), F32),
            pltpu.VMEM((3, 8, LANES), F32),
            pltpu.VMEM((FRONT + re + BACK, LANES), F32),
            pltpu.VMEM((FRONT + rd + BACK, LANES), F32),
            pltpu.VMEM((ne, UNIT, D), BF),
            pltpu.VMEM((nd, UNIT, D), BF),
            pltpu.VMEM((ge, 4, UNIT, D), BF),
            pltpu.VMEM((gd, 4, UNIT, D), BF),
            pltpu.VMEM((N_VEC, 8, LANES), F32),
            pltpu.VMEM((8, LANES), F32),
            pltpu.VMEM((n, 8, LANES), F32),
            dma((N_PAIR,)),
            dma((N_PAIR,)),
            pltpu.SemaphoreType.REGULAR,
            dma((N_PAIR, 5)),
            dma((N_PAIR, 5)),
            dma((N_PAIR, 2)),
            dma((2, max(ne, nd))),
            dma((2, max(ge, gd), 4)),
            dma((6,)),
            dma((6,)),
            dma((2,)),
            dma((N_VEC,)),
            dma((n,)),
            dma((n,)),
            dma((2,)),
            pltpu.VMEM((RING, 2, 4, 2, 2, UNIT, D), BF),
            pltpu.VMEM((4, 2, 2, 2, 8, LANES), F32),
            pltpu.VMEM((32, D), F32),
            pltpu.VMEM((8, D), F32),
            pltpu.VMEM((W_RING, D, D), BF),
            pltpu.VMEM((rows, D), F32),
            pltpu.VMEM((frames, D), F32),
            pltpu.VMEM((rows, D), F32),
            pltpu.VMEM((4, tall, D), BF),
            pltpu.VMEM((A_RING, rows, D), BF),
            pltpu.VMEM((rows, D), BF),
            pltpu.VMEM((rows, D), F32),
            pltpu.VMEM((tall, D), F32),
            pltpu.VMEM((tall, D), F32),
            pltpu.VMEM((tall, D), F32),
            pltpu.VMEM((tall, tall), F32),
            pltpu.VMEM((tall // 128, 8, 2 * LANES), F32),
            pltpu.VMEM((rows, D), BF),
            pltpu.VMEM((frames, D), BF),
            pltpu.VMEM((frames, D), F32),
            dma((6,)),
            dma((W_RING,)),
            dma((A_RING,)),
            dma((2,)),
        ],
        compiler_params=pltpu.CompilerParams(collective_id=1, has_side_effects=True, vmem_limit_bytes=61 << 20),
        name="backward",
    )(weights, vectors, seg[None, :], seg[:, None], ein, din, ecot, dcot, *kept)


def attention_plan(prefix, width):
    return [
        (prefix + "wq", width, width),
        (prefix + "bq", width, 0),
        (prefix + "wk", width, width),
        (prefix + "wv", width, width),
        (prefix + "bv", width, 0),
        (prefix + "wo", width, width),
        (prefix + "bo", width, 0),
    ]


def feed_plan(width, hidden):
    return [
        ("fc1_weight", width, hidden),
        ("fc1_bias", hidden, 0),
        ("fc2_weight", hidden, width),
        ("fc2_bias", width, 0),
    ]


def encoder_layout(width, hidden):
    return (
        [("ln1_gain", width, 0), ("ln1_bias", width, 0)]
        + attention_plan("att_", width)
        + [("ln2_gain", width, 0), ("ln2_bias", width, 0)]
        + feed_plan(width, hidden)
    )


def decoder_layout(width, hidden):
    return (
        [("ln1_gain", width, 0), ("ln1_bias", width, 0)]
        + attention_plan("self_", width)
        + [("ln2_gain", width, 0), ("ln2_bias", width, 0)]
        + attention_plan("cross_", width)
        + [("ln3_gain", width, 0), ("ln3_bias", width, 0)]
        + feed_plan(width, hidden)
    )


def unpack(flat, layout):
    params = {}
    offset = 0
    for name, rows, cols in layout:
        count = rows * cols if cols > 0 else rows
        piece = flat[offset : offset + count]
        params[name] = piece.reshape(rows, cols) if cols > 0 else piece
        offset = offset + count
    return params


def pack(grads, layout):
    return jnp.concatenate([grads[name].reshape(-1) for name, rows, cols in layout])


def dot_plain(left, right):
    return jnp.dot(left, right, preferred_element_type=jnp.float32)


def dot_left(left, right):
    return lax.dot_general(
        left, right, (((0,), (0,)), ((), ())), preferred_element_type=jnp.float32
    )


def dot_right(left, right):
    return lax.dot_general(
        left, right, (((1,), (1,)), ((), ())), preferred_element_type=jnp.float32
    )


def layer_norm(values, gain, shift):
    centred = values - jnp.mean(values, axis=-1, keepdims=True)
    spread = jnp.mean(centred * centred, axis=-1, keepdims=True)
    return centred * lax.rsqrt(spread + 1e-05) * gain + shift


def norm_forward(params, prefix, values):
    gain = params[prefix + "_gain"].astype(jnp.float32)
    shift = params[prefix + "_bias"].astype(jnp.float32)
    return layer_norm(values, gain, shift).astype(jnp.bfloat16)


def norm_backward(params, prefix, values, grad):
    gain = params[prefix + "_gain"].astype(jnp.float32)
    shift = params[prefix + "_bias"].astype(jnp.float32)
    unused, pullback = jax.vjp(layer_norm, values, gain, shift)
    value_grad, gain_grad, shift_grad = pullback(grad)
    return (value_grad, {prefix + "_gain": gain_grad, prefix + "_bias": shift_grad})


def block_rows(total):
    return total if total <= 1024 else 512


def attend_forward(queries, keys_low, values, allowed_fn):
    total, width = queries.shape
    heads = width // HEAD_DIM
    rows = block_rows(total)
    blocks = total // rows
    scale = HEAD_DIM ** (-0.5)
    query_heads = queries.reshape(blocks, rows, heads, HEAD_DIM)
    key_heads = keys_low.reshape(keys_low.shape[0], heads, HEAD_DIM)
    value_heads = values.reshape(values.shape[0], heads, HEAD_DIM)
    starts = jnp.arange(blocks, dtype=jnp.int32) * rows

    def one_block(inputs):
        block, start = inputs
        scores = (
            jnp.einsum("qhd,khd->hqk", block, key_heads, preferred_element_type=jnp.float32) * scale
        )
        if allowed_fn is not None:
            scores = jnp.where(allowed_fn(start, rows)[None], scores, -1000000000.0)
        peak = jnp.max(scores, axis=-1, keepdims=True)
        weights = jnp.exp(scores - peak)
        totals = jnp.sum(weights, axis=-1, keepdims=True)
        probs = (weights / totals).astype(jnp.bfloat16)
        mixed = jnp.einsum("hqk,khd->qhd", probs, value_heads, preferred_element_type=jnp.float32)
        return (mixed.reshape(rows, width).astype(jnp.bfloat16), (peak + jnp.log(totals))[..., 0])

    mixed, logsum = lax.map(one_block, (query_heads, starts))
    return (mixed.reshape(total, width), logsum)


def attend_backward(queries, keys_low, values, logsum, mixed_grad, allowed_fn):
    total, width = queries.shape
    heads = width // HEAD_DIM
    rows = block_rows(total)
    blocks = total // rows
    scale = HEAD_DIM ** (-0.5)
    query_heads = queries.reshape(blocks, rows, heads, HEAD_DIM)
    grad_heads = mixed_grad.reshape(blocks, rows, heads, HEAD_DIM)
    key_heads = keys_low.reshape(keys_low.shape[0], heads, HEAD_DIM)
    value_heads = values.reshape(values.shape[0], heads, HEAD_DIM)
    starts = jnp.arange(blocks, dtype=jnp.int32) * rows

    def one_block(carry, inputs):
        key_grad, value_grad = carry
        block, grad_block, block_sum, start = inputs
        scores = (
            jnp.einsum("qhd,khd->hqk", block, key_heads, preferred_element_type=jnp.float32) * scale
        )
        if allowed_fn is not None:
            scores = jnp.where(allowed_fn(start, rows)[None], scores, -1000000000.0)
        probs = jnp.exp(scores - block_sum[..., None])
        prob_grad = jnp.einsum(
            "qhd,khd->hqk", grad_block, value_heads, preferred_element_type=jnp.float32
        )
        value_grad = value_grad + jnp.einsum(
            "hqk,qhd->khd",
            probs.astype(jnp.bfloat16),
            grad_block,
            preferred_element_type=jnp.float32,
        )
        score_grad = probs * (prob_grad - jnp.sum(probs * prob_grad, axis=-1, keepdims=True))
        raw_grad = (score_grad * scale).astype(jnp.bfloat16)
        query_grad = jnp.einsum(
            "hqk,khd->qhd", raw_grad, key_heads, preferred_element_type=jnp.float32
        )
        key_grad = key_grad + jnp.einsum(
            "hqk,qhd->khd", raw_grad, block, preferred_element_type=jnp.float32
        )
        return ((key_grad, value_grad), query_grad.reshape(rows, width))

    zeros = jnp.zeros(key_heads.shape, jnp.float32)
    (key_grad, value_grad), query_grad = lax.scan(
        one_block, (zeros, zeros), (query_heads, grad_heads, logsum, starts)
    )
    return (
        query_grad.reshape(total, width),
        key_grad.reshape(keys_low.shape[0], width),
        value_grad.reshape(values.shape[0], width),
    )


def attention_forward(params, prefix, query_rows, key_rows, allowed_fn):
    queries = (dot_plain(query_rows, params[prefix + "wq"]) + params[prefix + "bq"]).astype(
        jnp.bfloat16
    )
    keys_low = dot_plain(key_rows, params[prefix + "wk"]).astype(jnp.bfloat16)
    values = (dot_plain(key_rows, params[prefix + "wv"]) + params[prefix + "bv"]).astype(
        jnp.bfloat16
    )
    mixed, logsum = attend_forward(queries, keys_low, values, allowed_fn)
    output = dot_plain(mixed, params[prefix + "wo"]) + params[prefix + "bo"]
    return (output, (queries, keys_low, values, mixed, logsum))


def attention_backward(params, prefix, query_rows, key_rows, kept, out_grad, allowed_fn):
    queries, keys_low, values, mixed, logsum = kept
    out_round = out_grad.astype(jnp.bfloat16)
    mixed_grad = dot_right(out_round, params[prefix + "wo"]).astype(jnp.bfloat16)
    query_grad, key_grad, value_grad = attend_backward(
        queries, keys_low, values, logsum, mixed_grad, allowed_fn
    )
    query_round = query_grad.astype(jnp.bfloat16)
    key_round = key_grad.astype(jnp.bfloat16)
    value_round = value_grad.astype(jnp.bfloat16)
    grads = {
        prefix + "wq": dot_left(query_rows, query_round),
        prefix + "bq": jnp.sum(query_grad, axis=0),
        prefix + "wk": dot_left(key_rows, key_round),
        prefix + "wv": dot_left(key_rows, value_round),
        prefix + "bv": jnp.sum(value_grad, axis=0),
        prefix + "wo": dot_left(mixed, out_round),
        prefix + "bo": jnp.sum(out_grad, axis=0),
    }
    query_side = dot_right(query_round, params[prefix + "wq"])
    key_side = dot_right(key_round, params[prefix + "wk"]) + dot_right(
        value_round, params[prefix + "wv"]
    )
    return (grads, query_side, key_side)


def feed_forward(params, normed):
    pre = dot_plain(normed, params["fc1_weight"]) + params["fc1_bias"]
    activated = jax.nn.gelu(pre, approximate=False).astype(jnp.bfloat16)
    return (dot_plain(activated, params["fc2_weight"]) + params["fc2_bias"], (pre, activated))


def feed_backward(params, normed, kept, out_grad):
    pre, activated = kept
    out_round = out_grad.astype(jnp.bfloat16)
    act_grad = dot_right(out_round, params["fc2_weight"])
    unused, gelu_back = jax.vjp(partial(jax.nn.gelu, approximate=False), pre)
    pre_grad = gelu_back(act_grad)[0]
    pre_round = pre_grad.astype(jnp.bfloat16)
    grads = {
        "fc1_weight": dot_left(normed, pre_round),
        "fc1_bias": jnp.sum(pre_grad, axis=0),
        "fc2_weight": dot_left(activated, out_round),
        "fc2_bias": jnp.sum(out_grad, axis=0),
    }
    return (grads, dot_right(pre_round, params["fc1_weight"]))


def encoder_forward(params, frames):
    normed = norm_forward(params, "ln1", frames)
    attended, attend_kept = attention_forward(params, "att_", normed, normed, None)
    after = frames + attended
    normed_two = norm_forward(params, "ln2", after)
    fed, feed_kept = feed_forward(params, normed_two)
    return (after + fed, (normed, attend_kept, after, normed_two, feed_kept))


def encoder_backward(params, frames, kept, out_grad):
    normed, attend_kept, after, normed_two, feed_kept = kept
    grads, normed_grad = feed_backward(params, normed_two, feed_kept, out_grad)
    part, norm_grads = norm_backward(params, "ln2", after, normed_grad)
    grads.update(norm_grads)
    after_grad = out_grad + part
    attend_grads, query_side, key_side = attention_backward(
        params, "att_", normed, normed, attend_kept, after_grad, None
    )
    grads.update(attend_grads)
    part, norm_grads = norm_backward(params, "ln1", frames, query_side + key_side)
    grads.update(norm_grads)
    return (grads, after_grad + part)


def decoder_forward(params, tokens, memory_low, allowed_fn):
    normed = norm_forward(params, "ln1", tokens)
    attended, self_kept = attention_forward(params, "self_", normed, normed, allowed_fn)
    after = tokens + attended
    normed_two = norm_forward(params, "ln2", after)
    crossed, cross_kept = attention_forward(params, "cross_", normed_two, memory_low, None)
    after_two = after + crossed
    normed_three = norm_forward(params, "ln3", after_two)
    fed, feed_kept = feed_forward(params, normed_three)
    return (
        after_two + fed,
        (normed, self_kept, after, normed_two, cross_kept, after_two, normed_three, feed_kept),
    )


def decoder_backward(params, tokens, memory_low, kept, out_grad, allowed_fn):
    normed, self_kept, after, normed_two, cross_kept, after_two, normed_three, feed_kept = kept
    grads, normed_grad = feed_backward(params, normed_three, feed_kept, out_grad)
    part, norm_grads = norm_backward(params, "ln3", after_two, normed_grad)
    grads.update(norm_grads)
    after_two_grad = out_grad + part
    cross_grads, query_side, memory_grad = attention_backward(
        params, "cross_", normed_two, memory_low, cross_kept, after_two_grad, None
    )
    grads.update(cross_grads)
    part, norm_grads = norm_backward(params, "ln2", after, query_side)
    grads.update(norm_grads)
    after_grad = after_two_grad + part
    self_grads, query_side, key_side = attention_backward(
        params, "self_", normed, normed, self_kept, after_grad, allowed_fn
    )
    grads.update(self_grads)
    part, norm_grads = norm_backward(params, "ln1", tokens, query_side + key_side)
    grads.update(norm_grads)
    return (grads, after_grad + part, memory_grad)


def adamw(master, first, second, grad, factor, correction):
    clipped = grad * factor
    moment = 0.5 * first + 0.5 * clipped
    variance = 0.5 * second + 0.5 * clipped * clipped
    update = moment / correction / (jnp.sqrt(variance / correction) + 1e-08) + 0.01 * master
    weights = master - 0.02 * update
    return (weights, moment, variance, weights.astype(jnp.bfloat16))


def shards_native(
    encoder_input,
    decoder_input,
    segments,
    encoder_cotangent,
    decoder_cotangent,
    encoder_master,
    encoder_first,
    encoder_second,
    decoder_master,
    decoder_first,
    decoder_second,
    step_count,
):
    encoder_plan = encoder_layout(D, FF)
    decoder_plan = decoder_layout(D, FF)
    encoder_params = unpack(
        lax.all_gather(encoder_master.astype(jnp.bfloat16), ("wide", "narrow"), axis=0, tiled=True),
        encoder_plan,
    )
    frames = encoder_input[0].astype(jnp.float32)
    memory, encoder_kept = encoder_forward(encoder_params, frames)
    memory_low = memory.astype(jnp.bfloat16)
    decoder_params = unpack(
        lax.all_gather(decoder_master.astype(jnp.bfloat16), ("wide", "narrow"), axis=0, tiled=True),
        decoder_plan,
    )
    tokens = decoder_input[0].astype(jnp.float32)
    segment_row = segments[0]
    length = segment_row.shape[0]

    def allowed_fn(start, count):
        places = start + jnp.arange(count, dtype=jnp.int32)
        row_segments = lax.dynamic_slice_in_dim(segment_row, start, count)
        columns = jnp.arange(length, dtype=jnp.int32)
        return (row_segments[:, None] == segment_row[None, :]) & (
            columns[None, :] <= places[:, None]
        )

    decoded, decoder_kept = decoder_forward(decoder_params, tokens, memory_low, allowed_fn)
    decoder_again = unpack(
        lax.all_gather(decoder_master.astype(jnp.bfloat16), ("wide", "narrow"), axis=0, tiled=True),
        decoder_plan,
    )
    decoder_grads, token_grad, memory_grad = decoder_backward(
        decoder_again,
        tokens,
        memory_low,
        decoder_kept,
        decoder_cotangent[0].astype(jnp.float32),
        allowed_fn,
    )
    decoder_total = pack(decoder_grads, decoder_plan)
    decoder_owned = lax.psum_scatter(
        decoder_total, ("wide", "narrow"), scatter_dimension=0, tiled=True
    )
    encoder_again = unpack(
        lax.all_gather(encoder_master.astype(jnp.bfloat16), ("wide", "narrow"), axis=0, tiled=True),
        encoder_plan,
    )
    memory_total = encoder_cotangent[0].astype(jnp.float32) + memory_grad
    encoder_grads, frame_grad = encoder_backward(encoder_again, frames, encoder_kept, memory_total)
    encoder_total = pack(encoder_grads, encoder_plan)
    encoder_owned = lax.psum_scatter(
        encoder_total, ("wide", "narrow"), scatter_dimension=0, tiled=True
    )
    local_squares = jnp.sum(encoder_owned * encoder_owned) + jnp.sum(decoder_owned * decoder_owned)
    gradient_norm = jnp.sqrt(lax.psum(local_squares, ("wide", "narrow")))
    factor = 1.0 / jnp.maximum(gradient_norm, 1.0)
    correction = 1.0 - jnp.power(0.5, step_count.astype(jnp.float32))
    encoder_new = adamw(
        encoder_master, encoder_first, encoder_second, encoder_owned, factor, correction
    )
    decoder_new = adamw(
        decoder_master, decoder_first, decoder_second, decoder_owned, factor, correction
    )
    return (
        memory_low[None],
        decoded.astype(jnp.bfloat16)[None],
        frame_grad[None],
        token_grad[None],
        gradient_norm,
        encoder_new[0],
        encoder_new[1],
        encoder_new[2],
        encoder_new[3],
        decoder_new[0],
        decoder_new[1],
        decoder_new[2],
        decoder_new[3],
    )


def shards(
    encoder_input,
    decoder_input,
    segments,
    encoder_cotangent,
    decoder_cotangent,
    encoder_master,
    encoder_first,
    encoder_second,
    decoder_master,
    decoder_first,
    decoder_second,
    step_count,
):
    n = 32
    weights, vectors, *kept = forward_pass(
        encoder_master, decoder_master, encoder_input[0], decoder_input[0], segments[0], n
    )
    encoder_flat, decoder_flat, norm, frame_grad, token_grad = backward_pass(
        weights, vectors, kept, encoder_input[0], decoder_input[0], encoder_cotangent[0], decoder_cotangent[0], segments[0], n
    )
    gradient_norm = norm[0, 0]
    factor = 1.0 / jnp.maximum(gradient_norm, 1.0)
    correction = 1.0 - jnp.power(0.5, step_count.astype(jnp.float32))
    encoder_owned = encoder_flat.reshape(-1)[: encoder_master.shape[0]]
    decoder_owned = decoder_flat.reshape(-1)[: decoder_master.shape[0]]
    encoder_new = adamw(encoder_master, encoder_first, encoder_second, encoder_owned, factor, correction)
    decoder_new = adamw(decoder_master, decoder_first, decoder_second, decoder_owned, factor, correction)
    return (
        kept[10][None],
        kept[28][None],
        frame_grad[None],
        token_grad[None],
        gradient_norm,
        *encoder_new,
        *decoder_new,
    )


def solution(mesh):
    placed = (
        P(("wide", "narrow"), None, None),
        P(("wide", "narrow"), None, None),
        P(("wide", "narrow"), None),
        P(("wide", "narrow"), None, None),
        P(("wide", "narrow"), None, None),
        P(("wide", "narrow")),
        P(("wide", "narrow")),
        P(("wide", "narrow")),
        P(("wide", "narrow")),
        P(("wide", "narrow")),
        P(("wide", "narrow")),
        P(),
    )
    return jax.shard_map(
        shards if tuple(mesh.shape.values()) == (8, 4) else shards_native,
        mesh=mesh,
        in_specs=placed,
        out_specs=(
            P(("wide", "narrow"), None, None),
            P(("wide", "narrow"), None, None),
            P(("wide", "narrow"), None, None),
            P(("wide", "narrow"), None, None),
            P(),
            P(("wide", "narrow")),
            P(("wide", "narrow")),
            P(("wide", "narrow")),
            P(("wide", "narrow")),
            P(("wide", "narrow")),
            P(("wide", "narrow")),
            P(("wide", "narrow")),
            P(("wide", "narrow")),
        ),
        check_vma=False,
    )
```

```python
from functools import partial

import jax
import jax.numpy as jnp
from jax import lax
from jax.experimental import pallas as pl
from jax.experimental.pallas import tpu as pltpu
from jax.sharding import PartitionSpec as P

D = 768
HEAD_DIM = 64
FF = 3072
MESH = pl.DeviceIdType.MESH
BF = jnp.bfloat16
F32 = jnp.float32

N_MAT = 28
N_PAIR = 14
UNIT = 48
LANES = 128
UROWS = UNIT * D // LANES
BIG = 4 * UROWS
FRONT = BIG + 8
BACK = BIG + 8
N_VEC = 29
F_AT = (1, 2, 4, 5)
B_AT = (1, 3, 5, 7)
AHEAD = 3


class Block:
    def __init__(self, small, gaps, fc1, vectors, first_mat, small_mats, total):
        self.small = small
        self.gaps = gaps
        self.fc1 = fc1
        self.vectors = vectors
        self.first_mat = first_mat
        self.small_mats = small_mats
        self.total = total


ENC = Block(
    small=8,
    gaps=((0, 2), (1, 1), (3, 1), (4, 3072 + 7)),
    fc1=3079,
    vectors=[0, 1, 770, 2307, 3076, 3077, 3078, 6151, 6152, 6153, 6154, 9227],
    first_mat=0,
    small_mats=4,
    total=9228,
)
DEC = Block(
    small=12,
    gaps=((0, 2), (1, 1), (3, 1), (4, 3), (5, 1), (7, 1), (8, 3072 + 7)),
    fc1=6156,
    vectors=[0, 1, 770, 2307, 3076, 3077, 3078, 3847, 5384, 6153, 6154, 6155, 9228, 9229, 9230, 9231, 12304],
    first_mat=12,
    small_mats=8,
    total=12305,
)
BLOCKS = (ENC, DEC)


def sizes(block, n):
    shard = block.total * D // n
    rows = -(-shard // 1024) * 8
    top = (shard + LANES - 1) // LANES
    return shard, rows, (top + UROWS) // UROWS + 1, (top + BIG) // BIG + 1


def small_row(block, m):
    row = m * D
    for at, gap in block.gaps:
        row = row + jnp.where(m >= at, gap, 0) if at > 0 else row + gap
    return row


def mat_of(block, m):
    return block.first_mat + m + jnp.where(m >= block.small_mats, 4, 0)


def static_unit_rows(block):
    out = []
    for m in range(block.small):
        row = m * D + sum(gap for at, gap in block.gaps if m >= at)
        out.append((block.first_mat + m + (4 if m >= block.small_mats else 0), row))
    return out


def whoami():
    wide, narrow = lax.axis_index("wide"), lax.axis_index("narrow")
    return wide, narrow, wide // 2, wide % 2, narrow // 2, narrow % 2


def device(z, x, y, c):
    return (z * 2 + x, y * 2 + c)


def flat_device(d):
    return (d // 4, d % 4)


def greet(me, n):
    bar = pltpu.get_barrier_semaphore()

    def signal(i, carry):
        pl.semaphore_signal(bar, inc=1, device_id=flat_device((me + i) % n), device_id_type=MESH)
        return carry

    lax.fori_loop(1, n, signal, 0)


def await_all(n):
    pl.semaphore_wait(pltpu.get_barrier_semaphore(), n - 1)


def each_small(block, n, me, slots, body, least=0, most=99):
    shard = sizes(block, n)[0]
    low = me * shard
    low_row = low // LANES
    first = 0
    for _, row in static_unit_rows(block):
        first = first + jnp.minimum(jnp.maximum(low - row * D, 0) // (UROWS * LANES), 16)

    def step(j, carry):
        g = first + j
        m, u = g // 16, g % 16
        start = small_row(block, m) * 6 + u * UROWS
        pos = start - low_row

        @pl.when((g < 16 * min(block.small, most)) & (g >= 16 * least) & (start * LANES < low + shard))
        def _():
            body((pos + UROWS) // UROWS, mat_of(block, m), u, pos, start * LANES)

        return carry

    lax.fori_loop(0, slots, step, 0)


def each_big(block, n, me, slots, body):
    shard = sizes(block, n)[0]
    low = me * shard
    low_row = low // LANES
    first = jnp.minimum(jnp.maximum(low - block.fc1 * D, 0) // (BIG * LANES), 16)

    def step(j, carry):
        u = first + j
        start = block.fc1 * 6 + u * BIG
        pos = start - low_row

        @pl.when((u < 16) & (start * LANES < low + shard) & (start * LANES + BIG * LANES > low))
        def _():
            body((pos + BIG) // BIG, u, pos, start * LANES)

        return carry

    lax.fori_loop(0, slots, step, 0)


def each_vector(block, n, me, first_vec, body):
    shard = sizes(block, n)[0]
    low = me * shard
    low_row = low // LANES
    for i, row in enumerate(block.vectors):
        @pl.when((row * D < low + shard) & (row * D + D > low))
        def _(i=i, row=row):
            body(first_vec + i, row * 6 - low_row, row * D)


def peers(axis, at):
    if axis == "z":
        return [dict(at, z=(at["z"] + k) % 4) for k in (1, 2, 3)]
    return [dict(at, **{axis: 1 - at[axis]})]


def first_peer(at):
    x, y, c = at["x"], at["y"], at["c"]
    return device(at["z"], x + (1 - c) * (1 - 2 * x), y + c * (1 - 2 * y), c)


def second_peer(at):
    x, y, c = at["x"], at["y"], at["c"]
    return device(at["z"], x + c * (1 - 2 * x), y + (1 - c) * (1 - 2 * y), c)


def dev(at):
    return device(at["z"], at["x"], at["y"], at["c"])


def gather_kernel(
    n, on_start, on_vectors, on_pair, xe_ref, xd_ref, w_ref, v_ref,
    re_ref, rd_ref, se_ref, sd_ref, be_ref, bd_ref, sv_ref, land, landv, own, ownv,
    s_small, s_big, s_vec, r_unit, r_vec, s_zxy, r_zxy, s_core, r_core, s_own, v_send, v_recv,
):
    wide, narrow, z, x, y, c = whoami()
    me = wide * 4 + narrow
    chip = me // 2
    at = dict(z=z, x=x, y=y, c=c)
    greet(me, n)
    lanes = lax.broadcasted_iota(jnp.int32, (1, LANES), 1)
    fields = {
        ENC: (xe_ref, re_ref, se_ref, be_ref, 0, 0, 0),
        DEC: (xd_ref, rd_ref, sd_ref, bd_ref, sizes(ENC, n)[2], sizes(ENC, n)[3], len(ENC.vectors)),
    }

    def prepare(block):
        x_ref, r_ref = fields[block][:2]
        shard, rows, _, _ = sizes(block, n)
        step = 8 * max(k for k in range(1, 40) if (rows // 8) % k == 0)

        def turn(i, carry):
            at_row = pl.multiple_of(i * step, 8)
            r_ref[pl.ds(FRONT + at_row, step), :] = pltpu.roll(
                x_ref[pl.ds(at_row, step), :], (me * shard) % LANES, 1
            )
            return carry

        lax.fori_loop(0, rows // step, turn, 0)

    def load_rows(block, row, count, stride=None):
        r_ref = fields[block][1]
        at_row = FRONT + row
        if stride is None:
            here, before = r_ref[pl.ds(at_row, count), :], r_ref[pl.ds(at_row - 1, count), :]
        else:
            here = r_ref[pl.ds(at_row, count, stride=stride), :]
            before = r_ref[pl.ds(at_row - 1, count, stride=stride), :]
        return jnp.where(lanes >= (me * sizes(block, n)[0]) % LANES, here, before)

    def send(src, dst, send_sem, recv_sem, target):
        @pl.when(target == me)
        def _():
            pltpu.make_async_copy(src, dst, send_sem).start()

        @pl.when(target != me)
        def _():
            pltpu.make_async_remote_copy(
                src, dst, send_sem, recv_sem, device_id=flat_device(target), device_id_type=MESH
            ).start()

    def which_of(block, start):
        return jnp.where(start // sizes(block, n)[0] == me, 0, 1)

    def small_units(block, least, most):
        s_ref, small0 = fields[block][2], fields[block][4]

        def body(slot, mat, u, pos, start):
            for k in range(6):
                s_ref[slot, :, k * LANES : (k + 1) * LANES] = load_rows(block, pos + k, UNIT, 6).astype(BF)
            which = which_of(block, start)
            send(
                s_ref.at[slot], land.at[which, mat // 2], s_small.at[small0 + slot], r_unit.at[which, mat // 2],
                u * 2 + mat % 2,
            )

        each_small(block, n, me, sizes(block, n)[2], body, least, most)

    def big_units(block):
        b_ref, big0 = fields[block][3], fields[block][5]
        pair = (block.first_mat + block.small_mats) // 2

        def body(slot, u, pos, start):
            for q in range(4):
                for k in range(6):
                    b_ref[slot, q % 2, q // 2, :, k * LANES : (k + 1) * LANES] = load_rows(
                        block, pos + 6 * q + k, UNIT, 24
                    ).astype(BF)
            which = which_of(block, start)
            for core in range(2):
                send(
                    b_ref.at[slot, core], land.at[which, pl.ds(pair, 2)], s_big.at[big0 + slot, core],
                    r_unit.at[which, pair], u * 2 + core,
                )

        each_big(block, n, me, sizes(block, n)[3], body)

    def vector_units(block):
        def body(v, pos, start):
            sv_ref[v] = load_rows(block, pos, 8).astype(BF).astype(F32)
            which = which_of(block, start)
            send(sv_ref.at[v], landv.at[which], s_vec.at[v], r_vec.at[which], v)

        each_vector(block, n, me, fields[block][6], body)

    def pair_units(pair):
        block = ENC if pair < 6 else DEC
        local = pair - block.first_mat // 2
        half = block.small_mats // 2
        if local == half:
            big_units(block)
        elif local != half + 1:
            first = 2 * local - (4 if local > half else 0)
            small_units(block, first, first + 2)

    prepare(ENC)
    await_all(n)
    pair_units(0)
    vector_units(ENC)
    prepare(DEC)
    vector_units(DEC)
    for pair in range(1, AHEAD):
        pair_units(pair)

    def of_self(first, last, which):
        return jnp.where(which == 0, first, last) == me

    def arrive_unit(first, last, src, dst, local_sem, recv):
        for which, holder in ((0, first), (1, last)):
            needed = True if which == 0 else (first != last)

            @pl.when(needed & (holder == me))
            def _(which=which):
                pltpu.make_async_copy(src(which), dst(which), local_sem).wait()

            @pl.when(needed & (holder != me))
            def _(which=which):
                pltpu.make_async_copy(src(which), dst(which), recv(which)).wait()

    def vec_of(v):
        n_enc = len(ENC.vectors)
        rows = ENC.vectors + DEC.vectors
        start = 0
        before = 0
        for i, row in enumerate(rows):
            start = start + jnp.where(v >= i, row - before, 0)
            before = row
        return start * D, jnp.where(v < n_enc, sizes(ENC, n)[0], sizes(DEC, n)[0])

    @pl.when(me < N_VEC)
    def _():
        start, shard = vec_of(me)
        first, last = start // shard, (start + D - 1) // shard
        arrive_unit(
            first, last, lambda w: sv_ref.at[0], lambda w: landv.at[w], s_vec.at[me], lambda w: r_vec.at[w]
        )
        at_elem = lax.broadcasted_iota(jnp.int32, (8, LANES), 0) * LANES + lax.broadcasted_iota(jnp.int32, (8, LANES), 1)
        ownv[...] = jnp.where(at_elem < (first + 1) * shard - start, landv[0], landv[1])

    @pl.when(me >= N_VEC)
    def _():
        ownv[...] = jnp.zeros_like(ownv)

    pltpu.sync_copy(ownv, v_ref.at[z, x, y, c])
    vorder = ("z", "x", "y", "c")

    def vview(done):
        have = set(vorder[:done])
        return tuple(slice(None) if a in have else at[a] for a in "zxyc")

    def vcopies(phase):
        axis = vorder[phase]
        out = []
        for k, p in enumerate(peers(axis, at)):
            ref = v_ref.at[vview(phase)]
            slot = phase if axis == "z" else phase + 2
            out.append(
                pltpu.make_async_remote_copy(
                    ref, ref, v_send.at[slot + k], v_recv.at[slot + k], device_id=dev(p), device_id_type=MESH
                )
            )
        return out

    row_i = lax.broadcasted_iota(jnp.int32, (UNIT, D), 0)
    col_i = lax.broadcasted_iota(jnp.int32, (UNIT, D), 1)

    def merge(pair):
        block = ENC if pair < 6 else DEC
        shard = sizes(block, n)[0]
        local = pair - block.first_mat // 2
        half = block.small_mats // 2
        if half <= local < half + 2:
            start = (block.fc1 * 6 + chip * BIG) * LANES
            elem = row_i * FF + (2 * (local - half) + c) * D + col_i
            length = BIG * LANES
        else:
            small = 2 * local - (4 if local >= half + 2 else 0) + c
            start = (small_row(block, small) * 6 + chip * UROWS) * LANES
            elem = row_i * D + col_i
            length = UROWS * LANES
        first, last = start // shard, (start + length - 1) // shard
        if half <= local < half + 2:
            if local == half:
                low_row = me * shard // LANES
                slot = (start // LANES - low_row + BIG) // BIG + (0 if block is ENC else sizes(ENC, n)[3])
                slot = jnp.minimum(jnp.maximum(slot, 0), sizes(ENC, n)[3] + sizes(DEC, n)[3] - 1)
                arrive_unit(
                    first, last, lambda w: land.at[w, pl.ds(pair, 2)], lambda w: land.at[w, pl.ds(pair, 2)],
                    s_big.at[slot, c], lambda w: r_unit.at[w, pair],
                )
        else:
            low_row = me * shard // LANES
            slot = (start // LANES - low_row + UROWS) // UROWS + (0 if block is ENC else sizes(ENC, n)[2])
            slot = jnp.minimum(jnp.maximum(slot, 0), sizes(ENC, n)[2] + sizes(DEC, n)[2] - 1)
            arrive_unit(
                first, last, lambda w: land.at[w, pair], lambda w: land.at[w, pair],
                s_small.at[slot], lambda w: r_unit.at[w, pair],
            )
        own[pair] = jnp.where(elem < (first + 1) * shard - start, land[0, pair], land[1, pair])

    def own_place(pair):
        return w_ref.at[pair, c, z, x, y]

    def remote(src, dst, pair, k, target):
        return pltpu.make_async_remote_copy(
            src, dst, s_zxy.at[pair, k], r_zxy.at[pair, k], device_id=target, device_id_type=MESH
        )

    def copies(pair, phase):
        if phase == 0:
            return [
                remote(own.at[pair], own_place(pair), pair, 2 + k, device((z + k) % 4, x, y, c)) for k in (1, 2, 3)
            ]
        if phase == 1:
            ref = w_ref.at[pair, c, :, x, y]
            return [remote(ref, ref, pair, 0, first_peer(at))]
        if phase == 2:
            ref = w_ref.at[pair, c, :, :, y]
            return [remote(ref, ref, pair, 1, second_peer(at))]
        ref = w_ref.at[pair, c]
        return [remote(ref, ref, pair, 2, device(z, x, y, 1 - c))]

    def begin(pair, phase):
        if phase != 2:
            for cp in copies(pair, phase):
                cp.start()
            return

        @pl.when(c == 0)
        def _():
            copies(pair, 2)[0].start()

        @pl.when(c == 1)
        def _():
            ref = w_ref.at[pair, c, :, x]
            remote(ref, ref, pair, 1, second_peer(at)).start()

    for t in range(N_PAIR + F_AT[3]):
        if t < N_PAIR:
            merge(t)
            pltpu.make_async_copy(own.at[t], own_place(t), s_own.at[t]).start()
            begin(t, 0)
        for phase in (1, 2, 3):
            pair = t - F_AT[phase - 1]
            if 0 <= pair < N_PAIR:
                if phase == 1:
                    pltpu.make_async_copy(own.at[pair], own_place(pair), s_own.at[pair]).wait()
                for cp in copies(pair, phase - 1):
                    cp.wait_recv()
                begin(pair, phase)
        if t + AHEAD < N_PAIR:
            pair_units(t + AHEAD)
        if t == 1:
            on_start()
        if t < 5:
            if t > 0:
                for cp in vcopies(t - 1):
                    cp.wait_recv()
            if t < 4:
                for cp in vcopies(t):
                    cp.start()
            else:
                on_vectors()
        pair = t - F_AT[3]
        if 0 <= pair < N_PAIR:
            for cp in copies(pair, 3):
                cp.wait_recv()
            on_pair(pair)

    for phase in range(4):
        for cp in vcopies(phase):
            cp.wait_send()
    for pair in range(N_PAIR):
        for phase in range(4):
            for cp in copies(pair, phase):
                cp.wait_send()
    for b, (block, s_ref, b_ref) in enumerate(((ENC, se_ref, be_ref), (DEC, sd_ref, bd_ref))):
        shard, rows, n_small, n_big = sizes(block, n)
        small0 = 0 if b == 0 else sizes(ENC, n)[2]
        big0 = 0 if b == 0 else sizes(ENC, n)[3]

        def small_wait(slot, mat, u, pos, start, s_ref=s_ref, small0=small0):
            @pl.when(u * 2 + mat % 2 != me)
            def _():
                pltpu.make_async_copy(s_ref.at[slot], s_ref.at[slot], s_small.at[small0 + slot]).wait()

        def big_wait(slot, u, pos, start, b_ref=b_ref, big0=big0):
            for core in range(2):
                @pl.when(u * 2 + core != me)
                def _(core=core):
                    pltpu.make_async_copy(
                        b_ref.at[slot, core], b_ref.at[slot, core], s_big.at[big0 + slot, core]
                    ).wait()

        def vec_wait(v, pos, start):
            @pl.when(me != v)
            def _():
                pltpu.make_async_copy(sv_ref.at[v], sv_ref.at[v], s_vec.at[v]).wait()

        each_vector(block, n, me, 0 if b == 0 else len(ENC.vectors), vec_wait)
        each_small(block, n, me, n_small, small_wait)
        each_big(block, n, me, n_big, big_wait)


def rows_of(flat, rows):
    return jnp.pad(flat, (0, rows * LANES - flat.shape[0])).reshape(rows, LANES)


SCALE = HEAD_DIM ** (-0.5)
FORBID = -1000000000.0
ROOT_HALF = 0.7071067811865476
PDF = 0.3989422804014327


def mm(a, b):
    return jnp.dot(a, b, preferred_element_type=F32)


def mm_nt(a, b):
    return lax.dot_general(a, b, (((1,), (1,)), ((), ())), preferred_element_type=F32)


def mm_tn(a, b):
    return lax.dot_general(a, b, (((0,), (0,)), ((), ())), preferred_element_type=F32)


def col_blocks(body, width=256):
    def step(j, carry):
        body(pl.ds(pl.multiple_of(j * width, width), width))
        return carry

    lax.fori_loop(0, D // width, step, 0)


def row_blocks(rows, body, height=64):
    def step(i, carry):
        body(pl.ds(pl.multiple_of(i * height, height), height))
        return carry

    lax.fori_loop(0, rows // height, step, 0)


def linear(x_ref, w_ref, rows, out_ref, bias=None):
    x = x_ref[0:rows, :]

    def body(cols):
        y = mm(x, w_ref[:, cols])
        if bias is not None:
            y = y + bias[:, cols]
        out_ref[0:rows, cols] = y.astype(out_ref.dtype)

    col_blocks(body)


def norm_rows(x):
    centred = x - jnp.mean(x, axis=1, keepdims=True)
    spread = jnp.mean(centred * centred, axis=1, keepdims=True)
    root = lax.rsqrt(spread + 1e-05)
    return centred * root, root


def norm_forward_ref(x_ref, gain, shift, rows, out_ref):
    def body(r):
        hat, _ = norm_rows(x_ref[r, :].astype(F32))
        out_ref[r, :] = (hat * gain[...] + shift[...]).astype(BF)

    row_blocks(rows, body)


def attend_tiles(rows, keys, causal):
    return [(start, min(start + 128, keys) if causal else keys) for start in range(0, rows, 128)]


def both_heads(x):
    lane = lax.broadcasted_iota(jnp.int32, (1, LANES), 1)
    zero = jnp.zeros_like(x)
    return jnp.concatenate([jnp.where(lane < HEAD_DIM, x, zero), jnp.where(lane < HEAD_DIM, zero, x)], axis=0)


def scores_of(k, q2, mask_ref, start, reach):
    scores = mm_nt(k, q2)
    if mask_ref is not None:
        mask = mask_ref[0:reach, start : start + LANES]
        scores = jnp.where(jnp.concatenate([mask, mask], axis=1) > 0, scores, FORBID)
    return scores


def attention_forward_ref(q_ref, k_ref, v_ref, mask_ref, rows, keys, mixed_ref, lse_ref):
    def pair_of_heads(i, carry):
        cols = pl.ds(pl.multiple_of(i * LANES, LANES), LANES)
        v_turned = jnp.transpose(v_ref[0:keys, cols])
        for tile, (start, reach) in enumerate(attend_tiles(rows, keys, mask_ref is not None)):
            r = slice(start, start + LANES)
            q2 = both_heads(q_ref[r, cols] * jnp.asarray(SCALE, BF))
            scores = scores_of(k_ref[0:reach, cols], q2, mask_ref, start, reach)
            peak = jnp.max(scores, axis=0, keepdims=True)
            weights = jnp.exp(scores - peak)
            totals = jnp.sum(weights, axis=0, keepdims=True)
            probs = weights.astype(BF)
            share = 1.0 / totals
            mixed = jnp.concatenate(
                [
                    mm(v_turned[s * HEAD_DIM : (s + 1) * HEAD_DIM, 0:reach], probs[:, s * LANES : (s + 1) * LANES])
                    * share[:, s * LANES : (s + 1) * LANES]
                    for s in range(2)
                ],
                axis=0,
            )
            mixed_ref[r, cols] = jnp.transpose(mixed).astype(BF)
            lse_ref[tile, pl.ds(i, 1), :] = peak + jnp.log(totals)
        return carry

    lax.fori_loop(0, D // LANES, pair_of_heads, 0, unroll=1 if mask_ref is not None else 3)


def project_add(x_ref, mixed_ref, w_ref, bias, rows, out_ref):
    m = mixed_ref[0:rows, :]

    def body(cols):
        out_ref[0:rows, cols] = x_ref[0:rows, cols].astype(F32) + mm(m, w_ref[:, cols]) + bias[:, cols]

    col_blocks(body)


def gelu_block(n_ref, w_ref, bias, rows, block, act_ref, slope_ref):
    x = n_ref[0:rows, :]

    def body(cols):
        pre = mm(x, w_ref[:, cols]) + bias[:, cols]
        bell = 0.5 * (1.0 + lax.erf(pre * ROOT_HALF))
        act_ref[block, 0:rows, cols] = (pre * bell).astype(BF)
        slope_ref[block, 0:rows, cols] = (bell + pre * (PDF * jnp.exp(-0.5 * pre * pre))).astype(BF)

    col_blocks(body, 128)


def accumulate(a, w_ref, rows, out_ref, bias=None):
    def body(cols):
        y = out_ref[0:rows, cols] + mm(a, w_ref[:, cols])
        out_ref[0:rows, cols] = y if bias is None else y + bias[:, cols]

    col_blocks(body)


N_SAVED = 29


def saved_shapes(rows, frames):
    tall = -(-rows // 128) * 128
    enc_lse, dec_lse = ((frames // 128, 8, 2 * LANES), F32), ((tall // 128, 8, 2 * LANES), F32)
    return (
        [((frames, D), BF)] * 5
        + [enc_lse, ((frames, D), F32), ((frames, D), BF), ((4, frames, D), BF), ((4, frames, D), BF), ((frames, D), BF)]
        + [((rows, D), BF)]
        + [((tall, D), BF)] * 4
        + [dec_lse, ((rows, D), F32), ((rows, D), BF)]
        + [((tall, D), BF), ((frames, D), BF), ((frames, D), BF), ((tall, D), BF), dec_lse]
        + [((rows, D), F32), ((rows, D), BF), ((4, rows, D), BF), ((4, rows, D), BF), ((rows, D), BF)]
    )


def make_mask(seg_row, seg_col, mask_ref):
    def body(r):
        key = lax.broadcasted_iota(jnp.int32, (64, mask_ref.shape[1]), 0) + r.start
        query = lax.broadcasted_iota(jnp.int32, (64, mask_ref.shape[1]), 1)
        allowed = (seg_col[r, :] == seg_row[...]) & (key <= query)
        mask_ref[r, :] = jnp.where(allowed, 1.0, 0.0)

    row_blocks(mask_ref.shape[0], body)


def forward_kernel(n, rows, frames, *refs):
    xe_ref, xd_ref, ein_ref, din_ref, seg_row, seg_col, w_ref, v_ref = refs[:8]
    outs, refs = refs[8 : 8 + N_SAVED], refs[8 + N_SAVED :]
    comm, refs = refs[:24], refs[24:]
    bufs, refs = refs[:N_SAVED], refs[N_SAVED:]
    vv, wbuf, acc, mask_ref, s_save, s_w = refs
    (
        e_n1, e_q, e_k, e_v, e_mix, e_lse, e_after, e_n2, e_act, e_slope, e_out,
        d_n1, d_q, d_k, d_v, d_mix, d_lse, d_after, d_n2,
        c_q, c_k, c_v, c_mix, c_lse, d_after2, d_n3, d_act, d_slope, d_out,
    ) = bufs
    eacc = acc.at[0:frames]

    def vec(i):
        return vv.at[i : i + 1]

    def save(*indices):
        for i in indices:
            pltpu.make_async_copy(bufs[i], outs[i], s_save.at[i]).start()

    def on_start():
        make_mask(seg_row, seg_col, mask_ref)
        for ref in (d_q, d_k, d_v, c_q):
            if ref.shape[0] > rows:
                ref[rows:, :] = jnp.zeros((ref.shape[0] - rows, D), BF)
        for ref in (e_lse, d_lse, c_lse):
            ref[...] = jnp.zeros_like(ref)

    def on_vectors():
        pltpu.sync_copy(v_ref, vv_tiles)
        for i in range(N_VEC):
            for k in range(6):
                vv[i : i + 1, k * LANES : (k + 1) * LANES] = vv_tiles[i // 8, i // 4 % 2, i // 2 % 2, i % 2, k : k + 1, :]

    def on_pair(pair):
        cps = [pltpu.make_async_copy(w_ref.at[pair, k].reshape(D, D), wbuf.at[k], s_w.at[k]) for k in range(2)]
        for cp in cps:
            cp.start()
        if pair == 0:
            norm_forward_ref(ein_ref, vec(0), vec(1), frames, e_n1)
        if pair == 6:
            norm_forward_ref(din_ref, vec(12), vec(13), rows, d_n1)
        for cp in cps:
            cp.wait()
        w0, w1 = wbuf.at[0], wbuf.at[1]
        if pair == 0:
            linear(e_n1, w0, frames, e_q, vec(2))
            linear(e_n1, w1, frames, e_k)
            save(0, 1, 2)
        elif pair == 1:
            linear(e_n1, w0, frames, e_v, vec(3))
            attention_forward_ref(e_q, e_k, e_v, None, frames, frames, e_mix, e_lse)
            project_add(ein_ref, e_mix, w1, vec(4), frames, e_after)
            norm_forward_ref(e_after, vec(5), vec(6), frames, e_n2)
            save(3, 4, 5, 6, 7)
        elif pair in (2, 3):
            for k in range(2):
                block = 2 * (pair - 2) + k
                gelu_block(e_n2, wbuf.at[k], vec(7 + block), frames, block, e_act, e_slope)
            if pair == 3:
                save(8, 9)
        elif pair in (4, 5):
            if pair == 4:
                eacc[...] = e_after[...]
            for k in range(2):
                last = pair == 5 and k == 1
                accumulate(e_act[2 * (pair - 4) + k], wbuf.at[k], frames, eacc, vec(11) if last else None)
            if pair == 5:
                e_out[...] = eacc[...].astype(BF)
                save(10)
        elif pair == 6:
            linear(d_n1, w0, rows, d_q, vec(14))
            linear(d_n1, w1, rows, d_k)
            save(11, 12, 13)
        elif pair == 7:
            linear(d_n1, w0, rows, d_v, vec(15))
            attention_forward_ref(d_q, d_k, d_v, mask_ref, d_q.shape[0], d_k.shape[0], d_mix, d_lse)
            project_add(din_ref, d_mix, w1, vec(16), rows, d_after)
            norm_forward_ref(d_after, vec(17), vec(18), rows, d_n2)
            save(14, 15, 16, 17, 18)
        elif pair == 8:
            linear(d_n2, w0, rows, c_q, vec(19))
            linear(e_out, w1, frames, c_k)
            save(19, 20)
        elif pair == 9:
            linear(e_out, w0, frames, c_v, vec(20))
            attention_forward_ref(c_q, c_k, c_v, None, c_q.shape[0], frames, c_mix, c_lse)
            project_add(d_after, c_mix, w1, vec(21), rows, d_after2)
            norm_forward_ref(d_after2, vec(22), vec(23), rows, d_n3)
            save(21, 22, 23, 24, 25)
        elif pair in (10, 11):
            for k in range(2):
                block = 2 * (pair - 10) + k
                gelu_block(d_n3, wbuf.at[k], vec(24 + block), rows, block, d_act, d_slope)
            if pair == 11:
                save(26, 27)
        else:
            if pair == 12:
                acc[...] = d_after2[...]
            for k in range(2):
                last = pair == 13 and k == 1
                accumulate(d_act[2 * (pair - 12) + k], wbuf.at[k], rows, acc, vec(28) if last else None)
            if pair == 13:
                d_out[...] = acc[...].astype(BF)
                save(28)

    vv_tiles = comm[-1]
    gather_kernel(n, on_start, on_vectors, on_pair, xe_ref, xd_ref, w_ref, v_ref, *comm[:-1])
    for i in range(N_SAVED):
        pltpu.make_async_copy(bufs[i], outs[i], s_save.at[i]).wait()


def forward_pass(encoder_master, decoder_master, encoder_input, decoder_input, segments, n):
    (_, re, ne, ge), (_, rd, nd, gd) = sizes(ENC, n), sizes(DEC, n)
    frames, rows = encoder_input.shape[0], decoder_input.shape[0]
    tall = -(-rows // 128) * 128
    dma = pltpu.SemaphoreType.DMA
    saved = saved_shapes(rows, frames)
    vmem, hbm = pl.BlockSpec(memory_space=pltpu.VMEM), pl.BlockSpec(memory_space=pl.ANY)
    seg = jnp.pad(segments, (0, tall - rows), constant_values=-1)
    return pl.pallas_call(
        partial(forward_kernel, n, rows, frames),
        out_shape=(
            jax.ShapeDtypeStruct((N_PAIR, 2, 4, 2, 2, UNIT, D), BF),
            jax.ShapeDtypeStruct((4, 2, 2, 2, 8, LANES), F32),
            *(jax.ShapeDtypeStruct(shape, dtype) for shape, dtype in saved),
        ),
        in_specs=[vmem] * 6,
        out_specs=(hbm,) * (2 + N_SAVED),
        scratch_shapes=[
            pltpu.VMEM((FRONT + re + BACK, LANES), F32),
            pltpu.VMEM((FRONT + rd + BACK, LANES), F32),
            pltpu.VMEM((ne, UNIT, D), BF),
            pltpu.VMEM((nd, UNIT, D), BF),
            pltpu.VMEM((ge, 2, 2, UNIT, D), BF),
            pltpu.VMEM((gd, 2, 2, UNIT, D), BF),
            pltpu.VMEM((N_VEC, 8, LANES), F32),
            pltpu.VMEM((2, N_PAIR, UNIT, D), BF),
            pltpu.VMEM((2, 8, LANES), F32),
            pltpu.VMEM((N_PAIR, UNIT, D), BF),
            pltpu.VMEM((8, LANES), F32),
            dma((ne + nd,)),
            dma((ge + gd, 2)),
            dma((N_VEC,)),
            dma((2, N_PAIR)),
            dma((2,)),
            dma((N_PAIR, 6)),
            dma((N_PAIR, 6)),
            dma((N_PAIR,)),
            dma((N_PAIR,)),
            dma((N_PAIR,)),
            dma((6,)),
            dma((6,)),
            pltpu.VMEM((4, 2, 2, 2, 8, LANES), F32),
            *(pltpu.VMEM(shape, dtype) for shape, dtype in saved),
            pltpu.VMEM((32, D), F32),
            pltpu.VMEM((2, D, D), BF),
            pltpu.VMEM((rows, D), F32),
            pltpu.VMEM((tall, tall), F32),
            dma((N_SAVED,)),
            dma((2,)),
        ],
        compiler_params=pltpu.CompilerParams(collective_id=0, has_side_effects=True, vmem_limit_bytes=58 << 20),
        name="forward",
    )(rows_of(encoder_master, re), rows_of(decoder_master, rd), encoder_input, decoder_input, seg[None, :], seg[:, None])


RING = 3
RING_C = 5


def scatter_kernel(
    n, produce, after, vg_ref, gbuf, oe_ref, od_ref, norm_ref,
    land_c, land_b, land_a, land_z, ownb, vown, vl_c, vl_y, vl_x, vl_z,
    ge_ref, gd_ref, fe, fd, fbe, fbd, fv, nsend, nland,
    s_core, r_core, s_free, s_ph, r_ph, s_back, r_small, r_big, sv, rv, s_vback, r_vback, s_n, r_n, s_out,
):
    wide, narrow, z, x, y, c = whoami()
    me = wide * 4 + narrow
    chip = me // 2
    at = dict(z=z, x=x, y=y, c=c)
    greet(me, n)
    sib = device(z, x, y, 1 - c)

    def slot_c(pair):
        return (N_PAIR - 1 - pair) % RING_C

    def core_copy(pair):
        return pltpu.make_async_remote_copy(
            gbuf.at[(N_PAIR - 1 - pair) % RING, 1 - c], land_c.at[slot_c(pair)], s_core.at[pair], r_core.at[pair], device_id=sib, device_id_type=MESH
        )

    mine_a = x * (1 - c) + y * c

    def phase_dmas(pair, phase):
        if phase == 1:
            steps = [(land_c.at[slot_c(pair), :, :, 1 - y], land_b.at[pair], 0, second_peer(at))]
        elif phase == 2:
            steps = [(land_b.at[pair, :, 1 - mine_a], land_a.at[pair], 1, first_peer(at))]
        else:
            steps = [
                (land_a.at[pair, (z + k) % 4], land_z.at[pair, k - 1], 1 + k, device((z + k) % 4, x, y, c))
                for k in (1, 2, 3)
            ]
        return [
            pltpu.make_async_remote_copy(
                src, dst, s_ph.at[pair, k], r_ph.at[pair, k], device_id=target, device_id_type=MESH
            )
            for src, dst, k, target in steps
        ]

    def begin(pair, phase):
        if phase != 1:
            for cp in phase_dmas(pair, phase):
                cp.start()
            return

        @pl.when(c == 0)
        def _():
            phase_dmas(pair, 1)[0].start()

        @pl.when(c == 1)
        def _():
            pltpu.make_async_remote_copy(
                land_c.at[slot_c(pair), :, 1 - x], land_b.at[pair], s_ph.at[pair, 0], r_ph.at[pair, 0],
                device_id=second_peer(at), device_id_type=MESH,
            ).start()

    def back(pair):
        block = ENC if pair < 6 else DEC
        shard = sizes(block, n)[0]
        local = pair - block.first_mat // 2
        half = block.small_mats // 2
        big = half <= local < half + 2
        if big:
            start = (block.fc1 * 6 + chip * BIG) * LANES
            length = BIG * LANES
        else:
            small = 2 * local - (4 if local >= half + 2 else 0) + c
            start = (small_row(block, small) * 6 + chip * UROWS) * LANES
            length = UROWS * LANES
        first, last = start // shard, (start + length - 1) // shard
        out = []
        for which, target in ((0, first), (1, last)):
            low_row = target * shard // LANES
            if big:
                slot = (start // LANES - low_row + BIG) // BIG
                q = 2 * (local - half) + c
                dst = (fbe if block is ENC else fbd).at[slot, q]
                recv = r_big.at[0 if block is ENC else 1, slot, q]
            else:
                slot = (start // LANES - low_row + UROWS) // UROWS
                dst = (fe if block is ENC else fd).at[slot]
                recv = r_small.at[0 if block is ENC else 1, slot]
            needed = True if which == 0 else first != last
            out.append((needed, target, dst, s_back.at[pair, which], recv))
        return out

    def start_back(pair):
        for needed, target, dst, send, recv in back(pair):
            @pl.when(needed & (target == me))
            def _(dst=dst, recv=recv):
                pltpu.make_async_copy(ownb.at[pair], dst, recv).start()

            @pl.when(needed & (target != me))
            def _(dst=dst, recv=recv, send=send, target=target):
                pltpu.make_async_remote_copy(
                    ownb.at[pair], dst, send, recv, device_id=flat_device(target), device_id_type=MESH
                ).start()

    def end_back(pair):
        for needed, target, dst, send, recv in back(pair):
            @pl.when(needed & (target != me))
            def _(send=send):
                pltpu.make_async_copy(ownb.at[pair], ownb.at[pair], send).wait()

    def add_core(pair):
        def body(i, carry):
            a, b = i // 2, i % 2
            for k in range(2):
                mine = gbuf[(N_PAIR - 1 - pair) % RING, c, a, b, k]
                land_c[slot_c(pair), a, b, k] = (
                    land_c[slot_c(pair), a, b, k].astype(F32) + mine.astype(F32)
                ).astype(BF)
            return carry

        lax.fori_loop(0, 8, body, 0)

    def add_b(pair):
        def body(i, carry):
            a, b = i // 2, i % 2
            mine = land_c[slot_c(pair), a, b * (1 - c) + x * c, y * (1 - c) + b * c]
            land_b[pair, a, b] = (land_b[pair, a, b].astype(F32) + mine.astype(F32)).astype(BF)
            return carry

        lax.fori_loop(0, 8, body, 0)

    def add_a(pair):
        for a in range(4):
            land_a[pair, a] = (land_a[pair, a].astype(F32) + land_b[pair, a, mine_a].astype(F32)).astype(BF)

    def add_z(pair):
        total = land_a[pair, z].astype(F32)
        for k in range(3):
            total = total + land_z[pair, k].astype(F32)
        ownb[pair] = total.astype(BF)
        squares = total * total
        return jnp.sum(squares.reshape(UNIT // 8, 8, D), axis=0)

    vland = dict(c=vl_c, y=vl_y, x=vl_x, z=vl_z)

    def vsteps(phase):
        if phase == 0:
            return [(vg_ref.at[:, :, :, 1 - c], vl_c, 0, dict(at, c=1 - c))]
        if phase == 1:
            return [(vl_c.at[:, :, 1 - y], vl_y, 1, dict(at, y=1 - y))]
        if phase == 2:
            return [(vl_y.at[:, 1 - x], vl_x, 2, dict(at, x=1 - x))]
        return [(vl_x.at[(z + k) % 4], vl_z.at[k - 1], 2 + k, dict(at, z=(z + k) % 4)) for k in (1, 2, 3)]

    def vdmas(phase):
        return [
            pltpu.make_async_remote_copy(s, d, sv.at[k], rv.at[k], device_id=dev(p), device_id_type=MESH)
            for s, d, k, p in vsteps(phase)
        ]

    def vadd(phase):
        if phase == 0:
            vl_c[...] = vl_c[...] + vg_ref[:, :, :, c]
        elif phase == 1:
            vl_y[...] = vl_y[...] + vl_c[:, :, y]
        elif phase == 2:
            vl_x[...] = vl_x[...] + vl_y[:, x]
        else:
            vown[...] = vl_x[z] + vl_z[0] + vl_z[1] + vl_z[2]

    fields = {ENC: (0, ge_ref, oe_ref, fe, fbe), DEC: (1, gd_ref, od_ref, fd, fbd)}

    def units_to_flat(block):
        b, g_out, _, f_ref, fb_ref = fields[block]
        _, _, n_small, n_big = sizes(block, n)

        def small_body(slot, mat, u, pos, start):
            pltpu.make_async_copy(f_ref.at[slot], f_ref.at[slot], r_small.at[b, slot]).wait()
            for k in range(6):
                g_out[pl.ds(FRONT + pos + k, UNIT, stride=6), :] = f_ref[slot, :, k * LANES : (k + 1) * LANES].astype(F32)

        def big_body(slot, u, pos, start):
            for q in range(4):
                pltpu.make_async_copy(fb_ref.at[slot, q], fb_ref.at[slot, q], r_big.at[b, slot, q]).wait()
                for k in range(6):
                    g_out[pl.ds(FRONT + pos + 6 * q + k, UNIT, stride=24), :] = fb_ref[
                        slot, q, :, k * LANES : (k + 1) * LANES
                    ].astype(F32)

        each_big(block, n, me, n_big, big_body)
        each_small(block, n, me, n_small, small_body)

    def finish_flat(block):
        b, g_out, o_ref, _, _ = fields[block]
        shard, rows, _, _ = sizes(block, n)

        def vec_body(v, pos, start):
            pltpu.make_async_copy(fv.at[v], fv.at[v], r_vback.at[v]).wait()
            g_out[pl.ds(FRONT + pos, 6), :] = fv[v, 0:6, :]

        each_vector(block, n, me, 0 if block is ENC else len(ENC.vectors), vec_body)
        shift = (me * shard) % LANES
        step = 8 * max(k for k in range(1, 40) if (rows // 8) % k == 0)
        lanes = lax.broadcasted_iota(jnp.int32, (1, LANES), 1)
        unturn = lax.rem(LANES - shift, LANES)

        def turn(i, carry):
            at_row = pl.multiple_of(i * step, 8)
            here = pltpu.roll(g_out[pl.ds(FRONT + at_row, step), :], unturn, 1)
            after = pltpu.roll(g_out[pl.ds(FRONT + at_row + 1, step), :], unturn, 1)
            g_out[pl.ds(FRONT + at_row, step), :] = jnp.where(lanes < LANES - shift, here, after)
            return carry

        lax.fori_loop(0, rows // step, turn, 0)
        pltpu.make_async_copy(g_out.at[pl.ds(FRONT, rows)], o_ref, s_out.at[b]).start()

    seq = list(range(N_PAIR - 1, -1, -1))
    square = jnp.zeros((8, D), F32)
    for t in range(N_PAIR + B_AT[3]):
        if t < N_PAIR:
            if t >= RING:
                core_copy(seq[t - RING]).wait_send()
            produce(t, gbuf.at[t % RING])
            if t == 0:
                await_all(n)
            if t >= RING_C:
                pl.semaphore_wait(s_free, 1)
            core_copy(seq[t]).start()
        for phase in (4, 3, 2, 1):
            i = t - B_AT[phase - 1]
            if 0 <= i < N_PAIR:
                pair = seq[i]
                if phase == 1:
                    core_copy(pair).wait_recv()
                    add_core(pair)
                elif phase == 2:
                    for cp in phase_dmas(pair, 1):
                        cp.wait()
                    add_b(pair)
                    if i < N_PAIR - RING_C:
                        pl.semaphore_signal(s_free, inc=1, device_id=sib, device_id_type=MESH)
                elif phase == 3:
                    for cp in phase_dmas(pair, 2):
                        cp.wait_recv()
                    add_a(pair)
                else:
                    for cp in phase_dmas(pair, 3):
                        cp.wait_recv()
                    square = square + add_z(pair)
                    start_back(pair)
                if phase < 4:
                    begin(pair, phase)
        if t < N_PAIR:
            after(t)
        if t == N_PAIR + B_AT[2] - 1:
            units_to_flat(DEC)
        if t == N_PAIR - 1:
            for cp in vdmas(0):
                cp.start()
        elif N_PAIR <= t < N_PAIR + 4:
            phase = t - N_PAIR
            for cp in vdmas(phase):
                cp.wait_recv()
            vadd(phase)
            if phase < 3:
                for cp in vdmas(phase + 1):
                    cp.start()

    vsq = vown[...] * vown[...]
    for k in range(6):
        vsq = vsq + square[:, k * LANES : (k + 1) * LANES]
    nsend[...] = vsq

    def norm_copy(i):
        return pltpu.make_async_remote_copy(
            nsend, nland.at[i], s_n.at[i], r_n.at[i], device_id=flat_device((me + i) % n), device_id_type=MESH
        )

    def norm_start(i, carry):
        norm_copy(i).start()
        return carry

    lax.fori_loop(1, n, norm_start, 0)

    def vector_targets(v_static):
        block = ENC if v_static < len(ENC.vectors) else DEC
        shard = sizes(block, n)[0]
        start = (ENC.vectors + DEC.vectors)[v_static] * D
        return start // shard, (start + D - 1) // shard

    for v in range(N_VEC):
        for which, target in enumerate(sorted(set(vector_targets(v)))):
            if target == v:
                @pl.when(me == v)
                def _(v=v):
                    pltpu.make_async_copy(vown, fv.at[v], r_vback.at[v]).start()
            else:
                @pl.when(me == v)
                def _(v=v, target=target, which=which):
                    pltpu.make_async_remote_copy(
                        vown, fv.at[v], s_vback.at[which], r_vback.at[v], device_id=(target // 4, target % 4), device_id_type=MESH
                    ).start()

    units_to_flat(ENC)
    finish_flat(DEC)
    finish_flat(ENC)

    def norm_wait(i, total):
        norm_copy(i).wait()
        return total + nland[i]

    total = lax.fori_loop(1, n, norm_wait, nsend[...])
    norm_ref[...] = jnp.broadcast_to(jnp.sqrt(jnp.sum(total)), (8, LANES))

    for b, (g_out, o_ref) in enumerate(((ge_ref, oe_ref), (gd_ref, od_ref))):
        pltpu.make_async_copy(g_out.at[pl.ds(FRONT, o_ref.shape[0])], o_ref, s_out.at[b]).wait()
    for phase in range(4):
        for cp in vdmas(phase):
            cp.wait_send()
    for v in range(N_VEC):
        for which, target in enumerate(sorted(set(vector_targets(v)))):
            if target != v:
                @pl.when(me == v)
                def _(which=which):
                    pltpu.make_async_copy(vown, vown, s_vback.at[which]).wait()
    for pair in range(N_PAIR):
        if N_PAIR - 1 - pair >= N_PAIR - RING:
            core_copy(pair).wait_send()
        for phase in (2, 3):
            for cp in phase_dmas(pair, phase):
                cp.wait_send()
        end_back(pair)


def sum_rows(ref, rows, out_ref):
    def body(r):
        out_ref[...] += jnp.sum(ref[r, :].astype(F32), axis=0, keepdims=True)

    out_ref[...] = jnp.zeros_like(out_ref)
    row_blocks(rows, body)


def norm_backward_ref(x_ref, gain, dn_ref, rows, out_ref, gain_grad, shift_grad):
    gain_grad[...] = jnp.zeros_like(gain_grad)
    shift_grad[...] = jnp.zeros_like(shift_grad)

    def body(r):
        hat, root = norm_rows(x_ref[r, :].astype(F32))
        dn = dn_ref[r, :]
        gain_grad[...] += jnp.sum(dn * hat, axis=0, keepdims=True)
        shift_grad[...] += jnp.sum(dn, axis=0, keepdims=True)
        g = dn * gain[...]
        part = g - jnp.mean(g, axis=1, keepdims=True) - hat * jnp.mean(g * hat, axis=1, keepdims=True)
        out_ref[r, :] += root * part

    row_blocks(rows, body)


def round_rows(src_ref, rows, out_ref):
    def body(r):
        out_ref[r, :] = src_ref[r, :].astype(BF)

    row_blocks(rows, body)


def weight_grad(a_ref, b_ref, rows, g_ref):
    b = b_ref[0:rows, :]
    flat = g_ref.reshape(D, D)

    def body(cols):
        flat[cols, :] = mm_tn(a_ref[0:rows, cols], b).astype(BF)

    col_blocks(body)


def back_through(a_ref, w_ref, rows, out_ref, add):
    a = a_ref[0:rows, :]

    def body(cols):
        y = mm_nt(a, w_ref[cols, :])
        if add:
            y = y + out_ref[0:rows, cols]
        out_ref[0:rows, cols] = y.astype(out_ref.dtype)

    col_blocks(body)


def gelu_back(o_ref, w_ref, slope_ref, rows, out_ref, bias_grad):
    a = o_ref[0:rows, :]

    def body(cols):
        y = mm_nt(a, w_ref[cols, :]) * slope_ref[0:rows, cols].astype(F32)
        bias_grad[:, cols] = jnp.sum(y, axis=0, keepdims=True)
        out_ref[0:rows, cols] = y.astype(BF)

    col_blocks(body)


def attention_backward_ref(q_ref, k_ref, v_ref, dm_ref, lse_ref, mask_ref, rows, keys, dq_ref, dk_ref, dv_ref):
    def pair_of_heads(i, carry):
        cols = pl.ds(pl.multiple_of(i * LANES, LANES), LANES)
        dk_ref[:, cols] = jnp.zeros((dk_ref.shape[0], LANES), F32)
        dv_ref[:, cols] = jnp.zeros((dv_ref.shape[0], LANES), F32)
        k_turned = jnp.transpose(k_ref[0:keys, cols])
        for tile, (start, reach) in enumerate(attend_tiles(rows, keys, mask_ref is not None)):
            r = slice(start, start + LANES)
            q2 = both_heads(q_ref[r, cols] * jnp.asarray(SCALE, BF))
            dm2 = both_heads(dm_ref[r, cols])
            scores = scores_of(k_ref[0:reach, cols], q2, mask_ref, start, reach)
            probs = jnp.exp(scores - lse_ref[tile, pl.ds(i, 1), :])
            dp = mm_nt(v_ref[0:reach, cols], dm2)
            weighted = probs * dp
            ds = (weighted - probs * jnp.sum(weighted, axis=0, keepdims=True)).astype(BF)
            dk_ref[0:reach, cols] += mm(ds, q2)
            dv_ref[0:reach, cols] += mm(probs.astype(BF), dm2)
            dq = jnp.concatenate(
                [
                    mm(k_turned[s * HEAD_DIM : (s + 1) * HEAD_DIM, 0:reach], ds[:, s * LANES : (s + 1) * LANES])
                    for s in range(2)
                ],
                axis=0,
            )
            dq_ref[r, cols] = jnp.transpose(dq) * SCALE
        return carry

    lax.fori_loop(0, D // LANES, pair_of_heads, 0, unroll=1 if mask_ref is not None else 2)


W_ORDER = (26, 27, 22, 23, 24, 25, 20, 21, 19, 16, 17, 18, 15, 12, 13, 14, 10, 11, 6, 7, 8, 9, 4, 5, 3, 0, 1, 2)
W_RING = 4
A_RING = 4


def backward_kernel(n, rows, frames, *refs):
    w_ref, v_ref, seg_row, seg_col, ein, din, ecot, dcot = refs[:8]
    kept, refs = refs[8 : 8 + N_SAVED], refs[8 + N_SAVED :]
    oe_ref, od_ref, norm_ref, fgrad, tgrad = refs[:5]
    refs = refs[5:]
    comm, refs = refs[:34], refs[34:]
    (
        gbuf, vg, vgr, gains, wbuf, outg, eoutg, dn, pool, abuf, nbuf, xbuf,
        dq, dk, dv, mask_ref, lse, orow, mem, mgrad, s_l, s_w, s_a, s_o,
    ) = refs
    tall = mask_ref.shape[0]

    a_order = (
        [kept[26].at[k] for k in (2, 3, 0, 1)]
        + [kept[27].at[k] for k in (2, 3, 0, 1)]
        + [kept[22].at[0:rows], kept[15].at[0:rows], din]
        + [kept[8].at[k] for k in (2, 3, 0, 1)]
        + [kept[9].at[k] for k in (2, 3, 0, 1)]
        + [kept[4], ein]
    )
    used = [0, 0]

    def w_copy(u):
        m = W_ORDER[u]
        return pltpu.make_async_copy(w_ref.at[m // 2, m % 2].reshape(D, D), wbuf.at[u % W_RING], s_w.at[u % W_RING])

    def a_copy(u):
        src = a_order[u]
        return pltpu.make_async_copy(src, abuf.at[u % A_RING, 0 : src.shape[0]], s_a.at[u % A_RING])

    def with_w(mat, body):
        u = used[0]
        used[0] += 1
        assert W_ORDER[u] == mat
        w_copy(u).wait()
        body(wbuf.at[u % W_RING])
        if u + W_RING < len(W_ORDER):
            w_copy(u + W_RING).start()

    def with_a(body):
        u = used[1]
        used[1] += 1
        a_copy(u).wait()
        body(abuf.at[u % A_RING])
        if u + A_RING < len(a_order):
            a_copy(u + A_RING).start()

    def side(k, src, dst):
        return pltpu.make_async_copy(src, dst, s_l.at[k])

    def x_copy(i):
        return side(0, kept[i], xbuf.at[0 : kept[i].shape[0]])

    def n_copy(i):
        return side(1, kept[i], nbuf.at[0 : kept[i].shape[0]])

    def vrow(i):
        return vgr.at[i : i + 1]

    def feed(step, g, count, first_mat, first_vec, n_i):
        if step < 2:
            for j in range(2):
                with_a(lambda a, j=j: weight_grad(a, orow, count, g.at[j]))
            return
        ks = (2, 3) if step == 2 else (0, 1)
        for j, k in enumerate(ks):
            with_w(
                first_mat + 4 + k,
                lambda w, k=k: with_a(lambda a: gelu_back(orow, w, a, count, pool.at[k], vrow(first_vec + k))),
            )
            if step == 2 and j == 0:
                n_copy(n_i).wait()
            weight_grad(nbuf, pool.at[k], count, g.at[j])

    def feed_after(step, count, first_mat):
        ks = (2, 3) if step == 2 else (0, 1)
        for j, k in enumerate(ks):
            with_w(first_mat + k, lambda w, j=j, k=k: back_through(pool.at[k], w, count, dn, not (step == 2 and j == 0)))

    def attend(g, count, padded, keys, padded_keys, out_ref, wo, q_i, lse_i, masked, bo, bq, bv):
        cps = [side(2 + k, kept[q_i + k], pool.at[k, 0 : kept[q_i + k].shape[0]]) for k in range(3)]
        cps.append(side(5, kept[lse_i], lse.at[0 : kept[lse_i].shape[0]]))
        for cp in cps:
            cp.start()
        round_rows(out_ref, count, orow)
        sum_rows(out_ref, count, vrow(bo))
        with_a(lambda a: weight_grad(a, orow, count, g.at[1]))
        with_w(wo, lambda w: back_through(orow, w, count, pool.at[3], False))
        if padded > count:
            pool[3, count:padded, :] = jnp.zeros((padded - count, D), BF)
        for cp in cps:
            cp.wait()
        attention_backward_ref(
            pool.at[0], pool.at[1], pool.at[2], pool.at[3], lse, mask_ref if masked else None, padded, padded_keys,
            dq, dk.at[0:padded_keys], dv.at[0:padded_keys],
        )
        round_rows(dv, keys, pool.at[2])
        round_rows(dq, count, pool.at[0])
        round_rows(dk, keys, pool.at[1])
        sum_rows(dq, count, vrow(bq))
        sum_rows(dv, keys, vrow(bv))

    def start():
        o_copy = side(2, dcot, orow)
        o_copy.start()
        for u in range(A_RING):
            a_copy(u).start()
        for u in range(W_RING):
            w_copy(u).start()
        n_copy(25).start()
        x_copy(24).start()
        mem_copy = side(3, kept[10], mem)
        mem_copy.start()
        for i, v in enumerate((0, 5, 12, 17, 22)):
            for k in range(6):
                gains[i : i + 1, k * LANES : (k + 1) * LANES] = v_ref[v // 8, v // 4 % 2, v // 2 % 2, v % 2, k : k + 1, :]
        o_copy.wait()
        mem_copy.wait()

    def widen():
        def body(r):
            outg[r, :] = orow[r, :].astype(F32)

        row_blocks(rows, body)
        sum_rows(outg, rows, vrow(28))

    def produce(t, g):
        if t == 0:
            start()
        if t < 4:
            feed(t, g, rows, 20, 24, 25)
            if t == 3:
                n_copy(18).start()
        elif t == 4:
            attend(g, rows, tall, frames, frames, outg, 19, 19, 23, False, 21, 19, 20)
            weight_grad(mem, pool.at[2], frames, g.at[0])
        elif t == 5:
            n_copy(18).wait()
            weight_grad(nbuf, pool.at[0], rows, g.at[0])
            weight_grad(mem, pool.at[1], frames, g.at[1])
            n_copy(11).start()
        elif t == 6:
            attend(g, rows, tall, rows, tall, outg, 15, 12, 16, True, 16, 14, 15)
            n_copy(11).wait()
            weight_grad(nbuf, pool.at[2], rows, g.at[0])
        elif t == 7:
            weight_grad(nbuf, pool.at[0], rows, g.at[0])
            weight_grad(nbuf, pool.at[1], rows, g.at[1])
            n_copy(7).start()
        elif t < 12:
            feed(t - 8, g, frames, 4, 7, 7)
            if t == 11:
                n_copy(0).start()
        elif t == 12:
            attend(g, frames, frames, frames, frames, eoutg, 3, 1, 5, False, 4, 2, 3)
            n_copy(0).wait()
            weight_grad(nbuf, pool.at[2], frames, g.at[0])
        else:
            weight_grad(nbuf, pool.at[0], frames, g.at[0])
            weight_grad(nbuf, pool.at[1], frames, g.at[1])

    def after(t):
        if t == 0:
            widen()
            make_mask(seg_row, seg_col, mask_ref)
        elif t in (2, 3):
            feed_after(t, rows, 20)
            if t == 3:
                x_copy(24).wait()
                norm_backward_ref(xbuf, gains.at[4:5], dn, rows, outg, vrow(22), vrow(23))
                x_copy(17).start()
        elif t == 5:
            with_w(16, lambda w: back_through(pool.at[0], w, rows, dn, False))
            with_w(17, lambda w: back_through(pool.at[1], w, frames, mgrad, False))
            with_w(18, lambda w: back_through(pool.at[2], w, frames, mgrad, True))
            x_copy(17).wait()
            norm_backward_ref(xbuf, gains.at[3:4], dn, rows, outg, vrow(17), vrow(18))
            x_copy(6).start()
        elif t == 7:
            cot = side(2, ecot, orow.at[0:frames])
            cot.start()
            with_w(12, lambda w: back_through(pool.at[0], w, rows, dn, False))
            with_w(13, lambda w: back_through(pool.at[1], w, rows, dn, True))
            with_w(14, lambda w: back_through(pool.at[2], w, rows, dn, True))
            with_a(lambda a: norm_backward_ref(a, gains.at[2:3], dn, rows, outg, vrow(12), vrow(13)))
            pltpu.make_async_copy(outg, tgrad, s_o.at[0]).start()
            cot.wait()

            def body(r):
                total = orow[r, :].astype(F32) + mgrad[r, :]
                eoutg[r, :] = total
                orow[r, :] = total.astype(BF)

            row_blocks(frames, body)
        elif t == 9:
            sum_rows(eoutg, frames, vrow(11))
        elif t in (10, 11):
            feed_after(t - 8, frames, 4)
            if t == 11:
                x_copy(6).wait()
                norm_backward_ref(xbuf, gains.at[1:2], dn, frames, eoutg, vrow(5), vrow(6))
        elif t == 13:
            with_w(0, lambda w: back_through(pool.at[0], w, frames, dn, False))
            with_w(1, lambda w: back_through(pool.at[1], w, frames, dn, True))
            with_w(2, lambda w: back_through(pool.at[2], w, frames, dn, True))
            with_a(lambda a: norm_backward_ref(a, gains.at[0:1], dn, frames, eoutg, vrow(0), vrow(1)))
            pltpu.make_async_copy(eoutg, fgrad, s_o.at[1]).start()
            for v in range(32):
                at = (v // 8, v // 4 % 2, v // 2 % 2, v % 2)
                if v < N_VEC:
                    vg[at + (slice(6, 8), slice(None))] = jnp.zeros((2, LANES), F32)
                    for k in range(6):
                        vg[at + (slice(k, k + 1), slice(None))] = vgr[v : v + 1, k * LANES : (k + 1) * LANES]
                else:
                    vg[at] = jnp.zeros((8, LANES), F32)

    scatter_kernel(n, produce, after, vg, gbuf, oe_ref, od_ref, norm_ref, *comm)
    pltpu.make_async_copy(outg, tgrad, s_o.at[0]).wait()
    pltpu.make_async_copy(eoutg, fgrad, s_o.at[1]).wait()


def backward_pass(weights, vectors, kept, ein, din, ecot, dcot, segments, n):
    (_, re, ne, ge), (_, rd, nd, gd) = sizes(ENC, n), sizes(DEC, n)
    frames, rows = ein.shape[0], din.shape[0]
    tall = -(-rows // 128) * 128
    dma = pltpu.SemaphoreType.DMA
    vmem, hbm = pl.BlockSpec(memory_space=pltpu.VMEM), pl.BlockSpec(memory_space=pl.ANY)
    seg = jnp.pad(segments, (0, tall - rows), constant_values=-1)
    return pl.pallas_call(
        partial(backward_kernel, n, rows, frames),
        out_shape=(
            jax.ShapeDtypeStruct((re, LANES), F32),
            jax.ShapeDtypeStruct((rd, LANES), F32),
            jax.ShapeDtypeStruct((8, LANES), F32),
            jax.ShapeDtypeStruct((frames, D), F32),
            jax.ShapeDtypeStruct((rows, D), F32),
        ),
        in_specs=[hbm] + [vmem] * 3 + [hbm] * (4 + N_SAVED),
        out_specs=(hbm, hbm, vmem, hbm, hbm),
        scratch_shapes=[
            pltpu.VMEM((RING_C, 4, 2, 2, UNIT, D), BF),
            pltpu.VMEM((N_PAIR, 4, 2, UNIT, D), BF),
            pltpu.VMEM((N_PAIR, 4, UNIT, D), BF),
            pltpu.VMEM((N_PAIR, 3, UNIT, D), BF),
            pltpu.VMEM((N_PAIR, UNIT, D), BF),
            pltpu.VMEM((8, LANES), F32),
            pltpu.VMEM((4, 2, 2, 8, LANES), F32),
            pltpu.VMEM((4, 2, 8, LANES), F32),
            pltpu.VMEM((4, 8, LANES), F32),
            pltpu.VMEM((3, 8, LANES), F32),
            pltpu.VMEM((FRONT + re + BACK, LANES), F32),
            pltpu.VMEM((FRONT + rd + BACK, LANES), F32),
            pltpu.VMEM((ne, UNIT, D), BF),
            pltpu.VMEM((nd, UNIT, D), BF),
            pltpu.VMEM((ge, 4, UNIT, D), BF),
            pltpu.VMEM((gd, 4, UNIT, D), BF),
            pltpu.VMEM((N_VEC, 8, LANES), F32),
            pltpu.VMEM((8, LANES), F32),
            pltpu.VMEM((n, 8, LANES), F32),
            dma((N_PAIR,)),
            dma((N_PAIR,)),
            pltpu.SemaphoreType.REGULAR,
            dma((N_PAIR, 5)),
            dma((N_PAIR, 5)),
            dma((N_PAIR, 2)),
            dma((2, max(ne, nd))),
            dma((2, max(ge, gd), 4)),
            dma((6,)),
            dma((6,)),
            dma((2,)),
            dma((N_VEC,)),
            dma((n,)),
            dma((n,)),
            dma((2,)),
            pltpu.VMEM((RING, 2, 4, 2, 2, UNIT, D), BF),
            pltpu.VMEM((4, 2, 2, 2, 8, LANES), F32),
            pltpu.VMEM((32, D), F32),
            pltpu.VMEM((8, D), F32),
            pltpu.VMEM((W_RING, D, D), BF),
            pltpu.VMEM((rows, D), F32),
            pltpu.VMEM((frames, D), F32),
            pltpu.VMEM((rows, D), F32),
            pltpu.VMEM((4, tall, D), BF),
            pltpu.VMEM((A_RING, rows, D), BF),
            pltpu.VMEM((rows, D), BF),
            pltpu.VMEM((rows, D), F32),
            pltpu.VMEM((tall, D), F32),
            pltpu.VMEM((tall, D), F32),
            pltpu.VMEM((tall, D), F32),
            pltpu.VMEM((tall, tall), F32),
            pltpu.VMEM((tall // 128, 8, 2 * LANES), F32),
            pltpu.VMEM((rows, D), BF),
            pltpu.VMEM((frames, D), BF),
            pltpu.VMEM((frames, D), F32),
            dma((6,)),
            dma((W_RING,)),
            dma((A_RING,)),
            dma((2,)),
        ],
        compiler_params=pltpu.CompilerParams(collective_id=1, has_side_effects=True, vmem_limit_bytes=61 << 20),
        name="backward",
    )(weights, vectors, seg[None, :], seg[:, None], ein, din, ecot, dcot, *kept)


def attention_plan(prefix, width):
    return [
        (prefix + "wq", width, width),
        (prefix + "bq", width, 0),
        (prefix + "wk", width, width),
        (prefix + "wv", width, width),
        (prefix + "bv", width, 0),
        (prefix + "wo", width, width),
        (prefix + "bo", width, 0),
    ]


def feed_plan(width, hidden):
    return [
        ("fc1_weight", width, hidden),
        ("fc1_bias", hidden, 0),
        ("fc2_weight", hidden, width),
        ("fc2_bias", width, 0),
    ]


def encoder_layout(width, hidden):
    return (
        [("ln1_gain", width, 0), ("ln1_bias", width, 0)]
        + attention_plan("att_", width)
        + [("ln2_gain", width, 0), ("ln2_bias", width, 0)]
        + feed_plan(width, hidden)
    )


def decoder_layout(width, hidden):
    return (
        [("ln1_gain", width, 0), ("ln1_bias", width, 0)]
        + attention_plan("self_", width)
        + [("ln2_gain", width, 0), ("ln2_bias", width, 0)]
        + attention_plan("cross_", width)
        + [("ln3_gain", width, 0), ("ln3_bias", width, 0)]
        + feed_plan(width, hidden)
    )


def unpack(flat, layout):
    params = {}
    offset = 0
    for name, rows, cols in layout:
        count = rows * cols if cols > 0 else rows
        piece = flat[offset : offset + count]
        params[name] = piece.reshape(rows, cols) if cols > 0 else piece
        offset = offset + count
    return params


def pack(grads, layout):
    return jnp.concatenate([grads[name].reshape(-1) for name, rows, cols in layout])


def dot_plain(left, right):
    return jnp.dot(left, right, preferred_element_type=jnp.float32)


def dot_left(left, right):
    return lax.dot_general(
        left, right, (((0,), (0,)), ((), ())), preferred_element_type=jnp.float32
    )


def dot_right(left, right):
    return lax.dot_general(
        left, right, (((1,), (1,)), ((), ())), preferred_element_type=jnp.float32
    )


def layer_norm(values, gain, shift):
    centred = values - jnp.mean(values, axis=-1, keepdims=True)
    spread = jnp.mean(centred * centred, axis=-1, keepdims=True)
    return centred * lax.rsqrt(spread + 1e-05) * gain + shift


def norm_forward(params, prefix, values):
    gain = params[prefix + "_gain"].astype(jnp.float32)
    shift = params[prefix + "_bias"].astype(jnp.float32)
    return layer_norm(values, gain, shift).astype(jnp.bfloat16)


def norm_backward(params, prefix, values, grad):
    gain = params[prefix + "_gain"].astype(jnp.float32)
    shift = params[prefix + "_bias"].astype(jnp.float32)
    unused, pullback = jax.vjp(layer_norm, values, gain, shift)
    value_grad, gain_grad, shift_grad = pullback(grad)
    return (value_grad, {prefix + "_gain": gain_grad, prefix + "_bias": shift_grad})


def block_rows(total):
    return total if total <= 1024 else 512


def attend_forward(queries, keys_low, values, allowed_fn):
    total, width = queries.shape
    heads = width // HEAD_DIM
    rows = block_rows(total)
    blocks = total // rows
    scale = HEAD_DIM ** (-0.5)
    query_heads = queries.reshape(blocks, rows, heads, HEAD_DIM)
    key_heads = keys_low.reshape(keys_low.shape[0], heads, HEAD_DIM)
    value_heads = values.reshape(values.shape[0], heads, HEAD_DIM)
    starts = jnp.arange(blocks, dtype=jnp.int32) * rows

    def one_block(inputs):
        block, start = inputs
        scores = (
            jnp.einsum("qhd,khd->hqk", block, key_heads, preferred_element_type=jnp.float32) * scale
        )
        if allowed_fn is not None:
            scores = jnp.where(allowed_fn(start, rows)[None], scores, -1000000000.0)
        peak = jnp.max(scores, axis=-1, keepdims=True)
        weights = jnp.exp(scores - peak)
        totals = jnp.sum(weights, axis=-1, keepdims=True)
        probs = (weights / totals).astype(jnp.bfloat16)
        mixed = jnp.einsum("hqk,khd->qhd", probs, value_heads, preferred_element_type=jnp.float32)
        return (mixed.reshape(rows, width).astype(jnp.bfloat16), (peak + jnp.log(totals))[..., 0])

    mixed, logsum = lax.map(one_block, (query_heads, starts))
    return (mixed.reshape(total, width), logsum)


def attend_backward(queries, keys_low, values, logsum, mixed_grad, allowed_fn):
    total, width = queries.shape
    heads = width // HEAD_DIM
    rows = block_rows(total)
    blocks = total // rows
    scale = HEAD_DIM ** (-0.5)
    query_heads = queries.reshape(blocks, rows, heads, HEAD_DIM)
    grad_heads = mixed_grad.reshape(blocks, rows, heads, HEAD_DIM)
    key_heads = keys_low.reshape(keys_low.shape[0], heads, HEAD_DIM)
    value_heads = values.reshape(values.shape[0], heads, HEAD_DIM)
    starts = jnp.arange(blocks, dtype=jnp.int32) * rows

    def one_block(carry, inputs):
        key_grad, value_grad = carry
        block, grad_block, block_sum, start = inputs
        scores = (
            jnp.einsum("qhd,khd->hqk", block, key_heads, preferred_element_type=jnp.float32) * scale
        )
        if allowed_fn is not None:
            scores = jnp.where(allowed_fn(start, rows)[None], scores, -1000000000.0)
        probs = jnp.exp(scores - block_sum[..., None])
        prob_grad = jnp.einsum(
            "qhd,khd->hqk", grad_block, value_heads, preferred_element_type=jnp.float32
        )
        value_grad = value_grad + jnp.einsum(
            "hqk,qhd->khd",
            probs.astype(jnp.bfloat16),
            grad_block,
            preferred_element_type=jnp.float32,
        )
        score_grad = probs * (prob_grad - jnp.sum(probs * prob_grad, axis=-1, keepdims=True))
        raw_grad = (score_grad * scale).astype(jnp.bfloat16)
        query_grad = jnp.einsum(
            "hqk,khd->qhd", raw_grad, key_heads, preferred_element_type=jnp.float32
        )
        key_grad = key_grad + jnp.einsum(
            "hqk,qhd->khd", raw_grad, block, preferred_element_type=jnp.float32
        )
        return ((key_grad, value_grad), query_grad.reshape(rows, width))

    zeros = jnp.zeros(key_heads.shape, jnp.float32)
    (key_grad, value_grad), query_grad = lax.scan(
        one_block, (zeros, zeros), (query_heads, grad_heads, logsum, starts)
    )
    return (
        query_grad.reshape(total, width),
        key_grad.reshape(keys_low.shape[0], width),
        value_grad.reshape(values.shape[0], width),
    )


def attention_forward(params, prefix, query_rows, key_rows, allowed_fn):
    queries = (dot_plain(query_rows, params[prefix + "wq"]) + params[prefix + "bq"]).astype(
        jnp.bfloat16
    )
    keys_low = dot_plain(key_rows, params[prefix + "wk"]).astype(jnp.bfloat16)
    values = (dot_plain(key_rows, params[prefix + "wv"]) + params[prefix + "bv"]).astype(
        jnp.bfloat16
    )
    mixed, logsum = attend_forward(queries, keys_low, values, allowed_fn)
    output = dot_plain(mixed, params[prefix + "wo"]) + params[prefix + "bo"]
    return (output, (queries, keys_low, values, mixed, logsum))


def attention_backward(params, prefix, query_rows, key_rows, kept, out_grad, allowed_fn):
    queries, keys_low, values, mixed, logsum = kept
    out_round = out_grad.astype(jnp.bfloat16)
    mixed_grad = dot_right(out_round, params[prefix + "wo"]).astype(jnp.bfloat16)
    query_grad, key_grad, value_grad = attend_backward(
        queries, keys_low, values, logsum, mixed_grad, allowed_fn
    )
    query_round = query_grad.astype(jnp.bfloat16)
    key_round = key_grad.astype(jnp.bfloat16)
    value_round = value_grad.astype(jnp.bfloat16)
    grads = {
        prefix + "wq": dot_left(query_rows, query_round),
        prefix + "bq": jnp.sum(query_grad, axis=0),
        prefix + "wk": dot_left(key_rows, key_round),
        prefix + "wv": dot_left(key_rows, value_round),
        prefix + "bv": jnp.sum(value_grad, axis=0),
        prefix + "wo": dot_left(mixed, out_round),
        prefix + "bo": jnp.sum(out_grad, axis=0),
    }
    query_side = dot_right(query_round, params[prefix + "wq"])
    key_side = dot_right(key_round, params[prefix + "wk"]) + dot_right(
        value_round, params[prefix + "wv"]
    )
    return (grads, query_side, key_side)


def feed_forward(params, normed):
    pre = dot_plain(normed, params["fc1_weight"]) + params["fc1_bias"]
    activated = jax.nn.gelu(pre, approximate=False).astype(jnp.bfloat16)
    return (dot_plain(activated, params["fc2_weight"]) + params["fc2_bias"], (pre, activated))


def feed_backward(params, normed, kept, out_grad):
    pre, activated = kept
    out_round = out_grad.astype(jnp.bfloat16)
    act_grad = dot_right(out_round, params["fc2_weight"])
    unused, gelu_back = jax.vjp(partial(jax.nn.gelu, approximate=False), pre)
    pre_grad = gelu_back(act_grad)[0]
    pre_round = pre_grad.astype(jnp.bfloat16)
    grads = {
        "fc1_weight": dot_left(normed, pre_round),
        "fc1_bias": jnp.sum(pre_grad, axis=0),
        "fc2_weight": dot_left(activated, out_round),
        "fc2_bias": jnp.sum(out_grad, axis=0),
    }
    return (grads, dot_right(pre_round, params["fc1_weight"]))


def encoder_forward(params, frames):
    normed = norm_forward(params, "ln1", frames)
    attended, attend_kept = attention_forward(params, "att_", normed, normed, None)
    after = frames + attended
    normed_two = norm_forward(params, "ln2", after)
    fed, feed_kept = feed_forward(params, normed_two)
    return (after + fed, (normed, attend_kept, after, normed_two, feed_kept))


def encoder_backward(params, frames, kept, out_grad):
    normed, attend_kept, after, normed_two, feed_kept = kept
    grads, normed_grad = feed_backward(params, normed_two, feed_kept, out_grad)
    part, norm_grads = norm_backward(params, "ln2", after, normed_grad)
    grads.update(norm_grads)
    after_grad = out_grad + part
    attend_grads, query_side, key_side = attention_backward(
        params, "att_", normed, normed, attend_kept, after_grad, None
    )
    grads.update(attend_grads)
    part, norm_grads = norm_backward(params, "ln1", frames, query_side + key_side)
    grads.update(norm_grads)
    return (grads, after_grad + part)


def decoder_forward(params, tokens, memory_low, allowed_fn):
    normed = norm_forward(params, "ln1", tokens)
    attended, self_kept = attention_forward(params, "self_", normed, normed, allowed_fn)
    after = tokens + attended
    normed_two = norm_forward(params, "ln2", after)
    crossed, cross_kept = attention_forward(params, "cross_", normed_two, memory_low, None)
    after_two = after + crossed
    normed_three = norm_forward(params, "ln3", after_two)
    fed, feed_kept = feed_forward(params, normed_three)
    return (
        after_two + fed,
        (normed, self_kept, after, normed_two, cross_kept, after_two, normed_three, feed_kept),
    )


def decoder_backward(params, tokens, memory_low, kept, out_grad, allowed_fn):
    normed, self_kept, after, normed_two, cross_kept, after_two, normed_three, feed_kept = kept
    grads, normed_grad = feed_backward(params, normed_three, feed_kept, out_grad)
    part, norm_grads = norm_backward(params, "ln3", after_two, normed_grad)
    grads.update(norm_grads)
    after_two_grad = out_grad + part
    cross_grads, query_side, memory_grad = attention_backward(
        params, "cross_", normed_two, memory_low, cross_kept, after_two_grad, None
    )
    grads.update(cross_grads)
    part, norm_grads = norm_backward(params, "ln2", after, query_side)
    grads.update(norm_grads)
    after_grad = after_two_grad + part
    self_grads, query_side, key_side = attention_backward(
        params, "self_", normed, normed, self_kept, after_grad, allowed_fn
    )
    grads.update(self_grads)
    part, norm_grads = norm_backward(params, "ln1", tokens, query_side + key_side)
    grads.update(norm_grads)
    return (grads, after_grad + part, memory_grad)


def adamw(master, first, second, grad, factor, correction):
    clipped = grad * factor
    moment = 0.5 * first + 0.5 * clipped
    variance = 0.5 * second + 0.5 * clipped * clipped
    update = moment / correction / (jnp.sqrt(variance / correction) + 1e-08) + 0.01 * master
    weights = master - 0.02 * update
    return (weights, moment, variance, weights.astype(jnp.bfloat16))


def shards_native(
    encoder_input,
    decoder_input,
    segments,
    encoder_cotangent,
    decoder_cotangent,
    encoder_master,
    encoder_first,
    encoder_second,
    decoder_master,
    decoder_first,
    decoder_second,
    step_count,
):
    encoder_plan = encoder_layout(D, FF)
    decoder_plan = decoder_layout(D, FF)
    encoder_params = unpack(
        lax.all_gather(encoder_master.astype(jnp.bfloat16), ("wide", "narrow"), axis=0, tiled=True),
        encoder_plan,
    )
    frames = encoder_input[0].astype(jnp.float32)
    memory, encoder_kept = encoder_forward(encoder_params, frames)
    memory_low = memory.astype(jnp.bfloat16)
    decoder_params = unpack(
        lax.all_gather(decoder_master.astype(jnp.bfloat16), ("wide", "narrow"), axis=0, tiled=True),
        decoder_plan,
    )
    tokens = decoder_input[0].astype(jnp.float32)
    segment_row = segments[0]
    length = segment_row.shape[0]

    def allowed_fn(start, count):
        places = start + jnp.arange(count, dtype=jnp.int32)
        row_segments = lax.dynamic_slice_in_dim(segment_row, start, count)
        columns = jnp.arange(length, dtype=jnp.int32)
        return (row_segments[:, None] == segment_row[None, :]) & (
            columns[None, :] <= places[:, None]
        )

    decoded, decoder_kept = decoder_forward(decoder_params, tokens, memory_low, allowed_fn)
    decoder_again = unpack(
        lax.all_gather(decoder_master.astype(jnp.bfloat16), ("wide", "narrow"), axis=0, tiled=True),
        decoder_plan,
    )
    decoder_grads, token_grad, memory_grad = decoder_backward(
        decoder_again,
        tokens,
        memory_low,
        decoder_kept,
        decoder_cotangent[0].astype(jnp.float32),
        allowed_fn,
    )
    decoder_total = pack(decoder_grads, decoder_plan)
    decoder_owned = lax.psum_scatter(
        decoder_total, ("wide", "narrow"), scatter_dimension=0, tiled=True
    )
    encoder_again = unpack(
        lax.all_gather(encoder_master.astype(jnp.bfloat16), ("wide", "narrow"), axis=0, tiled=True),
        encoder_plan,
    )
    memory_total = encoder_cotangent[0].astype(jnp.float32) + memory_grad
    encoder_grads, frame_grad = encoder_backward(encoder_again, frames, encoder_kept, memory_total)
    encoder_total = pack(encoder_grads, encoder_plan)
    encoder_owned = lax.psum_scatter(
        encoder_total, ("wide", "narrow"), scatter_dimension=0, tiled=True
    )
    local_squares = jnp.sum(encoder_owned * encoder_owned) + jnp.sum(decoder_owned * decoder_owned)
    gradient_norm = jnp.sqrt(lax.psum(local_squares, ("wide", "narrow")))
    factor = 1.0 / jnp.maximum(gradient_norm, 1.0)
    correction = 1.0 - jnp.power(0.5, step_count.astype(jnp.float32))
    encoder_new = adamw(
        encoder_master, encoder_first, encoder_second, encoder_owned, factor, correction
    )
    decoder_new = adamw(
        decoder_master, decoder_first, decoder_second, decoder_owned, factor, correction
    )
    return (
        memory_low[None],
        decoded.astype(jnp.bfloat16)[None],
        frame_grad[None],
        token_grad[None],
        gradient_norm,
        encoder_new[0],
        encoder_new[1],
        encoder_new[2],
        encoder_new[3],
        decoder_new[0],
        decoder_new[1],
        decoder_new[2],
        decoder_new[3],
    )


def shards(
    encoder_input,
    decoder_input,
    segments,
    encoder_cotangent,
    decoder_cotangent,
    encoder_master,
    encoder_first,
    encoder_second,
    decoder_master,
    decoder_first,
    decoder_second,
    step_count,
):
    n = 32
    weights, vectors, *kept = forward_pass(
        encoder_master, decoder_master, encoder_input[0], decoder_input[0], segments[0], n
    )
    encoder_flat, decoder_flat, norm, frame_grad, token_grad = backward_pass(
        weights, vectors, kept, encoder_input[0], decoder_input[0], encoder_cotangent[0], decoder_cotangent[0], segments[0], n
    )
    gradient_norm = norm[0, 0]
    factor = 1.0 / jnp.maximum(gradient_norm, 1.0)
    correction = 1.0 - jnp.power(0.5, step_count.astype(jnp.float32))
    encoder_owned = encoder_flat.reshape(-1)[: encoder_master.shape[0]]
    decoder_owned = decoder_flat.reshape(-1)[: decoder_master.shape[0]]
    encoder_new = adamw(encoder_master, encoder_first, encoder_second, encoder_owned, factor, correction)
    decoder_new = adamw(decoder_master, decoder_first, decoder_second, decoder_owned, factor, correction)
    return (
        kept[10][None],
        kept[28][None],
        frame_grad[None],
        token_grad[None],
        gradient_norm,
        *encoder_new,
        *decoder_new,
    )


def solution(mesh):
    placed = (
        P(("wide", "narrow"), None, None),
        P(("wide", "narrow"), None, None),
        P(("wide", "narrow"), None),
        P(("wide", "narrow"), None, None),
        P(("wide", "narrow"), None, None),
        P(("wide", "narrow")),
        P(("wide", "narrow")),
        P(("wide", "narrow")),
        P(("wide", "narrow")),
        P(("wide", "narrow")),
        P(("wide", "narrow")),
        P(),
    )
    return jax.shard_map(
        shards if tuple(mesh.shape.values()) == (8, 4) else shards_native,
        mesh=mesh,
        in_specs=placed,
        out_specs=(
            P(("wide", "narrow"), None, None),
            P(("wide", "narrow"), None, None),
            P(("wide", "narrow"), None, None),
            P(("wide", "narrow"), None, None),
            P(),
            P(("wide", "narrow")),
            P(("wide", "narrow")),
            P(("wide", "narrow")),
            P(("wide", "narrow")),
            P(("wide", "narrow")),
            P(("wide", "narrow")),
            P(("wide", "narrow")),
            P(("wide", "narrow")),
        ),
        check_vma=False,
    )
```

```python
from functools import partial

import jax
import jax.numpy as jnp
from jax import lax
from jax.experimental import pallas as pl
from jax.experimental.pallas import tpu as pltpu
from jax.sharding import PartitionSpec as P

D = 768
HEAD_DIM = 64
FF = 3072
MESH = pl.DeviceIdType.MESH
BF = jnp.bfloat16
F32 = jnp.float32

N_MAT = 28
N_PAIR = 14
UNIT = 48
LANES = 128
UROWS = UNIT * D // LANES
BIG = 4 * UROWS
FRONT = BIG + 8
BACK = BIG + 8
N_VEC = 29
F_AT = (1, 2, 4, 5)
B_AT = (1, 3, 5, 8)
AHEAD = 3


class Block:
    def __init__(self, small, gaps, fc1, vectors, first_mat, small_mats, total):
        self.small = small
        self.gaps = gaps
        self.fc1 = fc1
        self.vectors = vectors
        self.first_mat = first_mat
        self.small_mats = small_mats
        self.total = total


ENC = Block(
    small=8,
    gaps=((0, 2), (1, 1), (3, 1), (4, 3072 + 7)),
    fc1=3079,
    vectors=[0, 1, 770, 2307, 3076, 3077, 3078, 6151, 6152, 6153, 6154, 9227],
    first_mat=0,
    small_mats=4,
    total=9228,
)
DEC = Block(
    small=12,
    gaps=((0, 2), (1, 1), (3, 1), (4, 3), (5, 1), (7, 1), (8, 3072 + 7)),
    fc1=6156,
    vectors=[0, 1, 770, 2307, 3076, 3077, 3078, 3847, 5384, 6153, 6154, 6155, 9228, 9229, 9230, 9231, 12304],
    first_mat=12,
    small_mats=8,
    total=12305,
)
BLOCKS = (ENC, DEC)


def sizes(block, n):
    shard = block.total * D // n
    rows = -(-shard // 1024) * 8
    top = (shard + LANES - 1) // LANES
    return shard, rows, (top + UROWS) // UROWS + 1, (top + BIG) // BIG + 1


def small_row(block, m):
    row = m * D
    for at, gap in block.gaps:
        row = row + jnp.where(m >= at, gap, 0) if at > 0 else row + gap
    return row


def mat_of(block, m):
    return block.first_mat + m + jnp.where(m >= block.small_mats, 4, 0)


def static_unit_rows(block):
    out = []
    for m in range(block.small):
        row = m * D + sum(gap for at, gap in block.gaps if m >= at)
        out.append((block.first_mat + m + (4 if m >= block.small_mats else 0), row))
    return out


def whoami():
    wide, narrow = lax.axis_index("wide"), lax.axis_index("narrow")
    return wide, narrow, wide // 2, wide % 2, narrow // 2, narrow % 2


def device(z, x, y, c):
    return (z * 2 + x, y * 2 + c)


def flat_device(d):
    return (d // 4, d % 4)


def greet(me, n):
    bar = pltpu.get_barrier_semaphore()

    def signal(i, carry):
        pl.semaphore_signal(bar, inc=1, device_id=flat_device((me + i) % n), device_id_type=MESH)
        return carry

    lax.fori_loop(1, n, signal, 0)


def await_all(n):
    pl.semaphore_wait(pltpu.get_barrier_semaphore(), n - 1)


def each_small(block, n, me, slots, body, least=0, most=99):
    shard = sizes(block, n)[0]
    low = me * shard
    low_row = low // LANES
    first = 0
    for _, row in static_unit_rows(block):
        first = first + jnp.minimum(jnp.maximum(low - row * D, 0) // (UROWS * LANES), 16)

    def step(j, carry):
        g = first + j
        m, u = g // 16, g % 16
        start = small_row(block, m) * 6 + u * UROWS
        pos = start - low_row

        @pl.when((g < 16 * min(block.small, most)) & (g >= 16 * least) & (start * LANES < low + shard))
        def _():
            body((pos + UROWS) // UROWS, mat_of(block, m), u, pos, start * LANES)

        return carry

    lax.fori_loop(0, slots, step, 0)


def each_big(block, n, me, slots, body):
    shard = sizes(block, n)[0]
    low = me * shard
    low_row = low // LANES
    first = jnp.minimum(jnp.maximum(low - block.fc1 * D, 0) // (BIG * LANES), 16)

    def step(j, carry):
        u = first + j
        start = block.fc1 * 6 + u * BIG
        pos = start - low_row

        @pl.when((u < 16) & (start * LANES < low + shard) & (start * LANES + BIG * LANES > low))
        def _():
            body((pos + BIG) // BIG, u, pos, start * LANES)

        return carry

    lax.fori_loop(0, slots, step, 0)


def each_vector(block, n, me, first_vec, body):
    shard = sizes(block, n)[0]
    low = me * shard
    low_row = low // LANES
    for i, row in enumerate(block.vectors):
        @pl.when((row * D < low + shard) & (row * D + D > low))
        def _(i=i, row=row):
            body(first_vec + i, row * 6 - low_row, row * D)


def peers(axis, at):
    if axis == "z":
        return [dict(at, z=(at["z"] + k) % 4) for k in (1, 2, 3)]
    return [dict(at, **{axis: 1 - at[axis]})]


def first_peer(at):
    x, y, c = at["x"], at["y"], at["c"]
    return device(at["z"], x + (1 - c) * (1 - 2 * x), y + c * (1 - 2 * y), c)


def second_peer(at):
    x, y, c = at["x"], at["y"], at["c"]
    return device(at["z"], x + c * (1 - 2 * x), y + (1 - c) * (1 - 2 * y), c)


def dev(at):
    return device(at["z"], at["x"], at["y"], at["c"])


def gather_kernel(
    n, on_start, on_vectors, on_pair, on_last, xe_ref, xd_ref, w_ref, v_ref,
    re_ref, rd_ref, se_ref, sd_ref, be_ref, bd_ref, sv_ref, land, landv, own, ownv,
    s_small, s_big, s_vec, r_unit, r_vec, s_zxy, r_zxy, s_core, r_core, s_own, v_send, v_recv,
):
    wide, narrow, z, x, y, c = whoami()
    me = wide * 4 + narrow
    chip = me // 2
    at = dict(z=z, x=x, y=y, c=c)
    greet(me, n)
    lanes = lax.broadcasted_iota(jnp.int32, (1, LANES), 1)
    fields = {
        ENC: (xe_ref, re_ref, se_ref, be_ref, 0, 0, 0),
        DEC: (xd_ref, rd_ref, sd_ref, bd_ref, sizes(ENC, n)[2], sizes(ENC, n)[3], len(ENC.vectors)),
    }

    def prepare(block):
        x_ref, r_ref = fields[block][:2]
        shard, rows, _, _ = sizes(block, n)
        step = 8 * max(k for k in range(1, 40) if (rows // 8) % k == 0)

        def turn(i, carry):
            at_row = pl.multiple_of(i * step, 8)
            r_ref[pl.ds(FRONT + at_row, step), :] = pltpu.roll(
                x_ref[pl.ds(at_row, step), :], (me * shard) % LANES, 1
            )
            return carry

        lax.fori_loop(0, rows // step, turn, 0)

    def load_rows(block, row, count, stride=None):
        r_ref = fields[block][1]
        at_row = FRONT + row
        if stride is None:
            here, before = r_ref[pl.ds(at_row, count), :], r_ref[pl.ds(at_row - 1, count), :]
        else:
            here = r_ref[pl.ds(at_row, count, stride=stride), :]
            before = r_ref[pl.ds(at_row - 1, count, stride=stride), :]
        return jnp.where(lanes >= (me * sizes(block, n)[0]) % LANES, here, before)

    def send(src, dst, send_sem, recv_sem, target):
        @pl.when(target == me)
        def _():
            pltpu.make_async_copy(src, dst, send_sem).start()

        @pl.when(target != me)
        def _():
            pltpu.make_async_remote_copy(
                src, dst, send_sem, recv_sem, device_id=flat_device(target), device_id_type=MESH
            ).start()

    def which_of(block, start):
        return jnp.where(start // sizes(block, n)[0] == me, 0, 1)

    def small_units(block, least, most):
        s_ref, small0 = fields[block][2], fields[block][4]

        def body(slot, mat, u, pos, start):
            for k in range(6):
                s_ref[slot, :, k * LANES : (k + 1) * LANES] = load_rows(block, pos + k, UNIT, 6).astype(BF)
            which = which_of(block, start)
            send(
                s_ref.at[slot], land.at[which, mat // 2], s_small.at[small0 + slot], r_unit.at[which, mat // 2],
                u * 2 + mat % 2,
            )

        each_small(block, n, me, sizes(block, n)[2], body, least, most)

    def big_units(block):
        b_ref, big0 = fields[block][3], fields[block][5]
        pair = (block.first_mat + block.small_mats) // 2

        def body(slot, u, pos, start):
            for q in range(4):
                for k in range(6):
                    b_ref[slot, q % 2, q // 2, :, k * LANES : (k + 1) * LANES] = load_rows(
                        block, pos + 6 * q + k, UNIT, 24
                    ).astype(BF)
            which = which_of(block, start)
            for core in range(2):
                send(
                    b_ref.at[slot, core], land.at[which, pl.ds(pair, 2)], s_big.at[big0 + slot, core],
                    r_unit.at[which, pair], u * 2 + core,
                )

        each_big(block, n, me, sizes(block, n)[3], body)

    def vector_units(block):
        def body(v, pos, start):
            sv_ref[v] = load_rows(block, pos, 8).astype(BF).astype(F32)
            which = which_of(block, start)
            send(sv_ref.at[v], landv.at[which], s_vec.at[v], r_vec.at[which], v)

        each_vector(block, n, me, fields[block][6], body)

    def pair_units(pair):
        block = ENC if pair < 6 else DEC
        local = pair - block.first_mat // 2
        half = block.small_mats // 2
        if local == half:
            big_units(block)
        elif local != half + 1:
            first = 2 * local - (4 if local > half else 0)
            small_units(block, first, first + 2)

    prepare(ENC)
    await_all(n)
    pair_units(0)
    vector_units(ENC)
    prepare(DEC)
    vector_units(DEC)
    for pair in range(1, AHEAD):
        pair_units(pair)

    def of_self(first, last, which):
        return jnp.where(which == 0, first, last) == me

    def arrive_unit(first, last, src, dst, local_sem, recv):
        for which, holder in ((0, first), (1, last)):
            needed = True if which == 0 else (first != last)

            @pl.when(needed & (holder == me))
            def _(which=which):
                pltpu.make_async_copy(src(which), dst(which), local_sem).wait()

            @pl.when(needed & (holder != me))
            def _(which=which):
                pltpu.make_async_copy(src(which), dst(which), recv(which)).wait()

    def vec_of(v):
        n_enc = len(ENC.vectors)
        rows = ENC.vectors + DEC.vectors
        start = 0
        before = 0
        for i, row in enumerate(rows):
            start = start + jnp.where(v >= i, row - before, 0)
            before = row
        return start * D, jnp.where(v < n_enc, sizes(ENC, n)[0], sizes(DEC, n)[0])

    @pl.when(me < N_VEC)
    def _():
        start, shard = vec_of(me)
        first, last = start // shard, (start + D - 1) // shard
        arrive_unit(
            first, last, lambda w: sv_ref.at[0], lambda w: landv.at[w], s_vec.at[me], lambda w: r_vec.at[w]
        )
        at_elem = lax.broadcasted_iota(jnp.int32, (8, LANES), 0) * LANES + lax.broadcasted_iota(jnp.int32, (8, LANES), 1)
        ownv[...] = jnp.where(at_elem < (first + 1) * shard - start, landv[0], landv[1])

    @pl.when(me >= N_VEC)
    def _():
        ownv[...] = jnp.zeros_like(ownv)

    pltpu.sync_copy(ownv, v_ref.at[z, x, y, c])
    vorder = ("z", "x", "y", "c")

    def vview(done):
        have = set(vorder[:done])
        return tuple(slice(None) if a in have else at[a] for a in "zxyc")

    def vcopies(phase):
        axis = vorder[phase]
        out = []
        for k, p in enumerate(peers(axis, at)):
            ref = v_ref.at[vview(phase)]
            slot = phase if axis == "z" else phase + 2
            out.append(
                pltpu.make_async_remote_copy(
                    ref, ref, v_send.at[slot + k], v_recv.at[slot + k], device_id=dev(p), device_id_type=MESH
                )
            )
        return out

    row_i = lax.broadcasted_iota(jnp.int32, (UNIT, D), 0)
    col_i = lax.broadcasted_iota(jnp.int32, (UNIT, D), 1)

    def merge(pair):
        block = ENC if pair < 6 else DEC
        shard = sizes(block, n)[0]
        local = pair - block.first_mat // 2
        half = block.small_mats // 2
        if half <= local < half + 2:
            start = (block.fc1 * 6 + chip * BIG) * LANES
            elem = row_i * FF + (2 * (local - half) + c) * D + col_i
            length = BIG * LANES
        else:
            small = 2 * local - (4 if local >= half + 2 else 0) + c
            start = (small_row(block, small) * 6 + chip * UROWS) * LANES
            elem = row_i * D + col_i
            length = UROWS * LANES
        first, last = start // shard, (start + length - 1) // shard
        if half <= local < half + 2:
            if local == half:
                low_row = me * shard // LANES
                slot = (start // LANES - low_row + BIG) // BIG + (0 if block is ENC else sizes(ENC, n)[3])
                slot = jnp.minimum(jnp.maximum(slot, 0), sizes(ENC, n)[3] + sizes(DEC, n)[3] - 1)
                arrive_unit(
                    first, last, lambda w: land.at[w, pl.ds(pair, 2)], lambda w: land.at[w, pl.ds(pair, 2)],
                    s_big.at[slot, c], lambda w: r_unit.at[w, pair],
                )
        else:
            low_row = me * shard // LANES
            slot = (start // LANES - low_row + UROWS) // UROWS + (0 if block is ENC else sizes(ENC, n)[2])
            slot = jnp.minimum(jnp.maximum(slot, 0), sizes(ENC, n)[2] + sizes(DEC, n)[2] - 1)
            arrive_unit(
                first, last, lambda w: land.at[w, pair], lambda w: land.at[w, pair],
                s_small.at[slot], lambda w: r_unit.at[w, pair],
            )
        own[pair] = jnp.where(elem < (first + 1) * shard - start, land[0, pair], land[1, pair])

    def own_place(pair):
        return w_ref.at[pair, c, z, x, y]

    def remote(src, dst, pair, k, target):
        return pltpu.make_async_remote_copy(
            src, dst, s_zxy.at[pair, k], r_zxy.at[pair, k], device_id=target, device_id_type=MESH
        )

    def copies(pair, phase):
        if phase == 0:
            return [
                remote(own.at[pair], own_place(pair), pair, 2 + k, device((z + k) % 4, x, y, c)) for k in (1, 2, 3)
            ]
        if phase == 1:
            ref = w_ref.at[pair, c, :, x, y]
            return [remote(ref, ref, pair, 0, first_peer(at))]
        if phase == 2:
            ref = w_ref.at[pair, c, :, :, y]
            return [remote(ref, ref, pair, 1, second_peer(at))]
        ref = w_ref.at[pair, c]
        return [remote(ref, ref, pair, 2, device(z, x, y, 1 - c))]

    def begin(pair, phase):
        if phase != 2:
            for cp in copies(pair, phase):
                cp.start()
            return

        @pl.when(c == 0)
        def _():
            copies(pair, 2)[0].start()

        @pl.when(c == 1)
        def _():
            ref = w_ref.at[pair, c, :, x]
            remote(ref, ref, pair, 1, second_peer(at)).start()

    for t in range(N_PAIR + F_AT[3]):
        if t < N_PAIR:
            merge(t)
            pltpu.make_async_copy(own.at[t], own_place(t), s_own.at[t]).start()
            begin(t, 0)
        for phase in (1, 2, 3):
            pair = t - F_AT[phase - 1]
            if 0 <= pair < N_PAIR:
                if phase == 1:
                    pltpu.make_async_copy(own.at[pair], own_place(pair), s_own.at[pair]).wait()
                for cp in copies(pair, phase - 1):
                    cp.wait_recv()
                begin(pair, phase)
        if t + AHEAD < N_PAIR:
            pair_units(t + AHEAD)
        if t == 1:
            on_start()
        if t < 5:
            if t > 0:
                for cp in vcopies(t - 1):
                    cp.wait_recv()
            if t < 4:
                for cp in vcopies(t):
                    cp.start()
            else:
                on_vectors()
        pair = t - F_AT[3]
        if pair == N_PAIR - 1:
            on_last()
        if 0 <= pair < N_PAIR:
            for cp in copies(pair, 3):
                cp.wait_recv()
            on_pair(pair)

    for phase in range(4):
        for cp in vcopies(phase):
            cp.wait_send()
    for pair in range(N_PAIR):
        for phase in range(4):
            for cp in copies(pair, phase):
                cp.wait_send()
    for b, (block, s_ref, b_ref) in enumerate(((ENC, se_ref, be_ref), (DEC, sd_ref, bd_ref))):
        shard, rows, n_small, n_big = sizes(block, n)
        small0 = 0 if b == 0 else sizes(ENC, n)[2]
        big0 = 0 if b == 0 else sizes(ENC, n)[3]

        def small_wait(slot, mat, u, pos, start, s_ref=s_ref, small0=small0):
            @pl.when(u * 2 + mat % 2 != me)
            def _():
                pltpu.make_async_copy(s_ref.at[slot], s_ref.at[slot], s_small.at[small0 + slot]).wait()

        def big_wait(slot, u, pos, start, b_ref=b_ref, big0=big0):
            for core in range(2):
                @pl.when(u * 2 + core != me)
                def _(core=core):
                    pltpu.make_async_copy(
                        b_ref.at[slot, core], b_ref.at[slot, core], s_big.at[big0 + slot, core]
                    ).wait()

        def vec_wait(v, pos, start):
            @pl.when(me != v)
            def _():
                pltpu.make_async_copy(sv_ref.at[v], sv_ref.at[v], s_vec.at[v]).wait()

        each_vector(block, n, me, 0 if b == 0 else len(ENC.vectors), vec_wait)
        each_small(block, n, me, n_small, small_wait)
        each_big(block, n, me, n_big, big_wait)


def rows_of(flat, rows):
    return jnp.pad(flat, (0, rows * LANES - flat.shape[0])).reshape(rows, LANES)


SCALE = HEAD_DIM ** (-0.5)
FORBID = -1000000000.0
ROOT_HALF = 0.7071067811865476
PDF = 0.3989422804014327


def mm(a, b):
    return jnp.dot(a, b, preferred_element_type=F32)


def mm_nt(a, b):
    return lax.dot_general(a, b, (((1,), (1,)), ((), ())), preferred_element_type=F32)


def mm_tn(a, b):
    return lax.dot_general(a, b, (((0,), (0,)), ((), ())), preferred_element_type=F32)


def col_blocks(body, width=256):
    def step(j, carry):
        body(pl.ds(pl.multiple_of(j * width, width), width))
        return carry

    lax.fori_loop(0, D // width, step, 0)


def row_blocks(rows, body, height=64):
    def step(i, carry):
        body(pl.ds(pl.multiple_of(i * height, height), height))
        return carry

    lax.fori_loop(0, rows // height, step, 0)


def linear(x_ref, w_ref, rows, out_ref, bias=None):
    x = x_ref[0:rows, :]

    def body(cols):
        y = mm(x, w_ref[:, cols])
        if bias is not None:
            y = y + bias[:, cols]
        out_ref[0:rows, cols] = y.astype(out_ref.dtype)

    col_blocks(body)


def norm_rows(x):
    centred = x - jnp.mean(x, axis=1, keepdims=True)
    spread = jnp.mean(centred * centred, axis=1, keepdims=True)
    root = lax.rsqrt(spread + 1e-05)
    return centred * root, root


def norm_forward_ref(x_ref, gain, shift, rows, out_ref):
    def body(r):
        hat, _ = norm_rows(x_ref[r, :].astype(F32))
        out_ref[r, :] = (hat * gain[...] + shift[...]).astype(BF)

    row_blocks(rows, body)


def attend_tiles(rows, keys, causal):
    return [(start, min(start + 128, keys) if causal else keys) for start in range(0, rows, 128)]


def both_heads(x):
    lane = lax.broadcasted_iota(jnp.int32, (1, LANES), 1)
    zero = jnp.zeros_like(x)
    return jnp.concatenate([jnp.where(lane < HEAD_DIM, x, zero), jnp.where(lane < HEAD_DIM, zero, x)], axis=0)


def scores_of(k, q2, mask_ref, start, reach):
    scores = mm_nt(k, q2)
    if mask_ref is not None:
        mask = mask_ref[0:reach, start : start + LANES]
        scores = jnp.where(jnp.concatenate([mask, mask], axis=1) > 0, scores, FORBID)
    return scores


def attention_forward_ref(q_ref, k_ref, v_ref, mask_ref, rows, keys, mixed_ref, lse_ref):
    def pair_of_heads(i, carry):
        cols = pl.ds(pl.multiple_of(i * LANES, LANES), LANES)
        v_turned = jnp.transpose(v_ref[0:keys, cols])
        for tile, (start, reach) in enumerate(attend_tiles(rows, keys, mask_ref is not None)):
            r = slice(start, start + LANES)
            q2 = both_heads(q_ref[r, cols] * jnp.asarray(SCALE, BF))
            scores = scores_of(k_ref[0:reach, cols], q2, mask_ref, start, reach)
            peak = jnp.max(scores, axis=0, keepdims=True)
            weights = jnp.exp(scores - peak)
            totals = jnp.sum(weights, axis=0, keepdims=True)
            probs = weights.astype(BF)
            share = 1.0 / totals
            mixed = jnp.concatenate(
                [
                    mm(v_turned[s * HEAD_DIM : (s + 1) * HEAD_DIM, 0:reach], probs[:, s * LANES : (s + 1) * LANES])
                    * share[:, s * LANES : (s + 1) * LANES]
                    for s in range(2)
                ],
                axis=0,
            )
            mixed_ref[r, cols] = jnp.transpose(mixed).astype(BF)
            lse_ref[tile, pl.ds(i, 1), :] = peak + jnp.log(totals)
        return carry

    lax.fori_loop(0, D // LANES, pair_of_heads, 0, unroll=1 if mask_ref is not None else 2)


def project_add(x_ref, mixed_ref, w_ref, bias, rows, out_ref):
    m = mixed_ref[0:rows, :]

    def body(cols):
        out_ref[0:rows, cols] = x_ref[0:rows, cols].astype(F32) + mm(m, w_ref[:, cols]) + bias[:, cols]

    col_blocks(body)


def gelu_block(n_ref, w_ref, bias, rows, block, act_ref, slope_ref):
    x = n_ref[0:rows, :]

    def body(cols):
        pre = mm(x, w_ref[:, cols]) + bias[:, cols]
        bell = 0.5 * (1.0 + lax.erf(pre * ROOT_HALF))
        act_ref[block, 0:rows, cols] = (pre * bell).astype(BF)
        slope_ref[block, 0:rows, cols] = (bell + pre * (PDF * jnp.exp(-0.5 * pre * pre))).astype(BF)

    col_blocks(body, 128)


def accumulate(a_ref, w_ref, rows, out_ref):
    a = a_ref[0:rows, :]

    def body(cols):
        out_ref[0:rows, cols] += mm(a, w_ref[:, cols])

    col_blocks(body)


def add_row(out_ref, x_ref, row_ref, r):
    out_ref[r, :] = x_ref[r, :] + row_ref[...]


def both(body):
    def step(k, carry):
        body(k)
        return carry

    lax.fori_loop(0, 2, step, 0)


N_SAVED = 28


def saved_shapes(rows, frames):
    tall = -(-rows // 128) * 128
    enc_lse, dec_lse = ((frames // 128, 8, 2 * LANES), F32), ((tall // 128, 8, 2 * LANES), F32)
    return (
        [((frames, D), BF)] * 5
        + [enc_lse, ((frames, D), F32), ((frames, D), BF), ((4, frames, D), BF), ((4, frames, D), BF), ((frames, D), BF)]
        + [((rows, D), BF)]
        + [((tall, D), BF)] * 4
        + [dec_lse, ((rows, D), F32), ((rows, D), BF)]
        + [((tall, D), BF), ((frames, D), BF), ((frames, D), BF), ((tall, D), BF), dec_lse]
        + [((rows, D), F32), ((rows, D), BF), ((4, rows, D), BF), ((4, rows, D), BF)]
    )


def make_mask(seg_ref, row_ref, col_ref, mask_ref):
    rows, tall = seg_ref.shape[1], mask_ref.shape[0]
    row_ref[...] = jnp.full(row_ref.shape, -1.0, F32)
    row_ref[0:1, 0:rows] = seg_ref[...].astype(F32)
    for i in range(tall // LANES):
        part = slice(i * LANES, (i + 1) * LANES)
        col_ref[part, :] = jnp.transpose(jnp.broadcast_to(row_ref[0:1, part], (LANES, LANES)))

    def body(r):
        key = lax.broadcasted_iota(jnp.int32, (64, tall), 0) + r.start
        query = lax.broadcasted_iota(jnp.int32, (64, tall), 1)
        allowed = (col_ref[r, 0:1] == row_ref[0:1, :]) & (key <= query)
        mask_ref[r, :] = jnp.where(allowed, 1.0, 0.0)

    row_blocks(tall, body)


def forward_kernel(n, rows, frames, *refs):
    xe_ref, xd_ref, ein_ref, din_ref, seg_ref, dcot_ref, w_ref, v_ref = refs[:8]
    outs, refs = refs[8 : 8 + N_SAVED], refs[8 + N_SAVED :]
    early_ref, refs = refs[0], refs[1:]
    comm, refs = refs[:24], refs[24:]
    bufs, refs = refs[:N_SAVED], refs[N_SAVED:]
    vv, wbuf, acc, mask_ref, seg_row, seg_col, s_save, s_w, cot, gown, gsum, s_g, r_g, s_early = refs
    _, _, z, x, y, c = whoami()
    (
        e_n1, e_q, e_k, e_v, e_mix, e_lse, e_after, e_n2, e_act, e_slope, e_out,
        d_n1, d_q, d_k, d_v, d_mix, d_lse, d_after, d_n2,
        c_q, c_k, c_v, c_mix, c_lse, d_after2, d_n3, d_act, d_slope,
    ) = bufs
    eacc = acc.at[0:frames]

    def vec(i):
        return vv.at[pl.ds(i, 1)]

    def save(*indices):
        for i in indices:
            pltpu.make_async_copy(bufs[i], outs[i], s_save.at[i]).start()

    def cot_copy():
        return pltpu.make_async_copy(dcot_ref, cot, s_early.at[0])

    def early_core(i):
        return pltpu.make_async_remote_copy(
            gown.at[i, 1 - c], gsum.at[i], s_g.at[i], r_g.at[i], device_id=device(z, x, y, 1 - c), device_id_type=MESH
        )

    def early_save(i):
        return pltpu.make_async_copy(gsum.at[i], early_ref.at[i], s_early.at[i])

    def early_grad(i):
        both(lambda k: weight_grad(d_act.at[2 - 2 * i + k], cot, rows, gown.at[i, k]))
        early_core(i).start()

    def early_sum(i):
        early_core(i).wait_recv()

        def body(j, carry):
            a, b = j // 2, j % 2
            for k in range(2):
                gsum[i, a, b, k] = (gsum[i, a, b, k].astype(F32) + gown[i, c, a, b, k].astype(F32)).astype(BF)
            return carry

        lax.fori_loop(0, 8, body, 0)
        early_save(i).start()

    def on_last():
        early_sum(0)
        early_sum(1)

    def on_start():
        cot_copy().start()
        make_mask(seg_ref, seg_row, seg_col, mask_ref)
        for ref in (d_q, d_k, d_v, c_q):
            if ref.shape[0] > rows:
                ref[rows:, :] = jnp.zeros((ref.shape[0] - rows, D), BF)
        for ref in (e_lse, d_lse, c_lse):
            ref[...] = jnp.zeros_like(ref)

    def on_vectors():
        pltpu.sync_copy(v_ref, vv_tiles)
        for i in range(N_VEC):
            for k in range(6):
                vv[i : i + 1, k * LANES : (k + 1) * LANES] = vv_tiles[i // 8, i // 4 % 2, i // 2 % 2, i % 2, k : k + 1, :]

    def on_pair(pair):
        if pair == 12:
            cot_copy().wait()
            early_grad(0)
            early_grad(1)
        if pair > 11:
            return
        cps = [pltpu.make_async_copy(w_ref.at[pair, k].reshape(D, D), wbuf.at[k], s_w.at[k]) for k in range(2)]
        for cp in cps:
            cp.start()
        if pair == 0:
            norm_forward_ref(ein_ref, vec(0), vec(1), frames, e_n1)
        if pair == 6:
            norm_forward_ref(din_ref, vec(12), vec(13), rows, d_n1)
        for cp in cps:
            cp.wait()
        w0, w1 = wbuf.at[0], wbuf.at[1]
        if pair == 0:
            linear(e_n1, w0, frames, e_q, vec(2))
            linear(e_n1, w1, frames, e_k)
            save(0, 1, 2)
        elif pair == 1:
            linear(e_n1, w0, frames, e_v, vec(3))
            attention_forward_ref(e_q, e_k, e_v, None, frames, frames, e_mix, e_lse)
            project_add(ein_ref, e_mix, w1, vec(4), frames, e_after)
            norm_forward_ref(e_after, vec(5), vec(6), frames, e_n2)
            save(3, 4, 5, 6, 7)
        elif pair in (2, 3):
            both(lambda k: gelu_block(
                e_n2, wbuf.at[k], vec(7 + 2 * (pair - 2) + k), frames, 2 * (pair - 2) + k, e_act, e_slope
            ))
            if pair == 3:
                save(8, 9)
        elif pair in (4, 5):
            if pair == 4:
                eacc[...] = e_after[...] + vec(11)[...]
            both(lambda k: accumulate(e_act.at[2 * (pair - 4) + k], wbuf.at[k], frames, eacc))
            if pair == 5:
                e_out[...] = eacc[...].astype(BF)
                save(10)
        elif pair == 6:
            linear(d_n1, w0, rows, d_q, vec(14))
            linear(d_n1, w1, rows, d_k)
            save(11, 12, 13)
        elif pair == 7:
            linear(d_n1, w0, rows, d_v, vec(15))
            attention_forward_ref(d_q, d_k, d_v, mask_ref, d_q.shape[0], d_k.shape[0], d_mix, d_lse)
            project_add(din_ref, d_mix, w1, vec(16), rows, d_after)
            norm_forward_ref(d_after, vec(17), vec(18), rows, d_n2)
            save(14, 15, 16, 17, 18)
        elif pair == 8:
            linear(d_n2, w0, rows, c_q, vec(19))
            linear(e_out, w1, frames, c_k)
            save(19, 20)
        elif pair == 9:
            linear(e_out, w0, frames, c_v, vec(20))
            attention_forward_ref(c_q, c_k, c_v, None, c_q.shape[0], frames, c_mix, c_lse)
            project_add(d_after, c_mix, w1, vec(21), rows, d_after2)
            norm_forward_ref(d_after2, vec(22), vec(23), rows, d_n3)
            save(21, 22, 23, 24, 25)
        elif pair in (10, 11):
            both(lambda k: gelu_block(
                d_n3, wbuf.at[k], vec(24 + 2 * (pair - 10) + k), rows, 2 * (pair - 10) + k, d_act, d_slope
            ))
            if pair == 11:
                save(26, 27)

    vv_tiles = comm[-1]
    gather_kernel(n, on_start, on_vectors, on_pair, on_last, xe_ref, xd_ref, w_ref, v_ref, *comm[:-1])
    for i in range(N_SAVED):
        pltpu.make_async_copy(bufs[i], outs[i], s_save.at[i]).wait()
    for i in range(2):
        early_core(i).wait_send()
        early_save(i).wait()


def forward_pass(encoder_master, decoder_master, encoder_input, decoder_input, segments, decoder_cotangent, n):
    (_, re, ne, ge), (_, rd, nd, gd) = sizes(ENC, n), sizes(DEC, n)
    frames, rows = encoder_input.shape[0], decoder_input.shape[0]
    tall = -(-rows // 128) * 128
    dma = pltpu.SemaphoreType.DMA
    saved = saved_shapes(rows, frames)
    vmem, hbm = pl.BlockSpec(memory_space=pltpu.VMEM), pl.BlockSpec(memory_space=pl.ANY)
    return pl.pallas_call(
        partial(forward_kernel, n, rows, frames),
        out_shape=(
            jax.ShapeDtypeStruct((N_PAIR, 2, 4, 2, 2, UNIT, D), BF),
            jax.ShapeDtypeStruct((4, 2, 2, 2, 8, LANES), F32),
            *(jax.ShapeDtypeStruct(shape, dtype) for shape, dtype in saved),
            jax.ShapeDtypeStruct((2, 4, 2, 2, UNIT, D), BF),
        ),
        in_specs=[vmem] * 5 + [hbm],
        out_specs=(hbm,) * (3 + N_SAVED),
        scratch_shapes=[
            pltpu.VMEM((FRONT + re + BACK, LANES), F32),
            pltpu.VMEM((FRONT + rd + BACK, LANES), F32),
            pltpu.VMEM((ne, UNIT, D), BF),
            pltpu.VMEM((nd, UNIT, D), BF),
            pltpu.VMEM((ge, 2, 2, UNIT, D), BF),
            pltpu.VMEM((gd, 2, 2, UNIT, D), BF),
            pltpu.VMEM((N_VEC, 8, LANES), F32),
            pltpu.VMEM((2, N_PAIR, UNIT, D), BF),
            pltpu.VMEM((2, 8, LANES), F32),
            pltpu.VMEM((N_PAIR, UNIT, D), BF),
            pltpu.VMEM((8, LANES), F32),
            dma((ne + nd,)),
            dma((ge + gd, 2)),
            dma((N_VEC,)),
            dma((2, N_PAIR)),
            dma((2,)),
            dma((N_PAIR, 6)),
            dma((N_PAIR, 6)),
            dma((N_PAIR,)),
            dma((N_PAIR,)),
            dma((N_PAIR,)),
            dma((6,)),
            dma((6,)),
            pltpu.VMEM((4, 2, 2, 2, 8, LANES), F32),
            *(pltpu.VMEM(shape, dtype) for shape, dtype in saved),
            pltpu.VMEM((32, D), F32),
            pltpu.VMEM((2, D, D), BF),
            pltpu.VMEM((rows, D), F32),
            pltpu.VMEM((tall, tall), F32),
            pltpu.VMEM((8, tall), F32),
            pltpu.VMEM((tall, LANES), F32),
            dma((N_SAVED,)),
            dma((2,)),
            pltpu.VMEM((rows, D), BF),
            pltpu.VMEM((2, 2, 4, 2, 2, UNIT, D), BF),
            pltpu.VMEM((2, 4, 2, 2, UNIT, D), BF),
            dma((2,)),
            dma((2,)),
            dma((2,)),
        ],
        compiler_params=pltpu.CompilerParams(collective_id=0, has_side_effects=True, vmem_limit_bytes=58 << 20),
        name="forward",
    )(rows_of(encoder_master, re), rows_of(decoder_master, rd), encoder_input, decoder_input, segments,
      decoder_cotangent)


RING = 3
RING_C = 5
EARLY = 2


def scatter_kernel(
    n, begin_loads, produce, after, early_ref, vg_ref, gbuf, oe_ref, od_ref, norm_ref,
    land_c, land_b, land_a, land_z, ownb, vown, vl_c, vl_y, vl_x, vl_z,
    ge_ref, gd_ref, fe, fd, fbe, fbd, fv, nsend, nland,
    s_core, r_core, s_free, s_ph, r_ph, s_back, r_small, r_big, sv, rv, s_vback, r_vback, s_n, r_n, s_out,
):
    wide, narrow, z, x, y, c = whoami()
    me = wide * 4 + narrow
    chip = me // 2
    at = dict(z=z, x=x, y=y, c=c)
    greet(me, n)
    sib = device(z, x, y, 1 - c)

    def slot_c(pair):
        return (N_PAIR - 1 - pair) % RING_C

    def core_copy(pair):
        return pltpu.make_async_remote_copy(
            gbuf.at[(N_PAIR - 1 - pair) % RING, 1 - c], land_c.at[slot_c(pair)], s_core.at[pair], r_core.at[pair], device_id=sib, device_id_type=MESH
        )

    mine_a = x * (1 - c) + y * c

    def phase_dmas(pair, phase):
        if phase == 1:
            steps = [(land_c.at[slot_c(pair), :, :, 1 - y], land_b.at[pair], 0, second_peer(at))]
        elif phase == 2:
            steps = [(land_b.at[pair, :, 1 - mine_a], land_a.at[pair], 1, first_peer(at))]
        else:
            steps = [
                (land_a.at[pair, (z + k) % 4], land_z.at[pair, k - 1], 1 + k, device((z + k) % 4, x, y, c))
                for k in (1, 2, 3)
            ]
        return [
            pltpu.make_async_remote_copy(
                src, dst, s_ph.at[pair, k], r_ph.at[pair, k], device_id=target, device_id_type=MESH
            )
            for src, dst, k, target in steps
        ]

    def begin(pair, phase):
        if phase != 1:
            for cp in phase_dmas(pair, phase):
                cp.start()
            return

        @pl.when(c == 0)
        def _():
            phase_dmas(pair, 1)[0].start()

        @pl.when(c == 1)
        def _():
            pltpu.make_async_remote_copy(
                land_c.at[slot_c(pair), :, 1 - x], land_b.at[pair], s_ph.at[pair, 0], r_ph.at[pair, 0],
                device_id=second_peer(at), device_id_type=MESH,
            ).start()

    def back(pair):
        block = ENC if pair < 6 else DEC
        shard = sizes(block, n)[0]
        local = pair - block.first_mat // 2
        half = block.small_mats // 2
        big = half <= local < half + 2
        if big:
            start = (block.fc1 * 6 + chip * BIG) * LANES
            length = BIG * LANES
        else:
            small = 2 * local - (4 if local >= half + 2 else 0) + c
            start = (small_row(block, small) * 6 + chip * UROWS) * LANES
            length = UROWS * LANES
        first, last = start // shard, (start + length - 1) // shard
        out = []
        for which, target in ((0, first), (1, last)):
            low_row = target * shard // LANES
            if big:
                slot = (start // LANES - low_row + BIG) // BIG
                q = 2 * (local - half) + c
                dst = (fbe if block is ENC else fbd).at[slot, q]
                recv = r_big.at[0 if block is ENC else 1, slot, q]
            else:
                slot = (start // LANES - low_row + UROWS) // UROWS
                dst = (fe if block is ENC else fd).at[slot]
                recv = r_small.at[0 if block is ENC else 1, slot]
            needed = True if which == 0 else first != last
            out.append((needed, target, dst, s_back.at[pair, which], recv))
        return out

    def start_back(pair):
        for needed, target, dst, send, recv in back(pair):
            @pl.when(needed & (target == me))
            def _(dst=dst, recv=recv):
                pltpu.make_async_copy(ownb.at[pair], dst, recv).start()

            @pl.when(needed & (target != me))
            def _(dst=dst, recv=recv, send=send, target=target):
                pltpu.make_async_remote_copy(
                    ownb.at[pair], dst, send, recv, device_id=flat_device(target), device_id_type=MESH
                ).start()

    def end_back(pair):
        for needed, target, dst, send, recv in back(pair):
            @pl.when(needed & (target != me))
            def _(send=send):
                pltpu.make_async_copy(ownb.at[pair], ownb.at[pair], send).wait()

    def add_core(pair):
        def body(i, carry):
            a, b = i // 2, i % 2
            for k in range(2):
                mine = gbuf[(N_PAIR - 1 - pair) % RING, c, a, b, k]
                land_c[slot_c(pair), a, b, k] = (
                    land_c[slot_c(pair), a, b, k].astype(F32) + mine.astype(F32)
                ).astype(BF)
            return carry

        lax.fori_loop(0, 8, body, 0)

    def add_b(pair):
        def body(i, carry):
            a, b = i // 2, i % 2
            mine = land_c[slot_c(pair), a, b * (1 - c) + x * c, y * (1 - c) + b * c]
            land_b[pair, a, b] = (land_b[pair, a, b].astype(F32) + mine.astype(F32)).astype(BF)
            return carry

        lax.fori_loop(0, 8, body, 0)

    def add_a(pair):
        for a in range(4):
            land_a[pair, a] = (land_a[pair, a].astype(F32) + land_b[pair, a, mine_a].astype(F32)).astype(BF)

    def add_z(pair):
        total = land_a[pair, z].astype(F32)
        for k in range(3):
            total = total + land_z[pair, k].astype(F32)
        ownb[pair] = total.astype(BF)
        squares = total * total
        return jnp.sum(squares.reshape(UNIT // 8, 8, D), axis=0)

    vland = dict(c=vl_c, y=vl_y, x=vl_x, z=vl_z)

    def vsteps(phase):
        if phase == 0:
            return [(vg_ref.at[:, :, :, 1 - c], vl_c, 0, dict(at, c=1 - c))]
        if phase == 1:
            return [(vl_c.at[:, :, 1 - y], vl_y, 1, dict(at, y=1 - y))]
        if phase == 2:
            return [(vl_y.at[:, 1 - x], vl_x, 2, dict(at, x=1 - x))]
        return [(vl_x.at[(z + k) % 4], vl_z.at[k - 1], 2 + k, dict(at, z=(z + k) % 4)) for k in (1, 2, 3)]

    def vdmas(phase):
        return [
            pltpu.make_async_remote_copy(s, d, sv.at[k], rv.at[k], device_id=dev(p), device_id_type=MESH)
            for s, d, k, p in vsteps(phase)
        ]

    def vadd(phase):
        if phase == 0:
            vl_c[...] = vl_c[...] + vg_ref[:, :, :, c]
        elif phase == 1:
            vl_y[...] = vl_y[...] + vl_c[:, :, y]
        elif phase == 2:
            vl_x[...] = vl_x[...] + vl_y[:, x]
        else:
            vown[...] = vl_x[z] + vl_z[0] + vl_z[1] + vl_z[2]

    fields = {ENC: (0, ge_ref, oe_ref, fe, fbe), DEC: (1, gd_ref, od_ref, fd, fbd)}

    def units_to_flat(block, least=0, most=99):
        b, g_out, _, f_ref, fb_ref = fields[block]
        _, _, n_small, n_big = sizes(block, n)

        def small_body(slot, mat, u, pos, start):
            pltpu.make_async_copy(f_ref.at[slot], f_ref.at[slot], r_small.at[b, slot]).wait()
            for k in range(6):
                g_out[pl.ds(FRONT + pos + k, UNIT, stride=6), :] = f_ref[slot, :, k * LANES : (k + 1) * LANES].astype(F32)

        def big_body(slot, u, pos, start):
            for q in range(4):
                pltpu.make_async_copy(fb_ref.at[slot, q], fb_ref.at[slot, q], r_big.at[b, slot, q]).wait()
                for k in range(6):
                    g_out[pl.ds(FRONT + pos + 6 * q + k, UNIT, stride=24), :] = fb_ref[
                        slot, q, :, k * LANES : (k + 1) * LANES
                    ].astype(F32)

        if most > block.small_mats:
            each_big(block, n, me, n_big, big_body)
        each_small(block, n, me, n_small, small_body, least, most)

    def finish_flat(block):
        b, g_out, o_ref, _, _ = fields[block]
        shard, rows, _, _ = sizes(block, n)

        def vec_body(v, pos, start):
            pltpu.make_async_copy(fv.at[v], fv.at[v], r_vback.at[v]).wait()
            g_out[pl.ds(FRONT + pos, 6), :] = fv[v, 0:6, :]

        each_vector(block, n, me, 0 if block is ENC else len(ENC.vectors), vec_body)
        shift = (me * shard) % LANES
        step = 8 * max(k for k in range(1, 40) if (rows // 8) % k == 0)
        lanes = lax.broadcasted_iota(jnp.int32, (1, LANES), 1)
        unturn = lax.rem(LANES - shift, LANES)

        def turn(i, carry):
            at_row = pl.multiple_of(i * step, 8)
            here = pltpu.roll(g_out[pl.ds(FRONT + at_row, step), :], unturn, 1)
            after = pltpu.roll(g_out[pl.ds(FRONT + at_row + 1, step), :], unturn, 1)
            g_out[pl.ds(FRONT + at_row, step), :] = jnp.where(lanes < LANES - shift, here, after)
            return carry

        lax.fori_loop(0, rows // step, turn, 0)
        pltpu.make_async_copy(g_out.at[pl.ds(FRONT, rows)], o_ref, s_out.at[b]).start()

    def vector_targets(v_static):
        block = ENC if v_static < len(ENC.vectors) else DEC
        shard = sizes(block, n)[0]
        start = (ENC.vectors + DEC.vectors)[v_static] * D
        return start // shard, (start + D - 1) // shard

    def vectors_back():
        for v in range(N_VEC):
            for which, target in enumerate(sorted(set(vector_targets(v)))):
                if target == v:
                    @pl.when(me == v)
                    def _(v=v):
                        pltpu.make_async_copy(vown, fv.at[v], r_vback.at[v]).start()
                else:
                    @pl.when(me == v)
                    def _(v=v, target=target, which=which):
                        pltpu.make_async_remote_copy(
                            vown, fv.at[v], s_vback.at[which], r_vback.at[v], device_id=(target // 4, target % 4), device_id_type=MESH
                        ).start()

    seq = list(range(N_PAIR - 1, -1, -1))
    square = jnp.zeros((8, D), F32)
    def early_copy(i):
        return pltpu.make_async_copy(early_ref.at[i], land_c.at[i], s_core.at[i])

    for i in range(EARLY):
        early_copy(i).start()
    begin_loads()
    await_all(n)
    for i in range(EARLY):
        early_copy(i).wait()
        begin(seq[i], 1)
    for t in range(EARLY, N_PAIR + B_AT[3]):
        if t < N_PAIR:
            if t - RING >= EARLY:
                core_copy(seq[t - RING]).wait_send()
            produce(t, gbuf.at[t % RING])
            if t >= RING_C:
                pl.semaphore_wait(s_free, 1)
            core_copy(seq[t]).start()
        for phase in (4, 3, 2, 1):
            i = t - B_AT[phase - 1]
            if 0 <= i < N_PAIR:
                pair = seq[i]
                if phase == 1 and i < EARLY:
                    continue
                if phase == 1:
                    core_copy(pair).wait_recv()
                    add_core(pair)
                elif phase == 2:
                    for cp in phase_dmas(pair, 1):
                        cp.wait()
                    add_b(pair)
                    if i < N_PAIR - RING_C:
                        pl.semaphore_signal(s_free, inc=1, device_id=sib, device_id_type=MESH)
                elif phase == 3:
                    for cp in phase_dmas(pair, 2):
                        cp.wait_recv()
                    add_a(pair)
                else:
                    for cp in phase_dmas(pair, 3):
                        cp.wait_recv()
                    square = square + add_z(pair)
                    start_back(pair)
                if phase < 4:
                    begin(pair, phase)
        after(t)
        if t == N_PAIR + B_AT[2] - 1:
            units_to_flat(DEC)
        if t == N_PAIR + B_AT[3] - 1:
            finish_flat(DEC)
            units_to_flat(ENC, 2, 99)
        if t == N_PAIR - 1:
            for cp in vdmas(0):
                cp.start()
        elif N_PAIR <= t < N_PAIR + 4:
            phase = t - N_PAIR
            for cp in vdmas(phase):
                cp.wait_recv()
            vadd(phase)
            if phase < 3:
                for cp in vdmas(phase + 1):
                    cp.start()
            else:
                vectors_back()

    vsq = vown[...] * vown[...]
    for k in range(6):
        vsq = vsq + square[:, k * LANES : (k + 1) * LANES]
    nsend[...] = vsq

    def norm_copy(i):
        return pltpu.make_async_remote_copy(
            nsend, nland.at[i], s_n.at[i], r_n.at[i], device_id=flat_device((me + i) % n), device_id_type=MESH
        )

    def norm_start(i, carry):
        norm_copy(i).start()
        return carry

    lax.fori_loop(1, n, norm_start, 0)

    units_to_flat(ENC, 0, 2)
    finish_flat(ENC)

    def norm_wait(i, total):
        norm_copy(i).wait()
        return total + nland[i]

    total = lax.fori_loop(1, n, norm_wait, nsend[...])
    norm_ref[...] = jnp.broadcast_to(jnp.sqrt(jnp.sum(total)), (8, LANES))

    for b, (g_out, o_ref) in enumerate(((ge_ref, oe_ref), (gd_ref, od_ref))):
        pltpu.make_async_copy(g_out.at[pl.ds(FRONT, o_ref.shape[0])], o_ref, s_out.at[b]).wait()
    for phase in range(4):
        for cp in vdmas(phase):
            cp.wait_send()
    for v in range(N_VEC):
        for which, target in enumerate(sorted(set(vector_targets(v)))):
            if target != v:
                @pl.when(me == v)
                def _(which=which):
                    pltpu.make_async_copy(vown, vown, s_vback.at[which]).wait()
    for pair in range(N_PAIR):
        if N_PAIR - 1 - pair >= N_PAIR - RING:
            core_copy(pair).wait_send()
        for phase in (2, 3):
            for cp in phase_dmas(pair, phase):
                cp.wait_send()
        end_back(pair)


def sum_rows(ref, rows, out_ref):
    def body(r):
        out_ref[...] += jnp.sum(ref[r, :].astype(F32), axis=0, keepdims=True)

    out_ref[...] = jnp.zeros_like(out_ref)
    row_blocks(rows, body)


def norm_backward_ref(x_ref, gain, dn_ref, rows, out_ref, gain_grad, shift_grad):
    gain_grad[...] = jnp.zeros_like(gain_grad)
    shift_grad[...] = jnp.zeros_like(shift_grad)

    def body(r):
        hat, root = norm_rows(x_ref[r, :].astype(F32))
        dn = dn_ref[r, :]
        gain_grad[...] += jnp.sum(dn * hat, axis=0, keepdims=True)
        shift_grad[...] += jnp.sum(dn, axis=0, keepdims=True)
        g = dn * gain[...]
        part = g - jnp.mean(g, axis=1, keepdims=True) - hat * jnp.mean(g * hat, axis=1, keepdims=True)
        out_ref[r, :] += root * part

    row_blocks(rows, body)


def round_rows(src_ref, rows, out_ref):
    def body(r):
        out_ref[r, :] = src_ref[r, :].astype(BF)

    row_blocks(rows, body)


def weight_grad(a_ref, b_ref, rows, g_ref):
    b = b_ref[0:rows, :]
    flat = g_ref.reshape(D, D)

    def body(cols):
        flat[cols, :] = mm_tn(a_ref[0:rows, cols], b).astype(BF)

    col_blocks(body)


def back_through(a_ref, w_ref, rows, out_ref, add):
    a = a_ref[0:rows, :]

    def body(cols):
        y = mm_nt(a, w_ref[cols, :])
        if add:
            y = y + out_ref[0:rows, cols]
        out_ref[0:rows, cols] = y.astype(out_ref.dtype)

    col_blocks(body)


def gelu_back(o_ref, w_ref, slope_ref, rows, out_ref, bias_grad):
    a = o_ref[0:rows, :]

    def body(cols):
        y = mm_nt(a, w_ref[cols, :]) * slope_ref[0:rows, cols].astype(F32)
        bias_grad[:, cols] = jnp.sum(y, axis=0, keepdims=True)
        out_ref[0:rows, cols] = y.astype(BF)

    col_blocks(body)


def attention_backward_ref(q_ref, k_ref, v_ref, dm_ref, lse_ref, mask_ref, rows, keys, dq_ref, dk_ref, dv_ref):
    def pair_of_heads(i, carry):
        cols = pl.ds(pl.multiple_of(i * LANES, LANES), LANES)
        dk_ref[:, cols] = jnp.zeros((dk_ref.shape[0], LANES), F32)
        dv_ref[:, cols] = jnp.zeros((dv_ref.shape[0], LANES), F32)
        k_turned = jnp.transpose(k_ref[0:keys, cols])
        for tile, (start, reach) in enumerate(attend_tiles(rows, keys, mask_ref is not None)):
            r = slice(start, start + LANES)
            q2 = both_heads(q_ref[r, cols] * jnp.asarray(SCALE, BF))
            dm2 = both_heads(dm_ref[r, cols])
            scores = scores_of(k_ref[0:reach, cols], q2, mask_ref, start, reach)
            probs = jnp.exp(scores - lse_ref[tile, pl.ds(i, 1), :])
            dp = mm_nt(v_ref[0:reach, cols], dm2)
            weighted = probs * dp
            ds = (weighted - probs * jnp.sum(weighted, axis=0, keepdims=True)).astype(BF)
            dk_ref[0:reach, cols] += mm(ds, q2)
            dv_ref[0:reach, cols] += mm(probs.astype(BF), dm2)
            dq = jnp.concatenate(
                [
                    mm(k_turned[s * HEAD_DIM : (s + 1) * HEAD_DIM, 0:reach], ds[:, s * LANES : (s + 1) * LANES])
                    for s in range(2)
                ],
                axis=0,
            )
            dq_ref[r, cols] = jnp.transpose(dq) * SCALE
        return carry

    lax.fori_loop(0, D // LANES, pair_of_heads, 0, unroll=1 if mask_ref is not None else 2)


W_ORDER = (26, 27, 22, 23, 24, 25, 20, 21, 19, 16, 17, 18, 15, 12, 13, 14, 10, 11, 6, 7, 8, 9, 4, 5, 3, 0, 1, 2, 24, 25, 26, 27)
W_RING = 4
A_RING = 4


def backward_kernel(n, rows, frames, *refs):
    w_ref, v_ref, seg_ref, ein, din, ecot, dcot, early = refs[:8]
    kept, refs = refs[8 : 8 + N_SAVED], refs[8 + N_SAVED :]
    oe_ref, od_ref, norm_ref, fgrad, tgrad, dout = refs[:6]
    refs = refs[6:]
    comm, refs = refs[:34], refs[34:]
    (
        gbuf, vg, vgr, gains, wbuf, outg, eoutg, dn, pool, abuf, nbuf, xbuf,
        dq, dk, dv, mask_ref, seg_row, seg_col, lse, orow, mem, mgrad, s_l, s_w, s_a, s_o,
    ) = refs
    tall = mask_ref.shape[0]

    a_order = (
        [kept[27].at[k] for k in (2, 3, 0, 1)]
        + [kept[22].at[0:rows], kept[15].at[0:rows], din]
        + [kept[8].at[k] for k in (2, 3, 0, 1)]
        + [kept[9].at[k] for k in (2, 3, 0, 1)]
        + [kept[4], ein]
        + [kept[26].at[k] for k in range(4)]
    )
    used = [0, 0]

    def w_copy(u):
        m = W_ORDER[u]
        return pltpu.make_async_copy(w_ref.at[m // 2, m % 2].reshape(D, D), wbuf.at[u % W_RING], s_w.at[u % W_RING])

    def a_copy(u):
        src = a_order[u]
        return pltpu.make_async_copy(src, abuf.at[u % A_RING, 0 : src.shape[0]], s_a.at[u % A_RING])

    def with_w(mat, body):
        u = used[0]
        used[0] += 1
        assert W_ORDER[u] == mat
        w_copy(u).wait()
        body(wbuf.at[u % W_RING])
        if u + W_RING < len(W_ORDER):
            w_copy(u + W_RING).start()

    def with_a(body):
        u = used[1]
        used[1] += 1
        a_copy(u).wait()
        body(abuf.at[u % A_RING])
        if u + A_RING < len(a_order):
            a_copy(u + A_RING).start()

    def side(k, src, dst):
        return pltpu.make_async_copy(src, dst, s_l.at[k])

    def x_copy(i):
        return side(0, kept[i], xbuf.at[0 : kept[i].shape[0]])

    def n_copy(i):
        return side(1, kept[i], nbuf.at[0 : kept[i].shape[0]])

    def vrow(i):
        return vgr.at[i : i + 1]

    def take_two(which, copy, ring, total, body):
        u = used[which]
        used[which] += 2
        copy(u).wait()
        copy(u + 1).wait()
        body(lambda k: lax.rem(u + k, ring))
        for k in range(2):
            if u + k + ring < total:
                copy(u + k + ring).start()

    def two_w(mat, body):
        assert W_ORDER[used[0]] == mat
        take_two(0, w_copy, W_RING, len(W_ORDER), lambda slot: body(lambda k: wbuf.at[slot(k)]))

    def two_a(body):
        take_two(1, a_copy, A_RING, len(a_order), lambda slot: body(lambda k: abuf.at[slot(k)]))

    def feed(step, g, count, first_mat, first_vec, n_i):
        if step < 2:
            two_a(lambda a: both(lambda k: weight_grad(a(k), orow, count, g.at[k])))
            return
        first = 2 if step == 2 else 0
        if step == 2:
            n_copy(n_i).wait()

        def body(k, w, a):
            gelu_back(orow, w(k), a(k), count, pool.at[first + k], vgr.at[pl.ds(first_vec + first + k, 1)])
            weight_grad(nbuf, pool.at[first + k], count, g.at[k])

        two_w(first_mat + 4 + first, lambda w: two_a(lambda a: both(lambda k: body(k, w, a))))

    def feed_after(step, count, first_mat):
        first = 2 if step == 2 else 0
        if step == 2:
            dn[0:count, :] = jnp.zeros((count, D), F32)
        two_w(
            first_mat + first,
            lambda w: both(lambda k: back_through(pool.at[first + k], w(k), count, dn, True)),
        )

    def attend(g, count, padded, keys, padded_keys, out_ref, wo, q_i, lse_i, masked, bo, bq, bv):
        cps = [side(2 + k, kept[q_i + k], pool.at[k, 0 : kept[q_i + k].shape[0]]) for k in range(3)]
        cps.append(side(5, kept[lse_i], lse.at[0 : kept[lse_i].shape[0]]))
        for cp in cps:
            cp.start()
        round_rows(out_ref, count, orow)
        sum_rows(out_ref, count, vrow(bo))
        with_a(lambda a: weight_grad(a, orow, count, g.at[1]))
        with_w(wo, lambda w: back_through(orow, w, count, pool.at[3], False))
        if padded > count:
            pool[3, count:padded, :] = jnp.zeros((padded - count, D), BF)
        for cp in cps:
            cp.wait()
        attention_backward_ref(
            pool.at[0], pool.at[1], pool.at[2], pool.at[3], lse, mask_ref if masked else None, padded, padded_keys,
            dq, dk.at[0:padded_keys], dv.at[0:padded_keys],
        )
        round_rows(dv, keys, pool.at[2])
        round_rows(dq, count, pool.at[0])
        round_rows(dk, keys, pool.at[1])
        sum_rows(dq, count, vrow(bq))
        sum_rows(dv, keys, vrow(bv))

    def start():
        o_copy = side(2, dcot, orow)
        o_copy.start()
        for u in range(A_RING):
            a_copy(u).start()
        for u in range(W_RING):
            w_copy(u).start()
        n_copy(25).start()
        x_copy(24).start()
        mem_copy = side(3, kept[10], mem)
        mem_copy.start()
        for i, v in enumerate((0, 5, 12, 17, 22, 28)):
            for k in range(6):
                gains[i : i + 1, k * LANES : (k + 1) * LANES] = v_ref[v // 8, v // 4 % 2, v // 2 % 2, v % 2, k : k + 1, :]
        o_copy.wait()
        mem_copy.wait()

    def widen():
        def body(r):
            outg[r, :] = orow[r, :].astype(F32)

        row_blocks(rows, body)
        sum_rows(outg, rows, vrow(28))

    def produce(t, g):
        if t < 4:
            feed(t, g, rows, 20, 24, 25)
            if t == 3:
                n_copy(18).start()
        elif t == 4:
            attend(g, rows, tall, frames, frames, outg, 19, 19, 23, False, 21, 19, 20)
            weight_grad(mem, pool.at[2], frames, g.at[0])
        elif t == 5:
            n_copy(18).wait()
            weight_grad(nbuf, pool.at[0], rows, g.at[0])
            weight_grad(mem, pool.at[1], frames, g.at[1])
            n_copy(11).start()
        elif t == 6:
            attend(g, rows, tall, rows, tall, outg, 15, 12, 16, True, 16, 14, 15)
            n_copy(11).wait()
            weight_grad(nbuf, pool.at[2], rows, g.at[0])
        elif t == 7:
            weight_grad(nbuf, pool.at[0], rows, g.at[0])
            weight_grad(nbuf, pool.at[1], rows, g.at[1])
            n_copy(7).start()
        elif t < 12:
            feed(t - 8, g, frames, 4, 7, 7)
            if t == 11:
                n_copy(0).start()
        elif t == 12:
            attend(g, frames, frames, frames, frames, eoutg, 3, 1, 5, False, 4, 2, 3)
            n_copy(0).wait()
            weight_grad(nbuf, pool.at[2], frames, g.at[0])
        else:
            weight_grad(nbuf, pool.at[0], frames, g.at[0])
            weight_grad(nbuf, pool.at[1], frames, g.at[1])

    def after(t):
        if t in (2, 3):
            feed_after(t, rows, 20)
            if t == 2:
                widen()
                make_mask(seg_ref, seg_row, seg_col, mask_ref)
            if t == 3:
                x_copy(24).wait()
                norm_backward_ref(xbuf, gains.at[4:5], dn, rows, outg, vrow(22), vrow(23))
                x_copy(17).start()
        elif t == 5:
            with_w(16, lambda w: back_through(pool.at[0], w, rows, dn, False))
            with_w(17, lambda w: back_through(pool.at[1], w, frames, mgrad, False))
            with_w(18, lambda w: back_through(pool.at[2], w, frames, mgrad, True))
            x_copy(17).wait()
            norm_backward_ref(xbuf, gains.at[3:4], dn, rows, outg, vrow(17), vrow(18))
            x_copy(6).start()
        elif t == 7:
            cot = side(2, ecot, orow.at[0:frames])
            cot.start()
            with_w(12, lambda w: back_through(pool.at[0], w, rows, dn, False))
            with_w(13, lambda w: back_through(pool.at[1], w, rows, dn, True))
            with_w(14, lambda w: back_through(pool.at[2], w, rows, dn, True))
            with_a(lambda a: norm_backward_ref(a, gains.at[2:3], dn, rows, outg, vrow(12), vrow(13)))
            pltpu.make_async_copy(outg, tgrad, s_o.at[0]).start()
            cot.wait()

            def body(r):
                total = orow[r, :].astype(F32) + mgrad[r, :]
                eoutg[r, :] = total
                orow[r, :] = total.astype(BF)

            row_blocks(frames, body)
        elif t == 9:
            sum_rows(eoutg, frames, vrow(11))
        elif t in (10, 11):
            feed_after(t - 8, frames, 4)
            if t == 11:
                x_copy(6).wait()
                norm_backward_ref(xbuf, gains.at[1:2], dn, frames, eoutg, vrow(5), vrow(6))
                x_copy(24).start()
        elif t in (14, 15):
            if t == 14:
                x_copy(24).wait()
                row_blocks(rows, lambda r: add_row(dn, xbuf, gains.at[5:6], r))
            two_w(
                24 + 2 * (t - 14),
                lambda w: two_a(lambda a: both(lambda k: accumulate(a(k), w(k), rows, dn))),
            )
            if t == 15:
                round_rows(dn, rows, orow)
                pltpu.make_async_copy(orow, dout, s_o.at[2]).start()
        elif t == 13:
            with_w(0, lambda w: back_through(pool.at[0], w, frames, dn, False))
            with_w(1, lambda w: back_through(pool.at[1], w, frames, dn, True))
            with_w(2, lambda w: back_through(pool.at[2], w, frames, dn, True))
            with_a(lambda a: norm_backward_ref(a, gains.at[0:1], dn, frames, eoutg, vrow(0), vrow(1)))
            pltpu.make_async_copy(eoutg, fgrad, s_o.at[1]).start()
            for v in range(32):
                at = (v // 8, v // 4 % 2, v // 2 % 2, v % 2)
                if v < N_VEC:
                    vg[at + (slice(6, 8), slice(None))] = jnp.zeros((2, LANES), F32)
                    for k in range(6):
                        vg[at + (slice(k, k + 1), slice(None))] = vgr[v : v + 1, k * LANES : (k + 1) * LANES]
                else:
                    vg[at] = jnp.zeros((8, LANES), F32)

    scatter_kernel(n, start, produce, after, early, vg, gbuf, oe_ref, od_ref, norm_ref, *comm)
    pltpu.make_async_copy(outg, tgrad, s_o.at[0]).wait()
    pltpu.make_async_copy(eoutg, fgrad, s_o.at[1]).wait()
    pltpu.make_async_copy(orow, dout, s_o.at[2]).wait()


def backward_pass(weights, vectors, kept, early, ein, din, ecot, dcot, segments, n):
    (_, re, ne, ge), (_, rd, nd, gd) = sizes(ENC, n), sizes(DEC, n)
    frames, rows = ein.shape[0], din.shape[0]
    tall = -(-rows // 128) * 128
    dma = pltpu.SemaphoreType.DMA
    vmem, hbm = pl.BlockSpec(memory_space=pltpu.VMEM), pl.BlockSpec(memory_space=pl.ANY)
    return pl.pallas_call(
        partial(backward_kernel, n, rows, frames),
        out_shape=(
            jax.ShapeDtypeStruct((re, LANES), F32),
            jax.ShapeDtypeStruct((rd, LANES), F32),
            jax.ShapeDtypeStruct((8, LANES), F32),
            jax.ShapeDtypeStruct((frames, D), F32),
            jax.ShapeDtypeStruct((rows, D), F32),
            jax.ShapeDtypeStruct((rows, D), BF),
        ),
        in_specs=[hbm] + [vmem] * 2 + [hbm] * (5 + N_SAVED),
        out_specs=(hbm, hbm, vmem, hbm, hbm, hbm),
        scratch_shapes=[
            pltpu.VMEM((RING_C, 4, 2, 2, UNIT, D), BF),
            pltpu.VMEM((N_PAIR, 4, 2, UNIT, D), BF),
            pltpu.VMEM((N_PAIR, 4, UNIT, D), BF),
            pltpu.VMEM((N_PAIR, 3, UNIT, D), BF),
            pltpu.VMEM((N_PAIR, UNIT, D), BF),
            pltpu.VMEM((8, LANES), F32),
            pltpu.VMEM((4, 2, 2, 8, LANES), F32),
            pltpu.VMEM((4, 2, 8, LANES), F32),
            pltpu.VMEM((4, 8, LANES), F32),
            pltpu.VMEM((3, 8, LANES), F32),
            pltpu.VMEM((FRONT + re + BACK, LANES), F32),
            pltpu.VMEM((FRONT + rd + BACK, LANES), F32),
            pltpu.VMEM((ne, UNIT, D), BF),
            pltpu.VMEM((nd, UNIT, D), BF),
            pltpu.VMEM((ge, 4, UNIT, D), BF),
            pltpu.VMEM((gd, 4, UNIT, D), BF),
            pltpu.VMEM((N_VEC, 8, LANES), F32),
            pltpu.VMEM((8, LANES), F32),
            pltpu.VMEM((n, 8, LANES), F32),
            dma((N_PAIR,)),
            dma((N_PAIR,)),
            pltpu.SemaphoreType.REGULAR,
            dma((N_PAIR, 5)),
            dma((N_PAIR, 5)),
            dma((N_PAIR, 2)),
            dma((2, max(ne, nd))),
            dma((2, max(ge, gd), 4)),
            dma((6,)),
            dma((6,)),
            dma((2,)),
            dma((N_VEC,)),
            dma((n,)),
            dma((n,)),
            dma((2,)),
            pltpu.VMEM((RING, 2, 4, 2, 2, UNIT, D), BF),
            pltpu.VMEM((4, 2, 2, 2, 8, LANES), F32),
            pltpu.VMEM((32, D), F32),
            pltpu.VMEM((8, D), F32),
            pltpu.VMEM((W_RING, D, D), BF),
            pltpu.VMEM((rows, D), F32),
            pltpu.VMEM((frames, D), F32),
            pltpu.VMEM((rows, D), F32),
            pltpu.VMEM((4, tall, D), BF),
            pltpu.VMEM((A_RING, rows, D), BF),
            pltpu.VMEM((rows, D), BF),
            pltpu.VMEM((rows, D), F32),
            pltpu.VMEM((tall, D), F32),
            pltpu.VMEM((tall, D), F32),
            pltpu.VMEM((tall, D), F32),
            pltpu.VMEM((tall, tall), F32),
            pltpu.VMEM((8, tall), F32),
            pltpu.VMEM((tall, LANES), F32),
            pltpu.VMEM((tall // 128, 8, 2 * LANES), F32),
            pltpu.VMEM((rows, D), BF),
            pltpu.VMEM((frames, D), BF),
            pltpu.VMEM((frames, D), F32),
            dma((6,)),
            dma((W_RING,)),
            dma((A_RING,)),
            dma((3,)),
        ],
        compiler_params=pltpu.CompilerParams(collective_id=1, has_side_effects=True, vmem_limit_bytes=61 << 20),
        name="backward",
    )(weights, vectors, segments, ein, din, ecot, dcot, early, *kept)


def attention_plan(prefix, width):
    return [
        (prefix + "wq", width, width),
        (prefix + "bq", width, 0),
        (prefix + "wk", width, width),
        (prefix + "wv", width, width),
        (prefix + "bv", width, 0),
        (prefix + "wo", width, width),
        (prefix + "bo", width, 0),
    ]


def feed_plan(width, hidden):
    return [
        ("fc1_weight", width, hidden),
        ("fc1_bias", hidden, 0),
        ("fc2_weight", hidden, width),
        ("fc2_bias", width, 0),
    ]


def encoder_layout(width, hidden):
    return (
        [("ln1_gain", width, 0), ("ln1_bias", width, 0)]
        + attention_plan("att_", width)
        + [("ln2_gain", width, 0), ("ln2_bias", width, 0)]
        + feed_plan(width, hidden)
    )


def decoder_layout(width, hidden):
    return (
        [("ln1_gain", width, 0), ("ln1_bias", width, 0)]
        + attention_plan("self_", width)
        + [("ln2_gain", width, 0), ("ln2_bias", width, 0)]
        + attention_plan("cross_", width)
        + [("ln3_gain", width, 0), ("ln3_bias", width, 0)]
        + feed_plan(width, hidden)
    )


def unpack(flat, layout):
    params = {}
    offset = 0
    for name, rows, cols in layout:
        count = rows * cols if cols > 0 else rows
        piece = flat[offset : offset + count]
        params[name] = piece.reshape(rows, cols) if cols > 0 else piece
        offset = offset + count
    return params


def pack(grads, layout):
    return jnp.concatenate([grads[name].reshape(-1) for name, rows, cols in layout])


def dot_plain(left, right):
    return jnp.dot(left, right, preferred_element_type=jnp.float32)


def dot_left(left, right):
    return lax.dot_general(
        left, right, (((0,), (0,)), ((), ())), preferred_element_type=jnp.float32
    )


def dot_right(left, right):
    return lax.dot_general(
        left, right, (((1,), (1,)), ((), ())), preferred_element_type=jnp.float32
    )


def layer_norm(values, gain, shift):
    centred = values - jnp.mean(values, axis=-1, keepdims=True)
    spread = jnp.mean(centred * centred, axis=-1, keepdims=True)
    return centred * lax.rsqrt(spread + 1e-05) * gain + shift


def norm_forward(params, prefix, values):
    gain = params[prefix + "_gain"].astype(jnp.float32)
    shift = params[prefix + "_bias"].astype(jnp.float32)
    return layer_norm(values, gain, shift).astype(jnp.bfloat16)


def norm_backward(params, prefix, values, grad):
    gain = params[prefix + "_gain"].astype(jnp.float32)
    shift = params[prefix + "_bias"].astype(jnp.float32)
    unused, pullback = jax.vjp(layer_norm, values, gain, shift)
    value_grad, gain_grad, shift_grad = pullback(grad)
    return (value_grad, {prefix + "_gain": gain_grad, prefix + "_bias": shift_grad})


def block_rows(total):
    return total if total <= 1024 else 512


def attend_forward(queries, keys_low, values, allowed_fn):
    total, width = queries.shape
    heads = width // HEAD_DIM
    rows = block_rows(total)
    blocks = total // rows
    scale = HEAD_DIM ** (-0.5)
    query_heads = queries.reshape(blocks, rows, heads, HEAD_DIM)
    key_heads = keys_low.reshape(keys_low.shape[0], heads, HEAD_DIM)
    value_heads = values.reshape(values.shape[0], heads, HEAD_DIM)
    starts = jnp.arange(blocks, dtype=jnp.int32) * rows

    def one_block(inputs):
        block, start = inputs
        scores = (
            jnp.einsum("qhd,khd->hqk", block, key_heads, preferred_element_type=jnp.float32) * scale
        )
        if allowed_fn is not None:
            scores = jnp.where(allowed_fn(start, rows)[None], scores, -1000000000.0)
        peak = jnp.max(scores, axis=-1, keepdims=True)
        weights = jnp.exp(scores - peak)
        totals = jnp.sum(weights, axis=-1, keepdims=True)
        probs = (weights / totals).astype(jnp.bfloat16)
        mixed = jnp.einsum("hqk,khd->qhd", probs, value_heads, preferred_element_type=jnp.float32)
        return (mixed.reshape(rows, width).astype(jnp.bfloat16), (peak + jnp.log(totals))[..., 0])

    mixed, logsum = lax.map(one_block, (query_heads, starts))
    return (mixed.reshape(total, width), logsum)


def attend_backward(queries, keys_low, values, logsum, mixed_grad, allowed_fn):
    total, width = queries.shape
    heads = width // HEAD_DIM
    rows = block_rows(total)
    blocks = total // rows
    scale = HEAD_DIM ** (-0.5)
    query_heads = queries.reshape(blocks, rows, heads, HEAD_DIM)
    grad_heads = mixed_grad.reshape(blocks, rows, heads, HEAD_DIM)
    key_heads = keys_low.reshape(keys_low.shape[0], heads, HEAD_DIM)
    value_heads = values.reshape(values.shape[0], heads, HEAD_DIM)
    starts = jnp.arange(blocks, dtype=jnp.int32) * rows

    def one_block(carry, inputs):
        key_grad, value_grad = carry
        block, grad_block, block_sum, start = inputs
        scores = (
            jnp.einsum("qhd,khd->hqk", block, key_heads, preferred_element_type=jnp.float32) * scale
        )
        if allowed_fn is not None:
            scores = jnp.where(allowed_fn(start, rows)[None], scores, -1000000000.0)
        probs = jnp.exp(scores - block_sum[..., None])
        prob_grad = jnp.einsum(
            "qhd,khd->hqk", grad_block, value_heads, preferred_element_type=jnp.float32
        )
        value_grad = value_grad + jnp.einsum(
            "hqk,qhd->khd",
            probs.astype(jnp.bfloat16),
            grad_block,
            preferred_element_type=jnp.float32,
        )
        score_grad = probs * (prob_grad - jnp.sum(probs * prob_grad, axis=-1, keepdims=True))
        raw_grad = (score_grad * scale).astype(jnp.bfloat16)
        query_grad = jnp.einsum(
            "hqk,khd->qhd", raw_grad, key_heads, preferred_element_type=jnp.float32
        )
        key_grad = key_grad + jnp.einsum(
            "hqk,qhd->khd", raw_grad, block, preferred_element_type=jnp.float32
        )
        return ((key_grad, value_grad), query_grad.reshape(rows, width))

    zeros = jnp.zeros(key_heads.shape, jnp.float32)
    (key_grad, value_grad), query_grad = lax.scan(
        one_block, (zeros, zeros), (query_heads, grad_heads, logsum, starts)
    )
    return (
        query_grad.reshape(total, width),
        key_grad.reshape(keys_low.shape[0], width),
        value_grad.reshape(values.shape[0], width),
    )


def attention_forward(params, prefix, query_rows, key_rows, allowed_fn):
    queries = (dot_plain(query_rows, params[prefix + "wq"]) + params[prefix + "bq"]).astype(
        jnp.bfloat16
    )
    keys_low = dot_plain(key_rows, params[prefix + "wk"]).astype(jnp.bfloat16)
    values = (dot_plain(key_rows, params[prefix + "wv"]) + params[prefix + "bv"]).astype(
        jnp.bfloat16
    )
    mixed, logsum = attend_forward(queries, keys_low, values, allowed_fn)
    output = dot_plain(mixed, params[prefix + "wo"]) + params[prefix + "bo"]
    return (output, (queries, keys_low, values, mixed, logsum))


def attention_backward(params, prefix, query_rows, key_rows, kept, out_grad, allowed_fn):
    queries, keys_low, values, mixed, logsum = kept
    out_round = out_grad.astype(jnp.bfloat16)
    mixed_grad = dot_right(out_round, params[prefix + "wo"]).astype(jnp.bfloat16)
    query_grad, key_grad, value_grad = attend_backward(
        queries, keys_low, values, logsum, mixed_grad, allowed_fn
    )
    query_round = query_grad.astype(jnp.bfloat16)
    key_round = key_grad.astype(jnp.bfloat16)
    value_round = value_grad.astype(jnp.bfloat16)
    grads = {
        prefix + "wq": dot_left(query_rows, query_round),
        prefix + "bq": jnp.sum(query_grad, axis=0),
        prefix + "wk": dot_left(key_rows, key_round),
        prefix + "wv": dot_left(key_rows, value_round),
        prefix + "bv": jnp.sum(value_grad, axis=0),
        prefix + "wo": dot_left(mixed, out_round),
        prefix + "bo": jnp.sum(out_grad, axis=0),
    }
    query_side = dot_right(query_round, params[prefix + "wq"])
    key_side = dot_right(key_round, params[prefix + "wk"]) + dot_right(
        value_round, params[prefix + "wv"]
    )
    return (grads, query_side, key_side)


def feed_forward(params, normed):
    pre = dot_plain(normed, params["fc1_weight"]) + params["fc1_bias"]
    activated = jax.nn.gelu(pre, approximate=False).astype(jnp.bfloat16)
    return (dot_plain(activated, params["fc2_weight"]) + params["fc2_bias"], (pre, activated))


def feed_backward(params, normed, kept, out_grad):
    pre, activated = kept
    out_round = out_grad.astype(jnp.bfloat16)
    act_grad = dot_right(out_round, params["fc2_weight"])
    unused, gelu_back = jax.vjp(partial(jax.nn.gelu, approximate=False), pre)
    pre_grad = gelu_back(act_grad)[0]
    pre_round = pre_grad.astype(jnp.bfloat16)
    grads = {
        "fc1_weight": dot_left(normed, pre_round),
        "fc1_bias": jnp.sum(pre_grad, axis=0),
        "fc2_weight": dot_left(activated, out_round),
        "fc2_bias": jnp.sum(out_grad, axis=0),
    }
    return (grads, dot_right(pre_round, params["fc1_weight"]))


def encoder_forward(params, frames):
    normed = norm_forward(params, "ln1", frames)
    attended, attend_kept = attention_forward(params, "att_", normed, normed, None)
    after = frames + attended
    normed_two = norm_forward(params, "ln2", after)
    fed, feed_kept = feed_forward(params, normed_two)
    return (after + fed, (normed, attend_kept, after, normed_two, feed_kept))


def encoder_backward(params, frames, kept, out_grad):
    normed, attend_kept, after, normed_two, feed_kept = kept
    grads, normed_grad = feed_backward(params, normed_two, feed_kept, out_grad)
    part, norm_grads = norm_backward(params, "ln2", after, normed_grad)
    grads.update(norm_grads)
    after_grad = out_grad + part
    attend_grads, query_side, key_side = attention_backward(
        params, "att_", normed, normed, attend_kept, after_grad, None
    )
    grads.update(attend_grads)
    part, norm_grads = norm_backward(params, "ln1", frames, query_side + key_side)
    grads.update(norm_grads)
    return (grads, after_grad + part)


def decoder_forward(params, tokens, memory_low, allowed_fn):
    normed = norm_forward(params, "ln1", tokens)
    attended, self_kept = attention_forward(params, "self_", normed, normed, allowed_fn)
    after = tokens + attended
    normed_two = norm_forward(params, "ln2", after)
    crossed, cross_kept = attention_forward(params, "cross_", normed_two, memory_low, None)
    after_two = after + crossed
    normed_three = norm_forward(params, "ln3", after_two)
    fed, feed_kept = feed_forward(params, normed_three)
    return (
        after_two + fed,
        (normed, self_kept, after, normed_two, cross_kept, after_two, normed_three, feed_kept),
    )


def decoder_backward(params, tokens, memory_low, kept, out_grad, allowed_fn):
    normed, self_kept, after, normed_two, cross_kept, after_two, normed_three, feed_kept = kept
    grads, normed_grad = feed_backward(params, normed_three, feed_kept, out_grad)
    part, norm_grads = norm_backward(params, "ln3", after_two, normed_grad)
    grads.update(norm_grads)
    after_two_grad = out_grad + part
    cross_grads, query_side, memory_grad = attention_backward(
        params, "cross_", normed_two, memory_low, cross_kept, after_two_grad, None
    )
    grads.update(cross_grads)
    part, norm_grads = norm_backward(params, "ln2", after, query_side)
    grads.update(norm_grads)
    after_grad = after_two_grad + part
    self_grads, query_side, key_side = attention_backward(
        params, "self_", normed, normed, self_kept, after_grad, allowed_fn
    )
    grads.update(self_grads)
    part, norm_grads = norm_backward(params, "ln1", tokens, query_side + key_side)
    grads.update(norm_grads)
    return (grads, after_grad + part, memory_grad)


def adamw(master, first, second, grad, factor, correction):
    clipped = grad * factor
    moment = 0.5 * first + 0.5 * clipped
    variance = 0.5 * second + 0.5 * clipped * clipped
    update = moment / correction / (jnp.sqrt(variance / correction) + 1e-08) + 0.01 * master
    weights = master - 0.02 * update
    return (weights, moment, variance, weights.astype(jnp.bfloat16))


def shards_native(
    encoder_input,
    decoder_input,
    segments,
    encoder_cotangent,
    decoder_cotangent,
    encoder_master,
    encoder_first,
    encoder_second,
    decoder_master,
    decoder_first,
    decoder_second,
    step_count,
):
    encoder_plan = encoder_layout(D, FF)
    decoder_plan = decoder_layout(D, FF)
    encoder_params = unpack(
        lax.all_gather(encoder_master.astype(jnp.bfloat16), ("wide", "narrow"), axis=0, tiled=True),
        encoder_plan,
    )
    frames = encoder_input[0].astype(jnp.float32)
    memory, encoder_kept = encoder_forward(encoder_params, frames)
    memory_low = memory.astype(jnp.bfloat16)
    decoder_params = unpack(
        lax.all_gather(decoder_master.astype(jnp.bfloat16), ("wide", "narrow"), axis=0, tiled=True),
        decoder_plan,
    )
    tokens = decoder_input[0].astype(jnp.float32)
    segment_row = segments[0]
    length = segment_row.shape[0]

    def allowed_fn(start, count):
        places = start + jnp.arange(count, dtype=jnp.int32)
        row_segments = lax.dynamic_slice_in_dim(segment_row, start, count)
        columns = jnp.arange(length, dtype=jnp.int32)
        return (row_segments[:, None] == segment_row[None, :]) & (
            columns[None, :] <= places[:, None]
        )

    decoded, decoder_kept = decoder_forward(decoder_params, tokens, memory_low, allowed_fn)
    decoder_again = unpack(
        lax.all_gather(decoder_master.astype(jnp.bfloat16), ("wide", "narrow"), axis=0, tiled=True),
        decoder_plan,
    )
    decoder_grads, token_grad, memory_grad = decoder_backward(
        decoder_again,
        tokens,
        memory_low,
        decoder_kept,
        decoder_cotangent[0].astype(jnp.float32),
        allowed_fn,
    )
    decoder_total = pack(decoder_grads, decoder_plan)
    decoder_owned = lax.psum_scatter(
        decoder_total, ("wide", "narrow"), scatter_dimension=0, tiled=True
    )
    encoder_again = unpack(
        lax.all_gather(encoder_master.astype(jnp.bfloat16), ("wide", "narrow"), axis=0, tiled=True),
        encoder_plan,
    )
    memory_total = encoder_cotangent[0].astype(jnp.float32) + memory_grad
    encoder_grads, frame_grad = encoder_backward(encoder_again, frames, encoder_kept, memory_total)
    encoder_total = pack(encoder_grads, encoder_plan)
    encoder_owned = lax.psum_scatter(
        encoder_total, ("wide", "narrow"), scatter_dimension=0, tiled=True
    )
    local_squares = jnp.sum(encoder_owned * encoder_owned) + jnp.sum(decoder_owned * decoder_owned)
    gradient_norm = jnp.sqrt(lax.psum(local_squares, ("wide", "narrow")))
    factor = 1.0 / jnp.maximum(gradient_norm, 1.0)
    correction = 1.0 - jnp.power(0.5, step_count.astype(jnp.float32))
    encoder_new = adamw(
        encoder_master, encoder_first, encoder_second, encoder_owned, factor, correction
    )
    decoder_new = adamw(
        decoder_master, decoder_first, decoder_second, decoder_owned, factor, correction
    )
    return (
        memory_low[None],
        decoded.astype(jnp.bfloat16)[None],
        frame_grad[None],
        token_grad[None],
        gradient_norm,
        encoder_new[0],
        encoder_new[1],
        encoder_new[2],
        encoder_new[3],
        decoder_new[0],
        decoder_new[1],
        decoder_new[2],
        decoder_new[3],
    )


def shards(
    encoder_input,
    decoder_input,
    segments,
    encoder_cotangent,
    decoder_cotangent,
    encoder_master,
    encoder_first,
    encoder_second,
    decoder_master,
    decoder_first,
    decoder_second,
    step_count,
):
    n = 32
    weights, vectors, *kept, early = forward_pass(
        encoder_master, decoder_master, encoder_input[0], decoder_input[0], segments, decoder_cotangent[0], n
    )
    encoder_flat, decoder_flat, norm, frame_grad, token_grad, decoded = backward_pass(
        weights, vectors, kept, early, encoder_input[0], decoder_input[0], encoder_cotangent[0], decoder_cotangent[0], segments, n
    )
    gradient_norm = norm[0, 0]
    factor = 1.0 / jnp.maximum(gradient_norm, 1.0)
    correction = 1.0 - jnp.power(0.5, step_count.astype(jnp.float32))
    encoder_owned = encoder_flat.reshape(-1)[: encoder_master.shape[0]]
    decoder_owned = decoder_flat.reshape(-1)[: decoder_master.shape[0]]
    encoder_new = adamw(encoder_master, encoder_first, encoder_second, encoder_owned, factor, correction)
    decoder_new = adamw(decoder_master, decoder_first, decoder_second, decoder_owned, factor, correction)
    return (
        kept[10][None],
        decoded[None],
        frame_grad[None],
        token_grad[None],
        gradient_norm,
        *encoder_new,
        *decoder_new,
    )


def solution(mesh):
    placed = (
        P(("wide", "narrow"), None, None),
        P(("wide", "narrow"), None, None),
        P(("wide", "narrow"), None),
        P(("wide", "narrow"), None, None),
        P(("wide", "narrow"), None, None),
        P(("wide", "narrow")),
        P(("wide", "narrow")),
        P(("wide", "narrow")),
        P(("wide", "narrow")),
        P(("wide", "narrow")),
        P(("wide", "narrow")),
        P(),
    )
    return jax.shard_map(
        shards if tuple(mesh.shape.values()) == (8, 4) else shards_native,
        mesh=mesh,
        in_specs=placed,
        out_specs=(
            P(("wide", "narrow"), None, None),
            P(("wide", "narrow"), None, None),
            P(("wide", "narrow"), None, None),
            P(("wide", "narrow"), None, None),
            P(),
            P(("wide", "narrow")),
            P(("wide", "narrow")),
            P(("wide", "narrow")),
            P(("wide", "narrow")),
            P(("wide", "narrow")),
            P(("wide", "narrow")),
            P(("wide", "narrow")),
            P(("wide", "narrow")),
        ),
        check_vma=False,
    )
```

```python
from functools import partial

import jax
import jax.numpy as jnp
from jax import lax
from jax.experimental import pallas as pl
from jax.experimental.pallas import tpu as pltpu
from jax.sharding import PartitionSpec as P

D = 768
HEAD_DIM = 64
FF = 3072
MESH = pl.DeviceIdType.MESH
BF = jnp.bfloat16
F32 = jnp.float32

N_MAT = 28
N_PAIR = 14
UNIT = 48
LANES = 128
UROWS = UNIT * D // LANES
BIG = 4 * UROWS
FRONT = BIG + 8
BACK = BIG + 8
N_VEC = 29
F_AT = (1, 2, 4, 5)
B_AT = (1, 3, 5, 8)
AHEAD = 3


class Block:
    def __init__(self, small, gaps, fc1, vectors, first_mat, small_mats, total):
        self.small = small
        self.gaps = gaps
        self.fc1 = fc1
        self.vectors = vectors
        self.first_mat = first_mat
        self.small_mats = small_mats
        self.total = total


ENC = Block(
    small=8,
    gaps=((0, 2), (1, 1), (3, 1), (4, 3072 + 7)),
    fc1=3079,
    vectors=[0, 1, 770, 2307, 3076, 3077, 3078, 6151, 6152, 6153, 6154, 9227],
    first_mat=0,
    small_mats=4,
    total=9228,
)
DEC = Block(
    small=12,
    gaps=((0, 2), (1, 1), (3, 1), (4, 3), (5, 1), (7, 1), (8, 3072 + 7)),
    fc1=6156,
    vectors=[0, 1, 770, 2307, 3076, 3077, 3078, 3847, 5384, 6153, 6154, 6155, 9228, 9229, 9230, 9231, 12304],
    first_mat=12,
    small_mats=8,
    total=12305,
)
BLOCKS = (ENC, DEC)


def sizes(block, n):
    shard = block.total * D // n
    rows = -(-shard // 1024) * 8
    top = (shard + LANES - 1) // LANES
    return shard, rows, (top + UROWS) // UROWS + 1, (top + BIG) // BIG + 1


def small_row(block, m):
    row = m * D
    for at, gap in block.gaps:
        row = row + jnp.where(m >= at, gap, 0) if at > 0 else row + gap
    return row


def mat_of(block, m):
    return block.first_mat + m + jnp.where(m >= block.small_mats, 4, 0)


def static_unit_rows(block):
    out = []
    for m in range(block.small):
        row = m * D + sum(gap for at, gap in block.gaps if m >= at)
        out.append((block.first_mat + m + (4 if m >= block.small_mats else 0), row))
    return out


def whoami():
    wide, narrow = lax.axis_index("wide"), lax.axis_index("narrow")
    return wide, narrow, wide // 2, wide % 2, narrow // 2, narrow % 2


def device(z, x, y, c):
    return (z * 2 + x, y * 2 + c)


def flat_device(d):
    return (d // 4, d % 4)


def greet(me, n):
    bar = pltpu.get_barrier_semaphore()

    def signal(i, carry):
        pl.semaphore_signal(bar, inc=1, device_id=flat_device((me + i) % n), device_id_type=MESH)
        return carry

    lax.fori_loop(1, n, signal, 0)


def await_all(n):
    pl.semaphore_wait(pltpu.get_barrier_semaphore(), n - 1)


def each_small(block, n, me, slots, body, least=0, most=99):
    shard = sizes(block, n)[0]
    low = me * shard
    low_row = low // LANES
    first = 0
    for _, row in static_unit_rows(block):
        first = first + jnp.minimum(jnp.maximum(low - row * D, 0) // (UROWS * LANES), 16)

    def step(j, carry):
        g = first + j
        m, u = g // 16, g % 16
        start = small_row(block, m) * 6 + u * UROWS
        pos = start - low_row

        @pl.when((g < 16 * min(block.small, most)) & (g >= 16 * least) & (start * LANES < low + shard))
        def _():
            body((pos + UROWS) // UROWS, mat_of(block, m), u, pos, start * LANES)

        return carry

    lax.fori_loop(0, slots, step, 0)


def each_big(block, n, me, slots, body):
    shard = sizes(block, n)[0]
    low = me * shard
    low_row = low // LANES
    first = jnp.minimum(jnp.maximum(low - block.fc1 * D, 0) // (BIG * LANES), 16)

    def step(j, carry):
        u = first + j
        start = block.fc1 * 6 + u * BIG
        pos = start - low_row

        @pl.when((u < 16) & (start * LANES < low + shard) & (start * LANES + BIG * LANES > low))
        def _():
            body((pos + BIG) // BIG, u, pos, start * LANES)

        return carry

    lax.fori_loop(0, slots, step, 0)


def each_vector(block, n, me, first_vec, body):
    shard = sizes(block, n)[0]
    low = me * shard
    low_row = low // LANES
    for i, row in enumerate(block.vectors):
        @pl.when((row * D < low + shard) & (row * D + D > low))
        def _(i=i, row=row):
            body(first_vec + i, row * 6 - low_row, row * D)


def peers(axis, at):
    if axis == "z":
        return [dict(at, z=(at["z"] + k) % 4) for k in (1, 2, 3)]
    return [dict(at, **{axis: 1 - at[axis]})]


def first_peer(at):
    x, y, c = at["x"], at["y"], at["c"]
    return device(at["z"], x + (1 - c) * (1 - 2 * x), y + c * (1 - 2 * y), c)


def second_peer(at):
    x, y, c = at["x"], at["y"], at["c"]
    return device(at["z"], x + c * (1 - 2 * x), y + (1 - c) * (1 - 2 * y), c)


def dev(at):
    return device(at["z"], at["x"], at["y"], at["c"])


def gather_kernel(
    n, on_start, on_vectors, on_pair, on_last, xe_ref, xd_ref, w_ref, v_ref,
    re_ref, rd_ref, se_ref, sd_ref, be_ref, bd_ref, sv_ref, land, landv, own, ownv,
    s_small, s_big, s_vec, r_unit, r_vec, s_zxy, r_zxy, s_core, r_core, s_own, v_send, v_recv,
):
    wide, narrow, z, x, y, c = whoami()
    me = wide * 4 + narrow
    chip = me // 2
    at = dict(z=z, x=x, y=y, c=c)
    greet(me, n)
    lanes = lax.broadcasted_iota(jnp.int32, (1, LANES), 1)
    fields = {
        ENC: (xe_ref, re_ref, se_ref, be_ref, 0, 0, 0),
        DEC: (xd_ref, rd_ref, sd_ref, bd_ref, sizes(ENC, n)[2], sizes(ENC, n)[3], len(ENC.vectors)),
    }

    def prepare(block):
        x_ref, r_ref = fields[block][:2]
        shard, rows, _, _ = sizes(block, n)
        step = 8 * max(k for k in range(1, 40) if (rows // 8) % k == 0)

        def turn(i, carry):
            at_row = pl.multiple_of(i * step, 8)
            r_ref[pl.ds(FRONT + at_row, step), :] = pltpu.roll(
                x_ref[pl.ds(at_row, step), :], (me * shard) % LANES, 1
            )
            return carry

        lax.fori_loop(0, rows // step, turn, 0)

    def load_rows(block, row, count, stride=None):
        r_ref = fields[block][1]
        at_row = FRONT + row
        if stride is None:
            here, before = r_ref[pl.ds(at_row, count), :], r_ref[pl.ds(at_row - 1, count), :]
        else:
            here = r_ref[pl.ds(at_row, count, stride=stride), :]
            before = r_ref[pl.ds(at_row - 1, count, stride=stride), :]
        return jnp.where(lanes >= (me * sizes(block, n)[0]) % LANES, here, before)

    def send(src, dst, send_sem, recv_sem, target):
        @pl.when(target == me)
        def _():
            pltpu.make_async_copy(src, dst, send_sem).start()

        @pl.when(target != me)
        def _():
            pltpu.make_async_remote_copy(
                src, dst, send_sem, recv_sem, device_id=flat_device(target), device_id_type=MESH
            ).start()

    def which_of(block, start):
        return jnp.where(start // sizes(block, n)[0] == me, 0, 1)

    def small_units(block, least, most):
        s_ref, small0 = fields[block][2], fields[block][4]

        def body(slot, mat, u, pos, start):
            for k in range(6):
                s_ref[slot, :, k * LANES : (k + 1) * LANES] = load_rows(block, pos + k, UNIT, 6).astype(BF)
            which = which_of(block, start)
            send(
                s_ref.at[slot], land.at[which, mat // 2], s_small.at[small0 + slot], r_unit.at[which, mat // 2],
                u * 2 + mat % 2,
            )

        each_small(block, n, me, sizes(block, n)[2], body, least, most)

    def big_units(block):
        b_ref, big0 = fields[block][3], fields[block][5]
        pair = (block.first_mat + block.small_mats) // 2

        def body(slot, u, pos, start):
            for q in range(4):
                for k in range(6):
                    b_ref[slot, q % 2, q // 2, :, k * LANES : (k + 1) * LANES] = load_rows(
                        block, pos + 6 * q + k, UNIT, 24
                    ).astype(BF)
            which = which_of(block, start)
            for core in range(2):
                send(
                    b_ref.at[slot, core], land.at[which, pl.ds(pair, 2)], s_big.at[big0 + slot, core],
                    r_unit.at[which, pair], u * 2 + core,
                )

        each_big(block, n, me, sizes(block, n)[3], body)

    def vector_units(block):
        def body(v, pos, start):
            sv_ref[v] = load_rows(block, pos, 8).astype(BF).astype(F32)
            which = which_of(block, start)
            send(sv_ref.at[v], landv.at[which], s_vec.at[v], r_vec.at[which], v)

        each_vector(block, n, me, fields[block][6], body)

    def pair_units(pair):
        block = ENC if pair < 6 else DEC
        local = pair - block.first_mat // 2
        half = block.small_mats // 2
        if local == half:
            big_units(block)
        elif local != half + 1:
            first = 2 * local - (4 if local > half else 0)
            small_units(block, first, first + 2)

    prepare(ENC)
    await_all(n)
    pair_units(0)
    vector_units(ENC)
    prepare(DEC)
    vector_units(DEC)
    for pair in range(1, AHEAD):
        pair_units(pair)

    def of_self(first, last, which):
        return jnp.where(which == 0, first, last) == me

    def arrive_unit(first, last, src, dst, local_sem, recv):
        for which, holder in ((0, first), (1, last)):
            needed = True if which == 0 else (first != last)

            @pl.when(needed & (holder == me))
            def _(which=which):
                pltpu.make_async_copy(src(which), dst(which), local_sem).wait()

            @pl.when(needed & (holder != me))
            def _(which=which):
                pltpu.make_async_copy(src(which), dst(which), recv(which)).wait()

    def vec_of(v):
        n_enc = len(ENC.vectors)
        rows = ENC.vectors + DEC.vectors
        start = 0
        before = 0
        for i, row in enumerate(rows):
            start = start + jnp.where(v >= i, row - before, 0)
            before = row
        return start * D, jnp.where(v < n_enc, sizes(ENC, n)[0], sizes(DEC, n)[0])

    @pl.when(me < N_VEC)
    def _():
        start, shard = vec_of(me)
        first, last = start // shard, (start + D - 1) // shard
        arrive_unit(
            first, last, lambda w: sv_ref.at[0], lambda w: landv.at[w], s_vec.at[me], lambda w: r_vec.at[w]
        )
        at_elem = lax.broadcasted_iota(jnp.int32, (8, LANES), 0) * LANES + lax.broadcasted_iota(jnp.int32, (8, LANES), 1)
        ownv[...] = jnp.where(at_elem < (first + 1) * shard - start, landv[0], landv[1])

    @pl.when(me >= N_VEC)
    def _():
        ownv[...] = jnp.zeros_like(ownv)

    pltpu.sync_copy(ownv, v_ref.at[z, x, y, c])
    vorder = ("z", "x", "y", "c")

    def vview(done):
        have = set(vorder[:done])
        return tuple(slice(None) if a in have else at[a] for a in "zxyc")

    def vcopies(phase):
        axis = vorder[phase]
        out = []
        for k, p in enumerate(peers(axis, at)):
            ref = v_ref.at[vview(phase)]
            slot = phase if axis == "z" else phase + 2
            out.append(
                pltpu.make_async_remote_copy(
                    ref, ref, v_send.at[slot + k], v_recv.at[slot + k], device_id=dev(p), device_id_type=MESH
                )
            )
        return out

    row_i = lax.broadcasted_iota(jnp.int32, (UNIT, D), 0)
    col_i = lax.broadcasted_iota(jnp.int32, (UNIT, D), 1)

    def merge(pair):
        block = ENC if pair < 6 else DEC
        shard = sizes(block, n)[0]
        local = pair - block.first_mat // 2
        half = block.small_mats // 2
        if half <= local < half + 2:
            start = (block.fc1 * 6 + chip * BIG) * LANES
            elem = row_i * FF + (2 * (local - half) + c) * D + col_i
            length = BIG * LANES
        else:
            small = 2 * local - (4 if local >= half + 2 else 0) + c
            start = (small_row(block, small) * 6 + chip * UROWS) * LANES
            elem = row_i * D + col_i
            length = UROWS * LANES
        first, last = start // shard, (start + length - 1) // shard
        if half <= local < half + 2:
            if local == half:
                low_row = me * shard // LANES
                slot = (start // LANES - low_row + BIG) // BIG + (0 if block is ENC else sizes(ENC, n)[3])
                slot = jnp.minimum(jnp.maximum(slot, 0), sizes(ENC, n)[3] + sizes(DEC, n)[3] - 1)
                arrive_unit(
                    first, last, lambda w: land.at[w, pl.ds(pair, 2)], lambda w: land.at[w, pl.ds(pair, 2)],
                    s_big.at[slot, c], lambda w: r_unit.at[w, pair],
                )
        else:
            low_row = me * shard // LANES
            slot = (start // LANES - low_row + UROWS) // UROWS + (0 if block is ENC else sizes(ENC, n)[2])
            slot = jnp.minimum(jnp.maximum(slot, 0), sizes(ENC, n)[2] + sizes(DEC, n)[2] - 1)
            arrive_unit(
                first, last, lambda w: land.at[w, pair], lambda w: land.at[w, pair],
                s_small.at[slot], lambda w: r_unit.at[w, pair],
            )
        own[pair] = jnp.where(elem < (first + 1) * shard - start, land[0, pair], land[1, pair])

    def own_place(pair):
        return w_ref.at[pair, c, z, x, y]

    def remote(src, dst, pair, k, target):
        return pltpu.make_async_remote_copy(
            src, dst, s_zxy.at[pair, k], r_zxy.at[pair, k], device_id=target, device_id_type=MESH
        )

    def copies(pair, phase):
        if phase == 0:
            return [
                remote(own.at[pair], own_place(pair), pair, 2 + k, device((z + k) % 4, x, y, c)) for k in (1, 2, 3)
            ]
        if phase == 1:
            ref = w_ref.at[pair, c, :, x, y]
            return [remote(ref, ref, pair, 0, first_peer(at))]
        if phase == 2:
            ref = w_ref.at[pair, c, :, :, y]
            return [remote(ref, ref, pair, 1, second_peer(at))]
        ref = w_ref.at[pair, c]
        return [remote(ref, ref, pair, 2, device(z, x, y, 1 - c))]

    def begin(pair, phase):
        if phase != 2:
            for cp in copies(pair, phase):
                cp.start()
            return

        @pl.when(c == 0)
        def _():
            copies(pair, 2)[0].start()

        @pl.when(c == 1)
        def _():
            ref = w_ref.at[pair, c, :, x]
            remote(ref, ref, pair, 1, second_peer(at)).start()

    for t in range(N_PAIR + F_AT[3]):
        if t < N_PAIR:
            merge(t)
            pltpu.make_async_copy(own.at[t], own_place(t), s_own.at[t]).start()
            begin(t, 0)
        for phase in (1, 2, 3):
            pair = t - F_AT[phase - 1]
            if 0 <= pair < N_PAIR:
                if phase == 1:
                    pltpu.make_async_copy(own.at[pair], own_place(pair), s_own.at[pair]).wait()
                for cp in copies(pair, phase - 1):
                    cp.wait_recv()
                begin(pair, phase)
        if t + AHEAD < N_PAIR:
            pair_units(t + AHEAD)
        if t == 1:
            on_start()
        if t < 5:
            if t > 0:
                for cp in vcopies(t - 1):
                    cp.wait_recv()
            if t < 4:
                for cp in vcopies(t):
                    cp.start()
            else:
                on_vectors()
        pair = t - F_AT[3]
        if pair == N_PAIR - 1:
            on_last()
        if 0 <= pair < N_PAIR:
            for cp in copies(pair, 3):
                cp.wait_recv()
            on_pair(pair)

    for phase in range(4):
        for cp in vcopies(phase):
            cp.wait_send()
    for pair in range(N_PAIR):
        for phase in range(4):
            for cp in copies(pair, phase):
                cp.wait_send()
    for b, (block, s_ref, b_ref) in enumerate(((ENC, se_ref, be_ref), (DEC, sd_ref, bd_ref))):
        shard, rows, n_small, n_big = sizes(block, n)
        small0 = 0 if b == 0 else sizes(ENC, n)[2]
        big0 = 0 if b == 0 else sizes(ENC, n)[3]

        def small_wait(slot, mat, u, pos, start, s_ref=s_ref, small0=small0):
            @pl.when(u * 2 + mat % 2 != me)
            def _():
                pltpu.make_async_copy(s_ref.at[slot], s_ref.at[slot], s_small.at[small0 + slot]).wait()

        def big_wait(slot, u, pos, start, b_ref=b_ref, big0=big0):
            for core in range(2):
                @pl.when(u * 2 + core != me)
                def _(core=core):
                    pltpu.make_async_copy(
                        b_ref.at[slot, core], b_ref.at[slot, core], s_big.at[big0 + slot, core]
                    ).wait()

        def vec_wait(v, pos, start):
            @pl.when(me != v)
            def _():
                pltpu.make_async_copy(sv_ref.at[v], sv_ref.at[v], s_vec.at[v]).wait()

        each_vector(block, n, me, 0 if b == 0 else len(ENC.vectors), vec_wait)
        each_small(block, n, me, n_small, small_wait)
        each_big(block, n, me, n_big, big_wait)


def rows_of(flat, rows):
    return jnp.pad(flat, (0, rows * LANES - flat.shape[0])).reshape(rows, LANES)


SCALE = HEAD_DIM ** (-0.5)
FORBID = -1000000000.0
ROOT_HALF = 0.7071067811865476
PDF = 0.3989422804014327


def mm(a, b):
    return jnp.dot(a, b, preferred_element_type=F32)


def mm_nt(a, b):
    return lax.dot_general(a, b, (((1,), (1,)), ((), ())), preferred_element_type=F32)


def mm_tn(a, b):
    return lax.dot_general(a, b, (((0,), (0,)), ((), ())), preferred_element_type=F32)


def col_blocks(body, width=256):
    def step(j, carry):
        body(pl.ds(pl.multiple_of(j * width, width), width))
        return carry

    lax.fori_loop(0, D // width, step, 0)


def row_blocks(rows, body, height=64):
    def step(i, carry):
        body(pl.ds(pl.multiple_of(i * height, height), height))
        return carry

    lax.fori_loop(0, rows // height, step, 0)


def linear(x_ref, w_ref, rows, out_ref, bias=None):
    x = x_ref[0:rows, :]

    def body(cols):
        y = mm(x, w_ref[:, cols])
        if bias is not None:
            y = y + bias[:, cols]
        out_ref[0:rows, cols] = y.astype(out_ref.dtype)

    col_blocks(body)


def norm_rows(x):
    centred = x - jnp.mean(x, axis=1, keepdims=True)
    spread = jnp.mean(centred * centred, axis=1, keepdims=True)
    root = lax.rsqrt(spread + 1e-05)
    return centred * root, root


def norm_forward_ref(x_ref, gain, shift, rows, out_ref):
    def body(r):
        hat, _ = norm_rows(x_ref[r, :].astype(F32))
        out_ref[r, :] = (hat * gain[...] + shift[...]).astype(BF)

    row_blocks(rows, body)


def attend_tiles(rows, keys, causal):
    return [(start, min(start + 128, keys) if causal else keys) for start in range(0, rows, 128)]


def both_heads(x):
    lane = lax.broadcasted_iota(jnp.int32, (1, LANES), 1)
    zero = jnp.zeros_like(x)
    return jnp.concatenate([jnp.where(lane < HEAD_DIM, x, zero), jnp.where(lane < HEAD_DIM, zero, x)], axis=0)


def scores_of(k, q2, mask_ref, start, reach):
    scores = mm_nt(k, q2)
    if mask_ref is not None:
        mask = mask_ref[0:reach, start : start + LANES]
        scores = jnp.where(jnp.concatenate([mask, mask], axis=1) > 0, scores, FORBID)
    return scores


def attention_forward_ref(q_ref, k_ref, v_ref, mask_ref, rows, keys, mixed_ref, lse_ref):
    def pair_of_heads(i, carry):
        cols = pl.ds(pl.multiple_of(i * LANES, LANES), LANES)
        v_turned = jnp.transpose(v_ref[0:keys, cols])
        for tile, (start, reach) in enumerate(attend_tiles(rows, keys, mask_ref is not None)):
            r = slice(start, start + LANES)
            q2 = both_heads(q_ref[r, cols] * jnp.asarray(SCALE, BF))
            scores = scores_of(k_ref[0:reach, cols], q2, mask_ref, start, reach)
            peak = jnp.max(scores, axis=0, keepdims=True)
            weights = jnp.exp(scores - peak)
            totals = jnp.sum(weights, axis=0, keepdims=True)
            probs = weights.astype(BF)
            share = 1.0 / totals
            mixed = jnp.concatenate(
                [
                    mm(v_turned[s * HEAD_DIM : (s + 1) * HEAD_DIM, 0:reach], probs[:, s * LANES : (s + 1) * LANES])
                    * share[:, s * LANES : (s + 1) * LANES]
                    for s in range(2)
                ],
                axis=0,
            )
            mixed_ref[r, cols] = jnp.transpose(mixed).astype(BF)
            lse_ref[tile, pl.ds(i, 1), :] = peak + jnp.log(totals)
        return carry

    lax.fori_loop(0, D // LANES, pair_of_heads, 0, unroll=1 if mask_ref is not None else 2)


def project_add(x_ref, mixed_ref, w_ref, bias, rows, out_ref):
    m = mixed_ref[0:rows, :]

    def body(cols):
        out_ref[0:rows, cols] = x_ref[0:rows, cols].astype(F32) + mm(m, w_ref[:, cols]) + bias[:, cols]

    col_blocks(body)


def gelu_block(n_ref, w_ref, bias, rows, block, act_ref, slope_ref):
    x = n_ref[0:rows, :]

    def body(cols):
        pre = mm(x, w_ref[:, cols]) + bias[:, cols]
        bell = 0.5 * (1.0 + lax.erf(pre * ROOT_HALF))
        act_ref[block, 0:rows, cols] = (pre * bell).astype(BF)
        slope_ref[block, 0:rows, cols] = (bell + pre * (PDF * jnp.exp(-0.5 * pre * pre))).astype(BF)

    col_blocks(body, 128)


def accumulate(a_ref, w_ref, rows, out_ref):
    a = a_ref[0:rows, :]

    def body(cols):
        out_ref[0:rows, cols] += mm(a, w_ref[:, cols])

    col_blocks(body)


def add_row(out_ref, x_ref, row_ref, r):
    out_ref[r, :] = x_ref[r, :] + row_ref[...]


def both(body):
    def step(k, carry):
        body(k)
        return carry

    lax.fori_loop(0, 2, step, 0)


N_SAVED = 28


def saved_shapes(rows, frames):
    tall = -(-rows // 128) * 128
    enc_lse, dec_lse = ((frames // 128, 8, 2 * LANES), F32), ((tall // 128, 8, 2 * LANES), F32)
    return (
        [((frames, D), BF)] * 5
        + [enc_lse, ((frames, D), F32), ((frames, D), BF), ((4, frames, D), BF), ((4, frames, D), BF), ((frames, D), BF)]
        + [((rows, D), BF)]
        + [((tall, D), BF)] * 4
        + [dec_lse, ((rows, D), F32), ((rows, D), BF)]
        + [((tall, D), BF), ((frames, D), BF), ((frames, D), BF), ((tall, D), BF), dec_lse]
        + [((rows, D), F32), ((rows, D), BF), ((4, rows, D), BF), ((4, rows, D), BF)]
    )


def make_mask(seg_ref, row_ref, col_ref, mask_ref):
    rows, tall = seg_ref.shape[1], mask_ref.shape[0]
    row_ref[...] = jnp.full(row_ref.shape, -1.0, F32)
    row_ref[0:1, 0:rows] = seg_ref[...].astype(F32)
    for i in range(tall // LANES):
        part = slice(i * LANES, (i + 1) * LANES)
        col_ref[part, :] = jnp.transpose(jnp.broadcast_to(row_ref[0:1, part], (LANES, LANES)))

    def body(r):
        key = lax.broadcasted_iota(jnp.int32, (64, tall), 0) + r.start
        query = lax.broadcasted_iota(jnp.int32, (64, tall), 1)
        allowed = (col_ref[r, 0:1] == row_ref[0:1, :]) & (key <= query)
        mask_ref[r, :] = jnp.where(allowed, 1.0, 0.0)

    row_blocks(tall, body)


def forward_kernel(n, rows, frames, *refs):
    xe_ref, xd_ref, ein_ref, din_ref, seg_ref, dcot_ref, w_ref, v_ref = refs[:8]
    outs, refs = refs[8 : 8 + N_SAVED], refs[8 + N_SAVED :]
    early_ref, refs = refs[0], refs[1:]
    comm, refs = refs[:24], refs[24:]
    bufs, refs = refs[:N_SAVED], refs[N_SAVED:]
    vv, wbuf, acc, mask_ref, seg_row, seg_col, s_save, s_w, cot, gown, gsum, s_g, r_g, s_early = refs
    _, _, z, x, y, c = whoami()
    (
        e_n1, e_q, e_k, e_v, e_mix, e_lse, e_after, e_n2, e_act, e_slope, e_out,
        d_n1, d_q, d_k, d_v, d_mix, d_lse, d_after, d_n2,
        c_q, c_k, c_v, c_mix, c_lse, d_after2, d_n3, d_act, d_slope,
    ) = bufs
    eacc = acc.at[0:frames]

    def vec(i):
        return vv.at[pl.ds(i, 1)]

    def save(*indices):
        for i in indices:
            pltpu.make_async_copy(bufs[i], outs[i], s_save.at[i]).start()

    def cot_copy():
        return pltpu.make_async_copy(dcot_ref, cot, s_early.at[0])

    def early_core(i):
        return pltpu.make_async_remote_copy(
            gown.at[i, 1 - c], gsum.at[i], s_g.at[i], r_g.at[i], device_id=device(z, x, y, 1 - c), device_id_type=MESH
        )

    def early_save(i):
        return pltpu.make_async_copy(gsum.at[i], early_ref.at[i], s_early.at[i])

    def early_grad(i):
        both(lambda k: weight_grad(d_act.at[2 - 2 * i + k], cot, rows, gown.at[i, k]))
        early_core(i).start()

    def early_sum(i):
        early_core(i).wait_recv()

        def body(j, carry):
            a, b = j // 2, j % 2
            for k in range(2):
                gsum[i, a, b, k] = (gsum[i, a, b, k].astype(F32) + gown[i, c, a, b, k].astype(F32)).astype(BF)
            return carry

        lax.fori_loop(0, 8, body, 0)
        early_save(i).start()

    def on_last():
        early_sum(0)

    def on_start():
        cot_copy().start()
        make_mask(seg_ref, seg_row, seg_col, mask_ref)
        for ref in (d_q, d_k, d_v, c_q):
            if ref.shape[0] > rows:
                ref[rows:, :] = jnp.zeros((ref.shape[0] - rows, D), BF)
        for ref in (e_lse, d_lse, c_lse):
            ref[...] = jnp.zeros_like(ref)

    def on_vectors():
        pltpu.sync_copy(v_ref, vv_tiles)
        for i in range(N_VEC):
            for k in range(6):
                vv[i : i + 1, k * LANES : (k + 1) * LANES] = vv_tiles[i // 8, i // 4 % 2, i // 2 % 2, i % 2, k : k + 1, :]

    def on_pair(pair):
        if pair == 12:
            early_grad(0)
            early_sum(1)
        if pair > 11:
            return
        cps = [pltpu.make_async_copy(w_ref.at[pair, k].reshape(D, D), wbuf.at[k], s_w.at[k]) for k in range(2)]
        for cp in cps:
            cp.start()
        if pair == 0:
            norm_forward_ref(ein_ref, vec(0), vec(1), frames, e_n1)
        if pair == 6:
            norm_forward_ref(din_ref, vec(12), vec(13), rows, d_n1)
        if pair == 11:
            cot_copy().wait()
            early_grad(1)
        for cp in cps:
            cp.wait()
        w0, w1 = wbuf.at[0], wbuf.at[1]
        if pair == 0:
            linear(e_n1, w0, frames, e_q, vec(2))
            linear(e_n1, w1, frames, e_k)
            save(0, 1, 2)
        elif pair == 1:
            linear(e_n1, w0, frames, e_v, vec(3))
            attention_forward_ref(e_q, e_k, e_v, None, frames, frames, e_mix, e_lse)
            project_add(ein_ref, e_mix, w1, vec(4), frames, e_after)
            norm_forward_ref(e_after, vec(5), vec(6), frames, e_n2)
            save(3, 4, 5, 6, 7)
        elif pair in (2, 3):
            both(lambda k: gelu_block(
                e_n2, wbuf.at[k], vec(7 + 2 * (pair - 2) + k), frames, 2 * (pair - 2) + k, e_act, e_slope
            ))
            if pair == 3:
                save(8, 9)
        elif pair in (4, 5):
            if pair == 4:
                eacc[...] = e_after[...] + vec(11)[...]
            both(lambda k: accumulate(e_act.at[2 * (pair - 4) + k], wbuf.at[k], frames, eacc))
            if pair == 5:
                e_out[...] = eacc[...].astype(BF)
                save(10)
        elif pair == 6:
            linear(d_n1, w0, rows, d_q, vec(14))
            linear(d_n1, w1, rows, d_k)
            save(11, 12, 13)
        elif pair == 7:
            linear(d_n1, w0, rows, d_v, vec(15))
            attention_forward_ref(d_q, d_k, d_v, mask_ref, d_q.shape[0], d_k.shape[0], d_mix, d_lse)
            project_add(din_ref, d_mix, w1, vec(16), rows, d_after)
            norm_forward_ref(d_after, vec(17), vec(18), rows, d_n2)
            save(14, 15, 16, 17, 18)
        elif pair == 8:
            linear(d_n2, w0, rows, c_q, vec(19))
            linear(e_out, w1, frames, c_k)
            save(19, 20)
        elif pair == 9:
            linear(e_out, w0, frames, c_v, vec(20))
            attention_forward_ref(c_q, c_k, c_v, None, c_q.shape[0], frames, c_mix, c_lse)
            project_add(d_after, c_mix, w1, vec(21), rows, d_after2)
            norm_forward_ref(d_after2, vec(22), vec(23), rows, d_n3)
            save(21, 22, 23, 24, 25)
        elif pair in (10, 11):
            both(lambda k: gelu_block(
                d_n3, wbuf.at[k], vec(24 + 2 * (pair - 10) + k), rows, 2 * (pair - 10) + k, d_act, d_slope
            ))
            if pair == 11:
                save(26, 27)

    vv_tiles = comm[-1]
    gather_kernel(n, on_start, on_vectors, on_pair, on_last, xe_ref, xd_ref, w_ref, v_ref, *comm[:-1])
    for i in range(N_SAVED):
        pltpu.make_async_copy(bufs[i], outs[i], s_save.at[i]).wait()
    for i in range(2):
        early_core(i).wait_send()
        early_save(i).wait()


def forward_pass(encoder_master, decoder_master, encoder_input, decoder_input, segments, decoder_cotangent, n):
    (_, re, ne, ge), (_, rd, nd, gd) = sizes(ENC, n), sizes(DEC, n)
    frames, rows = encoder_input.shape[0], decoder_input.shape[0]
    tall = -(-rows // 128) * 128
    dma = pltpu.SemaphoreType.DMA
    saved = saved_shapes(rows, frames)
    vmem, hbm = pl.BlockSpec(memory_space=pltpu.VMEM), pl.BlockSpec(memory_space=pl.ANY)
    return pl.pallas_call(
        partial(forward_kernel, n, rows, frames),
        out_shape=(
            jax.ShapeDtypeStruct((N_PAIR, 2, 4, 2, 2, UNIT, D), BF),
            jax.ShapeDtypeStruct((4, 2, 2, 2, 8, LANES), F32),
            *(jax.ShapeDtypeStruct(shape, dtype) for shape, dtype in saved),
            jax.ShapeDtypeStruct((2, 4, 2, 2, UNIT, D), BF),
        ),
        in_specs=[vmem] * 5 + [hbm],
        out_specs=(hbm,) * (3 + N_SAVED),
        scratch_shapes=[
            pltpu.VMEM((FRONT + re + BACK, LANES), F32),
            pltpu.VMEM((FRONT + rd + BACK, LANES), F32),
            pltpu.VMEM((ne, UNIT, D), BF),
            pltpu.VMEM((nd, UNIT, D), BF),
            pltpu.VMEM((ge, 2, 2, UNIT, D), BF),
            pltpu.VMEM((gd, 2, 2, UNIT, D), BF),
            pltpu.VMEM((N_VEC, 8, LANES), F32),
            pltpu.VMEM((2, N_PAIR, UNIT, D), BF),
            pltpu.VMEM((2, 8, LANES), F32),
            pltpu.VMEM((N_PAIR, UNIT, D), BF),
            pltpu.VMEM((8, LANES), F32),
            dma((ne + nd,)),
            dma((ge + gd, 2)),
            dma((N_VEC,)),
            dma((2, N_PAIR)),
            dma((2,)),
            dma((N_PAIR, 6)),
            dma((N_PAIR, 6)),
            dma((N_PAIR,)),
            dma((N_PAIR,)),
            dma((N_PAIR,)),
            dma((6,)),
            dma((6,)),
            pltpu.VMEM((4, 2, 2, 2, 8, LANES), F32),
            *(pltpu.VMEM(shape, dtype) for shape, dtype in saved),
            pltpu.VMEM((32, D), F32),
            pltpu.VMEM((2, D, D), BF),
            pltpu.VMEM((rows, D), F32),
            pltpu.VMEM((tall, tall), F32),
            pltpu.VMEM((8, tall), F32),
            pltpu.VMEM((tall, LANES), F32),
            dma((N_SAVED,)),
            dma((2,)),
            pltpu.VMEM((rows, D), BF),
            pltpu.VMEM((2, 2, 4, 2, 2, UNIT, D), BF),
            pltpu.VMEM((2, 4, 2, 2, UNIT, D), BF),
            dma((2,)),
            dma((2,)),
            dma((2,)),
        ],
        compiler_params=pltpu.CompilerParams(collective_id=0, has_side_effects=True, vmem_limit_bytes=58 << 20),
        name="forward",
    )(rows_of(encoder_master, re), rows_of(decoder_master, rd), encoder_input, decoder_input, segments,
      decoder_cotangent)


RING = 3
RING_C = 5
EARLY = 2
TICKS = [(t, part) for t in range(EARLY, N_PAIR) for part in ((0, 1) if t in (4, 6) else (0,))]
SENT = list(range(EARLY)) + [
    EARLY + u for u, (t, part) in enumerate(TICKS) if part == 1 or (t, 1) not in TICKS
]


def scatter_kernel(
    n, begin_loads, produce, after, early_ref, vg_ref, gbuf, oe_ref, od_ref, norm_ref,
    land_c, land_b, land_a, land_z, ownb, vown, vl_c, vl_y, vl_x, vl_z,
    ge_ref, gd_ref, fe, fd, fbe, fbd, fv, nsend, nland,
    s_core, r_core, s_free, s_ph, r_ph, s_back, r_small, r_big, sv, rv, s_vback, r_vback, s_n, r_n, s_out,
):
    wide, narrow, z, x, y, c = whoami()
    me = wide * 4 + narrow
    chip = me // 2
    at = dict(z=z, x=x, y=y, c=c)
    greet(me, n)
    sib = device(z, x, y, 1 - c)

    def slot_c(pair):
        return (N_PAIR - 1 - pair) % RING_C

    def core_copy(pair):
        return pltpu.make_async_remote_copy(
            gbuf.at[(N_PAIR - 1 - pair) % RING, 1 - c], land_c.at[slot_c(pair)], s_core.at[pair], r_core.at[pair], device_id=sib, device_id_type=MESH
        )

    mine_a = x * (1 - c) + y * c

    def phase_dmas(pair, phase):
        if phase == 1:
            steps = [(land_c.at[slot_c(pair), :, :, 1 - y], land_b.at[pair], 0, second_peer(at))]
        elif phase == 2:
            steps = [(land_b.at[pair, :, 1 - mine_a], land_a.at[pair], 1, first_peer(at))]
        else:
            steps = [
                (land_a.at[pair, (z + k) % 4], land_z.at[pair, k - 1], 1 + k, device((z + k) % 4, x, y, c))
                for k in (1, 2, 3)
            ]
        return [
            pltpu.make_async_remote_copy(
                src, dst, s_ph.at[pair, k], r_ph.at[pair, k], device_id=target, device_id_type=MESH
            )
            for src, dst, k, target in steps
        ]

    def begin(pair, phase):
        if phase != 1:
            for cp in phase_dmas(pair, phase):
                cp.start()
            return

        @pl.when(c == 0)
        def _():
            phase_dmas(pair, 1)[0].start()

        @pl.when(c == 1)
        def _():
            pltpu.make_async_remote_copy(
                land_c.at[slot_c(pair), :, 1 - x], land_b.at[pair], s_ph.at[pair, 0], r_ph.at[pair, 0],
                device_id=second_peer(at), device_id_type=MESH,
            ).start()

    def back(pair):
        block = ENC if pair < 6 else DEC
        shard = sizes(block, n)[0]
        local = pair - block.first_mat // 2
        half = block.small_mats // 2
        big = half <= local < half + 2
        if big:
            start = (block.fc1 * 6 + chip * BIG) * LANES
            length = BIG * LANES
        else:
            small = 2 * local - (4 if local >= half + 2 else 0) + c
            start = (small_row(block, small) * 6 + chip * UROWS) * LANES
            length = UROWS * LANES
        first, last = start // shard, (start + length - 1) // shard
        out = []
        for which, target in ((0, first), (1, last)):
            low_row = target * shard // LANES
            if big:
                slot = (start // LANES - low_row + BIG) // BIG
                q = 2 * (local - half) + c
                dst = (fbe if block is ENC else fbd).at[slot, q]
                recv = r_big.at[0 if block is ENC else 1, slot, q]
            else:
                slot = (start // LANES - low_row + UROWS) // UROWS
                dst = (fe if block is ENC else fd).at[slot]
                recv = r_small.at[0 if block is ENC else 1, slot]
            needed = True if which == 0 else first != last
            out.append((needed, target, dst, s_back.at[pair, which], recv))
        return out

    def start_back(pair):
        for needed, target, dst, send, recv in back(pair):
            @pl.when(needed & (target == me))
            def _(dst=dst, recv=recv):
                pltpu.make_async_copy(ownb.at[pair], dst, recv).start()

            @pl.when(needed & (target != me))
            def _(dst=dst, recv=recv, send=send, target=target):
                pltpu.make_async_remote_copy(
                    ownb.at[pair], dst, send, recv, device_id=flat_device(target), device_id_type=MESH
                ).start()

    def end_back(pair):
        for needed, target, dst, send, recv in back(pair):
            @pl.when(needed & (target != me))
            def _(send=send):
                pltpu.make_async_copy(ownb.at[pair], ownb.at[pair], send).wait()

    def add_core(pair):
        def body(i, carry):
            a, b = i // 2, i % 2
            for k in range(2):
                mine = gbuf[(N_PAIR - 1 - pair) % RING, c, a, b, k]
                land_c[slot_c(pair), a, b, k] = (
                    land_c[slot_c(pair), a, b, k].astype(F32) + mine.astype(F32)
                ).astype(BF)
            return carry

        lax.fori_loop(0, 8, body, 0)

    def add_b(pair):
        def body(i, carry):
            a, b = i // 2, i % 2
            mine = land_c[slot_c(pair), a, b * (1 - c) + x * c, y * (1 - c) + b * c]
            land_b[pair, a, b] = (land_b[pair, a, b].astype(F32) + mine.astype(F32)).astype(BF)
            return carry

        lax.fori_loop(0, 8, body, 0)

    def add_a(pair):
        for a in range(4):
            land_a[pair, a] = (land_a[pair, a].astype(F32) + land_b[pair, a, mine_a].astype(F32)).astype(BF)

    def add_z(pair):
        total = land_a[pair, z].astype(F32)
        for k in range(3):
            total = total + land_z[pair, k].astype(F32)
        ownb[pair] = total.astype(BF)
        squares = total * total
        return jnp.sum(squares.reshape(UNIT // 8, 8, D), axis=0)

    vland = dict(c=vl_c, y=vl_y, x=vl_x, z=vl_z)

    def vsteps(phase):
        if phase == 0:
            return [(vg_ref.at[:, :, :, 1 - c], vl_c, 0, dict(at, c=1 - c))]
        if phase == 1:
            return [(vl_c.at[:, :, 1 - y], vl_y, 1, dict(at, y=1 - y))]
        if phase == 2:
            return [(vl_y.at[:, 1 - x], vl_x, 2, dict(at, x=1 - x))]
        return [(vl_x.at[(z + k) % 4], vl_z.at[k - 1], 2 + k, dict(at, z=(z + k) % 4)) for k in (1, 2, 3)]

    def vdmas(phase):
        return [
            pltpu.make_async_remote_copy(s, d, sv.at[k], rv.at[k], device_id=dev(p), device_id_type=MESH)
            for s, d, k, p in vsteps(phase)
        ]

    def vadd(phase):
        if phase == 0:
            vl_c[...] = vl_c[...] + vg_ref[:, :, :, c]
        elif phase == 1:
            vl_y[...] = vl_y[...] + vl_c[:, :, y]
        elif phase == 2:
            vl_x[...] = vl_x[...] + vl_y[:, x]
        else:
            vown[...] = vl_x[z] + vl_z[0] + vl_z[1] + vl_z[2]

    fields = {ENC: (0, ge_ref, oe_ref, fe, fbe), DEC: (1, gd_ref, od_ref, fd, fbd)}

    def units_to_flat(block, least=0, most=99):
        b, g_out, _, f_ref, fb_ref = fields[block]
        _, _, n_small, n_big = sizes(block, n)

        def small_body(slot, mat, u, pos, start):
            pltpu.make_async_copy(f_ref.at[slot], f_ref.at[slot], r_small.at[b, slot]).wait()
            for k in range(6):
                g_out[pl.ds(FRONT + pos + k, UNIT, stride=6), :] = f_ref[slot, :, k * LANES : (k + 1) * LANES].astype(F32)

        def big_body(slot, u, pos, start):
            for q in range(4):
                pltpu.make_async_copy(fb_ref.at[slot, q], fb_ref.at[slot, q], r_big.at[b, slot, q]).wait()
                for k in range(6):
                    g_out[pl.ds(FRONT + pos + 6 * q + k, UNIT, stride=24), :] = fb_ref[
                        slot, q, :, k * LANES : (k + 1) * LANES
                    ].astype(F32)

        if most > block.small_mats:
            each_big(block, n, me, n_big, big_body)
        each_small(block, n, me, n_small, small_body, least, most)

    def finish_flat(block):
        b, g_out, o_ref, _, _ = fields[block]
        shard, rows, _, _ = sizes(block, n)

        def vec_body(v, pos, start):
            pltpu.make_async_copy(fv.at[v], fv.at[v], r_vback.at[v]).wait()
            g_out[pl.ds(FRONT + pos, 6), :] = fv[v, 0:6, :]

        each_vector(block, n, me, 0 if block is ENC else len(ENC.vectors), vec_body)
        shift = (me * shard) % LANES
        step = 8 * max(k for k in range(1, 40) if (rows // 8) % k == 0)
        lanes = lax.broadcasted_iota(jnp.int32, (1, LANES), 1)
        unturn = lax.rem(LANES - shift, LANES)

        def turn(i, carry):
            at_row = pl.multiple_of(i * step, 8)
            here = pltpu.roll(g_out[pl.ds(FRONT + at_row, step), :], unturn, 1)
            after = pltpu.roll(g_out[pl.ds(FRONT + at_row + 1, step), :], unturn, 1)
            g_out[pl.ds(FRONT + at_row, step), :] = jnp.where(lanes < LANES - shift, here, after)
            return carry

        lax.fori_loop(0, rows // step, turn, 0)
        pltpu.make_async_copy(g_out.at[pl.ds(FRONT, rows)], o_ref, s_out.at[b]).start()

    def vector_targets(v_static):
        block = ENC if v_static < len(ENC.vectors) else DEC
        shard = sizes(block, n)[0]
        start = (ENC.vectors + DEC.vectors)[v_static] * D
        return start // shard, (start + D - 1) // shard

    def vectors_back():
        for v in range(N_VEC):
            for which, target in enumerate(sorted(set(vector_targets(v)))):
                if target == v:
                    @pl.when(me == v)
                    def _(v=v):
                        pltpu.make_async_copy(vown, fv.at[v], r_vback.at[v]).start()
                else:
                    @pl.when(me == v)
                    def _(v=v, target=target, which=which):
                        pltpu.make_async_remote_copy(
                            vown, fv.at[v], s_vback.at[which], r_vback.at[v], device_id=(target // 4, target % 4), device_id_type=MESH
                        ).start()

    seq = list(range(N_PAIR - 1, -1, -1))
    square = jnp.zeros((8, D), F32)
    def early_copy(i):
        return pltpu.make_async_copy(early_ref.at[i], land_c.at[i], s_core.at[i])

    for i in range(EARLY):
        early_copy(i).start()
    begin_loads()
    await_all(n)
    for i in range(EARLY):
        early_copy(i).wait()
        begin(seq[i], 1)
    for u in range(EARLY, EARLY + len(TICKS) + B_AT[3]):
        t, part = TICKS[u - EARLY] if u - EARLY < len(TICKS) else (N_PAIR + u - EARLY - len(TICKS), 0)
        done = part == 1 or (t, 1) not in TICKS
        if t < N_PAIR:
            if part == 0 and t - RING >= EARLY:
                core_copy(seq[t - RING]).wait_send()
            produce(t, part, gbuf.at[t % RING])
            if done:
                if t >= RING_C:
                    pl.semaphore_wait(s_free, 1)
                core_copy(seq[t]).start()
        for phase in (4, 3, 2, 1):
            if u - B_AT[phase - 1] in SENT:
                i = SENT.index(u - B_AT[phase - 1])
                pair = seq[i]
                if phase == 1 and i < EARLY:
                    continue
                if phase == 1:
                    core_copy(pair).wait_recv()
                    add_core(pair)
                elif phase == 2:
                    for cp in phase_dmas(pair, 1):
                        cp.wait()
                    add_b(pair)
                    if i < N_PAIR - RING_C:
                        pl.semaphore_signal(s_free, inc=1, device_id=sib, device_id_type=MESH)
                elif phase == 3:
                    for cp in phase_dmas(pair, 2):
                        cp.wait_recv()
                    add_a(pair)
                else:
                    for cp in phase_dmas(pair, 3):
                        cp.wait_recv()
                    square = square + add_z(pair)
                    start_back(pair)
                if phase < 4:
                    begin(pair, phase)
        if done:
            after(t)
        if t == N_PAIR + B_AT[2] - 1:
            units_to_flat(DEC)
        if t == N_PAIR + B_AT[3] - 1:
            finish_flat(DEC)
            units_to_flat(ENC, 2, 99)
        if t == N_PAIR - 1:
            for cp in vdmas(0):
                cp.start()
        elif N_PAIR <= t < N_PAIR + 4:
            phase = t - N_PAIR
            for cp in vdmas(phase):
                cp.wait_recv()
            vadd(phase)
            if phase < 3:
                for cp in vdmas(phase + 1):
                    cp.start()
            else:
                vectors_back()

    vsq = vown[...] * vown[...]
    for k in range(6):
        vsq = vsq + square[:, k * LANES : (k + 1) * LANES]
    nsend[...] = vsq

    def norm_copy(i):
        return pltpu.make_async_remote_copy(
            nsend, nland.at[i], s_n.at[i], r_n.at[i], device_id=flat_device((me + i) % n), device_id_type=MESH
        )

    def norm_start(i, carry):
        norm_copy(i).start()
        return carry

    lax.fori_loop(1, n, norm_start, 0)

    units_to_flat(ENC, 0, 2)
    finish_flat(ENC)

    def norm_wait(i, total):
        norm_copy(i).wait()
        return total + nland[i]

    total = lax.fori_loop(1, n, norm_wait, nsend[...])
    norm_ref[...] = jnp.broadcast_to(jnp.sqrt(jnp.sum(total)), (8, LANES))

    for b, (g_out, o_ref) in enumerate(((ge_ref, oe_ref), (gd_ref, od_ref))):
        pltpu.make_async_copy(g_out.at[pl.ds(FRONT, o_ref.shape[0])], o_ref, s_out.at[b]).wait()
    for phase in range(4):
        for cp in vdmas(phase):
            cp.wait_send()
    for v in range(N_VEC):
        for which, target in enumerate(sorted(set(vector_targets(v)))):
            if target != v:
                @pl.when(me == v)
                def _(which=which):
                    pltpu.make_async_copy(vown, vown, s_vback.at[which]).wait()
    for pair in range(N_PAIR):
        if N_PAIR - 1 - pair >= N_PAIR - RING:
            core_copy(pair).wait_send()
        for phase in (2, 3):
            for cp in phase_dmas(pair, phase):
                cp.wait_send()
        end_back(pair)


def sum_rows(ref, rows, out_ref):
    def body(r):
        out_ref[...] += jnp.sum(ref[r, :].astype(F32), axis=0, keepdims=True)

    out_ref[...] = jnp.zeros_like(out_ref)
    row_blocks(rows, body)


def norm_backward_ref(x_ref, gain, dn_ref, rows, out_ref, gain_grad, shift_grad):
    gain_grad[...] = jnp.zeros_like(gain_grad)
    shift_grad[...] = jnp.zeros_like(shift_grad)

    def body(r):
        hat, root = norm_rows(x_ref[r, :].astype(F32))
        dn = dn_ref[r, :]
        gain_grad[...] += jnp.sum(dn * hat, axis=0, keepdims=True)
        shift_grad[...] += jnp.sum(dn, axis=0, keepdims=True)
        g = dn * gain[...]
        part = g - jnp.mean(g, axis=1, keepdims=True) - hat * jnp.mean(g * hat, axis=1, keepdims=True)
        out_ref[r, :] += root * part

    row_blocks(rows, body)


def round_rows(src_ref, rows, out_ref):
    def body(r):
        out_ref[r, :] = src_ref[r, :].astype(BF)

    row_blocks(rows, body)


def weight_grad(a_ref, b_ref, rows, g_ref):
    b = b_ref[0:rows, :]
    flat = g_ref.reshape(D, D)

    def body(cols):
        flat[cols, :] = mm_tn(a_ref[0:rows, cols], b).astype(BF)

    col_blocks(body)


def back_through(a_ref, w_ref, rows, out_ref, add):
    a = a_ref[0:rows, :]

    def body(cols):
        y = mm_nt(a, w_ref[cols, :])
        if add:
            y = y + out_ref[0:rows, cols]
        out_ref[0:rows, cols] = y.astype(out_ref.dtype)

    col_blocks(body)


def gelu_back(o_ref, w_ref, slope_ref, rows, out_ref, bias_grad):
    a = o_ref[0:rows, :]

    def body(cols):
        y = mm_nt(a, w_ref[cols, :]) * slope_ref[0:rows, cols].astype(F32)
        bias_grad[:, cols] = jnp.sum(y, axis=0, keepdims=True)
        out_ref[0:rows, cols] = y.astype(BF)

    col_blocks(body)


def attention_backward_ref(q_ref, k_ref, v_ref, dm_ref, lse_ref, mask_ref, rows, keys, dq_ref, dk_ref, dv_ref, low, high):
    def pair_of_heads(i, carry):
        cols = pl.ds(pl.multiple_of(i * LANES, LANES), LANES)
        dk_ref[:, cols] = jnp.zeros((dk_ref.shape[0], LANES), F32)
        dv_ref[:, cols] = jnp.zeros((dv_ref.shape[0], LANES), F32)
        k_turned = jnp.transpose(k_ref[0:keys, cols])
        for tile, (start, reach) in enumerate(attend_tiles(rows, keys, mask_ref is not None)):
            r = slice(start, start + LANES)
            q2 = both_heads(q_ref[r, cols] * jnp.asarray(SCALE, BF))
            dm2 = both_heads(dm_ref[r, cols])
            scores = scores_of(k_ref[0:reach, cols], q2, mask_ref, start, reach)
            probs = jnp.exp(scores - lse_ref[tile, pl.ds(i, 1), :])
            dp = mm_nt(v_ref[0:reach, cols], dm2)
            weighted = probs * dp
            ds = (weighted - probs * jnp.sum(weighted, axis=0, keepdims=True)).astype(BF)
            dk_ref[0:reach, cols] += mm(ds, q2)
            dv_ref[0:reach, cols] += mm(probs.astype(BF), dm2)
            dq = jnp.concatenate(
                [
                    mm(k_turned[s * HEAD_DIM : (s + 1) * HEAD_DIM, 0:reach], ds[:, s * LANES : (s + 1) * LANES])
                    for s in range(2)
                ],
                axis=0,
            )
            dq_ref[r, cols] = jnp.transpose(dq) * SCALE
        return carry

    lax.fori_loop(low, high, pair_of_heads, 0, unroll=1 if mask_ref is not None else 3)


W_ORDER = (26, 27, 22, 23, 24, 25, 20, 21, 19, 16, 17, 18, 15, 12, 13, 14, 10, 11, 6, 7, 8, 9, 4, 5, 3, 0, 1, 2, 24, 25, 26, 27)
W_RING = 4
A_RING = 4


def backward_kernel(n, rows, frames, *refs):
    w_ref, v_ref, seg_ref, ein, din, ecot, dcot, early = refs[:8]
    kept, refs = refs[8 : 8 + N_SAVED], refs[8 + N_SAVED :]
    oe_ref, od_ref, norm_ref, fgrad, tgrad, dout = refs[:6]
    refs = refs[6:]
    comm, refs = refs[:34], refs[34:]
    (
        gbuf, vg, vgr, gains, wbuf, outg, eoutg, dn, pool, abuf, nbuf, xbuf,
        dq, dk, dv, mask_ref, seg_row, seg_col, lse, orow, mem, mgrad, s_l, s_w, s_a, s_o,
    ) = refs
    tall = mask_ref.shape[0]

    a_order = (
        [kept[27].at[k] for k in (2, 3, 0, 1)]
        + [kept[22].at[0:rows], kept[15].at[0:rows], din]
        + [kept[8].at[k] for k in (2, 3, 0, 1)]
        + [kept[9].at[k] for k in (2, 3, 0, 1)]
        + [kept[4], ein]
        + [kept[26].at[k] for k in range(4)]
    )
    used = [0, 0]

    def w_copy(u):
        m = W_ORDER[u]
        return pltpu.make_async_copy(w_ref.at[m // 2, m % 2].reshape(D, D), wbuf.at[u % W_RING], s_w.at[u % W_RING])

    def a_copy(u):
        src = a_order[u]
        return pltpu.make_async_copy(src, abuf.at[u % A_RING, 0 : src.shape[0]], s_a.at[u % A_RING])

    def with_w(mat, body):
        u = used[0]
        used[0] += 1
        assert W_ORDER[u] == mat
        w_copy(u).wait()
        body(wbuf.at[u % W_RING])
        if u + W_RING < len(W_ORDER):
            w_copy(u + W_RING).start()

    def with_a(body):
        u = used[1]
        used[1] += 1
        a_copy(u).wait()
        body(abuf.at[u % A_RING])
        if u + A_RING < len(a_order):
            a_copy(u + A_RING).start()

    def side(k, src, dst):
        return pltpu.make_async_copy(src, dst, s_l.at[k])

    def x_copy(i):
        return side(0, kept[i], xbuf.at[0 : kept[i].shape[0]])

    def n_copy(i):
        return side(1, kept[i], nbuf.at[0 : kept[i].shape[0]])

    def vrow(i):
        return vgr.at[i : i + 1]

    def take_two(which, copy, ring, total, body):
        u = used[which]
        used[which] += 2
        copy(u).wait()
        copy(u + 1).wait()
        body(lambda k: lax.rem(u + k, ring))
        for k in range(2):
            if u + k + ring < total:
                copy(u + k + ring).start()

    def two_w(mat, body):
        assert W_ORDER[used[0]] == mat
        take_two(0, w_copy, W_RING, len(W_ORDER), lambda slot: body(lambda k: wbuf.at[slot(k)]))

    def two_a(body):
        take_two(1, a_copy, A_RING, len(a_order), lambda slot: body(lambda k: abuf.at[slot(k)]))

    def feed(step, g, count, first_mat, first_vec, n_i):
        if step < 2:
            two_a(lambda a: both(lambda k: weight_grad(a(k), orow, count, g.at[k])))
            return
        first = 2 if step == 2 else 0
        if step == 2:
            n_copy(n_i).wait()

        def body(k, w, a):
            gelu_back(orow, w(k), a(k), count, pool.at[first + k], vgr.at[pl.ds(first_vec + first + k, 1)])
            weight_grad(nbuf, pool.at[first + k], count, g.at[k])

        two_w(first_mat + 4 + first, lambda w: two_a(lambda a: both(lambda k: body(k, w, a))))

    def feed_after(step, count, first_mat):
        first = 2 if step == 2 else 0
        if step == 2:
            dn[0:count, :] = jnp.zeros((count, D), F32)
        two_w(
            first_mat + first,
            lambda w: both(lambda k: back_through(pool.at[first + k], w(k), count, dn, True)),
        )

    def attend(part, *setting):
        g, count, padded, keys, padded_keys, out_ref, wo, q_i, lse_i, masked, bo, bq, bv = setting
        heads = partial(
            attention_backward_ref,
            pool.at[0], pool.at[1], pool.at[2], pool.at[3], lse, mask_ref if masked else None, padded, padded_keys,
            dq, dk.at[0:padded_keys], dv.at[0:padded_keys],
        )
        if part == 0:
            attend_start(*setting)
            heads(0, 3)
            return
        heads(3, 6)
        round_rows(dv, keys, pool.at[2])
        round_rows(dq, count, pool.at[0])
        round_rows(dk, keys, pool.at[1])
        sum_rows(dq, count, vrow(bq))
        sum_rows(dv, keys, vrow(bv))

    def attend_start(g, count, padded, keys, padded_keys, out_ref, wo, q_i, lse_i, masked, bo, bq, bv):
        cps = [side(2 + k, kept[q_i + k], pool.at[k, 0 : kept[q_i + k].shape[0]]) for k in range(3)]
        cps.append(side(5, kept[lse_i], lse.at[0 : kept[lse_i].shape[0]]))
        for cp in cps:
            cp.start()
        round_rows(out_ref, count, orow)
        sum_rows(out_ref, count, vrow(bo))
        with_a(lambda a: weight_grad(a, orow, count, g.at[1]))
        with_w(wo, lambda w: back_through(orow, w, count, pool.at[3], False))
        if padded > count:
            pool[3, count:padded, :] = jnp.zeros((padded - count, D), BF)
        for cp in cps:
            cp.wait()

    def start():
        o_copy = side(2, dcot, orow)
        o_copy.start()
        for u in range(A_RING):
            a_copy(u).start()
        for u in range(W_RING):
            w_copy(u).start()
        n_copy(25).start()
        x_copy(24).start()
        mem_copy = side(3, kept[10], mem)
        mem_copy.start()
        for i, v in enumerate((0, 5, 12, 17, 22, 28)):
            for k in range(6):
                gains[i : i + 1, k * LANES : (k + 1) * LANES] = v_ref[v // 8, v // 4 % 2, v // 2 % 2, v % 2, k : k + 1, :]
        o_copy.wait()
        mem_copy.wait()

    def widen():
        def body(r):
            outg[r, :] = orow[r, :].astype(F32)

        row_blocks(rows, body)
        sum_rows(outg, rows, vrow(28))

    def produce(t, part, g):
        if t < 4:
            feed(t, g, rows, 20, 24, 25)
            if t == 3:
                n_copy(18).start()
        elif t == 4:
            attend(part, g, rows, tall, frames, frames, outg, 19, 19, 23, False, 21, 19, 20)
            if part == 1:
                weight_grad(mem, pool.at[2], frames, g.at[0])
        elif t == 5:
            n_copy(18).wait()
            weight_grad(nbuf, pool.at[0], rows, g.at[0])
            weight_grad(mem, pool.at[1], frames, g.at[1])
            n_copy(11).start()
        elif t == 6:
            attend(part, g, rows, tall, rows, tall, outg, 15, 12, 16, True, 16, 14, 15)
            if part == 1:
                n_copy(11).wait()
                weight_grad(nbuf, pool.at[2], rows, g.at[0])
        elif t == 7:
            weight_grad(nbuf, pool.at[0], rows, g.at[0])
            weight_grad(nbuf, pool.at[1], rows, g.at[1])
            n_copy(7).start()
        elif t < 12:
            feed(t - 8, g, frames, 4, 7, 7)
            if t == 11:
                n_copy(0).start()
        elif t == 12:
            for half in range(2):
                attend(half, g, frames, frames, frames, frames, eoutg, 3, 1, 5, False, 4, 2, 3)
            n_copy(0).wait()
            weight_grad(nbuf, pool.at[2], frames, g.at[0])
        else:
            weight_grad(nbuf, pool.at[0], frames, g.at[0])
            weight_grad(nbuf, pool.at[1], frames, g.at[1])

    def after(t):
        if t in (2, 3):
            feed_after(t, rows, 20)
            if t == 2:
                widen()
                make_mask(seg_ref, seg_row, seg_col, mask_ref)
            if t == 3:
                x_copy(24).wait()
                norm_backward_ref(xbuf, gains.at[4:5], dn, rows, outg, vrow(22), vrow(23))
                x_copy(17).start()
        elif t == 5:
            with_w(16, lambda w: back_through(pool.at[0], w, rows, dn, False))
            with_w(17, lambda w: back_through(pool.at[1], w, frames, mgrad, False))
            with_w(18, lambda w: back_through(pool.at[2], w, frames, mgrad, True))
            x_copy(17).wait()
            norm_backward_ref(xbuf, gains.at[3:4], dn, rows, outg, vrow(17), vrow(18))
            x_copy(6).start()
        elif t == 7:
            cot = side(2, ecot, orow.at[0:frames])
            cot.start()
            with_w(12, lambda w: back_through(pool.at[0], w, rows, dn, False))
            with_w(13, lambda w: back_through(pool.at[1], w, rows, dn, True))
            with_w(14, lambda w: back_through(pool.at[2], w, rows, dn, True))
            with_a(lambda a: norm_backward_ref(a, gains.at[2:3], dn, rows, outg, vrow(12), vrow(13)))
            pltpu.make_async_copy(outg, tgrad, s_o.at[0]).start()
            cot.wait()

            def body(r):
                total = orow[r, :].astype(F32) + mgrad[r, :]
                eoutg[r, :] = total
                orow[r, :] = total.astype(BF)

            row_blocks(frames, body)
        elif t == 9:
            sum_rows(eoutg, frames, vrow(11))
        elif t in (10, 11):
            feed_after(t - 8, frames, 4)
            if t == 11:
                x_copy(6).wait()
                norm_backward_ref(xbuf, gains.at[1:2], dn, frames, eoutg, vrow(5), vrow(6))
                x_copy(24).start()
        elif t in (14, 15):
            if t == 14:
                x_copy(24).wait()
                row_blocks(rows, lambda r: add_row(dn, xbuf, gains.at[5:6], r))
            two_w(
                24 + 2 * (t - 14),
                lambda w: two_a(lambda a: both(lambda k: accumulate(a(k), w(k), rows, dn))),
            )
            if t == 15:
                round_rows(dn, rows, orow)
                pltpu.make_async_copy(orow, dout, s_o.at[2]).start()
        elif t == 13:
            with_w(0, lambda w: back_through(pool.at[0], w, frames, dn, False))
            with_w(1, lambda w: back_through(pool.at[1], w, frames, dn, True))
            with_w(2, lambda w: back_through(pool.at[2], w, frames, dn, True))
            with_a(lambda a: norm_backward_ref(a, gains.at[0:1], dn, frames, eoutg, vrow(0), vrow(1)))
            pltpu.make_async_copy(eoutg, fgrad, s_o.at[1]).start()
            for v in range(32):
                at = (v // 8, v // 4 % 2, v // 2 % 2, v % 2)
                if v < N_VEC:
                    vg[at + (slice(6, 8), slice(None))] = jnp.zeros((2, LANES), F32)
                    for k in range(6):
                        vg[at + (slice(k, k + 1), slice(None))] = vgr[v : v + 1, k * LANES : (k + 1) * LANES]
                else:
                    vg[at] = jnp.zeros((8, LANES), F32)

    scatter_kernel(n, start, produce, after, early, vg, gbuf, oe_ref, od_ref, norm_ref, *comm)
    pltpu.make_async_copy(outg, tgrad, s_o.at[0]).wait()
    pltpu.make_async_copy(eoutg, fgrad, s_o.at[1]).wait()
    pltpu.make_async_copy(orow, dout, s_o.at[2]).wait()


def backward_pass(weights, vectors, kept, early, ein, din, ecot, dcot, segments, n):
    (_, re, ne, ge), (_, rd, nd, gd) = sizes(ENC, n), sizes(DEC, n)
    frames, rows = ein.shape[0], din.shape[0]
    tall = -(-rows // 128) * 128
    dma = pltpu.SemaphoreType.DMA
    vmem, hbm = pl.BlockSpec(memory_space=pltpu.VMEM), pl.BlockSpec(memory_space=pl.ANY)
    return pl.pallas_call(
        partial(backward_kernel, n, rows, frames),
        out_shape=(
            jax.ShapeDtypeStruct((re, LANES), F32),
            jax.ShapeDtypeStruct((rd, LANES), F32),
            jax.ShapeDtypeStruct((8, LANES), F32),
            jax.ShapeDtypeStruct((frames, D), F32),
            jax.ShapeDtypeStruct((rows, D), F32),
            jax.ShapeDtypeStruct((rows, D), BF),
        ),
        in_specs=[hbm] + [vmem] * 2 + [hbm] * (5 + N_SAVED),
        out_specs=(hbm, hbm, vmem, hbm, hbm, hbm),
        scratch_shapes=[
            pltpu.VMEM((RING_C, 4, 2, 2, UNIT, D), BF),
            pltpu.VMEM((N_PAIR, 4, 2, UNIT, D), BF),
            pltpu.VMEM((N_PAIR, 4, UNIT, D), BF),
            pltpu.VMEM((N_PAIR, 3, UNIT, D), BF),
            pltpu.VMEM((N_PAIR, UNIT, D), BF),
            pltpu.VMEM((8, LANES), F32),
            pltpu.VMEM((4, 2, 2, 8, LANES), F32),
            pltpu.VMEM((4, 2, 8, LANES), F32),
            pltpu.VMEM((4, 8, LANES), F32),
            pltpu.VMEM((3, 8, LANES), F32),
            pltpu.VMEM((FRONT + re + BACK, LANES), F32),
            pltpu.VMEM((FRONT + rd + BACK, LANES), F32),
            pltpu.VMEM((ne, UNIT, D), BF),
            pltpu.VMEM((nd, UNIT, D), BF),
            pltpu.VMEM((ge, 4, UNIT, D), BF),
            pltpu.VMEM((gd, 4, UNIT, D), BF),
            pltpu.VMEM((N_VEC, 8, LANES), F32),
            pltpu.VMEM((8, LANES), F32),
            pltpu.VMEM((n, 8, LANES), F32),
            dma((N_PAIR,)),
            dma((N_PAIR,)),
            pltpu.SemaphoreType.REGULAR,
            dma((N_PAIR, 5)),
            dma((N_PAIR, 5)),
            dma((N_PAIR, 2)),
            dma((2, max(ne, nd))),
            dma((2, max(ge, gd), 4)),
            dma((6,)),
            dma((6,)),
            dma((2,)),
            dma((N_VEC,)),
            dma((n,)),
            dma((n,)),
            dma((2,)),
            pltpu.VMEM((RING, 2, 4, 2, 2, UNIT, D), BF),
            pltpu.VMEM((4, 2, 2, 2, 8, LANES), F32),
            pltpu.VMEM((32, D), F32),
            pltpu.VMEM((8, D), F32),
            pltpu.VMEM((W_RING, D, D), BF),
            pltpu.VMEM((rows, D), F32),
            pltpu.VMEM((frames, D), F32),
            pltpu.VMEM((rows, D), F32),
            pltpu.VMEM((4, tall, D), BF),
            pltpu.VMEM((A_RING, rows, D), BF),
            pltpu.VMEM((rows, D), BF),
            pltpu.VMEM((rows, D), F32),
            pltpu.VMEM((tall, D), F32),
            pltpu.VMEM((tall, D), F32),
            pltpu.VMEM((tall, D), F32),
            pltpu.VMEM((tall, tall), F32),
            pltpu.VMEM((8, tall), F32),
            pltpu.VMEM((tall, LANES), F32),
            pltpu.VMEM((tall // 128, 8, 2 * LANES), F32),
            pltpu.VMEM((rows, D), BF),
            pltpu.VMEM((frames, D), BF),
            pltpu.VMEM((frames, D), F32),
            dma((6,)),
            dma((W_RING,)),
            dma((A_RING,)),
            dma((3,)),
        ],
        compiler_params=pltpu.CompilerParams(collective_id=1, has_side_effects=True, vmem_limit_bytes=61 << 20),
        name="backward",
    )(weights, vectors, segments, ein, din, ecot, dcot, early, *kept)


def attention_plan(prefix, width):
    return [
        (prefix + "wq", width, width),
        (prefix + "bq", width, 0),
        (prefix + "wk", width, width),
        (prefix + "wv", width, width),
        (prefix + "bv", width, 0),
        (prefix + "wo", width, width),
        (prefix + "bo", width, 0),
    ]


def feed_plan(width, hidden):
    return [
        ("fc1_weight", width, hidden),
        ("fc1_bias", hidden, 0),
        ("fc2_weight", hidden, width),
        ("fc2_bias", width, 0),
    ]


def encoder_layout(width, hidden):
    return (
        [("ln1_gain", width, 0), ("ln1_bias", width, 0)]
        + attention_plan("att_", width)
        + [("ln2_gain", width, 0), ("ln2_bias", width, 0)]
        + feed_plan(width, hidden)
    )


def decoder_layout(width, hidden):
    return (
        [("ln1_gain", width, 0), ("ln1_bias", width, 0)]
        + attention_plan("self_", width)
        + [("ln2_gain", width, 0), ("ln2_bias", width, 0)]
        + attention_plan("cross_", width)
        + [("ln3_gain", width, 0), ("ln3_bias", width, 0)]
        + feed_plan(width, hidden)
    )


def unpack(flat, layout):
    params = {}
    offset = 0
    for name, rows, cols in layout:
        count = rows * cols if cols > 0 else rows
        piece = flat[offset : offset + count]
        params[name] = piece.reshape(rows, cols) if cols > 0 else piece
        offset = offset + count
    return params


def pack(grads, layout):
    return jnp.concatenate([grads[name].reshape(-1) for name, rows, cols in layout])


def dot_plain(left, right):
    return jnp.dot(left, right, preferred_element_type=jnp.float32)


def dot_left(left, right):
    return lax.dot_general(
        left, right, (((0,), (0,)), ((), ())), preferred_element_type=jnp.float32
    )


def dot_right(left, right):
    return lax.dot_general(
        left, right, (((1,), (1,)), ((), ())), preferred_element_type=jnp.float32
    )


def layer_norm(values, gain, shift):
    centred = values - jnp.mean(values, axis=-1, keepdims=True)
    spread = jnp.mean(centred * centred, axis=-1, keepdims=True)
    return centred * lax.rsqrt(spread + 1e-05) * gain + shift


def norm_forward(params, prefix, values):
    gain = params[prefix + "_gain"].astype(jnp.float32)
    shift = params[prefix + "_bias"].astype(jnp.float32)
    return layer_norm(values, gain, shift).astype(jnp.bfloat16)


def norm_backward(params, prefix, values, grad):
    gain = params[prefix + "_gain"].astype(jnp.float32)
    shift = params[prefix + "_bias"].astype(jnp.float32)
    unused, pullback = jax.vjp(layer_norm, values, gain, shift)
    value_grad, gain_grad, shift_grad = pullback(grad)
    return (value_grad, {prefix + "_gain": gain_grad, prefix + "_bias": shift_grad})


def block_rows(total):
    return total if total <= 1024 else 512


def attend_forward(queries, keys_low, values, allowed_fn):
    total, width = queries.shape
    heads = width // HEAD_DIM
    rows = block_rows(total)
    blocks = total // rows
    scale = HEAD_DIM ** (-0.5)
    query_heads = queries.reshape(blocks, rows, heads, HEAD_DIM)
    key_heads = keys_low.reshape(keys_low.shape[0], heads, HEAD_DIM)
    value_heads = values.reshape(values.shape[0], heads, HEAD_DIM)
    starts = jnp.arange(blocks, dtype=jnp.int32) * rows

    def one_block(inputs):
        block, start = inputs
        scores = (
            jnp.einsum("qhd,khd->hqk", block, key_heads, preferred_element_type=jnp.float32) * scale
        )
        if allowed_fn is not None:
            scores = jnp.where(allowed_fn(start, rows)[None], scores, -1000000000.0)
        peak = jnp.max(scores, axis=-1, keepdims=True)
        weights = jnp.exp(scores - peak)
        totals = jnp.sum(weights, axis=-1, keepdims=True)
        probs = (weights / totals).astype(jnp.bfloat16)
        mixed = jnp.einsum("hqk,khd->qhd", probs, value_heads, preferred_element_type=jnp.float32)
        return (mixed.reshape(rows, width).astype(jnp.bfloat16), (peak + jnp.log(totals))[..., 0])

    mixed, logsum = lax.map(one_block, (query_heads, starts))
    return (mixed.reshape(total, width), logsum)


def attend_backward(queries, keys_low, values, logsum, mixed_grad, allowed_fn):
    total, width = queries.shape
    heads = width // HEAD_DIM
    rows = block_rows(total)
    blocks = total // rows
    scale = HEAD_DIM ** (-0.5)
    query_heads = queries.reshape(blocks, rows, heads, HEAD_DIM)
    grad_heads = mixed_grad.reshape(blocks, rows, heads, HEAD_DIM)
    key_heads = keys_low.reshape(keys_low.shape[0], heads, HEAD_DIM)
    value_heads = values.reshape(values.shape[0], heads, HEAD_DIM)
    starts = jnp.arange(blocks, dtype=jnp.int32) * rows

    def one_block(carry, inputs):
        key_grad, value_grad = carry
        block, grad_block, block_sum, start = inputs
        scores = (
            jnp.einsum("qhd,khd->hqk", block, key_heads, preferred_element_type=jnp.float32) * scale
        )
        if allowed_fn is not None:
            scores = jnp.where(allowed_fn(start, rows)[None], scores, -1000000000.0)
        probs = jnp.exp(scores - block_sum[..., None])
        prob_grad = jnp.einsum(
            "qhd,khd->hqk", grad_block, value_heads, preferred_element_type=jnp.float32
        )
        value_grad = value_grad + jnp.einsum(
            "hqk,qhd->khd",
            probs.astype(jnp.bfloat16),
            grad_block,
            preferred_element_type=jnp.float32,
        )
        score_grad = probs * (prob_grad - jnp.sum(probs * prob_grad, axis=-1, keepdims=True))
        raw_grad = (score_grad * scale).astype(jnp.bfloat16)
        query_grad = jnp.einsum(
            "hqk,khd->qhd", raw_grad, key_heads, preferred_element_type=jnp.float32
        )
        key_grad = key_grad + jnp.einsum(
            "hqk,qhd->khd", raw_grad, block, preferred_element_type=jnp.float32
        )
        return ((key_grad, value_grad), query_grad.reshape(rows, width))

    zeros = jnp.zeros(key_heads.shape, jnp.float32)
    (key_grad, value_grad), query_grad = lax.scan(
        one_block, (zeros, zeros), (query_heads, grad_heads, logsum, starts)
    )
    return (
        query_grad.reshape(total, width),
        key_grad.reshape(keys_low.shape[0], width),
        value_grad.reshape(values.shape[0], width),
    )


def attention_forward(params, prefix, query_rows, key_rows, allowed_fn):
    queries = (dot_plain(query_rows, params[prefix + "wq"]) + params[prefix + "bq"]).astype(
        jnp.bfloat16
    )
    keys_low = dot_plain(key_rows, params[prefix + "wk"]).astype(jnp.bfloat16)
    values = (dot_plain(key_rows, params[prefix + "wv"]) + params[prefix + "bv"]).astype(
        jnp.bfloat16
    )
    mixed, logsum = attend_forward(queries, keys_low, values, allowed_fn)
    output = dot_plain(mixed, params[prefix + "wo"]) + params[prefix + "bo"]
    return (output, (queries, keys_low, values, mixed, logsum))


def attention_backward(params, prefix, query_rows, key_rows, kept, out_grad, allowed_fn):
    queries, keys_low, values, mixed, logsum = kept
    out_round = out_grad.astype(jnp.bfloat16)
    mixed_grad = dot_right(out_round, params[prefix + "wo"]).astype(jnp.bfloat16)
    query_grad, key_grad, value_grad = attend_backward(
        queries, keys_low, values, logsum, mixed_grad, allowed_fn
    )
    query_round = query_grad.astype(jnp.bfloat16)
    key_round = key_grad.astype(jnp.bfloat16)
    value_round = value_grad.astype(jnp.bfloat16)
    grads = {
        prefix + "wq": dot_left(query_rows, query_round),
        prefix + "bq": jnp.sum(query_grad, axis=0),
        prefix + "wk": dot_left(key_rows, key_round),
        prefix + "wv": dot_left(key_rows, value_round),
        prefix + "bv": jnp.sum(value_grad, axis=0),
        prefix + "wo": dot_left(mixed, out_round),
        prefix + "bo": jnp.sum(out_grad, axis=0),
    }
    query_side = dot_right(query_round, params[prefix + "wq"])
    key_side = dot_right(key_round, params[prefix + "wk"]) + dot_right(
        value_round, params[prefix + "wv"]
    )
    return (grads, query_side, key_side)


def feed_forward(params, normed):
    pre = dot_plain(normed, params["fc1_weight"]) + params["fc1_bias"]
    activated = jax.nn.gelu(pre, approximate=False).astype(jnp.bfloat16)
    return (dot_plain(activated, params["fc2_weight"]) + params["fc2_bias"], (pre, activated))


def feed_backward(params, normed, kept, out_grad):
    pre, activated = kept
    out_round = out_grad.astype(jnp.bfloat16)
    act_grad = dot_right(out_round, params["fc2_weight"])
    unused, gelu_back = jax.vjp(partial(jax.nn.gelu, approximate=False), pre)
    pre_grad = gelu_back(act_grad)[0]
    pre_round = pre_grad.astype(jnp.bfloat16)
    grads = {
        "fc1_weight": dot_left(normed, pre_round),
        "fc1_bias": jnp.sum(pre_grad, axis=0),
        "fc2_weight": dot_left(activated, out_round),
        "fc2_bias": jnp.sum(out_grad, axis=0),
    }
    return (grads, dot_right(pre_round, params["fc1_weight"]))


def encoder_forward(params, frames):
    normed = norm_forward(params, "ln1", frames)
    attended, attend_kept = attention_forward(params, "att_", normed, normed, None)
    after = frames + attended
    normed_two = norm_forward(params, "ln2", after)
    fed, feed_kept = feed_forward(params, normed_two)
    return (after + fed, (normed, attend_kept, after, normed_two, feed_kept))


def encoder_backward(params, frames, kept, out_grad):
    normed, attend_kept, after, normed_two, feed_kept = kept
    grads, normed_grad = feed_backward(params, normed_two, feed_kept, out_grad)
    part, norm_grads = norm_backward(params, "ln2", after, normed_grad)
    grads.update(norm_grads)
    after_grad = out_grad + part
    attend_grads, query_side, key_side = attention_backward(
        params, "att_", normed, normed, attend_kept, after_grad, None
    )
    grads.update(attend_grads)
    part, norm_grads = norm_backward(params, "ln1", frames, query_side + key_side)
    grads.update(norm_grads)
    return (grads, after_grad + part)


def decoder_forward(params, tokens, memory_low, allowed_fn):
    normed = norm_forward(params, "ln1", tokens)
    attended, self_kept = attention_forward(params, "self_", normed, normed, allowed_fn)
    after = tokens + attended
    normed_two = norm_forward(params, "ln2", after)
    crossed, cross_kept = attention_forward(params, "cross_", normed_two, memory_low, None)
    after_two = after + crossed
    normed_three = norm_forward(params, "ln3", after_two)
    fed, feed_kept = feed_forward(params, normed_three)
    return (
        after_two + fed,
        (normed, self_kept, after, normed_two, cross_kept, after_two, normed_three, feed_kept),
    )


def decoder_backward(params, tokens, memory_low, kept, out_grad, allowed_fn):
    normed, self_kept, after, normed_two, cross_kept, after_two, normed_three, feed_kept = kept
    grads, normed_grad = feed_backward(params, normed_three, feed_kept, out_grad)
    part, norm_grads = norm_backward(params, "ln3", after_two, normed_grad)
    grads.update(norm_grads)
    after_two_grad = out_grad + part
    cross_grads, query_side, memory_grad = attention_backward(
        params, "cross_", normed_two, memory_low, cross_kept, after_two_grad, None
    )
    grads.update(cross_grads)
    part, norm_grads = norm_backward(params, "ln2", after, query_side)
    grads.update(norm_grads)
    after_grad = after_two_grad + part
    self_grads, query_side, key_side = attention_backward(
        params, "self_", normed, normed, self_kept, after_grad, allowed_fn
    )
    grads.update(self_grads)
    part, norm_grads = norm_backward(params, "ln1", tokens, query_side + key_side)
    grads.update(norm_grads)
    return (grads, after_grad + part, memory_grad)


def adamw(master, first, second, grad, factor, correction):
    clipped = grad * factor
    moment = 0.5 * first + 0.5 * clipped
    variance = 0.5 * second + 0.5 * clipped * clipped
    update = moment / correction / (jnp.sqrt(variance / correction) + 1e-08) + 0.01 * master
    weights = master - 0.02 * update
    return (weights, moment, variance, weights.astype(jnp.bfloat16))


def shards_native(
    encoder_input,
    decoder_input,
    segments,
    encoder_cotangent,
    decoder_cotangent,
    encoder_master,
    encoder_first,
    encoder_second,
    decoder_master,
    decoder_first,
    decoder_second,
    step_count,
):
    encoder_plan = encoder_layout(D, FF)
    decoder_plan = decoder_layout(D, FF)
    encoder_params = unpack(
        lax.all_gather(encoder_master.astype(jnp.bfloat16), ("wide", "narrow"), axis=0, tiled=True),
        encoder_plan,
    )
    frames = encoder_input[0].astype(jnp.float32)
    memory, encoder_kept = encoder_forward(encoder_params, frames)
    memory_low = memory.astype(jnp.bfloat16)
    decoder_params = unpack(
        lax.all_gather(decoder_master.astype(jnp.bfloat16), ("wide", "narrow"), axis=0, tiled=True),
        decoder_plan,
    )
    tokens = decoder_input[0].astype(jnp.float32)
    segment_row = segments[0]
    length = segment_row.shape[0]

    def allowed_fn(start, count):
        places = start + jnp.arange(count, dtype=jnp.int32)
        row_segments = lax.dynamic_slice_in_dim(segment_row, start, count)
        columns = jnp.arange(length, dtype=jnp.int32)
        return (row_segments[:, None] == segment_row[None, :]) & (
            columns[None, :] <= places[:, None]
        )

    decoded, decoder_kept = decoder_forward(decoder_params, tokens, memory_low, allowed_fn)
    decoder_again = unpack(
        lax.all_gather(decoder_master.astype(jnp.bfloat16), ("wide", "narrow"), axis=0, tiled=True),
        decoder_plan,
    )
    decoder_grads, token_grad, memory_grad = decoder_backward(
        decoder_again,
        tokens,
        memory_low,
        decoder_kept,
        decoder_cotangent[0].astype(jnp.float32),
        allowed_fn,
    )
    decoder_total = pack(decoder_grads, decoder_plan)
    decoder_owned = lax.psum_scatter(
        decoder_total, ("wide", "narrow"), scatter_dimension=0, tiled=True
    )
    encoder_again = unpack(
        lax.all_gather(encoder_master.astype(jnp.bfloat16), ("wide", "narrow"), axis=0, tiled=True),
        encoder_plan,
    )
    memory_total = encoder_cotangent[0].astype(jnp.float32) + memory_grad
    encoder_grads, frame_grad = encoder_backward(encoder_again, frames, encoder_kept, memory_total)
    encoder_total = pack(encoder_grads, encoder_plan)
    encoder_owned = lax.psum_scatter(
        encoder_total, ("wide", "narrow"), scatter_dimension=0, tiled=True
    )
    local_squares = jnp.sum(encoder_owned * encoder_owned) + jnp.sum(decoder_owned * decoder_owned)
    gradient_norm = jnp.sqrt(lax.psum(local_squares, ("wide", "narrow")))
    factor = 1.0 / jnp.maximum(gradient_norm, 1.0)
    correction = 1.0 - jnp.power(0.5, step_count.astype(jnp.float32))
    encoder_new = adamw(
        encoder_master, encoder_first, encoder_second, encoder_owned, factor, correction
    )
    decoder_new = adamw(
        decoder_master, decoder_first, decoder_second, decoder_owned, factor, correction
    )
    return (
        memory_low[None],
        decoded.astype(jnp.bfloat16)[None],
        frame_grad[None],
        token_grad[None],
        gradient_norm,
        encoder_new[0],
        encoder_new[1],
        encoder_new[2],
        encoder_new[3],
        decoder_new[0],
        decoder_new[1],
        decoder_new[2],
        decoder_new[3],
    )


def shards(
    encoder_input,
    decoder_input,
    segments,
    encoder_cotangent,
    decoder_cotangent,
    encoder_master,
    encoder_first,
    encoder_second,
    decoder_master,
    decoder_first,
    decoder_second,
    step_count,
):
    n = 32
    weights, vectors, *kept, early = forward_pass(
        encoder_master, decoder_master, encoder_input[0], decoder_input[0], segments, decoder_cotangent[0], n
    )
    encoder_flat, decoder_flat, norm, frame_grad, token_grad, decoded = backward_pass(
        weights, vectors, kept, early, encoder_input[0], decoder_input[0], encoder_cotangent[0], decoder_cotangent[0], segments, n
    )
    gradient_norm = norm[0, 0]
    factor = 1.0 / jnp.maximum(gradient_norm, 1.0)
    correction = 1.0 - jnp.power(0.5, step_count.astype(jnp.float32))
    encoder_owned = encoder_flat.reshape(-1)[: encoder_master.shape[0]]
    decoder_owned = decoder_flat.reshape(-1)[: decoder_master.shape[0]]
    encoder_new = adamw(encoder_master, encoder_first, encoder_second, encoder_owned, factor, correction)
    decoder_new = adamw(decoder_master, decoder_first, decoder_second, decoder_owned, factor, correction)
    return (
        kept[10][None],
        decoded[None],
        frame_grad[None],
        token_grad[None],
        gradient_norm,
        *encoder_new,
        *decoder_new,
    )


def solution(mesh):
    placed = (
        P(("wide", "narrow"), None, None),
        P(("wide", "narrow"), None, None),
        P(("wide", "narrow"), None),
        P(("wide", "narrow"), None, None),
        P(("wide", "narrow"), None, None),
        P(("wide", "narrow")),
        P(("wide", "narrow")),
        P(("wide", "narrow")),
        P(("wide", "narrow")),
        P(("wide", "narrow")),
        P(("wide", "narrow")),
        P(),
    )
    return jax.shard_map(
        shards if tuple(mesh.shape.values()) == (8, 4) else shards_native,
        mesh=mesh,
        in_specs=placed,
        out_specs=(
            P(("wide", "narrow"), None, None),
            P(("wide", "narrow"), None, None),
            P(("wide", "narrow"), None, None),
            P(("wide", "narrow"), None, None),
            P(),
            P(("wide", "narrow")),
            P(("wide", "narrow")),
            P(("wide", "narrow")),
            P(("wide", "narrow")),
            P(("wide", "narrow")),
            P(("wide", "narrow")),
            P(("wide", "narrow")),
            P(("wide", "narrow")),
        ),
        check_vma=False,
    )
```

```python
from functools import partial

import jax
import jax.numpy as jnp
from jax import lax
from jax.experimental import pallas as pl
from jax.experimental.pallas import tpu as pltpu
from jax.sharding import PartitionSpec as P

D = 768
HEAD_DIM = 64
FF = 3072
MESH = pl.DeviceIdType.MESH
BF = jnp.bfloat16
F32 = jnp.float32

N_MAT = 28
N_PAIR = 14
UNIT = 48
LANES = 128
UROWS = UNIT * D // LANES
BIG = 4 * UROWS
FRONT = BIG + 8
BACK = BIG + 8
N_VEC = 29
F_AT = (1, 2, 4, 5)
B_AT = (1, 3, 5, 8)
AHEAD = 3


class Block:
    def __init__(self, small, gaps, fc1, vectors, first_mat, small_mats, total):
        self.small = small
        self.gaps = gaps
        self.fc1 = fc1
        self.vectors = vectors
        self.first_mat = first_mat
        self.small_mats = small_mats
        self.total = total


ENC = Block(
    small=8,
    gaps=((0, 2), (1, 1), (3, 1), (4, 3072 + 7)),
    fc1=3079,
    vectors=[0, 1, 770, 2307, 3076, 3077, 3078, 6151, 6152, 6153, 6154, 9227],
    first_mat=0,
    small_mats=4,
    total=9228,
)
DEC = Block(
    small=12,
    gaps=((0, 2), (1, 1), (3, 1), (4, 3), (5, 1), (7, 1), (8, 3072 + 7)),
    fc1=6156,
    vectors=[0, 1, 770, 2307, 3076, 3077, 3078, 3847, 5384, 6153, 6154, 6155, 9228, 9229, 9230, 9231, 12304],
    first_mat=12,
    small_mats=8,
    total=12305,
)
BLOCKS = (ENC, DEC)


def sizes(block, n):
    shard = block.total * D // n
    rows = -(-shard // 1024) * 8
    top = (shard + LANES - 1) // LANES
    return shard, rows, (top + UROWS) // UROWS + 1, (top + BIG) // BIG + 1


def small_row(block, m):
    row = m * D
    for at, gap in block.gaps:
        row = row + jnp.where(m >= at, gap, 0) if at > 0 else row + gap
    return row


def mat_of(block, m):
    return block.first_mat + m + jnp.where(m >= block.small_mats, 4, 0)


def static_unit_rows(block):
    out = []
    for m in range(block.small):
        row = m * D + sum(gap for at, gap in block.gaps if m >= at)
        out.append((block.first_mat + m + (4 if m >= block.small_mats else 0), row))
    return out


def whoami():
    wide, narrow = lax.axis_index("wide"), lax.axis_index("narrow")
    return wide, narrow, wide // 2, wide % 2, narrow // 2, narrow % 2


def device(z, x, y, c):
    return (z * 2 + x, y * 2 + c)


def flat_device(d):
    return (d // 4, d % 4)


def greet(me, n):
    bar = pltpu.get_barrier_semaphore()

    def signal(i, carry):
        pl.semaphore_signal(bar, inc=1, device_id=flat_device((me + i) % n), device_id_type=MESH)
        return carry

    lax.fori_loop(1, n, signal, 0)


def await_all(n):
    pl.semaphore_wait(pltpu.get_barrier_semaphore(), n - 1)


def each_small(block, n, me, slots, body, least=0, most=99):
    shard = sizes(block, n)[0]
    low = me * shard
    low_row = low // LANES
    first = 0
    for _, row in static_unit_rows(block):
        first = first + jnp.minimum(jnp.maximum(low - row * D, 0) // (UROWS * LANES), 16)

    def step(j, carry):
        g = first + j
        m, u = g // 16, g % 16
        start = small_row(block, m) * 6 + u * UROWS
        pos = start - low_row

        @pl.when((g < 16 * min(block.small, most)) & (g >= 16 * least) & (start * LANES < low + shard))
        def _():
            body((pos + UROWS) // UROWS, mat_of(block, m), u, pos, start * LANES)

        return carry

    lax.fori_loop(0, slots, step, 0)


def each_big(block, n, me, slots, body):
    shard = sizes(block, n)[0]
    low = me * shard
    low_row = low // LANES
    first = jnp.minimum(jnp.maximum(low - block.fc1 * D, 0) // (BIG * LANES), 16)

    def step(j, carry):
        u = first + j
        start = block.fc1 * 6 + u * BIG
        pos = start - low_row

        @pl.when((u < 16) & (start * LANES < low + shard) & (start * LANES + BIG * LANES > low))
        def _():
            body((pos + BIG) // BIG, u, pos, start * LANES)

        return carry

    lax.fori_loop(0, slots, step, 0)


def each_vector(block, n, me, first_vec, body):
    shard = sizes(block, n)[0]
    low = me * shard
    low_row = low // LANES
    for i, row in enumerate(block.vectors):
        @pl.when((row * D < low + shard) & (row * D + D > low))
        def _(i=i, row=row):
            body(first_vec + i, row * 6 - low_row, row * D)


def peers(axis, at):
    if axis == "z":
        return [dict(at, z=(at["z"] + k) % 4) for k in (1, 2, 3)]
    return [dict(at, **{axis: 1 - at[axis]})]


def first_peer(at):
    x, y, c = at["x"], at["y"], at["c"]
    return device(at["z"], x + (1 - c) * (1 - 2 * x), y + c * (1 - 2 * y), c)


def second_peer(at):
    x, y, c = at["x"], at["y"], at["c"]
    return device(at["z"], x + c * (1 - 2 * x), y + (1 - c) * (1 - 2 * y), c)


def dev(at):
    return device(at["z"], at["x"], at["y"], at["c"])


def gather_kernel(
    n, on_start, on_vectors, on_pair, on_last, xe_ref, xd_ref, w_ref, v_ref,
    re_ref, rd_ref, se_ref, sd_ref, be_ref, bd_ref, sv_ref, land, landv, own, ownv,
    s_small, s_big, s_vec, r_unit, r_vec, s_zxy, r_zxy, s_core, r_core, s_own, v_send, v_recv,
):
    wide, narrow, z, x, y, c = whoami()
    me = wide * 4 + narrow
    chip = me // 2
    at = dict(z=z, x=x, y=y, c=c)
    greet(me, n)
    lanes = lax.broadcasted_iota(jnp.int32, (1, LANES), 1)
    fields = {
        ENC: (xe_ref, re_ref, se_ref, be_ref, 0, 0, 0),
        DEC: (xd_ref, rd_ref, sd_ref, bd_ref, sizes(ENC, n)[2], sizes(ENC, n)[3], len(ENC.vectors)),
    }

    def prepare(block):
        x_ref, r_ref = fields[block][:2]
        shard, rows, _, _ = sizes(block, n)
        step = 8 * max(k for k in range(1, 40) if (rows // 8) % k == 0)

        def turn(i, carry):
            at_row = pl.multiple_of(i * step, 8)
            r_ref[pl.ds(FRONT + at_row, step), :] = pltpu.roll(
                x_ref[pl.ds(at_row, step), :], (me * shard) % LANES, 1
            )
            return carry

        lax.fori_loop(0, rows // step, turn, 0)

    def load_rows(block, row, count, stride=None):
        r_ref = fields[block][1]
        at_row = FRONT + row
        if stride is None:
            here, before = r_ref[pl.ds(at_row, count), :], r_ref[pl.ds(at_row - 1, count), :]
        else:
            here = r_ref[pl.ds(at_row, count, stride=stride), :]
            before = r_ref[pl.ds(at_row - 1, count, stride=stride), :]
        return jnp.where(lanes >= (me * sizes(block, n)[0]) % LANES, here, before)

    def send(src, dst, send_sem, recv_sem, target):
        @pl.when(target == me)
        def _():
            pltpu.make_async_copy(src, dst, send_sem).start()

        @pl.when(target != me)
        def _():
            pltpu.make_async_remote_copy(
                src, dst, send_sem, recv_sem, device_id=flat_device(target), device_id_type=MESH
            ).start()

    def which_of(block, start):
        return jnp.where(start // sizes(block, n)[0] == me, 0, 1)

    def small_units(block, least, most):
        s_ref, small0 = fields[block][2], fields[block][4]

        def body(slot, mat, u, pos, start):
            for k in range(6):
                s_ref[slot, :, k * LANES : (k + 1) * LANES] = load_rows(block, pos + k, UNIT, 6).astype(BF)
            which = which_of(block, start)
            send(
                s_ref.at[slot], land.at[which, mat // 2], s_small.at[small0 + slot], r_unit.at[which, mat // 2],
                u * 2 + mat % 2,
            )

        each_small(block, n, me, sizes(block, n)[2], body, least, most)

    def big_units(block):
        b_ref, big0 = fields[block][3], fields[block][5]
        pair = (block.first_mat + block.small_mats) // 2

        def body(slot, u, pos, start):
            for q in range(4):
                for k in range(6):
                    b_ref[slot, q % 2, q // 2, :, k * LANES : (k + 1) * LANES] = load_rows(
                        block, pos + 6 * q + k, UNIT, 24
                    ).astype(BF)
            which = which_of(block, start)
            for core in range(2):
                send(
                    b_ref.at[slot, core], land.at[which, pl.ds(pair, 2)], s_big.at[big0 + slot, core],
                    r_unit.at[which, pair], u * 2 + core,
                )

        each_big(block, n, me, sizes(block, n)[3], body)

    def vector_units(block):
        def body(v, pos, start):
            sv_ref[v] = load_rows(block, pos, 8).astype(BF).astype(F32)
            which = which_of(block, start)
            send(sv_ref.at[v], landv.at[which], s_vec.at[v], r_vec.at[which], v)

        each_vector(block, n, me, fields[block][6], body)

    def pair_units(pair):
        block = ENC if pair < 6 else DEC
        local = pair - block.first_mat // 2
        half = block.small_mats // 2
        if local == half:
            big_units(block)
        elif local != half + 1:
            first = 2 * local - (4 if local > half else 0)
            small_units(block, first, first + 2)

    prepare(ENC)
    await_all(n)
    pair_units(0)
    vector_units(ENC)
    prepare(DEC)
    vector_units(DEC)
    for pair in range(1, AHEAD):
        pair_units(pair)

    def of_self(first, last, which):
        return jnp.where(which == 0, first, last) == me

    def arrive_unit(first, last, src, dst, local_sem, recv):
        for which, holder in ((0, first), (1, last)):
            needed = True if which == 0 else (first != last)

            @pl.when(needed & (holder == me))
            def _(which=which):
                pltpu.make_async_copy(src(which), dst(which), local_sem).wait()

            @pl.when(needed & (holder != me))
            def _(which=which):
                pltpu.make_async_copy(src(which), dst(which), recv(which)).wait()

    def vec_of(v):
        n_enc = len(ENC.vectors)
        rows = ENC.vectors + DEC.vectors
        start = 0
        before = 0
        for i, row in enumerate(rows):
            start = start + jnp.where(v >= i, row - before, 0)
            before = row
        return start * D, jnp.where(v < n_enc, sizes(ENC, n)[0], sizes(DEC, n)[0])

    @pl.when(me < N_VEC)
    def _():
        start, shard = vec_of(me)
        first, last = start // shard, (start + D - 1) // shard
        arrive_unit(
            first, last, lambda w: sv_ref.at[0], lambda w: landv.at[w], s_vec.at[me], lambda w: r_vec.at[w]
        )
        at_elem = lax.broadcasted_iota(jnp.int32, (8, LANES), 0) * LANES + lax.broadcasted_iota(jnp.int32, (8, LANES), 1)
        ownv[...] = jnp.where(at_elem < (first + 1) * shard - start, landv[0], landv[1])

    @pl.when(me >= N_VEC)
    def _():
        ownv[...] = jnp.zeros_like(ownv)

    pltpu.sync_copy(ownv, v_ref.at[z, x, y, c])
    vorder = ("z", "x", "y", "c")

    def vview(done):
        have = set(vorder[:done])
        return tuple(slice(None) if a in have else at[a] for a in "zxyc")

    def vcopies(phase):
        axis = vorder[phase]
        out = []
        for k, p in enumerate(peers(axis, at)):
            ref = v_ref.at[vview(phase)]
            slot = phase if axis == "z" else phase + 2
            out.append(
                pltpu.make_async_remote_copy(
                    ref, ref, v_send.at[slot + k], v_recv.at[slot + k], device_id=dev(p), device_id_type=MESH
                )
            )
        return out

    row_i = lax.broadcasted_iota(jnp.int32, (UNIT, D), 0)
    col_i = lax.broadcasted_iota(jnp.int32, (UNIT, D), 1)

    def merge(pair):
        block = ENC if pair < 6 else DEC
        shard = sizes(block, n)[0]
        local = pair - block.first_mat // 2
        half = block.small_mats // 2
        if half <= local < half + 2:
            start = (block.fc1 * 6 + chip * BIG) * LANES
            elem = row_i * FF + (2 * (local - half) + c) * D + col_i
            length = BIG * LANES
        else:
            small = 2 * local - (4 if local >= half + 2 else 0) + c
            start = (small_row(block, small) * 6 + chip * UROWS) * LANES
            elem = row_i * D + col_i
            length = UROWS * LANES
        first, last = start // shard, (start + length - 1) // shard
        if half <= local < half + 2:
            if local == half:
                low_row = me * shard // LANES
                slot = (start // LANES - low_row + BIG) // BIG + (0 if block is ENC else sizes(ENC, n)[3])
                slot = jnp.minimum(jnp.maximum(slot, 0), sizes(ENC, n)[3] + sizes(DEC, n)[3] - 1)
                arrive_unit(
                    first, last, lambda w: land.at[w, pl.ds(pair, 2)], lambda w: land.at[w, pl.ds(pair, 2)],
                    s_big.at[slot, c], lambda w: r_unit.at[w, pair],
                )
        else:
            low_row = me * shard // LANES
            slot = (start // LANES - low_row + UROWS) // UROWS + (0 if block is ENC else sizes(ENC, n)[2])
            slot = jnp.minimum(jnp.maximum(slot, 0), sizes(ENC, n)[2] + sizes(DEC, n)[2] - 1)
            arrive_unit(
                first, last, lambda w: land.at[w, pair], lambda w: land.at[w, pair],
                s_small.at[slot], lambda w: r_unit.at[w, pair],
            )
        own[pair] = jnp.where(elem < (first + 1) * shard - start, land[0, pair], land[1, pair])

    def own_place(pair):
        return w_ref.at[pair, c, z, x, y]

    def remote(src, dst, pair, k, target):
        return pltpu.make_async_remote_copy(
            src, dst, s_zxy.at[pair, k], r_zxy.at[pair, k], device_id=target, device_id_type=MESH
        )

    def copies(pair, phase):
        if phase == 0:
            return [
                remote(own.at[pair], own_place(pair), pair, 2 + k, device((z + k) % 4, x, y, c)) for k in (1, 2, 3)
            ]
        if phase == 1:
            ref = w_ref.at[pair, c, :, x, y]
            return [remote(ref, ref, pair, 0, first_peer(at))]
        if phase == 2:
            ref = w_ref.at[pair, c, :, :, y]
            return [remote(ref, ref, pair, 1, second_peer(at))]
        ref = w_ref.at[pair, c]
        return [remote(ref, ref, pair, 2, device(z, x, y, 1 - c))]

    def begin(pair, phase):
        if phase != 2:
            for cp in copies(pair, phase):
                cp.start()
            return

        @pl.when(c == 0)
        def _():
            copies(pair, 2)[0].start()

        @pl.when(c == 1)
        def _():
            ref = w_ref.at[pair, c, :, x]
            remote(ref, ref, pair, 1, second_peer(at)).start()

    for t in range(N_PAIR + F_AT[3]):
        if t < N_PAIR:
            merge(t)
            pltpu.make_async_copy(own.at[t], own_place(t), s_own.at[t]).start()
            begin(t, 0)
        for phase in (1, 2, 3):
            pair = t - F_AT[phase - 1]
            if 0 <= pair < N_PAIR:
                if phase == 1:
                    pltpu.make_async_copy(own.at[pair], own_place(pair), s_own.at[pair]).wait()
                for cp in copies(pair, phase - 1):
                    cp.wait_recv()
                begin(pair, phase)
        if t + AHEAD < N_PAIR:
            pair_units(t + AHEAD)
        if t == 1:
            on_start()
        if t < 5:
            if t > 0:
                for cp in vcopies(t - 1):
                    cp.wait_recv()
            if t < 4:
                for cp in vcopies(t):
                    cp.start()
            else:
                on_vectors()
        pair = t - F_AT[3]
        if pair == N_PAIR - 1:
            on_last()
        if 0 <= pair < N_PAIR:
            for cp in copies(pair, 3):
                cp.wait_recv()
            on_pair(pair)

    for phase in range(4):
        for cp in vcopies(phase):
            cp.wait_send()
    for pair in range(N_PAIR):
        for phase in range(4):
            for cp in copies(pair, phase):
                cp.wait_send()
    for b, (block, s_ref, b_ref) in enumerate(((ENC, se_ref, be_ref), (DEC, sd_ref, bd_ref))):
        shard, rows, n_small, n_big = sizes(block, n)
        small0 = 0 if b == 0 else sizes(ENC, n)[2]
        big0 = 0 if b == 0 else sizes(ENC, n)[3]

        def small_wait(slot, mat, u, pos, start, s_ref=s_ref, small0=small0):
            @pl.when(u * 2 + mat % 2 != me)
            def _():
                pltpu.make_async_copy(s_ref.at[slot], s_ref.at[slot], s_small.at[small0 + slot]).wait()

        def big_wait(slot, u, pos, start, b_ref=b_ref, big0=big0):
            for core in range(2):
                @pl.when(u * 2 + core != me)
                def _(core=core):
                    pltpu.make_async_copy(
                        b_ref.at[slot, core], b_ref.at[slot, core], s_big.at[big0 + slot, core]
                    ).wait()

        def vec_wait(v, pos, start):
            @pl.when(me != v)
            def _():
                pltpu.make_async_copy(sv_ref.at[v], sv_ref.at[v], s_vec.at[v]).wait()

        each_vector(block, n, me, 0 if b == 0 else len(ENC.vectors), vec_wait)
        each_small(block, n, me, n_small, small_wait)
        each_big(block, n, me, n_big, big_wait)


def rows_of(flat, rows):
    return jnp.pad(flat, (0, rows * LANES - flat.shape[0])).reshape(rows, LANES)


SCALE = HEAD_DIM ** (-0.5)
FORBID = -1000000000.0
ROOT_HALF = 0.7071067811865476
PDF = 0.3989422804014327


def mm(a, b):
    return jnp.dot(a, b, preferred_element_type=F32)


def mm_nt(a, b):
    return lax.dot_general(a, b, (((1,), (1,)), ((), ())), preferred_element_type=F32)


def mm_tn(a, b):
    return lax.dot_general(a, b, (((0,), (0,)), ((), ())), preferred_element_type=F32)


def col_blocks(body, width=256):
    def step(j, carry):
        body(pl.ds(pl.multiple_of(j * width, width), width))
        return carry

    lax.fori_loop(0, D // width, step, 0)


def row_blocks(rows, body, height=64):
    def step(i, carry):
        body(pl.ds(pl.multiple_of(i * height, height), height))
        return carry

    lax.fori_loop(0, rows // height, step, 0)


def linear(x_ref, w_ref, rows, out_ref, bias=None):
    x = x_ref[0:rows, :]

    def body(cols):
        y = mm(x, w_ref[:, cols])
        if bias is not None:
            y = y + bias[:, cols]
        out_ref[0:rows, cols] = y.astype(out_ref.dtype)

    col_blocks(body)


def norm_rows(x):
    centred = x - jnp.mean(x, axis=1, keepdims=True)
    spread = jnp.mean(centred * centred, axis=1, keepdims=True)
    root = lax.rsqrt(spread + 1e-05)
    return centred * root, root


def norm_forward_ref(x_ref, gain, shift, rows, out_ref):
    def body(r):
        hat, _ = norm_rows(x_ref[r, :].astype(F32))
        out_ref[r, :] = (hat * gain[...] + shift[...]).astype(BF)

    row_blocks(rows, body)


def attend_tiles(rows, keys, causal):
    return [(start, min(start + 128, keys) if causal else keys) for start in range(0, rows, 128)]


def both_heads(x):
    lane = lax.broadcasted_iota(jnp.int32, (1, LANES), 1)
    zero = jnp.zeros_like(x)
    return jnp.concatenate([jnp.where(lane < HEAD_DIM, x, zero), jnp.where(lane < HEAD_DIM, zero, x)], axis=0)


def scores_of(k, q2, mask_ref, start, reach):
    scores = mm_nt(k, q2)
    if mask_ref is not None:
        mask = mask_ref[0:reach, start : start + LANES]
        scores = jnp.where(jnp.concatenate([mask, mask], axis=1) > 0, scores, FORBID)
    return scores


def attention_forward_ref(q_ref, k_ref, v_ref, mask_ref, rows, keys, mixed_ref, lse_ref):
    def pair_of_heads(i, carry):
        cols = pl.ds(pl.multiple_of(i * LANES, LANES), LANES)
        v_turned = jnp.transpose(v_ref[0:keys, cols])
        for tile, (start, reach) in enumerate(attend_tiles(rows, keys, mask_ref is not None)):
            r = slice(start, start + LANES)
            q2 = both_heads(q_ref[r, cols] * jnp.asarray(SCALE, BF))
            scores = scores_of(k_ref[0:reach, cols], q2, mask_ref, start, reach)
            peak = jnp.max(scores, axis=0, keepdims=True)
            weights = jnp.exp(scores - peak)
            totals = jnp.sum(weights, axis=0, keepdims=True)
            probs = weights.astype(BF)
            share = 1.0 / totals
            mixed = jnp.concatenate(
                [
                    mm(v_turned[s * HEAD_DIM : (s + 1) * HEAD_DIM, 0:reach], probs[:, s * LANES : (s + 1) * LANES])
                    * share[:, s * LANES : (s + 1) * LANES]
                    for s in range(2)
                ],
                axis=0,
            )
            mixed_ref[r, cols] = jnp.transpose(mixed).astype(BF)
            lse_ref[tile, pl.ds(i, 1), :] = peak + jnp.log(totals)
        return carry

    lax.fori_loop(0, D // LANES, pair_of_heads, 0, unroll=1 if mask_ref is not None else 2)


def project_add(x_ref, mixed_ref, w_ref, bias, rows, out_ref):
    m = mixed_ref[0:rows, :]

    def body(cols):
        out_ref[0:rows, cols] = x_ref[0:rows, cols].astype(F32) + mm(m, w_ref[:, cols]) + bias[:, cols]

    col_blocks(body)


def gelu_block(n_ref, w_ref, bias, rows, block, act_ref, slope_ref):
    x = n_ref[0:rows, :]

    def body(cols):
        pre = mm(x, w_ref[:, cols]) + bias[:, cols]
        bell = 0.5 * (1.0 + lax.erf(pre * ROOT_HALF))
        act_ref[block, 0:rows, cols] = (pre * bell).astype(BF)
        slope_ref[block, 0:rows, cols] = (bell + pre * (PDF * jnp.exp(-0.5 * pre * pre))).astype(BF)

    col_blocks(body, 128)


def accumulate(a_ref, w_ref, rows, out_ref):
    a = a_ref[0:rows, :]

    def body(cols):
        out_ref[0:rows, cols] += mm(a, w_ref[:, cols])

    col_blocks(body)


def add_row(out_ref, x_ref, row_ref, r):
    out_ref[r, :] = x_ref[r, :] + row_ref[...]


def both(body):
    def step(k, carry):
        body(k)
        return carry

    lax.fori_loop(0, 2, step, 0)


N_SAVED = 28


def saved_shapes(rows, frames):
    tall = -(-rows // 128) * 128
    enc_lse, dec_lse = ((frames // 128, 8, 2 * LANES), F32), ((tall // 128, 8, 2 * LANES), F32)
    return (
        [((frames, D), BF)] * 5
        + [enc_lse, ((frames, D), F32), ((frames, D), BF), ((4, frames, D), BF), ((4, frames, D), BF), ((frames, D), BF)]
        + [((rows, D), BF)]
        + [((tall, D), BF)] * 4
        + [dec_lse, ((rows, D), F32), ((rows, D), BF)]
        + [((tall, D), BF), ((frames, D), BF), ((frames, D), BF), ((tall, D), BF), dec_lse]
        + [((rows, D), F32), ((rows, D), BF), ((4, rows, D), BF), ((4, rows, D), BF)]
    )


def make_mask(seg_ref, row_ref, col_ref, mask_ref):
    rows, tall = seg_ref.shape[1], mask_ref.shape[0]
    row_ref[...] = jnp.full(row_ref.shape, -1.0, F32)
    row_ref[0:1, 0:rows] = seg_ref[...].astype(F32)
    for i in range(tall // LANES):
        part = slice(i * LANES, (i + 1) * LANES)
        col_ref[part, :] = jnp.transpose(jnp.broadcast_to(row_ref[0:1, part], (LANES, LANES)))

    def body(r):
        key = lax.broadcasted_iota(jnp.int32, (64, tall), 0) + r.start
        query = lax.broadcasted_iota(jnp.int32, (64, tall), 1)
        allowed = (col_ref[r, 0:1] == row_ref[0:1, :]) & (key <= query)
        mask_ref[r, :] = jnp.where(allowed, 1.0, 0.0)

    row_blocks(tall, body)


def forward_kernel(n, rows, frames, *refs):
    xe_ref, xd_ref, ein_ref, din_ref, seg_ref, dcot_ref, w_ref, v_ref = refs[:8]
    outs, refs = refs[8 : 8 + N_SAVED], refs[8 + N_SAVED :]
    early_ref, refs = refs[0], refs[1:]
    comm, refs = refs[:24], refs[24:]
    bufs, refs = refs[:N_SAVED], refs[N_SAVED:]
    vv, wbuf, acc, mask_ref, seg_row, seg_col, s_save, s_w, cot, gown, gsum, s_g, r_g, s_early = refs
    _, _, z, x, y, c = whoami()
    (
        e_n1, e_q, e_k, e_v, e_mix, e_lse, e_after, e_n2, e_act, e_slope, e_out,
        d_n1, d_q, d_k, d_v, d_mix, d_lse, d_after, d_n2,
        c_q, c_k, c_v, c_mix, c_lse, d_after2, d_n3, d_act, d_slope,
    ) = bufs
    eacc = acc.at[0:frames]

    def vec(i):
        return vv.at[pl.ds(i, 1)]

    def save(*indices):
        for i in indices:
            pltpu.make_async_copy(bufs[i], outs[i], s_save.at[i]).start()

    def cot_copy():
        return pltpu.make_async_copy(dcot_ref, cot, s_early.at[0])

    def early_core(i):
        return pltpu.make_async_remote_copy(
            gown.at[i, 1 - c], gsum.at[i], s_g.at[i], r_g.at[i], device_id=device(z, x, y, 1 - c), device_id_type=MESH
        )

    def early_save(i):
        return pltpu.make_async_copy(gsum.at[i], early_ref.at[i], s_early.at[i])

    def early_grad(i):
        both(lambda k: weight_grad(d_act.at[2 - 2 * i + k], cot, rows, gown.at[i, k]))
        early_core(i).start()

    def early_sum(i):
        early_core(i).wait_recv()

        def body(j, carry):
            a, b = j // 2, j % 2
            for k in range(2):
                gsum[i, a, b, k] = (gsum[i, a, b, k].astype(F32) + gown[i, c, a, b, k].astype(F32)).astype(BF)
            return carry

        lax.fori_loop(0, 8, body, 0)
        early_save(i).start()

    def on_last():
        early_sum(0)

    def on_start():
        cot_copy().start()
        make_mask(seg_ref, seg_row, seg_col, mask_ref)
        for ref in (d_q, d_k, d_v, c_q):
            if ref.shape[0] > rows:
                ref[rows:, :] = jnp.zeros((ref.shape[0] - rows, D), BF)
        for ref in (e_lse, d_lse, c_lse):
            ref[...] = jnp.zeros_like(ref)

    def on_vectors():
        pltpu.sync_copy(v_ref, vv_tiles)
        for i in range(N_VEC):
            for k in range(6):
                vv[i : i + 1, k * LANES : (k + 1) * LANES] = vv_tiles[i // 8, i // 4 % 2, i // 2 % 2, i % 2, k : k + 1, :]

    def on_pair(pair):
        if pair == 12:
            early_grad(0)
            early_sum(1)
        if pair > 11:
            return
        cps = [pltpu.make_async_copy(w_ref.at[pair, k].reshape(D, D), wbuf.at[k], s_w.at[k]) for k in range(2)]
        for cp in cps:
            cp.start()
        if pair == 0:
            norm_forward_ref(ein_ref, vec(0), vec(1), frames, e_n1)
        if pair == 6:
            norm_forward_ref(din_ref, vec(12), vec(13), rows, d_n1)
        if pair == 11:
            cot_copy().wait()
            early_grad(1)
        for cp in cps:
            cp.wait()
        w0, w1 = wbuf.at[0], wbuf.at[1]
        if pair == 0:
            linear(e_n1, w0, frames, e_q, vec(2))
            linear(e_n1, w1, frames, e_k)
            save(0, 1, 2)
        elif pair == 1:
            linear(e_n1, w0, frames, e_v, vec(3))
            attention_forward_ref(e_q, e_k, e_v, None, frames, frames, e_mix, e_lse)
            project_add(ein_ref, e_mix, w1, vec(4), frames, e_after)
            norm_forward_ref(e_after, vec(5), vec(6), frames, e_n2)
            save(3, 4, 5, 6, 7)
        elif pair in (2, 3):
            both(lambda k: gelu_block(
                e_n2, wbuf.at[k], vec(7 + 2 * (pair - 2) + k), frames, 2 * (pair - 2) + k, e_act, e_slope
            ))
            if pair == 3:
                save(8, 9)
        elif pair in (4, 5):
            if pair == 4:
                eacc[...] = e_after[...] + vec(11)[...]
            both(lambda k: accumulate(e_act.at[2 * (pair - 4) + k], wbuf.at[k], frames, eacc))
            if pair == 5:
                e_out[...] = eacc[...].astype(BF)
                save(10)
        elif pair == 6:
            linear(d_n1, w0, rows, d_q, vec(14))
            linear(d_n1, w1, rows, d_k)
            save(11, 12, 13)
        elif pair == 7:
            linear(d_n1, w0, rows, d_v, vec(15))
            attention_forward_ref(d_q, d_k, d_v, mask_ref, d_q.shape[0], d_k.shape[0], d_mix, d_lse)
            project_add(din_ref, d_mix, w1, vec(16), rows, d_after)
            norm_forward_ref(d_after, vec(17), vec(18), rows, d_n2)
            save(14, 15, 16, 17, 18)
        elif pair == 8:
            linear(d_n2, w0, rows, c_q, vec(19))
            linear(e_out, w1, frames, c_k)
            save(19, 20)
        elif pair == 9:
            linear(e_out, w0, frames, c_v, vec(20))
            attention_forward_ref(c_q, c_k, c_v, None, c_q.shape[0], frames, c_mix, c_lse)
            project_add(d_after, c_mix, w1, vec(21), rows, d_after2)
            norm_forward_ref(d_after2, vec(22), vec(23), rows, d_n3)
            save(21, 22, 23, 24, 25)
        elif pair in (10, 11):
            both(lambda k: gelu_block(
                d_n3, wbuf.at[k], vec(24 + 2 * (pair - 10) + k), rows, 2 * (pair - 10) + k, d_act, d_slope
            ))
            if pair == 11:
                save(26, 27)

    vv_tiles = comm[-1]
    gather_kernel(n, on_start, on_vectors, on_pair, on_last, xe_ref, xd_ref, w_ref, v_ref, *comm[:-1])
    for i in range(N_SAVED):
        pltpu.make_async_copy(bufs[i], outs[i], s_save.at[i]).wait()
    for i in range(2):
        early_core(i).wait_send()
        early_save(i).wait()


def forward_pass(encoder_master, decoder_master, encoder_input, decoder_input, segments, decoder_cotangent, n):
    (_, re, ne, ge), (_, rd, nd, gd) = sizes(ENC, n), sizes(DEC, n)
    frames, rows = encoder_input.shape[0], decoder_input.shape[0]
    tall = -(-rows // 128) * 128
    dma = pltpu.SemaphoreType.DMA
    saved = saved_shapes(rows, frames)
    vmem, hbm = pl.BlockSpec(memory_space=pltpu.VMEM), pl.BlockSpec(memory_space=pl.ANY)
    return pl.pallas_call(
        partial(forward_kernel, n, rows, frames),
        out_shape=(
            jax.ShapeDtypeStruct((N_PAIR, 2, 4, 2, 2, UNIT, D), BF),
            jax.ShapeDtypeStruct((4, 2, 2, 2, 8, LANES), F32),
            *(jax.ShapeDtypeStruct(shape, dtype) for shape, dtype in saved),
            jax.ShapeDtypeStruct((2, 4, 2, 2, UNIT, D), BF),
        ),
        in_specs=[vmem] * 5 + [hbm],
        out_specs=(hbm,) * (3 + N_SAVED),
        scratch_shapes=[
            pltpu.VMEM((FRONT + re + BACK, LANES), F32),
            pltpu.VMEM((FRONT + rd + BACK, LANES), F32),
            pltpu.VMEM((ne, UNIT, D), BF),
            pltpu.VMEM((nd, UNIT, D), BF),
            pltpu.VMEM((ge, 2, 2, UNIT, D), BF),
            pltpu.VMEM((gd, 2, 2, UNIT, D), BF),
            pltpu.VMEM((N_VEC, 8, LANES), F32),
            pltpu.VMEM((2, N_PAIR, UNIT, D), BF),
            pltpu.VMEM((2, 8, LANES), F32),
            pltpu.VMEM((N_PAIR, UNIT, D), BF),
            pltpu.VMEM((8, LANES), F32),
            dma((ne + nd,)),
            dma((ge + gd, 2)),
            dma((N_VEC,)),
            dma((2, N_PAIR)),
            dma((2,)),
            dma((N_PAIR, 6)),
            dma((N_PAIR, 6)),
            dma((N_PAIR,)),
            dma((N_PAIR,)),
            dma((N_PAIR,)),
            dma((6,)),
            dma((6,)),
            pltpu.VMEM((4, 2, 2, 2, 8, LANES), F32),
            *(pltpu.VMEM(shape, dtype) for shape, dtype in saved),
            pltpu.VMEM((32, D), F32),
            pltpu.VMEM((2, D, D), BF),
            pltpu.VMEM((rows, D), F32),
            pltpu.VMEM((tall, tall), F32),
            pltpu.VMEM((8, tall), F32),
            pltpu.VMEM((tall, LANES), F32),
            dma((N_SAVED,)),
            dma((2,)),
            pltpu.VMEM((rows, D), BF),
            pltpu.VMEM((2, 2, 4, 2, 2, UNIT, D), BF),
            pltpu.VMEM((2, 4, 2, 2, UNIT, D), BF),
            dma((2,)),
            dma((2,)),
            dma((2,)),
        ],
        compiler_params=pltpu.CompilerParams(collective_id=0, has_side_effects=True, vmem_limit_bytes=58 << 20),
        name="forward",
    )(rows_of(encoder_master, re), rows_of(decoder_master, rd), encoder_input, decoder_input, segments,
      decoder_cotangent)


RING = 3
RING_C = 5
EARLY = 2
TICKS = [(t, part) for t in range(EARLY, N_PAIR) for part in ((0, 1) if t in (4, 6) else (0,))]
SENT = list(range(EARLY)) + [
    EARLY + u for u, (t, part) in enumerate(TICKS) if part == 1 or (t, 1) not in TICKS
]


def scatter_kernel(
    n, begin_loads, produce, after, early_ref, vg_ref, gbuf, oe_ref, od_ref, norm_ref,
    land_c, land_b, land_a, land_z, ownb, vown, vl_c, vl_y, vl_x, vl_z,
    ge_ref, gd_ref, fe, fd, fbe, fbd, fv, nsend, nland,
    s_core, r_core, s_free, s_ph, r_ph, s_back, r_small, r_big, sv, rv, s_vback, r_vback, s_n, r_n, s_out,
):
    wide, narrow, z, x, y, c = whoami()
    me = wide * 4 + narrow
    chip = me // 2
    at = dict(z=z, x=x, y=y, c=c)
    greet(me, n)
    sib = device(z, x, y, 1 - c)

    def slot_c(pair):
        return (N_PAIR - 1 - pair) % RING_C

    def core_copy(pair):
        return pltpu.make_async_remote_copy(
            gbuf.at[(N_PAIR - 1 - pair) % RING, 1 - c], land_c.at[slot_c(pair)], s_core.at[pair], r_core.at[pair], device_id=sib, device_id_type=MESH
        )

    mine_a = x * (1 - c) + y * c

    def phase_dmas(pair, phase):
        if phase == 1:
            steps = [(land_c.at[slot_c(pair), :, :, 1 - y], land_b.at[pair], 0, second_peer(at))]
        elif phase == 2:
            steps = [(land_b.at[pair, :, 1 - mine_a], land_a.at[pair], 1, first_peer(at))]
        else:
            steps = [
                (land_a.at[pair, (z + k) % 4], land_z.at[pair, k - 1], 1 + k, device((z + k) % 4, x, y, c))
                for k in (1, 2, 3)
            ]
        return [
            pltpu.make_async_remote_copy(
                src, dst, s_ph.at[pair, k], r_ph.at[pair, k], device_id=target, device_id_type=MESH
            )
            for src, dst, k, target in steps
        ]

    def begin(pair, phase):
        if phase != 1:
            for cp in phase_dmas(pair, phase):
                cp.start()
            return

        @pl.when(c == 0)
        def _():
            phase_dmas(pair, 1)[0].start()

        @pl.when(c == 1)
        def _():
            pltpu.make_async_remote_copy(
                land_c.at[slot_c(pair), :, 1 - x], land_b.at[pair], s_ph.at[pair, 0], r_ph.at[pair, 0],
                device_id=second_peer(at), device_id_type=MESH,
            ).start()

    def back(pair):
        block = ENC if pair < 6 else DEC
        shard = sizes(block, n)[0]
        local = pair - block.first_mat // 2
        half = block.small_mats // 2
        big = half <= local < half + 2
        if big:
            start = (block.fc1 * 6 + chip * BIG) * LANES
            length = BIG * LANES
        else:
            small = 2 * local - (4 if local >= half + 2 else 0) + c
            start = (small_row(block, small) * 6 + chip * UROWS) * LANES
            length = UROWS * LANES
        first, last = start // shard, (start + length - 1) // shard
        out = []
        for which, target in ((0, first), (1, last)):
            low_row = target * shard // LANES
            if big:
                slot = (start // LANES - low_row + BIG) // BIG
                q = 2 * (local - half) + c
                dst = (fbe if block is ENC else fbd).at[slot, q]
                recv = r_big.at[0 if block is ENC else 1, slot, q]
            else:
                slot = (start // LANES - low_row + UROWS) // UROWS
                dst = (fe if block is ENC else fd).at[slot]
                recv = r_small.at[0 if block is ENC else 1, slot]
            needed = True if which == 0 else first != last
            out.append((needed, target, dst, s_back.at[pair, which], recv))
        return out

    def start_back(pair):
        for needed, target, dst, send, recv in back(pair):
            @pl.when(needed & (target == me))
            def _(dst=dst, recv=recv):
                pltpu.make_async_copy(ownb.at[pair], dst, recv).start()

            @pl.when(needed & (target != me))
            def _(dst=dst, recv=recv, send=send, target=target):
                pltpu.make_async_remote_copy(
                    ownb.at[pair], dst, send, recv, device_id=flat_device(target), device_id_type=MESH
                ).start()

    def end_back(pair):
        for needed, target, dst, send, recv in back(pair):
            @pl.when(needed & (target != me))
            def _(send=send):
                pltpu.make_async_copy(ownb.at[pair], ownb.at[pair], send).wait()

    def add_core(pair):
        def body(i, carry):
            a, b = i // 2, i % 2
            for k in range(2):
                mine = gbuf[(N_PAIR - 1 - pair) % RING, c, a, b, k]
                land_c[slot_c(pair), a, b, k] = (
                    land_c[slot_c(pair), a, b, k].astype(F32) + mine.astype(F32)
                ).astype(BF)
            return carry

        lax.fori_loop(0, 8, body, 0)

    def add_b(pair):
        def body(i, carry):
            a, b = i // 2, i % 2
            mine = land_c[slot_c(pair), a, b * (1 - c) + x * c, y * (1 - c) + b * c]
            land_b[pair, a, b] = (land_b[pair, a, b].astype(F32) + mine.astype(F32)).astype(BF)
            return carry

        lax.fori_loop(0, 8, body, 0)

    def add_a(pair):
        for a in range(4):
            land_a[pair, a] = (land_a[pair, a].astype(F32) + land_b[pair, a, mine_a].astype(F32)).astype(BF)

    def add_z(pair):
        total = land_a[pair, z].astype(F32)
        for k in range(3):
            total = total + land_z[pair, k].astype(F32)
        ownb[pair] = total.astype(BF)
        squares = total * total
        return jnp.sum(squares.reshape(UNIT // 8, 8, D), axis=0)

    vland = dict(c=vl_c, y=vl_y, x=vl_x, z=vl_z)

    def vsteps(phase):
        if phase == 0:
            return [(vg_ref.at[:, :, :, 1 - c], vl_c, 0, dict(at, c=1 - c))]
        if phase == 1:
            return [(vl_c.at[:, :, 1 - y], vl_y, 1, dict(at, y=1 - y))]
        if phase == 2:
            return [(vl_y.at[:, 1 - x], vl_x, 2, dict(at, x=1 - x))]
        return [(vl_x.at[(z + k) % 4], vl_z.at[k - 1], 2 + k, dict(at, z=(z + k) % 4)) for k in (1, 2, 3)]

    def vdmas(phase):
        return [
            pltpu.make_async_remote_copy(s, d, sv.at[k], rv.at[k], device_id=dev(p), device_id_type=MESH)
            for s, d, k, p in vsteps(phase)
        ]

    def vadd(phase):
        if phase == 0:
            vl_c[...] = vl_c[...] + vg_ref[:, :, :, c]
        elif phase == 1:
            vl_y[...] = vl_y[...] + vl_c[:, :, y]
        elif phase == 2:
            vl_x[...] = vl_x[...] + vl_y[:, x]
        else:
            vown[...] = vl_x[z] + vl_z[0] + vl_z[1] + vl_z[2]

    fields = {ENC: (0, ge_ref, oe_ref, fe, fbe), DEC: (1, gd_ref, od_ref, fd, fbd)}

    def units_to_flat(block, least=0, most=99):
        b, g_out, _, f_ref, fb_ref = fields[block]
        _, _, n_small, n_big = sizes(block, n)

        def small_body(slot, mat, u, pos, start):
            pltpu.make_async_copy(f_ref.at[slot], f_ref.at[slot], r_small.at[b, slot]).wait()
            for k in range(6):
                g_out[pl.ds(FRONT + pos + k, UNIT, stride=6), :] = f_ref[slot, :, k * LANES : (k + 1) * LANES].astype(F32)

        def big_body(slot, u, pos, start):
            for q in range(4):
                pltpu.make_async_copy(fb_ref.at[slot, q], fb_ref.at[slot, q], r_big.at[b, slot, q]).wait()
                for k in range(6):
                    g_out[pl.ds(FRONT + pos + 6 * q + k, UNIT, stride=24), :] = fb_ref[
                        slot, q, :, k * LANES : (k + 1) * LANES
                    ].astype(F32)

        if most > block.small_mats:
            each_big(block, n, me, n_big, big_body)
        each_small(block, n, me, n_small, small_body, least, most)

    def finish_flat(block):
        b, g_out, o_ref, _, _ = fields[block]
        shard, rows, _, _ = sizes(block, n)

        def vec_body(v, pos, start):
            pltpu.make_async_copy(fv.at[v], fv.at[v], r_vback.at[v]).wait()
            g_out[pl.ds(FRONT + pos, 6), :] = fv[v, 0:6, :]

        each_vector(block, n, me, 0 if block is ENC else len(ENC.vectors), vec_body)
        shift = (me * shard) % LANES
        step = 8 * max(k for k in range(1, 40) if (rows // 8) % k == 0)
        lanes = lax.broadcasted_iota(jnp.int32, (1, LANES), 1)
        unturn = lax.rem(LANES - shift, LANES)

        def turn(i, carry):
            at_row = pl.multiple_of(i * step, 8)
            here = pltpu.roll(g_out[pl.ds(FRONT + at_row, step), :], unturn, 1)
            after = pltpu.roll(g_out[pl.ds(FRONT + at_row + 1, step), :], unturn, 1)
            g_out[pl.ds(FRONT + at_row, step), :] = jnp.where(lanes < LANES - shift, here, after)
            return carry

        lax.fori_loop(0, rows // step, turn, 0)
        pltpu.make_async_copy(g_out.at[pl.ds(FRONT, rows)], o_ref, s_out.at[b]).start()

    def vector_targets(v_static):
        block = ENC if v_static < len(ENC.vectors) else DEC
        shard = sizes(block, n)[0]
        start = (ENC.vectors + DEC.vectors)[v_static] * D
        return start // shard, (start + D - 1) // shard

    def vectors_back():
        for v in range(N_VEC):
            for which, target in enumerate(sorted(set(vector_targets(v)))):
                if target == v:
                    @pl.when(me == v)
                    def _(v=v):
                        pltpu.make_async_copy(vown, fv.at[v], r_vback.at[v]).start()
                else:
                    @pl.when(me == v)
                    def _(v=v, target=target, which=which):
                        pltpu.make_async_remote_copy(
                            vown, fv.at[v], s_vback.at[which], r_vback.at[v], device_id=(target // 4, target % 4), device_id_type=MESH
                        ).start()

    seq = list(range(N_PAIR - 1, -1, -1))
    square = jnp.zeros((8, D), F32)
    def early_copy(i):
        return pltpu.make_async_copy(early_ref.at[i], land_c.at[i], s_core.at[i])

    for i in range(EARLY):
        early_copy(i).start()
    begin_loads()
    await_all(n)
    for i in range(EARLY):
        early_copy(i).wait()
        begin(seq[i], 1)
    for u in range(EARLY, EARLY + len(TICKS) + B_AT[3]):
        t, part = TICKS[u - EARLY] if u - EARLY < len(TICKS) else (N_PAIR + u - EARLY - len(TICKS), 0)
        done = part == 1 or (t, 1) not in TICKS
        if t < N_PAIR:
            if part == 0 and t - RING >= EARLY:
                core_copy(seq[t - RING]).wait_send()
            produce(t, part, gbuf.at[t % RING])
            if done:
                if t >= RING_C:
                    pl.semaphore_wait(s_free, 1)
                core_copy(seq[t]).start()
        for phase in (4, 3, 2, 1):
            if u - B_AT[phase - 1] in SENT:
                i = SENT.index(u - B_AT[phase - 1])
                pair = seq[i]
                if phase == 1 and i < EARLY:
                    continue
                if phase == 1:
                    core_copy(pair).wait_recv()
                    add_core(pair)
                elif phase == 2:
                    for cp in phase_dmas(pair, 1):
                        cp.wait()
                    add_b(pair)
                    if i < N_PAIR - RING_C:
                        pl.semaphore_signal(s_free, inc=1, device_id=sib, device_id_type=MESH)
                elif phase == 3:
                    for cp in phase_dmas(pair, 2):
                        cp.wait_recv()
                    add_a(pair)
                else:
                    for cp in phase_dmas(pair, 3):
                        cp.wait_recv()
                    square = square + add_z(pair)
                    start_back(pair)
                if phase < 4:
                    begin(pair, phase)
        if done:
            after(t)
        if t == N_PAIR + B_AT[2] - 1:
            units_to_flat(DEC)
        if t == N_PAIR + B_AT[3] - 1:
            finish_flat(DEC)
            units_to_flat(ENC, 2, 99)
        if t == N_PAIR - 1:
            for cp in vdmas(0):
                cp.start()
        elif N_PAIR <= t < N_PAIR + 4:
            phase = t - N_PAIR
            for cp in vdmas(phase):
                cp.wait_recv()
            vadd(phase)
            if phase < 3:
                for cp in vdmas(phase + 1):
                    cp.start()
            else:
                vectors_back()

    vsq = vown[...] * vown[...]
    for k in range(6):
        vsq = vsq + square[:, k * LANES : (k + 1) * LANES]
    nsend[...] = vsq

    def norm_copy(i):
        return pltpu.make_async_remote_copy(
            nsend, nland.at[i], s_n.at[i], r_n.at[i], device_id=flat_device((me + i) % n), device_id_type=MESH
        )

    def norm_start(i, carry):
        norm_copy(i).start()
        return carry

    lax.fori_loop(1, n, norm_start, 0)

    units_to_flat(ENC, 0, 2)
    finish_flat(ENC)

    def norm_wait(i, total):
        norm_copy(i).wait()
        return total + nland[i]

    total = lax.fori_loop(1, n, norm_wait, nsend[...])
    norm_ref[...] = jnp.broadcast_to(jnp.sqrt(jnp.sum(total)), (8, LANES))

    for b, (g_out, o_ref) in enumerate(((ge_ref, oe_ref), (gd_ref, od_ref))):
        pltpu.make_async_copy(g_out.at[pl.ds(FRONT, o_ref.shape[0])], o_ref, s_out.at[b]).wait()
    for phase in range(4):
        for cp in vdmas(phase):
            cp.wait_send()
    for v in range(N_VEC):
        for which, target in enumerate(sorted(set(vector_targets(v)))):
            if target != v:
                @pl.when(me == v)
                def _(which=which):
                    pltpu.make_async_copy(vown, vown, s_vback.at[which]).wait()
    for pair in range(N_PAIR):
        if N_PAIR - 1 - pair >= N_PAIR - RING:
            core_copy(pair).wait_send()
        for phase in (2, 3):
            for cp in phase_dmas(pair, phase):
                cp.wait_send()
        end_back(pair)


def sum_rows(ref, rows, out_ref):
    def body(r):
        out_ref[...] += jnp.sum(ref[r, :].astype(F32), axis=0, keepdims=True)

    out_ref[...] = jnp.zeros_like(out_ref)
    row_blocks(rows, body)


def norm_backward_ref(x_ref, gain, dn_ref, rows, out_ref, gain_grad, shift_grad):
    gain_grad[...] = jnp.zeros_like(gain_grad)
    shift_grad[...] = jnp.zeros_like(shift_grad)

    def body(r):
        hat, root = norm_rows(x_ref[r, :].astype(F32))
        dn = dn_ref[r, :]
        gain_grad[...] += jnp.sum(dn * hat, axis=0, keepdims=True)
        shift_grad[...] += jnp.sum(dn, axis=0, keepdims=True)
        g = dn * gain[...]
        part = g - jnp.mean(g, axis=1, keepdims=True) - hat * jnp.mean(g * hat, axis=1, keepdims=True)
        out_ref[r, :] += root * part

    row_blocks(rows, body)


def round_rows(src_ref, rows, out_ref):
    def body(r):
        out_ref[r, :] = src_ref[r, :].astype(BF)

    row_blocks(rows, body)


def weight_grad(a_ref, b_ref, rows, g_ref):
    b = b_ref[0:rows, :]
    flat = g_ref.reshape(D, D)

    def body(cols):
        flat[cols, :] = mm_tn(a_ref[0:rows, cols], b).astype(BF)

    col_blocks(body)


def back_through(a_ref, w_ref, rows, out_ref, add):
    a = a_ref[0:rows, :]

    def body(cols):
        y = mm_nt(a, w_ref[cols, :])
        if add:
            y = y + out_ref[0:rows, cols]
        out_ref[0:rows, cols] = y.astype(out_ref.dtype)

    col_blocks(body)


def gelu_back(o_ref, w_ref, slope_ref, rows, out_ref, bias_grad):
    a = o_ref[0:rows, :]

    def body(cols):
        y = mm_nt(a, w_ref[cols, :]) * slope_ref[0:rows, cols].astype(F32)
        bias_grad[:, cols] = jnp.sum(y, axis=0, keepdims=True)
        out_ref[0:rows, cols] = y.astype(BF)

    col_blocks(body)


def attention_backward_ref(q_ref, k_ref, v_ref, dm_ref, lse_ref, mask_ref, rows, keys, dq_ref, dk_ref, dv_ref, low, high):
    def pair_of_heads(i, carry):
        cols = pl.ds(pl.multiple_of(i * LANES, LANES), LANES)
        dk_ref[:, cols] = jnp.zeros((dk_ref.shape[0], LANES), F32)
        dv_ref[:, cols] = jnp.zeros((dv_ref.shape[0], LANES), F32)
        k_turned = jnp.transpose(k_ref[0:keys, cols])
        for tile, (start, reach) in enumerate(attend_tiles(rows, keys, mask_ref is not None)):
            r = slice(start, start + LANES)
            q2 = both_heads(q_ref[r, cols] * jnp.asarray(SCALE, BF))
            dm2 = both_heads(dm_ref[r, cols])
            scores = scores_of(k_ref[0:reach, cols], q2, mask_ref, start, reach)
            probs = jnp.exp(scores - lse_ref[tile, pl.ds(i, 1), :])
            dp = mm_nt(v_ref[0:reach, cols], dm2)
            weighted = probs * dp
            ds = (weighted - probs * jnp.sum(weighted, axis=0, keepdims=True)).astype(BF)
            dk_ref[0:reach, cols] += mm(ds, q2)
            dv_ref[0:reach, cols] += mm(probs.astype(BF), dm2)
            dq = jnp.concatenate(
                [
                    mm(k_turned[s * HEAD_DIM : (s + 1) * HEAD_DIM, 0:reach], ds[:, s * LANES : (s + 1) * LANES])
                    for s in range(2)
                ],
                axis=0,
            )
            dq_ref[r, cols] = jnp.transpose(dq) * SCALE
        return carry

    lax.fori_loop(low, high, pair_of_heads, 0, unroll=1)


W_ORDER = (26, 27, 22, 23, 24, 25, 20, 21, 19, 16, 17, 18, 15, 12, 13, 14, 10, 11, 6, 7, 8, 9, 4, 5, 3, 0, 1, 2, 24, 25, 26, 27)
W_RING = 4
A_RING = 4


def backward_kernel(n, rows, frames, *refs):
    w_ref, v_ref, seg_ref, ein, din, ecot, dcot, early = refs[:8]
    kept, refs = refs[8 : 8 + N_SAVED], refs[8 + N_SAVED :]
    oe_ref, od_ref, norm_ref, fgrad, tgrad, dout = refs[:6]
    refs = refs[6:]
    comm, refs = refs[:34], refs[34:]
    (
        gbuf, vg, vgr, gains, wbuf, outg, eoutg, dn, pool, abuf, nbuf, xbuf,
        dq, dk, dv, mask_ref, seg_row, seg_col, lse, orow, mem, mgrad, s_l, s_w, s_a, s_o,
    ) = refs
    tall = mask_ref.shape[0]

    a_order = (
        [kept[27].at[k] for k in (2, 3, 0, 1)]
        + [kept[22].at[0:rows], kept[15].at[0:rows], din]
        + [kept[8].at[k] for k in (2, 3, 0, 1)]
        + [kept[9].at[k] for k in (2, 3, 0, 1)]
        + [kept[4], ein]
        + [kept[26].at[k] for k in range(4)]
    )
    used = [0, 0]

    def w_copy(u):
        m = W_ORDER[u]
        return pltpu.make_async_copy(w_ref.at[m // 2, m % 2].reshape(D, D), wbuf.at[u % W_RING], s_w.at[u % W_RING])

    def a_copy(u):
        src = a_order[u]
        return pltpu.make_async_copy(src, abuf.at[u % A_RING, 0 : src.shape[0]], s_a.at[u % A_RING])

    def with_w(mat, body):
        u = used[0]
        used[0] += 1
        assert W_ORDER[u] == mat
        w_copy(u).wait()
        body(wbuf.at[u % W_RING])
        if u + W_RING < len(W_ORDER):
            w_copy(u + W_RING).start()

    def with_a(body):
        u = used[1]
        used[1] += 1
        a_copy(u).wait()
        body(abuf.at[u % A_RING])
        if u + A_RING < len(a_order):
            a_copy(u + A_RING).start()

    def side(k, src, dst):
        return pltpu.make_async_copy(src, dst, s_l.at[k])

    def x_copy(i):
        return side(0, kept[i], xbuf.at[0 : kept[i].shape[0]])

    def n_copy(i):
        return side(1, kept[i], nbuf.at[0 : kept[i].shape[0]])

    def vrow(i):
        return vgr.at[i : i + 1]

    def take_two(which, copy, ring, total, body):
        u = used[which]
        used[which] += 2
        copy(u).wait()
        copy(u + 1).wait()
        body(lambda k: lax.rem(u + k, ring))
        for k in range(2):
            if u + k + ring < total:
                copy(u + k + ring).start()

    def two_w(mat, body):
        assert W_ORDER[used[0]] == mat
        take_two(0, w_copy, W_RING, len(W_ORDER), lambda slot: body(lambda k: wbuf.at[slot(k)]))

    def two_a(body):
        take_two(1, a_copy, A_RING, len(a_order), lambda slot: body(lambda k: abuf.at[slot(k)]))

    def feed(step, g, count, first_mat, first_vec, n_i):
        if step < 2:
            two_a(lambda a: both(lambda k: weight_grad(a(k), orow, count, g.at[k])))
            return
        first = 2 if step == 2 else 0
        if step == 2:
            n_copy(n_i).wait()

        def body(k, w, a):
            gelu_back(orow, w(k), a(k), count, pool.at[first + k], vgr.at[pl.ds(first_vec + first + k, 1)])
            weight_grad(nbuf, pool.at[first + k], count, g.at[k])

        two_w(first_mat + 4 + first, lambda w: two_a(lambda a: both(lambda k: body(k, w, a))))

    def feed_after(step, count, first_mat):
        first = 2 if step == 2 else 0
        if step == 2:
            dn[0:count, :] = jnp.zeros((count, D), F32)
        two_w(
            first_mat + first,
            lambda w: both(lambda k: back_through(pool.at[first + k], w(k), count, dn, True)),
        )

    def attend(part, *setting):
        g, count, padded, keys, padded_keys, out_ref, wo, q_i, lse_i, masked, bo, bq, bv = setting
        heads = partial(
            attention_backward_ref,
            pool.at[0], pool.at[1], pool.at[2], pool.at[3], lse, mask_ref if masked else None, padded, padded_keys,
            dq, dk.at[0:padded_keys], dv.at[0:padded_keys],
        )
        if part == 0:
            attend_start(*setting)
            heads(0, 3)
            return
        heads(3, 6)
        round_rows(dv, keys, pool.at[2])
        round_rows(dq, count, pool.at[0])
        round_rows(dk, keys, pool.at[1])
        sum_rows(dq, count, vrow(bq))
        sum_rows(dv, keys, vrow(bv))

    def attend_start(g, count, padded, keys, padded_keys, out_ref, wo, q_i, lse_i, masked, bo, bq, bv):
        cps = [side(2 + k, kept[q_i + k], pool.at[k, 0 : kept[q_i + k].shape[0]]) for k in range(3)]
        cps.append(side(5, kept[lse_i], lse.at[0 : kept[lse_i].shape[0]]))
        for cp in cps:
            cp.start()
        round_rows(out_ref, count, orow)
        sum_rows(out_ref, count, vrow(bo))
        with_a(lambda a: weight_grad(a, orow, count, g.at[1]))
        with_w(wo, lambda w: back_through(orow, w, count, pool.at[3], False))
        if padded > count:
            pool[3, count:padded, :] = jnp.zeros((padded - count, D), BF)
        for cp in cps:
            cp.wait()

    def start():
        o_copy = side(2, dcot, orow)
        o_copy.start()
        for u in range(A_RING):
            a_copy(u).start()
        for u in range(W_RING):
            w_copy(u).start()
        n_copy(25).start()
        x_copy(24).start()
        mem_copy = side(3, kept[10], mem)
        mem_copy.start()
        for i, v in enumerate((0, 5, 12, 17, 22, 28)):
            for k in range(6):
                gains[i : i + 1, k * LANES : (k + 1) * LANES] = v_ref[v // 8, v // 4 % 2, v // 2 % 2, v % 2, k : k + 1, :]
        o_copy.wait()
        mem_copy.wait()

    def widen():
        def body(r):
            outg[r, :] = orow[r, :].astype(F32)

        row_blocks(rows, body)
        sum_rows(outg, rows, vrow(28))

    def produce(t, part, g):
        if t < 4:
            feed(t, g, rows, 20, 24, 25)
            if t == 3:
                n_copy(18).start()
        elif t == 4:
            attend(part, g, rows, tall, frames, frames, outg, 19, 19, 23, False, 21, 19, 20)
            if part == 1:
                weight_grad(mem, pool.at[2], frames, g.at[0])
        elif t == 5:
            n_copy(18).wait()
            weight_grad(nbuf, pool.at[0], rows, g.at[0])
            weight_grad(mem, pool.at[1], frames, g.at[1])
            n_copy(11).start()
        elif t == 6:
            attend(part, g, rows, tall, rows, tall, outg, 15, 12, 16, True, 16, 14, 15)
            if part == 1:
                n_copy(11).wait()
                weight_grad(nbuf, pool.at[2], rows, g.at[0])
        elif t == 7:
            weight_grad(nbuf, pool.at[0], rows, g.at[0])
            weight_grad(nbuf, pool.at[1], rows, g.at[1])
            n_copy(7).start()
        elif t < 12:
            feed(t - 8, g, frames, 4, 7, 7)
            if t == 11:
                n_copy(0).start()
        elif t == 12:
            for half in range(2):
                attend(half, g, frames, frames, frames, frames, eoutg, 3, 1, 5, False, 4, 2, 3)
            n_copy(0).wait()
            weight_grad(nbuf, pool.at[2], frames, g.at[0])
        else:
            weight_grad(nbuf, pool.at[0], frames, g.at[0])
            weight_grad(nbuf, pool.at[1], frames, g.at[1])

    def after(t):
        if t in (2, 3):
            feed_after(t, rows, 20)
            if t == 2:
                widen()
                make_mask(seg_ref, seg_row, seg_col, mask_ref)
            if t == 3:
                x_copy(24).wait()
                norm_backward_ref(xbuf, gains.at[4:5], dn, rows, outg, vrow(22), vrow(23))
                x_copy(17).start()
        elif t == 5:
            with_w(16, lambda w: back_through(pool.at[0], w, rows, dn, False))
            with_w(17, lambda w: back_through(pool.at[1], w, frames, mgrad, False))
            with_w(18, lambda w: back_through(pool.at[2], w, frames, mgrad, True))
            x_copy(17).wait()
            norm_backward_ref(xbuf, gains.at[3:4], dn, rows, outg, vrow(17), vrow(18))
            x_copy(6).start()
        elif t == 7:
            cot = side(2, ecot, orow.at[0:frames])
            cot.start()
            with_w(12, lambda w: back_through(pool.at[0], w, rows, dn, False))
            with_w(13, lambda w: back_through(pool.at[1], w, rows, dn, True))
            with_w(14, lambda w: back_through(pool.at[2], w, rows, dn, True))
            with_a(lambda a: norm_backward_ref(a, gains.at[2:3], dn, rows, outg, vrow(12), vrow(13)))
            pltpu.make_async_copy(outg, tgrad, s_o.at[0]).start()
            cot.wait()

            def body(r):
                total = orow[r, :].astype(F32) + mgrad[r, :]
                eoutg[r, :] = total
                orow[r, :] = total.astype(BF)

            row_blocks(frames, body)
        elif t == 9:
            sum_rows(eoutg, frames, vrow(11))
        elif t in (10, 11):
            feed_after(t - 8, frames, 4)
            if t == 11:
                x_copy(6).wait()
                norm_backward_ref(xbuf, gains.at[1:2], dn, frames, eoutg, vrow(5), vrow(6))
                x_copy(24).start()
        elif t in (14, 15):
            if t == 14:
                x_copy(24).wait()
                row_blocks(rows, lambda r: add_row(dn, xbuf, gains.at[5:6], r))
            two_w(
                24 + 2 * (t - 14),
                lambda w: two_a(lambda a: both(lambda k: accumulate(a(k), w(k), rows, dn))),
            )
            if t == 15:
                round_rows(dn, rows, orow)
                pltpu.make_async_copy(orow, dout, s_o.at[2]).start()
        elif t == 13:
            with_w(0, lambda w: back_through(pool.at[0], w, frames, dn, False))
            with_w(1, lambda w: back_through(pool.at[1], w, frames, dn, True))
            with_w(2, lambda w: back_through(pool.at[2], w, frames, dn, True))
            with_a(lambda a: norm_backward_ref(a, gains.at[0:1], dn, frames, eoutg, vrow(0), vrow(1)))
            pltpu.make_async_copy(eoutg, fgrad, s_o.at[1]).start()
            for v in range(32):
                at = (v // 8, v // 4 % 2, v // 2 % 2, v % 2)
                if v < N_VEC:
                    vg[at + (slice(6, 8), slice(None))] = jnp.zeros((2, LANES), F32)
                    for k in range(6):
                        vg[at + (slice(k, k + 1), slice(None))] = vgr[v : v + 1, k * LANES : (k + 1) * LANES]
                else:
                    vg[at] = jnp.zeros((8, LANES), F32)

    scatter_kernel(n, start, produce, after, early, vg, gbuf, oe_ref, od_ref, norm_ref, *comm)
    pltpu.make_async_copy(outg, tgrad, s_o.at[0]).wait()
    pltpu.make_async_copy(eoutg, fgrad, s_o.at[1]).wait()
    pltpu.make_async_copy(orow, dout, s_o.at[2]).wait()


def backward_pass(weights, vectors, kept, early, ein, din, ecot, dcot, segments, n):
    (_, re, ne, ge), (_, rd, nd, gd) = sizes(ENC, n), sizes(DEC, n)
    frames, rows = ein.shape[0], din.shape[0]
    tall = -(-rows // 128) * 128
    dma = pltpu.SemaphoreType.DMA
    vmem, hbm = pl.BlockSpec(memory_space=pltpu.VMEM), pl.BlockSpec(memory_space=pl.ANY)
    return pl.pallas_call(
        partial(backward_kernel, n, rows, frames),
        out_shape=(
            jax.ShapeDtypeStruct((re, LANES), F32),
            jax.ShapeDtypeStruct((rd, LANES), F32),
            jax.ShapeDtypeStruct((8, LANES), F32),
            jax.ShapeDtypeStruct((frames, D), F32),
            jax.ShapeDtypeStruct((rows, D), F32),
            jax.ShapeDtypeStruct((rows, D), BF),
        ),
        in_specs=[hbm] + [vmem] * 2 + [hbm] * (5 + N_SAVED),
        out_specs=(hbm, hbm, vmem, hbm, hbm, hbm),
        scratch_shapes=[
            pltpu.VMEM((RING_C, 4, 2, 2, UNIT, D), BF),
            pltpu.VMEM((N_PAIR, 4, 2, UNIT, D), BF),
            pltpu.VMEM((N_PAIR, 4, UNIT, D), BF),
            pltpu.VMEM((N_PAIR, 3, UNIT, D), BF),
            pltpu.VMEM((N_PAIR, UNIT, D), BF),
            pltpu.VMEM((8, LANES), F32),
            pltpu.VMEM((4, 2, 2, 8, LANES), F32),
            pltpu.VMEM((4, 2, 8, LANES), F32),
            pltpu.VMEM((4, 8, LANES), F32),
            pltpu.VMEM((3, 8, LANES), F32),
            pltpu.VMEM((FRONT + re + BACK, LANES), F32),
            pltpu.VMEM((FRONT + rd + BACK, LANES), F32),
            pltpu.VMEM((ne, UNIT, D), BF),
            pltpu.VMEM((nd, UNIT, D), BF),
            pltpu.VMEM((ge, 4, UNIT, D), BF),
            pltpu.VMEM((gd, 4, UNIT, D), BF),
            pltpu.VMEM((N_VEC, 8, LANES), F32),
            pltpu.VMEM((8, LANES), F32),
            pltpu.VMEM((n, 8, LANES), F32),
            dma((N_PAIR,)),
            dma((N_PAIR,)),
            pltpu.SemaphoreType.REGULAR,
            dma((N_PAIR, 5)),
            dma((N_PAIR, 5)),
            dma((N_PAIR, 2)),
            dma((2, max(ne, nd))),
            dma((2, max(ge, gd), 4)),
            dma((6,)),
            dma((6,)),
            dma((2,)),
            dma((N_VEC,)),
            dma((n,)),
            dma((n,)),
            dma((2,)),
            pltpu.VMEM((RING, 2, 4, 2, 2, UNIT, D), BF),
            pltpu.VMEM((4, 2, 2, 2, 8, LANES), F32),
            pltpu.VMEM((32, D), F32),
            pltpu.VMEM((8, D), F32),
            pltpu.VMEM((W_RING, D, D), BF),
            pltpu.VMEM((rows, D), F32),
            pltpu.VMEM((frames, D), F32),
            pltpu.VMEM((rows, D), F32),
            pltpu.VMEM((4, tall, D), BF),
            pltpu.VMEM((A_RING, rows, D), BF),
            pltpu.VMEM((rows, D), BF),
            pltpu.VMEM((rows, D), F32),
            pltpu.VMEM((tall, D), F32),
            pltpu.VMEM((tall, D), F32),
            pltpu.VMEM((tall, D), F32),
            pltpu.VMEM((tall, tall), F32),
            pltpu.VMEM((8, tall), F32),
            pltpu.VMEM((tall, LANES), F32),
            pltpu.VMEM((tall // 128, 8, 2 * LANES), F32),
            pltpu.VMEM((rows, D), BF),
            pltpu.VMEM((frames, D), BF),
            pltpu.VMEM((frames, D), F32),
            dma((6,)),
            dma((W_RING,)),
            dma((A_RING,)),
            dma((3,)),
        ],
        compiler_params=pltpu.CompilerParams(collective_id=1, has_side_effects=True, vmem_limit_bytes=61 << 20),
        name="backward",
    )(weights, vectors, segments, ein, din, ecot, dcot, early, *kept)


def attention_plan(prefix, width):
    return [
        (prefix + "wq", width, width),
        (prefix + "bq", width, 0),
        (prefix + "wk", width, width),
        (prefix + "wv", width, width),
        (prefix + "bv", width, 0),
        (prefix + "wo", width, width),
        (prefix + "bo", width, 0),
    ]


def feed_plan(width, hidden):
    return [
        ("fc1_weight", width, hidden),
        ("fc1_bias", hidden, 0),
        ("fc2_weight", hidden, width),
        ("fc2_bias", width, 0),
    ]


def encoder_layout(width, hidden):
    return (
        [("ln1_gain", width, 0), ("ln1_bias", width, 0)]
        + attention_plan("att_", width)
        + [("ln2_gain", width, 0), ("ln2_bias", width, 0)]
        + feed_plan(width, hidden)
    )


def decoder_layout(width, hidden):
    return (
        [("ln1_gain", width, 0), ("ln1_bias", width, 0)]
        + attention_plan("self_", width)
        + [("ln2_gain", width, 0), ("ln2_bias", width, 0)]
        + attention_plan("cross_", width)
        + [("ln3_gain", width, 0), ("ln3_bias", width, 0)]
        + feed_plan(width, hidden)
    )


def unpack(flat, layout):
    params = {}
    offset = 0
    for name, rows, cols in layout:
        count = rows * cols if cols > 0 else rows
        piece = flat[offset : offset + count]
        params[name] = piece.reshape(rows, cols) if cols > 0 else piece
        offset = offset + count
    return params


def pack(grads, layout):
    return jnp.concatenate([grads[name].reshape(-1) for name, rows, cols in layout])


def dot_plain(left, right):
    return jnp.dot(left, right, preferred_element_type=jnp.float32)


def dot_left(left, right):
    return lax.dot_general(
        left, right, (((0,), (0,)), ((), ())), preferred_element_type=jnp.float32
    )


def dot_right(left, right):
    return lax.dot_general(
        left, right, (((1,), (1,)), ((), ())), preferred_element_type=jnp.float32
    )


def layer_norm(values, gain, shift):
    centred = values - jnp.mean(values, axis=-1, keepdims=True)
    spread = jnp.mean(centred * centred, axis=-1, keepdims=True)
    return centred * lax.rsqrt(spread + 1e-05) * gain + shift


def norm_forward(params, prefix, values):
    gain = params[prefix + "_gain"].astype(jnp.float32)
    shift = params[prefix + "_bias"].astype(jnp.float32)
    return layer_norm(values, gain, shift).astype(jnp.bfloat16)


def norm_backward(params, prefix, values, grad):
    gain = params[prefix + "_gain"].astype(jnp.float32)
    shift = params[prefix + "_bias"].astype(jnp.float32)
    unused, pullback = jax.vjp(layer_norm, values, gain, shift)
    value_grad, gain_grad, shift_grad = pullback(grad)
    return (value_grad, {prefix + "_gain": gain_grad, prefix + "_bias": shift_grad})


def block_rows(total):
    return total if total <= 1024 else 512


def attend_forward(queries, keys_low, values, allowed_fn):
    total, width = queries.shape
    heads = width // HEAD_DIM
    rows = block_rows(total)
    blocks = total // rows
    scale = HEAD_DIM ** (-0.5)
    query_heads = queries.reshape(blocks, rows, heads, HEAD_DIM)
    key_heads = keys_low.reshape(keys_low.shape[0], heads, HEAD_DIM)
    value_heads = values.reshape(values.shape[0], heads, HEAD_DIM)
    starts = jnp.arange(blocks, dtype=jnp.int32) * rows

    def one_block(inputs):
        block, start = inputs
        scores = (
            jnp.einsum("qhd,khd->hqk", block, key_heads, preferred_element_type=jnp.float32) * scale
        )
        if allowed_fn is not None:
            scores = jnp.where(allowed_fn(start, rows)[None], scores, -1000000000.0)
        peak = jnp.max(scores, axis=-1, keepdims=True)
        weights = jnp.exp(scores - peak)
        totals = jnp.sum(weights, axis=-1, keepdims=True)
        probs = (weights / totals).astype(jnp.bfloat16)
        mixed = jnp.einsum("hqk,khd->qhd", probs, value_heads, preferred_element_type=jnp.float32)
        return (mixed.reshape(rows, width).astype(jnp.bfloat16), (peak + jnp.log(totals))[..., 0])

    mixed, logsum = lax.map(one_block, (query_heads, starts))
    return (mixed.reshape(total, width), logsum)


def attend_backward(queries, keys_low, values, logsum, mixed_grad, allowed_fn):
    total, width = queries.shape
    heads = width // HEAD_DIM
    rows = block_rows(total)
    blocks = total // rows
    scale = HEAD_DIM ** (-0.5)
    query_heads = queries.reshape(blocks, rows, heads, HEAD_DIM)
    grad_heads = mixed_grad.reshape(blocks, rows, heads, HEAD_DIM)
    key_heads = keys_low.reshape(keys_low.shape[0], heads, HEAD_DIM)
    value_heads = values.reshape(values.shape[0], heads, HEAD_DIM)
    starts = jnp.arange(blocks, dtype=jnp.int32) * rows

    def one_block(carry, inputs):
        key_grad, value_grad = carry
        block, grad_block, block_sum, start = inputs
        scores = (
            jnp.einsum("qhd,khd->hqk", block, key_heads, preferred_element_type=jnp.float32) * scale
        )
        if allowed_fn is not None:
            scores = jnp.where(allowed_fn(start, rows)[None], scores, -1000000000.0)
        probs = jnp.exp(scores - block_sum[..., None])
        prob_grad = jnp.einsum(
            "qhd,khd->hqk", grad_block, value_heads, preferred_element_type=jnp.float32
        )
        value_grad = value_grad + jnp.einsum(
            "hqk,qhd->khd",
            probs.astype(jnp.bfloat16),
            grad_block,
            preferred_element_type=jnp.float32,
        )
        score_grad = probs * (prob_grad - jnp.sum(probs * prob_grad, axis=-1, keepdims=True))
        raw_grad = (score_grad * scale).astype(jnp.bfloat16)
        query_grad = jnp.einsum(
            "hqk,khd->qhd", raw_grad, key_heads, preferred_element_type=jnp.float32
        )
        key_grad = key_grad + jnp.einsum(
            "hqk,qhd->khd", raw_grad, block, preferred_element_type=jnp.float32
        )
        return ((key_grad, value_grad), query_grad.reshape(rows, width))

    zeros = jnp.zeros(key_heads.shape, jnp.float32)
    (key_grad, value_grad), query_grad = lax.scan(
        one_block, (zeros, zeros), (query_heads, grad_heads, logsum, starts)
    )
    return (
        query_grad.reshape(total, width),
        key_grad.reshape(keys_low.shape[0], width),
        value_grad.reshape(values.shape[0], width),
    )


def attention_forward(params, prefix, query_rows, key_rows, allowed_fn):
    queries = (dot_plain(query_rows, params[prefix + "wq"]) + params[prefix + "bq"]).astype(
        jnp.bfloat16
    )
    keys_low = dot_plain(key_rows, params[prefix + "wk"]).astype(jnp.bfloat16)
    values = (dot_plain(key_rows, params[prefix + "wv"]) + params[prefix + "bv"]).astype(
        jnp.bfloat16
    )
    mixed, logsum = attend_forward(queries, keys_low, values, allowed_fn)
    output = dot_plain(mixed, params[prefix + "wo"]) + params[prefix + "bo"]
    return (output, (queries, keys_low, values, mixed, logsum))


def attention_backward(params, prefix, query_rows, key_rows, kept, out_grad, allowed_fn):
    queries, keys_low, values, mixed, logsum = kept
    out_round = out_grad.astype(jnp.bfloat16)
    mixed_grad = dot_right(out_round, params[prefix + "wo"]).astype(jnp.bfloat16)
    query_grad, key_grad, value_grad = attend_backward(
        queries, keys_low, values, logsum, mixed_grad, allowed_fn
    )
    query_round = query_grad.astype(jnp.bfloat16)
    key_round = key_grad.astype(jnp.bfloat16)
    value_round = value_grad.astype(jnp.bfloat16)
    grads = {
        prefix + "wq": dot_left(query_rows, query_round),
        prefix + "bq": jnp.sum(query_grad, axis=0),
        prefix + "wk": dot_left(key_rows, key_round),
        prefix + "wv": dot_left(key_rows, value_round),
        prefix + "bv": jnp.sum(value_grad, axis=0),
        prefix + "wo": dot_left(mixed, out_round),
        prefix + "bo": jnp.sum(out_grad, axis=0),
    }
    query_side = dot_right(query_round, params[prefix + "wq"])
    key_side = dot_right(key_round, params[prefix + "wk"]) + dot_right(
        value_round, params[prefix + "wv"]
    )
    return (grads, query_side, key_side)


def feed_forward(params, normed):
    pre = dot_plain(normed, params["fc1_weight"]) + params["fc1_bias"]
    activated = jax.nn.gelu(pre, approximate=False).astype(jnp.bfloat16)
    return (dot_plain(activated, params["fc2_weight"]) + params["fc2_bias"], (pre, activated))


def feed_backward(params, normed, kept, out_grad):
    pre, activated = kept
    out_round = out_grad.astype(jnp.bfloat16)
    act_grad = dot_right(out_round, params["fc2_weight"])
    unused, gelu_back = jax.vjp(partial(jax.nn.gelu, approximate=False), pre)
    pre_grad = gelu_back(act_grad)[0]
    pre_round = pre_grad.astype(jnp.bfloat16)
    grads = {
        "fc1_weight": dot_left(normed, pre_round),
        "fc1_bias": jnp.sum(pre_grad, axis=0),
        "fc2_weight": dot_left(activated, out_round),
        "fc2_bias": jnp.sum(out_grad, axis=0),
    }
    return (grads, dot_right(pre_round, params["fc1_weight"]))


def encoder_forward(params, frames):
    normed = norm_forward(params, "ln1", frames)
    attended, attend_kept = attention_forward(params, "att_", normed, normed, None)
    after = frames + attended
    normed_two = norm_forward(params, "ln2", after)
    fed, feed_kept = feed_forward(params, normed_two)
    return (after + fed, (normed, attend_kept, after, normed_two, feed_kept))


def encoder_backward(params, frames, kept, out_grad):
    normed, attend_kept, after, normed_two, feed_kept = kept
    grads, normed_grad = feed_backward(params, normed_two, feed_kept, out_grad)
    part, norm_grads = norm_backward(params, "ln2", after, normed_grad)
    grads.update(norm_grads)
    after_grad = out_grad + part
    attend_grads, query_side, key_side = attention_backward(
        params, "att_", normed, normed, attend_kept, after_grad, None
    )
    grads.update(attend_grads)
    part, norm_grads = norm_backward(params, "ln1", frames, query_side + key_side)
    grads.update(norm_grads)
    return (grads, after_grad + part)


def decoder_forward(params, tokens, memory_low, allowed_fn):
    normed = norm_forward(params, "ln1", tokens)
    attended, self_kept = attention_forward(params, "self_", normed, normed, allowed_fn)
    after = tokens + attended
    normed_two = norm_forward(params, "ln2", after)
    crossed, cross_kept = attention_forward(params, "cross_", normed_two, memory_low, None)
    after_two = after + crossed
    normed_three = norm_forward(params, "ln3", after_two)
    fed, feed_kept = feed_forward(params, normed_three)
    return (
        after_two + fed,
        (normed, self_kept, after, normed_two, cross_kept, after_two, normed_three, feed_kept),
    )


def decoder_backward(params, tokens, memory_low, kept, out_grad, allowed_fn):
    normed, self_kept, after, normed_two, cross_kept, after_two, normed_three, feed_kept = kept
    grads, normed_grad = feed_backward(params, normed_three, feed_kept, out_grad)
    part, norm_grads = norm_backward(params, "ln3", after_two, normed_grad)
    grads.update(norm_grads)
    after_two_grad = out_grad + part
    cross_grads, query_side, memory_grad = attention_backward(
        params, "cross_", normed_two, memory_low, cross_kept, after_two_grad, None
    )
    grads.update(cross_grads)
    part, norm_grads = norm_backward(params, "ln2", after, query_side)
    grads.update(norm_grads)
    after_grad = after_two_grad + part
    self_grads, query_side, key_side = attention_backward(
        params, "self_", normed, normed, self_kept, after_grad, allowed_fn
    )
    grads.update(self_grads)
    part, norm_grads = norm_backward(params, "ln1", tokens, query_side + key_side)
    grads.update(norm_grads)
    return (grads, after_grad + part, memory_grad)


def adamw(master, first, second, grad, factor, correction):
    clipped = grad * factor
    moment = 0.5 * first + 0.5 * clipped
    variance = 0.5 * second + 0.5 * clipped * clipped
    update = moment / correction / (jnp.sqrt(variance / correction) + 1e-08) + 0.01 * master
    weights = master - 0.02 * update
    return (weights, moment, variance, weights.astype(jnp.bfloat16))


def shards_native(
    encoder_input,
    decoder_input,
    segments,
    encoder_cotangent,
    decoder_cotangent,
    encoder_master,
    encoder_first,
    encoder_second,
    decoder_master,
    decoder_first,
    decoder_second,
    step_count,
):
    encoder_plan = encoder_layout(D, FF)
    decoder_plan = decoder_layout(D, FF)
    encoder_params = unpack(
        lax.all_gather(encoder_master.astype(jnp.bfloat16), ("wide", "narrow"), axis=0, tiled=True),
        encoder_plan,
    )
    frames = encoder_input[0].astype(jnp.float32)
    memory, encoder_kept = encoder_forward(encoder_params, frames)
    memory_low = memory.astype(jnp.bfloat16)
    decoder_params = unpack(
        lax.all_gather(decoder_master.astype(jnp.bfloat16), ("wide", "narrow"), axis=0, tiled=True),
        decoder_plan,
    )
    tokens = decoder_input[0].astype(jnp.float32)
    segment_row = segments[0]
    length = segment_row.shape[0]

    def allowed_fn(start, count):
        places = start + jnp.arange(count, dtype=jnp.int32)
        row_segments = lax.dynamic_slice_in_dim(segment_row, start, count)
        columns = jnp.arange(length, dtype=jnp.int32)
        return (row_segments[:, None] == segment_row[None, :]) & (
            columns[None, :] <= places[:, None]
        )

    decoded, decoder_kept = decoder_forward(decoder_params, tokens, memory_low, allowed_fn)
    decoder_again = unpack(
        lax.all_gather(decoder_master.astype(jnp.bfloat16), ("wide", "narrow"), axis=0, tiled=True),
        decoder_plan,
    )
    decoder_grads, token_grad, memory_grad = decoder_backward(
        decoder_again,
        tokens,
        memory_low,
        decoder_kept,
        decoder_cotangent[0].astype(jnp.float32),
        allowed_fn,
    )
    decoder_total = pack(decoder_grads, decoder_plan)
    decoder_owned = lax.psum_scatter(
        decoder_total, ("wide", "narrow"), scatter_dimension=0, tiled=True
    )
    encoder_again = unpack(
        lax.all_gather(encoder_master.astype(jnp.bfloat16), ("wide", "narrow"), axis=0, tiled=True),
        encoder_plan,
    )
    memory_total = encoder_cotangent[0].astype(jnp.float32) + memory_grad
    encoder_grads, frame_grad = encoder_backward(encoder_again, frames, encoder_kept, memory_total)
    encoder_total = pack(encoder_grads, encoder_plan)
    encoder_owned = lax.psum_scatter(
        encoder_total, ("wide", "narrow"), scatter_dimension=0, tiled=True
    )
    local_squares = jnp.sum(encoder_owned * encoder_owned) + jnp.sum(decoder_owned * decoder_owned)
    gradient_norm = jnp.sqrt(lax.psum(local_squares, ("wide", "narrow")))
    factor = 1.0 / jnp.maximum(gradient_norm, 1.0)
    correction = 1.0 - jnp.power(0.5, step_count.astype(jnp.float32))
    encoder_new = adamw(
        encoder_master, encoder_first, encoder_second, encoder_owned, factor, correction
    )
    decoder_new = adamw(
        decoder_master, decoder_first, decoder_second, decoder_owned, factor, correction
    )
    return (
        memory_low[None],
        decoded.astype(jnp.bfloat16)[None],
        frame_grad[None],
        token_grad[None],
        gradient_norm,
        encoder_new[0],
        encoder_new[1],
        encoder_new[2],
        encoder_new[3],
        decoder_new[0],
        decoder_new[1],
        decoder_new[2],
        decoder_new[3],
    )


def shards(
    encoder_input,
    decoder_input,
    segments,
    encoder_cotangent,
    decoder_cotangent,
    encoder_master,
    encoder_first,
    encoder_second,
    decoder_master,
    decoder_first,
    decoder_second,
    step_count,
):
    n = 32
    weights, vectors, *kept, early = forward_pass(
        encoder_master, decoder_master, encoder_input[0], decoder_input[0], segments, decoder_cotangent[0], n
    )
    encoder_flat, decoder_flat, norm, frame_grad, token_grad, decoded = backward_pass(
        weights, vectors, kept, early, encoder_input[0], decoder_input[0], encoder_cotangent[0], decoder_cotangent[0], segments, n
    )
    gradient_norm = norm[0, 0]
    factor = 1.0 / jnp.maximum(gradient_norm, 1.0)
    correction = 1.0 - jnp.power(0.5, step_count.astype(jnp.float32))
    encoder_owned = encoder_flat.reshape(-1)[: encoder_master.shape[0]]
    decoder_owned = decoder_flat.reshape(-1)[: decoder_master.shape[0]]
    encoder_new = adamw(encoder_master, encoder_first, encoder_second, encoder_owned, factor, correction)
    decoder_new = adamw(decoder_master, decoder_first, decoder_second, decoder_owned, factor, correction)
    return (
        kept[10][None],
        decoded[None],
        frame_grad[None],
        token_grad[None],
        gradient_norm,
        *encoder_new,
        *decoder_new,
    )


def solution(mesh):
    placed = (
        P(("wide", "narrow"), None, None),
        P(("wide", "narrow"), None, None),
        P(("wide", "narrow"), None),
        P(("wide", "narrow"), None, None),
        P(("wide", "narrow"), None, None),
        P(("wide", "narrow")),
        P(("wide", "narrow")),
        P(("wide", "narrow")),
        P(("wide", "narrow")),
        P(("wide", "narrow")),
        P(("wide", "narrow")),
        P(),
    )
    return jax.shard_map(
        shards if tuple(mesh.shape.values()) == (8, 4) else shards_native,
        mesh=mesh,
        in_specs=placed,
        out_specs=(
            P(("wide", "narrow"), None, None),
            P(("wide", "narrow"), None, None),
            P(("wide", "narrow"), None, None),
            P(("wide", "narrow"), None, None),
            P(),
            P(("wide", "narrow")),
            P(("wide", "narrow")),
            P(("wide", "narrow")),
            P(("wide", "narrow")),
            P(("wide", "narrow")),
            P(("wide", "narrow")),
            P(("wide", "narrow")),
            P(("wide", "narrow")),
        ),
        check_vma=False,
    )
```

```python
from functools import partial

import jax
import jax.numpy as jnp
from jax import lax
from jax.experimental import pallas as pl
from jax.experimental.pallas import tpu as pltpu
from jax.sharding import PartitionSpec as P

D = 768
HEAD_DIM = 64
FF = 3072
MESH = pl.DeviceIdType.MESH
BF = jnp.bfloat16
F32 = jnp.float32

N_MAT = 28
N_PAIR = 14
UNIT = 48
LANES = 128
UROWS = UNIT * D // LANES
BIG = 4 * UROWS
FRONT = BIG + 8
BACK = BIG + 8
N_VEC = 29
F_AT = (1, 2, 4, 5)
B_AT = (1, 3, 5, 8)
AHEAD = 3


class Block:
    def __init__(self, small, gaps, fc1, vectors, first_mat, small_mats, total):
        self.small = small
        self.gaps = gaps
        self.fc1 = fc1
        self.vectors = vectors
        self.first_mat = first_mat
        self.small_mats = small_mats
        self.total = total


ENC = Block(
    small=8,
    gaps=((0, 2), (1, 1), (3, 1), (4, 3072 + 7)),
    fc1=3079,
    vectors=[0, 1, 770, 2307, 3076, 3077, 3078, 6151, 6152, 6153, 6154, 9227],
    first_mat=0,
    small_mats=4,
    total=9228,
)
DEC = Block(
    small=12,
    gaps=((0, 2), (1, 1), (3, 1), (4, 3), (5, 1), (7, 1), (8, 3072 + 7)),
    fc1=6156,
    vectors=[0, 1, 770, 2307, 3076, 3077, 3078, 3847, 5384, 6153, 6154, 6155, 9228, 9229, 9230, 9231, 12304],
    first_mat=12,
    small_mats=8,
    total=12305,
)
BLOCKS = (ENC, DEC)


def sizes(block, n):
    shard = block.total * D // n
    rows = -(-shard // 1024) * 8
    top = (shard + LANES - 1) // LANES
    return shard, rows, (top + UROWS) // UROWS + 1, (top + BIG) // BIG + 1


def small_row(block, m):
    row = m * D
    for at, gap in block.gaps:
        row = row + jnp.where(m >= at, gap, 0) if at > 0 else row + gap
    return row


def mat_of(block, m):
    return block.first_mat + m + jnp.where(m >= block.small_mats, 4, 0)


def static_unit_rows(block):
    out = []
    for m in range(block.small):
        row = m * D + sum(gap for at, gap in block.gaps if m >= at)
        out.append((block.first_mat + m + (4 if m >= block.small_mats else 0), row))
    return out


def whoami():
    wide, narrow = lax.axis_index("wide"), lax.axis_index("narrow")
    return wide, narrow, wide // 2, wide % 2, narrow // 2, narrow % 2


def device(z, x, y, c):
    return (z * 2 + x, y * 2 + c)


def flat_device(d):
    return (d // 4, d % 4)


def greet(me, n):
    bar = pltpu.get_barrier_semaphore()

    def signal(i, carry):
        pl.semaphore_signal(bar, inc=1, device_id=flat_device((me + i) % n), device_id_type=MESH)
        return carry

    lax.fori_loop(1, n, signal, 0)


def await_all(n):
    pl.semaphore_wait(pltpu.get_barrier_semaphore(), n - 1)


def each_small(block, n, me, slots, body, least=0, most=99):
    shard = sizes(block, n)[0]
    low = me * shard
    low_row = low // LANES
    first = 0
    for _, row in static_unit_rows(block):
        first = first + jnp.minimum(jnp.maximum(low - row * D, 0) // (UROWS * LANES), 16)

    def step(j, carry):
        g = first + j
        m, u = g // 16, g % 16
        start = small_row(block, m) * 6 + u * UROWS
        pos = start - low_row

        @pl.when((g < 16 * min(block.small, most)) & (g >= 16 * least) & (start * LANES < low + shard))
        def _():
            body((pos + UROWS) // UROWS, mat_of(block, m), u, pos, start * LANES)

        return carry

    lax.fori_loop(0, slots, step, 0)


def each_big(block, n, me, slots, body):
    shard = sizes(block, n)[0]
    low = me * shard
    low_row = low // LANES
    first = jnp.minimum(jnp.maximum(low - block.fc1 * D, 0) // (BIG * LANES), 16)

    def step(j, carry):
        u = first + j
        start = block.fc1 * 6 + u * BIG
        pos = start - low_row

        @pl.when((u < 16) & (start * LANES < low + shard) & (start * LANES + BIG * LANES > low))
        def _():
            body((pos + BIG) // BIG, u, pos, start * LANES)

        return carry

    lax.fori_loop(0, slots, step, 0)


def each_vector(block, n, me, first_vec, body):
    shard = sizes(block, n)[0]
    low = me * shard
    low_row = low // LANES
    for i, row in enumerate(block.vectors):
        @pl.when((row * D < low + shard) & (row * D + D > low))
        def _(i=i, row=row):
            body(first_vec + i, row * 6 - low_row, row * D)


def peers(axis, at):
    if axis == "z":
        return [dict(at, z=(at["z"] + k) % 4) for k in (1, 2, 3)]
    return [dict(at, **{axis: 1 - at[axis]})]


def first_peer(at):
    x, y, c = at["x"], at["y"], at["c"]
    return device(at["z"], x + (1 - c) * (1 - 2 * x), y + c * (1 - 2 * y), c)


def second_peer(at):
    x, y, c = at["x"], at["y"], at["c"]
    return device(at["z"], x + c * (1 - 2 * x), y + (1 - c) * (1 - 2 * y), c)


def dev(at):
    return device(at["z"], at["x"], at["y"], at["c"])


def gather_kernel(
    n, on_start, on_vectors, on_pair, on_last, xe_ref, xd_ref, w_ref, v_ref,
    re_ref, rd_ref, se_ref, sd_ref, be_ref, bd_ref, sv_ref, land, landv, own, ownv,
    s_small, s_big, s_vec, r_unit, r_vec, s_zxy, r_zxy, s_core, r_core, s_own, v_send, v_recv,
):
    wide, narrow, z, x, y, c = whoami()
    me = wide * 4 + narrow
    chip = me // 2
    at = dict(z=z, x=x, y=y, c=c)
    greet(me, n)
    lanes = lax.broadcasted_iota(jnp.int32, (1, LANES), 1)
    fields = {
        ENC: (xe_ref, re_ref, se_ref, be_ref, 0, 0, 0),
        DEC: (xd_ref, rd_ref, sd_ref, bd_ref, sizes(ENC, n)[2], sizes(ENC, n)[3], len(ENC.vectors)),
    }

    def prepare(block):
        x_ref, r_ref = fields[block][:2]
        shard, rows, _, _ = sizes(block, n)
        step = 8 * max(k for k in range(1, 40) if (rows // 8) % k == 0)

        def turn(i, carry):
            at_row = pl.multiple_of(i * step, 8)
            r_ref[pl.ds(FRONT + at_row, step), :] = pltpu.roll(
                x_ref[pl.ds(at_row, step), :], (me * shard) % LANES, 1
            )
            return carry

        lax.fori_loop(0, rows // step, turn, 0)

    def load_rows(block, row, count, stride=None):
        r_ref = fields[block][1]
        at_row = FRONT + row
        if stride is None:
            here, before = r_ref[pl.ds(at_row, count), :], r_ref[pl.ds(at_row - 1, count), :]
        else:
            here = r_ref[pl.ds(at_row, count, stride=stride), :]
            before = r_ref[pl.ds(at_row - 1, count, stride=stride), :]
        return jnp.where(lanes >= (me * sizes(block, n)[0]) % LANES, here, before)

    def send(src, dst, send_sem, recv_sem, target):
        @pl.when(target == me)
        def _():
            pltpu.make_async_copy(src, dst, send_sem).start()

        @pl.when(target != me)
        def _():
            pltpu.make_async_remote_copy(
                src, dst, send_sem, recv_sem, device_id=flat_device(target), device_id_type=MESH
            ).start()

    def which_of(block, start):
        return jnp.where(start // sizes(block, n)[0] == me, 0, 1)

    def small_units(block, least, most):
        s_ref, small0 = fields[block][2], fields[block][4]

        def body(slot, mat, u, pos, start):
            for k in range(6):
                s_ref[slot, :, k * LANES : (k + 1) * LANES] = load_rows(block, pos + k, UNIT, 6).astype(BF)
            which = which_of(block, start)
            send(
                s_ref.at[slot], land.at[which, mat // 2], s_small.at[small0 + slot], r_unit.at[which, mat // 2],
                u * 2 + mat % 2,
            )

        each_small(block, n, me, sizes(block, n)[2], body, least, most)

    def big_units(block):
        b_ref, big0 = fields[block][3], fields[block][5]
        pair = (block.first_mat + block.small_mats) // 2

        def body(slot, u, pos, start):
            for q in range(4):
                for k in range(6):
                    b_ref[slot, q % 2, q // 2, :, k * LANES : (k + 1) * LANES] = load_rows(
                        block, pos + 6 * q + k, UNIT, 24
                    ).astype(BF)
            which = which_of(block, start)
            for core in range(2):
                send(
                    b_ref.at[slot, core], land.at[which, pl.ds(pair, 2)], s_big.at[big0 + slot, core],
                    r_unit.at[which, pair], u * 2 + core,
                )

        each_big(block, n, me, sizes(block, n)[3], body)

    def vector_units(block):
        def body(v, pos, start):
            sv_ref[v] = load_rows(block, pos, 8).astype(BF).astype(F32)
            which = which_of(block, start)
            send(sv_ref.at[v], landv.at[which], s_vec.at[v], r_vec.at[which], v)

        each_vector(block, n, me, fields[block][6], body)

    def pair_units(pair):
        block = ENC if pair < 6 else DEC
        local = pair - block.first_mat // 2
        half = block.small_mats // 2
        if local == half:
            big_units(block)
        elif local != half + 1:
            first = 2 * local - (4 if local > half else 0)
            small_units(block, first, first + 2)

    prepare(ENC)
    await_all(n)
    pair_units(0)
    vector_units(ENC)
    prepare(DEC)
    vector_units(DEC)
    for pair in range(1, AHEAD):
        pair_units(pair)

    def of_self(first, last, which):
        return jnp.where(which == 0, first, last) == me

    def arrive_unit(first, last, src, dst, local_sem, recv):
        for which, holder in ((0, first), (1, last)):
            needed = True if which == 0 else (first != last)

            @pl.when(needed & (holder == me))
            def _(which=which):
                pltpu.make_async_copy(src(which), dst(which), local_sem).wait()

            @pl.when(needed & (holder != me))
            def _(which=which):
                pltpu.make_async_copy(src(which), dst(which), recv(which)).wait()

    def vec_of(v):
        n_enc = len(ENC.vectors)
        rows = ENC.vectors + DEC.vectors
        start = 0
        before = 0
        for i, row in enumerate(rows):
            start = start + jnp.where(v >= i, row - before, 0)
            before = row
        return start * D, jnp.where(v < n_enc, sizes(ENC, n)[0], sizes(DEC, n)[0])

    @pl.when(me < N_VEC)
    def _():
        start, shard = vec_of(me)
        first, last = start // shard, (start + D - 1) // shard
        arrive_unit(
            first, last, lambda w: sv_ref.at[0], lambda w: landv.at[w], s_vec.at[me], lambda w: r_vec.at[w]
        )
        at_elem = lax.broadcasted_iota(jnp.int32, (8, LANES), 0) * LANES + lax.broadcasted_iota(jnp.int32, (8, LANES), 1)
        ownv[...] = jnp.where(at_elem < (first + 1) * shard - start, landv[0], landv[1])

    @pl.when(me >= N_VEC)
    def _():
        ownv[...] = jnp.zeros_like(ownv)

    pltpu.sync_copy(ownv, v_ref.at[z, x, y, c])
    vorder = ("z", "x", "y", "c")

    def vview(done):
        have = set(vorder[:done])
        return tuple(slice(None) if a in have else at[a] for a in "zxyc")

    def vcopies(phase):
        axis = vorder[phase]
        out = []
        for k, p in enumerate(peers(axis, at)):
            ref = v_ref.at[vview(phase)]
            slot = phase if axis == "z" else phase + 2
            out.append(
                pltpu.make_async_remote_copy(
                    ref, ref, v_send.at[slot + k], v_recv.at[slot + k], device_id=dev(p), device_id_type=MESH
                )
            )
        return out

    row_i = lax.broadcasted_iota(jnp.int32, (UNIT, D), 0)
    col_i = lax.broadcasted_iota(jnp.int32, (UNIT, D), 1)

    def merge(pair):
        block = ENC if pair < 6 else DEC
        shard = sizes(block, n)[0]
        local = pair - block.first_mat // 2
        half = block.small_mats // 2
        if half <= local < half + 2:
            start = (block.fc1 * 6 + chip * BIG) * LANES
            elem = row_i * FF + (2 * (local - half) + c) * D + col_i
            length = BIG * LANES
        else:
            small = 2 * local - (4 if local >= half + 2 else 0) + c
            start = (small_row(block, small) * 6 + chip * UROWS) * LANES
            elem = row_i * D + col_i
            length = UROWS * LANES
        first, last = start // shard, (start + length - 1) // shard
        if half <= local < half + 2:
            if local == half:
                low_row = me * shard // LANES
                slot = (start // LANES - low_row + BIG) // BIG + (0 if block is ENC else sizes(ENC, n)[3])
                slot = jnp.minimum(jnp.maximum(slot, 0), sizes(ENC, n)[3] + sizes(DEC, n)[3] - 1)
                arrive_unit(
                    first, last, lambda w: land.at[w, pl.ds(pair, 2)], lambda w: land.at[w, pl.ds(pair, 2)],
                    s_big.at[slot, c], lambda w: r_unit.at[w, pair],
                )
        else:
            low_row = me * shard // LANES
            slot = (start // LANES - low_row + UROWS) // UROWS + (0 if block is ENC else sizes(ENC, n)[2])
            slot = jnp.minimum(jnp.maximum(slot, 0), sizes(ENC, n)[2] + sizes(DEC, n)[2] - 1)
            arrive_unit(
                first, last, lambda w: land.at[w, pair], lambda w: land.at[w, pair],
                s_small.at[slot], lambda w: r_unit.at[w, pair],
            )
        own[pair] = jnp.where(elem < (first + 1) * shard - start, land[0, pair], land[1, pair])

    def own_place(pair):
        return w_ref.at[pair, c, z, x, y]

    def remote(src, dst, pair, k, target):
        return pltpu.make_async_remote_copy(
            src, dst, s_zxy.at[pair, k], r_zxy.at[pair, k], device_id=target, device_id_type=MESH
        )

    def copies(pair, phase):
        if phase == 0:
            return [
                remote(own.at[pair], own_place(pair), pair, 2 + k, device((z + k) % 4, x, y, c)) for k in (1, 2, 3)
            ]
        if phase == 1:
            ref = w_ref.at[pair, c, :, x, y]
            return [remote(ref, ref, pair, 0, first_peer(at))]
        if phase == 2:
            ref = w_ref.at[pair, c, :, :, y]
            return [remote(ref, ref, pair, 1, second_peer(at))]
        ref = w_ref.at[pair, c]
        return [remote(ref, ref, pair, 2, device(z, x, y, 1 - c))]

    def begin(pair, phase):
        if phase != 2:
            for cp in copies(pair, phase):
                cp.start()
            return

        @pl.when(c == 0)
        def _():
            copies(pair, 2)[0].start()

        @pl.when(c == 1)
        def _():
            ref = w_ref.at[pair, c, :, x]
            remote(ref, ref, pair, 1, second_peer(at)).start()

    for t in range(N_PAIR + F_AT[3]):
        if t < N_PAIR:
            merge(t)
            pltpu.make_async_copy(own.at[t], own_place(t), s_own.at[t]).start()
            begin(t, 0)
        for phase in (1, 2, 3):
            pair = t - F_AT[phase - 1]
            if 0 <= pair < N_PAIR:
                if phase == 1:
                    pltpu.make_async_copy(own.at[pair], own_place(pair), s_own.at[pair]).wait()
                for cp in copies(pair, phase - 1):
                    cp.wait_recv()
                begin(pair, phase)
        if t + AHEAD < N_PAIR:
            pair_units(t + AHEAD)
        if t == 1:
            on_start()
        if t < 5:
            if t > 0:
                for cp in vcopies(t - 1):
                    cp.wait_recv()
            if t < 4:
                for cp in vcopies(t):
                    cp.start()
            else:
                on_vectors()
        pair = t - F_AT[3]
        if pair == N_PAIR - 1:
            on_last()
        if 0 <= pair < N_PAIR:
            for cp in copies(pair, 3):
                cp.wait_recv()
            on_pair(pair)

    for phase in range(4):
        for cp in vcopies(phase):
            cp.wait_send()
    for pair in range(N_PAIR):
        for phase in range(4):
            for cp in copies(pair, phase):
                cp.wait_send()
    for b, (block, s_ref, b_ref) in enumerate(((ENC, se_ref, be_ref), (DEC, sd_ref, bd_ref))):
        shard, rows, n_small, n_big = sizes(block, n)
        small0 = 0 if b == 0 else sizes(ENC, n)[2]
        big0 = 0 if b == 0 else sizes(ENC, n)[3]

        def small_wait(slot, mat, u, pos, start, s_ref=s_ref, small0=small0):
            @pl.when(u * 2 + mat % 2 != me)
            def _():
                pltpu.make_async_copy(s_ref.at[slot], s_ref.at[slot], s_small.at[small0 + slot]).wait()

        def big_wait(slot, u, pos, start, b_ref=b_ref, big0=big0):
            for core in range(2):
                @pl.when(u * 2 + core != me)
                def _(core=core):
                    pltpu.make_async_copy(
                        b_ref.at[slot, core], b_ref.at[slot, core], s_big.at[big0 + slot, core]
                    ).wait()

        def vec_wait(v, pos, start):
            @pl.when(me != v)
            def _():
                pltpu.make_async_copy(sv_ref.at[v], sv_ref.at[v], s_vec.at[v]).wait()

        each_vector(block, n, me, 0 if b == 0 else len(ENC.vectors), vec_wait)
        each_small(block, n, me, n_small, small_wait)
        each_big(block, n, me, n_big, big_wait)


def rows_of(flat, rows):
    return jnp.pad(flat, (0, rows * LANES - flat.shape[0])).reshape(rows, LANES)


SCALE = HEAD_DIM ** (-0.5)
FORBID = -1000000000.0
ROOT_HALF = 0.7071067811865476
PDF = 0.3989422804014327


def mm(a, b):
    return jnp.dot(a, b, preferred_element_type=F32)


def mm_nt(a, b):
    return lax.dot_general(a, b, (((1,), (1,)), ((), ())), preferred_element_type=F32)


def mm_tn(a, b):
    return lax.dot_general(a, b, (((0,), (0,)), ((), ())), preferred_element_type=F32)


def col_blocks(body, width=256):
    def step(j, carry):
        body(pl.ds(pl.multiple_of(j * width, width), width))
        return carry

    lax.fori_loop(0, D // width, step, 0)


def row_blocks(rows, body, height=64):
    def step(i, carry):
        body(pl.ds(pl.multiple_of(i * height, height), height))
        return carry

    lax.fori_loop(0, rows // height, step, 0)


def linear(x_ref, w_ref, rows, out_ref, bias=None):
    x = x_ref[0:rows, :]

    def body(cols):
        y = mm(x, w_ref[:, cols])
        if bias is not None:
            y = y + bias[:, cols]
        out_ref[0:rows, cols] = y.astype(out_ref.dtype)

    col_blocks(body)


def norm_rows(x):
    centred = x - jnp.mean(x, axis=1, keepdims=True)
    spread = jnp.mean(centred * centred, axis=1, keepdims=True)
    root = lax.rsqrt(spread + 1e-05)
    return centred * root, root


def norm_forward_ref(x_ref, gain, shift, rows, out_ref):
    def body(r):
        hat, _ = norm_rows(x_ref[r, :].astype(F32))
        out_ref[r, :] = (hat * gain[...] + shift[...]).astype(BF)

    row_blocks(rows, body)


def attend_tiles(rows, keys, causal):
    return [(start, min(start + 128, keys) if causal else keys) for start in range(0, rows, 128)]


def both_heads(x):
    lane = lax.broadcasted_iota(jnp.int32, (1, LANES), 1)
    zero = jnp.zeros_like(x)
    return jnp.concatenate([jnp.where(lane < HEAD_DIM, x, zero), jnp.where(lane < HEAD_DIM, zero, x)], axis=0)


def scores_of(k, q2, mask_ref, start, reach):
    scores = mm_nt(k, q2)
    if mask_ref is not None:
        mask = mask_ref[0:reach, start : start + LANES]
        scores = jnp.where(jnp.concatenate([mask, mask], axis=1) > 0, scores, FORBID)
    return scores


def attention_forward_ref(q_ref, k_ref, v_ref, mask_ref, rows, keys, mixed_ref, lse_ref):
    def pair_of_heads(i, carry):
        cols = pl.ds(pl.multiple_of(i * LANES, LANES), LANES)
        v_turned = jnp.transpose(v_ref[0:keys, cols])
        for tile, (start, reach) in enumerate(attend_tiles(rows, keys, mask_ref is not None)):
            r = slice(start, start + LANES)
            q2 = both_heads(q_ref[r, cols] * jnp.asarray(SCALE, BF))
            scores = scores_of(k_ref[0:reach, cols], q2, mask_ref, start, reach)
            peak = jnp.max(scores, axis=0, keepdims=True)
            weights = jnp.exp(scores - peak)
            totals = jnp.sum(weights, axis=0, keepdims=True)
            probs = weights.astype(BF)
            share = 1.0 / totals
            mixed = jnp.concatenate(
                [
                    mm(v_turned[s * HEAD_DIM : (s + 1) * HEAD_DIM, 0:reach], probs[:, s * LANES : (s + 1) * LANES])
                    * share[:, s * LANES : (s + 1) * LANES]
                    for s in range(2)
                ],
                axis=0,
            )
            mixed_ref[r, cols] = jnp.transpose(mixed).astype(BF)
            lse_ref[tile, pl.ds(i, 1), :] = peak + jnp.log(totals)
        return carry

    lax.fori_loop(0, D // LANES, pair_of_heads, 0, unroll=1 if mask_ref is not None else 2)


def project_add(x_ref, mixed_ref, w_ref, bias, rows, out_ref):
    m = mixed_ref[0:rows, :]

    def body(cols):
        out_ref[0:rows, cols] = x_ref[0:rows, cols].astype(F32) + mm(m, w_ref[:, cols]) + bias[:, cols]

    col_blocks(body)


def gelu_block(n_ref, w_ref, bias, rows, block, act_ref, slope_ref):
    x = n_ref[0:rows, :]

    def body(cols):
        pre = mm(x, w_ref[:, cols]) + bias[:, cols]
        bell = 0.5 * (1.0 + lax.erf(pre * ROOT_HALF))
        act_ref[block, 0:rows, cols] = (pre * bell).astype(BF)
        slope_ref[block, 0:rows, cols] = (bell + pre * (PDF * jnp.exp(-0.5 * pre * pre))).astype(BF)

    col_blocks(body, 128)


def accumulate(a_ref, w_ref, rows, out_ref):
    a = a_ref[0:rows, :]

    def body(cols):
        out_ref[0:rows, cols] += mm(a, w_ref[:, cols])

    col_blocks(body)


def add_row(out_ref, x_ref, row_ref, r):
    out_ref[r, :] = x_ref[r, :] + row_ref[...]


def both(body):
    def step(k, carry):
        body(k)
        return carry

    lax.fori_loop(0, 2, step, 0)


N_SAVED = 28


def saved_shapes(rows, frames):
    tall = -(-rows // 128) * 128
    enc_lse, dec_lse = ((frames // 128, 8, 2 * LANES), F32), ((tall // 128, 8, 2 * LANES), F32)
    return (
        [((frames, D), BF)] * 5
        + [enc_lse, ((frames, D), F32), ((frames, D), BF), ((4, frames, D), BF), ((4, frames, D), BF), ((frames, D), BF)]
        + [((rows, D), BF)]
        + [((tall, D), BF)] * 4
        + [dec_lse, ((rows, D), F32), ((rows, D), BF)]
        + [((tall, D), BF), ((frames, D), BF), ((frames, D), BF), ((tall, D), BF), dec_lse]
        + [((rows, D), F32), ((rows, D), BF), ((4, rows, D), BF), ((4, rows, D), BF)]
    )


def make_mask(seg_ref, row_ref, col_ref, mask_ref):
    rows, tall = seg_ref.shape[1], mask_ref.shape[0]
    row_ref[...] = jnp.full(row_ref.shape, -1.0, F32)
    row_ref[0:1, 0:rows] = seg_ref[...].astype(F32)
    for i in range(tall // LANES):
        part = slice(i * LANES, (i + 1) * LANES)
        col_ref[part, :] = jnp.transpose(jnp.broadcast_to(row_ref[0:1, part], (LANES, LANES)))

    def body(r):
        key = lax.broadcasted_iota(jnp.int32, (64, tall), 0) + r.start
        query = lax.broadcasted_iota(jnp.int32, (64, tall), 1)
        allowed = (col_ref[r, 0:1] == row_ref[0:1, :]) & (key <= query)
        mask_ref[r, :] = jnp.where(allowed, 1.0, 0.0)

    row_blocks(tall, body)


def forward_kernel(n, rows, frames, *refs):
    xe_ref, xd_ref, ein_ref, din_ref, seg_ref, dcot_ref, w_ref, v_ref = refs[:8]
    outs, refs = refs[8 : 8 + N_SAVED], refs[8 + N_SAVED :]
    early_ref, refs = refs[0], refs[1:]
    comm, refs = refs[:24], refs[24:]
    bufs, refs = refs[:N_SAVED], refs[N_SAVED:]
    vv, wbuf, acc, mask_ref, seg_row, seg_col, s_save, s_w, cot, gown, gsum, s_g, r_g, s_early = refs
    _, _, z, x, y, c = whoami()
    (
        e_n1, e_q, e_k, e_v, e_mix, e_lse, e_after, e_n2, e_act, e_slope, e_out,
        d_n1, d_q, d_k, d_v, d_mix, d_lse, d_after, d_n2,
        c_q, c_k, c_v, c_mix, c_lse, d_after2, d_n3, d_act, d_slope,
    ) = bufs
    eacc = acc.at[0:frames]

    def vec(i):
        return vv.at[pl.ds(i, 1)]

    def save(*indices):
        for i in indices:
            pltpu.make_async_copy(bufs[i], outs[i], s_save.at[i]).start()

    def cot_copy():
        return pltpu.make_async_copy(dcot_ref, cot, s_early.at[0])

    def early_core(i):
        return pltpu.make_async_remote_copy(
            gown.at[i, 1 - c], gsum.at[i], s_g.at[i], r_g.at[i], device_id=device(z, x, y, 1 - c), device_id_type=MESH
        )

    def early_save(i):
        return pltpu.make_async_copy(gsum.at[i], early_ref.at[i], s_early.at[i])

    def early_grad(i):
        both(lambda k: weight_grad(d_act.at[2 - 2 * i + k], cot, rows, gown.at[i, k]))
        early_core(i).start()

    def early_sum(i):
        early_core(i).wait_recv()

        def body(j, carry):
            a, b = j // 2, j % 2
            for k in range(2):
                gsum[i, a, b, k] = (gsum[i, a, b, k].astype(F32) + gown[i, c, a, b, k].astype(F32)).astype(BF)
            return carry

        lax.fori_loop(0, 8, body, 0)
        early_save(i).start()

    def on_last():
        early_sum(0)

    def on_start():
        cot_copy().start()
        make_mask(seg_ref, seg_row, seg_col, mask_ref)
        for ref in (d_q, d_k, d_v, c_q):
            if ref.shape[0] > rows:
                ref[rows:, :] = jnp.zeros((ref.shape[0] - rows, D), BF)
        for ref in (e_lse, d_lse, c_lse):
            ref[...] = jnp.zeros_like(ref)

    def on_vectors():
        pltpu.sync_copy(v_ref, vv_tiles)
        for i in range(N_VEC):
            for k in range(6):
                vv[i : i + 1, k * LANES : (k + 1) * LANES] = vv_tiles[i // 8, i // 4 % 2, i // 2 % 2, i % 2, k : k + 1, :]

    def on_pair(pair):
        if pair == 12:
            early_grad(0)
            early_sum(1)
        if pair > 11:
            return
        cps = [pltpu.make_async_copy(w_ref.at[pair, k].reshape(D, D), wbuf.at[k], s_w.at[k]) for k in range(2)]
        for cp in cps:
            cp.start()
        if pair == 0:
            norm_forward_ref(ein_ref, vec(0), vec(1), frames, e_n1)
        if pair == 6:
            norm_forward_ref(din_ref, vec(12), vec(13), rows, d_n1)
        if pair == 11:
            cot_copy().wait()
            early_grad(1)
        cps[0].wait()
        w0 = wbuf.at[0]
        if pair in (2, 3, 4, 5, 10, 11):
            cps[1].wait()

        def second():
            cps[1].wait()
            return wbuf.at[1]

        if pair == 0:
            linear(e_n1, w0, frames, e_q, vec(2))
            linear(e_n1, second(), frames, e_k)
            save(0, 1, 2)
        elif pair == 1:
            linear(e_n1, w0, frames, e_v, vec(3))
            attention_forward_ref(e_q, e_k, e_v, None, frames, frames, e_mix, e_lse)
            project_add(ein_ref, e_mix, second(), vec(4), frames, e_after)
            norm_forward_ref(e_after, vec(5), vec(6), frames, e_n2)
            save(3, 4, 5, 6, 7)
        elif pair in (2, 3):
            both(lambda k: gelu_block(
                e_n2, wbuf.at[k], vec(7 + 2 * (pair - 2) + k), frames, 2 * (pair - 2) + k, e_act, e_slope
            ))
            if pair == 3:
                save(8, 9)
        elif pair in (4, 5):
            if pair == 4:
                eacc[...] = e_after[...] + vec(11)[...]
            both(lambda k: accumulate(e_act.at[2 * (pair - 4) + k], wbuf.at[k], frames, eacc))
            if pair == 5:
                e_out[...] = eacc[...].astype(BF)
                save(10)
        elif pair == 6:
            linear(d_n1, w0, rows, d_q, vec(14))
            linear(d_n1, second(), rows, d_k)
            save(11, 12, 13)
        elif pair == 7:
            linear(d_n1, w0, rows, d_v, vec(15))
            attention_forward_ref(d_q, d_k, d_v, mask_ref, d_q.shape[0], d_k.shape[0], d_mix, d_lse)
            project_add(din_ref, d_mix, second(), vec(16), rows, d_after)
            norm_forward_ref(d_after, vec(17), vec(18), rows, d_n2)
            save(14, 15, 16, 17, 18)
        elif pair == 8:
            linear(d_n2, w0, rows, c_q, vec(19))
            linear(e_out, second(), frames, c_k)
            save(19, 20)
        elif pair == 9:
            linear(e_out, w0, frames, c_v, vec(20))
            attention_forward_ref(c_q, c_k, c_v, None, c_q.shape[0], frames, c_mix, c_lse)
            project_add(d_after, c_mix, second(), vec(21), rows, d_after2)
            norm_forward_ref(d_after2, vec(22), vec(23), rows, d_n3)
            save(21, 22, 23, 24, 25)
        elif pair in (10, 11):
            both(lambda k: gelu_block(
                d_n3, wbuf.at[k], vec(24 + 2 * (pair - 10) + k), rows, 2 * (pair - 10) + k, d_act, d_slope
            ))
            if pair == 11:
                save(26, 27)

    vv_tiles = comm[-1]
    gather_kernel(n, on_start, on_vectors, on_pair, on_last, xe_ref, xd_ref, w_ref, v_ref, *comm[:-1])
    for i in range(N_SAVED):
        pltpu.make_async_copy(bufs[i], outs[i], s_save.at[i]).wait()
    for i in range(2):
        early_core(i).wait_send()
        early_save(i).wait()


def forward_pass(encoder_master, decoder_master, encoder_input, decoder_input, segments, decoder_cotangent, n):
    (_, re, ne, ge), (_, rd, nd, gd) = sizes(ENC, n), sizes(DEC, n)
    frames, rows = encoder_input.shape[0], decoder_input.shape[0]
    tall = -(-rows // 128) * 128
    dma = pltpu.SemaphoreType.DMA
    saved = saved_shapes(rows, frames)
    vmem, hbm = pl.BlockSpec(memory_space=pltpu.VMEM), pl.BlockSpec(memory_space=pl.ANY)
    return pl.pallas_call(
        partial(forward_kernel, n, rows, frames),
        out_shape=(
            jax.ShapeDtypeStruct((N_PAIR, 2, 4, 2, 2, UNIT, D), BF),
            jax.ShapeDtypeStruct((4, 2, 2, 2, 8, LANES), F32),
            *(jax.ShapeDtypeStruct(shape, dtype) for shape, dtype in saved),
            jax.ShapeDtypeStruct((2, 4, 2, 2, UNIT, D), BF),
        ),
        in_specs=[vmem] * 5 + [hbm],
        out_specs=(hbm,) * (3 + N_SAVED),
        scratch_shapes=[
            pltpu.VMEM((FRONT + re + BACK, LANES), F32),
            pltpu.VMEM((FRONT + rd + BACK, LANES), F32),
            pltpu.VMEM((ne, UNIT, D), BF),
            pltpu.VMEM((nd, UNIT, D), BF),
            pltpu.VMEM((ge, 2, 2, UNIT, D), BF),
            pltpu.VMEM((gd, 2, 2, UNIT, D), BF),
            pltpu.VMEM((N_VEC, 8, LANES), F32),
            pltpu.VMEM((2, N_PAIR, UNIT, D), BF),
            pltpu.VMEM((2, 8, LANES), F32),
            pltpu.VMEM((N_PAIR, UNIT, D), BF),
            pltpu.VMEM((8, LANES), F32),
            dma((ne + nd,)),
            dma((ge + gd, 2)),
            dma((N_VEC,)),
            dma((2, N_PAIR)),
            dma((2,)),
            dma((N_PAIR, 6)),
            dma((N_PAIR, 6)),
            dma((N_PAIR,)),
            dma((N_PAIR,)),
            dma((N_PAIR,)),
            dma((6,)),
            dma((6,)),
            pltpu.VMEM((4, 2, 2, 2, 8, LANES), F32),
            *(pltpu.VMEM(shape, dtype) for shape, dtype in saved),
            pltpu.VMEM((32, D), F32),
            pltpu.VMEM((2, D, D), BF),
            pltpu.VMEM((rows, D), F32),
            pltpu.VMEM((tall, tall), F32),
            pltpu.VMEM((8, tall), F32),
            pltpu.VMEM((tall, LANES), F32),
            dma((N_SAVED,)),
            dma((2,)),
            pltpu.VMEM((rows, D), BF),
            pltpu.VMEM((2, 2, 4, 2, 2, UNIT, D), BF),
            pltpu.VMEM((2, 4, 2, 2, UNIT, D), BF),
            dma((2,)),
            dma((2,)),
            dma((2,)),
        ],
        compiler_params=pltpu.CompilerParams(collective_id=0, has_side_effects=True, vmem_limit_bytes=58 << 20),
        name="forward",
    )(rows_of(encoder_master, re), rows_of(decoder_master, rd), encoder_input, decoder_input, segments,
      decoder_cotangent)


RING = 3
RING_C = 5
EARLY = 2
TICKS = [(t, part) for t in range(EARLY, N_PAIR) for part in ((0, 1) if t in (4, 6) else (0,))]
SENT = list(range(EARLY)) + [
    EARLY + u for u, (t, part) in enumerate(TICKS) if part == 1 or (t, 1) not in TICKS
]


def scatter_kernel(
    n, begin_loads, produce, after, early_ref, vg_ref, gbuf, oe_ref, od_ref, norm_ref,
    land_c, land_b, land_a, land_z, ownb, vown, vl_c, vl_y, vl_x, vl_z,
    ge_ref, gd_ref, fe, fd, fbe, fbd, fv, nsend, nland,
    s_core, r_core, s_free, s_ph, r_ph, s_back, r_small, r_big, sv, rv, s_vback, r_vback, s_n, r_n, s_out,
):
    wide, narrow, z, x, y, c = whoami()
    me = wide * 4 + narrow
    chip = me // 2
    at = dict(z=z, x=x, y=y, c=c)
    greet(me, n)
    sib = device(z, x, y, 1 - c)

    def slot_c(pair):
        return (N_PAIR - 1 - pair) % RING_C

    def core_copy(pair):
        return pltpu.make_async_remote_copy(
            gbuf.at[(N_PAIR - 1 - pair) % RING, 1 - c], land_c.at[slot_c(pair)], s_core.at[pair], r_core.at[pair], device_id=sib, device_id_type=MESH
        )

    mine_a = x * (1 - c) + y * c

    def phase_dmas(pair, phase):
        if phase == 1:
            steps = [(land_c.at[slot_c(pair), :, :, 1 - y], land_b.at[pair], 0, second_peer(at))]
        elif phase == 2:
            steps = [(land_b.at[pair, :, 1 - mine_a], land_a.at[pair], 1, first_peer(at))]
        else:
            steps = [
                (land_a.at[pair, (z + k) % 4], land_z.at[pair, k - 1], 1 + k, device((z + k) % 4, x, y, c))
                for k in (1, 2, 3)
            ]
        return [
            pltpu.make_async_remote_copy(
                src, dst, s_ph.at[pair, k], r_ph.at[pair, k], device_id=target, device_id_type=MESH
            )
            for src, dst, k, target in steps
        ]

    def begin(pair, phase):
        if phase != 1:
            for cp in phase_dmas(pair, phase):
                cp.start()
            return

        @pl.when(c == 0)
        def _():
            phase_dmas(pair, 1)[0].start()

        @pl.when(c == 1)
        def _():
            pltpu.make_async_remote_copy(
                land_c.at[slot_c(pair), :, 1 - x], land_b.at[pair], s_ph.at[pair, 0], r_ph.at[pair, 0],
                device_id=second_peer(at), device_id_type=MESH,
            ).start()

    def back(pair):
        block = ENC if pair < 6 else DEC
        shard = sizes(block, n)[0]
        local = pair - block.first_mat // 2
        half = block.small_mats // 2
        big = half <= local < half + 2
        if big:
            start = (block.fc1 * 6 + chip * BIG) * LANES
            length = BIG * LANES
        else:
            small = 2 * local - (4 if local >= half + 2 else 0) + c
            start = (small_row(block, small) * 6 + chip * UROWS) * LANES
            length = UROWS * LANES
        first, last = start // shard, (start + length - 1) // shard
        out = []
        for which, target in ((0, first), (1, last)):
            low_row = target * shard // LANES
            if big:
                slot = (start // LANES - low_row + BIG) // BIG
                q = 2 * (local - half) + c
                dst = (fbe if block is ENC else fbd).at[slot, q]
                recv = r_big.at[0 if block is ENC else 1, slot, q]
            else:
                slot = (start // LANES - low_row + UROWS) // UROWS
                dst = (fe if block is ENC else fd).at[slot]
                recv = r_small.at[0 if block is ENC else 1, slot]
            needed = True if which == 0 else first != last
            out.append((needed, target, dst, s_back.at[pair, which], recv))
        return out

    def start_back(pair):
        for needed, target, dst, send, recv in back(pair):
            @pl.when(needed & (target == me))
            def _(dst=dst, recv=recv):
                pltpu.make_async_copy(ownb.at[pair], dst, recv).start()

            @pl.when(needed & (target != me))
            def _(dst=dst, recv=recv, send=send, target=target):
                pltpu.make_async_remote_copy(
                    ownb.at[pair], dst, send, recv, device_id=flat_device(target), device_id_type=MESH
                ).start()

    def end_back(pair):
        for needed, target, dst, send, recv in back(pair):
            @pl.when(needed & (target != me))
            def _(send=send):
                pltpu.make_async_copy(ownb.at[pair], ownb.at[pair], send).wait()

    def add_core(pair):
        def body(i, carry):
            a, b = i // 2, i % 2
            for k in range(2):
                mine = gbuf[(N_PAIR - 1 - pair) % RING, c, a, b, k]
                land_c[slot_c(pair), a, b, k] = (
                    land_c[slot_c(pair), a, b, k].astype(F32) + mine.astype(F32)
                ).astype(BF)
            return carry

        lax.fori_loop(0, 8, body, 0)

    def add_b(pair):
        def body(i, carry):
            a, b = i // 2, i % 2
            mine = land_c[slot_c(pair), a, b * (1 - c) + x * c, y * (1 - c) + b * c]
            land_b[pair, a, b] = (land_b[pair, a, b].astype(F32) + mine.astype(F32)).astype(BF)
            return carry

        lax.fori_loop(0, 8, body, 0)

    def add_a(pair):
        for a in range(4):
            land_a[pair, a] = (land_a[pair, a].astype(F32) + land_b[pair, a, mine_a].astype(F32)).astype(BF)

    def add_z(pair):
        total = land_a[pair, z].astype(F32)
        for k in range(3):
            total = total + land_z[pair, k].astype(F32)
        ownb[pair] = total.astype(BF)
        squares = total * total
        return jnp.sum(squares.reshape(UNIT // 8, 8, D), axis=0)

    vland = dict(c=vl_c, y=vl_y, x=vl_x, z=vl_z)

    def vsteps(phase):
        if phase == 0:
            return [(vg_ref.at[:, :, :, 1 - c], vl_c, 0, dict(at, c=1 - c))]
        if phase == 1:
            return [(vl_c.at[:, :, 1 - y], vl_y, 1, dict(at, y=1 - y))]
        if phase == 2:
            return [(vl_y.at[:, 1 - x], vl_x, 2, dict(at, x=1 - x))]
        return [(vl_x.at[(z + k) % 4], vl_z.at[k - 1], 2 + k, dict(at, z=(z + k) % 4)) for k in (1, 2, 3)]

    def vdmas(phase):
        return [
            pltpu.make_async_remote_copy(s, d, sv.at[k], rv.at[k], device_id=dev(p), device_id_type=MESH)
            for s, d, k, p in vsteps(phase)
        ]

    def vadd(phase):
        if phase == 0:
            vl_c[...] = vl_c[...] + vg_ref[:, :, :, c]
        elif phase == 1:
            vl_y[...] = vl_y[...] + vl_c[:, :, y]
        elif phase == 2:
            vl_x[...] = vl_x[...] + vl_y[:, x]
        else:
            vown[...] = vl_x[z] + vl_z[0] + vl_z[1] + vl_z[2]

    fields = {ENC: (0, ge_ref, oe_ref, fe, fbe), DEC: (1, gd_ref, od_ref, fd, fbd)}

    def units_to_flat(block, least=0, most=99):
        b, g_out, _, f_ref, fb_ref = fields[block]
        _, _, n_small, n_big = sizes(block, n)

        def small_body(slot, mat, u, pos, start):
            pltpu.make_async_copy(f_ref.at[slot], f_ref.at[slot], r_small.at[b, slot]).wait()
            for k in range(6):
                g_out[pl.ds(FRONT + pos + k, UNIT, stride=6), :] = f_ref[slot, :, k * LANES : (k + 1) * LANES].astype(F32)

        def big_body(slot, u, pos, start):
            for q in range(4):
                pltpu.make_async_copy(fb_ref.at[slot, q], fb_ref.at[slot, q], r_big.at[b, slot, q]).wait()
                for k in range(6):
                    g_out[pl.ds(FRONT + pos + 6 * q + k, UNIT, stride=24), :] = fb_ref[
                        slot, q, :, k * LANES : (k + 1) * LANES
                    ].astype(F32)

        if most > block.small_mats:
            each_big(block, n, me, n_big, big_body)
        each_small(block, n, me, n_small, small_body, least, most)

    def finish_flat(block):
        b, g_out, o_ref, _, _ = fields[block]
        shard, rows, _, _ = sizes(block, n)

        def vec_body(v, pos, start):
            pltpu.make_async_copy(fv.at[v], fv.at[v], r_vback.at[v]).wait()
            g_out[pl.ds(FRONT + pos, 6), :] = fv[v, 0:6, :]

        each_vector(block, n, me, 0 if block is ENC else len(ENC.vectors), vec_body)
        shift = (me * shard) % LANES
        step = 8 * max(k for k in range(1, 40) if (rows // 8) % k == 0)
        lanes = lax.broadcasted_iota(jnp.int32, (1, LANES), 1)
        unturn = lax.rem(LANES - shift, LANES)

        def turn(i, carry):
            at_row = pl.multiple_of(i * step, 8)
            here = pltpu.roll(g_out[pl.ds(FRONT + at_row, step), :], unturn, 1)
            after = pltpu.roll(g_out[pl.ds(FRONT + at_row + 1, step), :], unturn, 1)
            g_out[pl.ds(FRONT + at_row, step), :] = jnp.where(lanes < LANES - shift, here, after)
            return carry

        lax.fori_loop(0, rows // step, turn, 0)
        pltpu.make_async_copy(g_out.at[pl.ds(FRONT, rows)], o_ref, s_out.at[b]).start()

    def vector_targets(v_static):
        block = ENC if v_static < len(ENC.vectors) else DEC
        shard = sizes(block, n)[0]
        start = (ENC.vectors + DEC.vectors)[v_static] * D
        return start // shard, (start + D - 1) // shard

    def vectors_back():
        for v in range(N_VEC):
            for which, target in enumerate(sorted(set(vector_targets(v)))):
                if target == v:
                    @pl.when(me == v)
                    def _(v=v):
                        pltpu.make_async_copy(vown, fv.at[v], r_vback.at[v]).start()
                else:
                    @pl.when(me == v)
                    def _(v=v, target=target, which=which):
                        pltpu.make_async_remote_copy(
                            vown, fv.at[v], s_vback.at[which], r_vback.at[v], device_id=(target // 4, target % 4), device_id_type=MESH
                        ).start()

    seq = list(range(N_PAIR - 1, -1, -1))
    square = jnp.zeros((8, D), F32)
    def early_copy(i):
        return pltpu.make_async_copy(early_ref.at[i], land_c.at[i], s_core.at[i])

    for i in range(EARLY):
        early_copy(i).start()
    begin_loads()
    await_all(n)
    for i in range(EARLY):
        early_copy(i).wait()
        begin(seq[i], 1)
    for u in range(EARLY, EARLY + len(TICKS) + B_AT[3]):
        t, part = TICKS[u - EARLY] if u - EARLY < len(TICKS) else (N_PAIR + u - EARLY - len(TICKS), 0)
        done = part == 1 or (t, 1) not in TICKS
        if t < N_PAIR:
            if part == 0 and t - RING >= EARLY:
                core_copy(seq[t - RING]).wait_send()
            produce(t, part, gbuf.at[t % RING])
            if done:
                if t >= RING_C:
                    pl.semaphore_wait(s_free, 1)
                core_copy(seq[t]).start()
        for phase in (4, 3, 2, 1):
            if u - B_AT[phase - 1] in SENT:
                i = SENT.index(u - B_AT[phase - 1])
                pair = seq[i]
                if phase == 1 and i < EARLY:
                    continue
                if phase == 1:
                    core_copy(pair).wait_recv()
                    add_core(pair)
                elif phase == 2:
                    for cp in phase_dmas(pair, 1):
                        cp.wait()
                    add_b(pair)
                    if i < N_PAIR - RING_C:
                        pl.semaphore_signal(s_free, inc=1, device_id=sib, device_id_type=MESH)
                elif phase == 3:
                    for cp in phase_dmas(pair, 2):
                        cp.wait_recv()
                    add_a(pair)
                else:
                    for cp in phase_dmas(pair, 3):
                        cp.wait_recv()
                    square = square + add_z(pair)
                    start_back(pair)
                if phase < 4:
                    begin(pair, phase)
        if done:
            after(t)
        if t == N_PAIR + B_AT[2] - 1:
            units_to_flat(DEC)
        if t == N_PAIR + B_AT[3] - 1:
            finish_flat(DEC)
            units_to_flat(ENC, 2, 99)
        if t == N_PAIR - 1:
            for cp in vdmas(0):
                cp.start()
        elif N_PAIR <= t < N_PAIR + 4:
            phase = t - N_PAIR
            for cp in vdmas(phase):
                cp.wait_recv()
            vadd(phase)
            if phase < 3:
                for cp in vdmas(phase + 1):
                    cp.start()
            else:
                vectors_back()

    vsq = vown[...] * vown[...]
    for k in range(6):
        vsq = vsq + square[:, k * LANES : (k + 1) * LANES]
    nsend[...] = vsq

    def norm_copy(i):
        return pltpu.make_async_remote_copy(
            nsend, nland.at[i], s_n.at[i], r_n.at[i], device_id=flat_device((me + i) % n), device_id_type=MESH
        )

    def norm_start(i, carry):
        norm_copy(i).start()
        return carry

    lax.fori_loop(1, n, norm_start, 0)

    units_to_flat(ENC, 0, 2)
    finish_flat(ENC)

    def norm_wait(i, total):
        norm_copy(i).wait()
        return total + nland[i]

    total = lax.fori_loop(1, n, norm_wait, nsend[...])
    norm_ref[...] = jnp.broadcast_to(jnp.sqrt(jnp.sum(total)), (8, LANES))

    for b, (g_out, o_ref) in enumerate(((ge_ref, oe_ref), (gd_ref, od_ref))):
        pltpu.make_async_copy(g_out.at[pl.ds(FRONT, o_ref.shape[0])], o_ref, s_out.at[b]).wait()
    for phase in range(4):
        for cp in vdmas(phase):
            cp.wait_send()
    for v in range(N_VEC):
        for which, target in enumerate(sorted(set(vector_targets(v)))):
            if target != v:
                @pl.when(me == v)
                def _(which=which):
                    pltpu.make_async_copy(vown, vown, s_vback.at[which]).wait()
    for pair in range(N_PAIR):
        if N_PAIR - 1 - pair >= N_PAIR - RING:
            core_copy(pair).wait_send()
        for phase in (2, 3):
            for cp in phase_dmas(pair, phase):
                cp.wait_send()
        end_back(pair)


def sum_rows(ref, rows, out_ref):
    def body(r):
        out_ref[...] += jnp.sum(ref[r, :].astype(F32), axis=0, keepdims=True)

    out_ref[...] = jnp.zeros_like(out_ref)
    row_blocks(rows, body)


def norm_backward_ref(x_ref, gain, dn_ref, rows, out_ref, gain_grad, shift_grad):
    gain_grad[...] = jnp.zeros_like(gain_grad)
    shift_grad[...] = jnp.zeros_like(shift_grad)

    def body(r):
        hat, root = norm_rows(x_ref[r, :].astype(F32))
        dn = dn_ref[r, :]
        gain_grad[...] += jnp.sum(dn * hat, axis=0, keepdims=True)
        shift_grad[...] += jnp.sum(dn, axis=0, keepdims=True)
        g = dn * gain[...]
        part = g - jnp.mean(g, axis=1, keepdims=True) - hat * jnp.mean(g * hat, axis=1, keepdims=True)
        out_ref[r, :] += root * part

    row_blocks(rows, body)


def round_rows(src_ref, rows, out_ref):
    def body(r):
        out_ref[r, :] = src_ref[r, :].astype(BF)

    row_blocks(rows, body)


def weight_grad(a_ref, b_ref, rows, g_ref):
    b = b_ref[0:rows, :]
    flat = g_ref.reshape(D, D)

    def body(cols):
        flat[cols, :] = mm_tn(a_ref[0:rows, cols], b).astype(BF)

    col_blocks(body)


def back_through(a_ref, w_ref, rows, out_ref, add):
    a = a_ref[0:rows, :]

    def body(cols):
        y = mm_nt(a, w_ref[cols, :])
        if add:
            y = y + out_ref[0:rows, cols]
        out_ref[0:rows, cols] = y.astype(out_ref.dtype)

    col_blocks(body)


def gelu_back(o_ref, w_ref, slope_ref, rows, out_ref, bias_grad):
    a = o_ref[0:rows, :]

    def body(cols):
        y = mm_nt(a, w_ref[cols, :]) * slope_ref[0:rows, cols].astype(F32)
        bias_grad[:, cols] = jnp.sum(y, axis=0, keepdims=True)
        out_ref[0:rows, cols] = y.astype(BF)

    col_blocks(body)


def attention_backward_ref(q_ref, k_ref, v_ref, dm_ref, lse_ref, mask_ref, rows, keys, dq_ref, dk_ref, dv_ref, low, high):
    def pair_of_heads(i, carry):
        cols = pl.ds(pl.multiple_of(i * LANES, LANES), LANES)
        dk_ref[:, cols] = jnp.zeros((dk_ref.shape[0], LANES), F32)
        dv_ref[:, cols] = jnp.zeros((dv_ref.shape[0], LANES), F32)
        k_turned = jnp.transpose(k_ref[0:keys, cols])
        for tile, (start, reach) in enumerate(attend_tiles(rows, keys, mask_ref is not None)):
            r = slice(start, start + LANES)
            q2 = both_heads(q_ref[r, cols] * jnp.asarray(SCALE, BF))
            dm2 = both_heads(dm_ref[r, cols])
            scores = scores_of(k_ref[0:reach, cols], q2, mask_ref, start, reach)
            probs = jnp.exp(scores - lse_ref[tile, pl.ds(i, 1), :])
            dp = mm_nt(v_ref[0:reach, cols], dm2)
            weighted = probs * dp
            ds = (weighted - probs * jnp.sum(weighted, axis=0, keepdims=True)).astype(BF)
            dk_ref[0:reach, cols] += mm(ds, q2)
            dv_ref[0:reach, cols] += mm(probs.astype(BF), dm2)
            dq = jnp.concatenate(
                [
                    mm(k_turned[s * HEAD_DIM : (s + 1) * HEAD_DIM, 0:reach], ds[:, s * LANES : (s + 1) * LANES])
                    for s in range(2)
                ],
                axis=0,
            )
            dq_ref[r, cols] = jnp.transpose(dq) * SCALE
        return carry

    lax.fori_loop(low, high, pair_of_heads, 0, unroll=1)


W_ORDER = (26, 27, 22, 23, 24, 25, 20, 21, 19, 16, 17, 18, 15, 12, 13, 14, 10, 11, 6, 7, 8, 9, 4, 5, 3, 0, 1, 2, 24, 25, 26, 27)
W_RING = 4
A_RING = 4


def backward_kernel(n, rows, frames, *refs):
    w_ref, v_ref, seg_ref, ein, din, ecot, dcot, early = refs[:8]
    kept, refs = refs[8 : 8 + N_SAVED], refs[8 + N_SAVED :]
    oe_ref, od_ref, norm_ref, fgrad, tgrad, dout = refs[:6]
    refs = refs[6:]
    comm, refs = refs[:34], refs[34:]
    (
        gbuf, vg, vgr, gains, wbuf, outg, eoutg, dn, pool, abuf, nbuf, xbuf,
        dq, dk, dv, mask_ref, seg_row, seg_col, lse, orow, mem, mgrad, s_l, s_w, s_a, s_o,
    ) = refs
    tall = mask_ref.shape[0]

    a_order = (
        [kept[27].at[k] for k in (2, 3, 0, 1)]
        + [kept[22].at[0:rows], kept[15].at[0:rows], din]
        + [kept[8].at[k] for k in (2, 3, 0, 1)]
        + [kept[9].at[k] for k in (2, 3, 0, 1)]
        + [kept[4], ein]
        + [kept[26].at[k] for k in range(4)]
    )
    used = [0, 0]

    def w_copy(u):
        m = W_ORDER[u]
        return pltpu.make_async_copy(w_ref.at[m // 2, m % 2].reshape(D, D), wbuf.at[u % W_RING], s_w.at[u % W_RING])

    def a_copy(u):
        src = a_order[u]
        return pltpu.make_async_copy(src, abuf.at[u % A_RING, 0 : src.shape[0]], s_a.at[u % A_RING])

    def with_w(mat, body):
        u = used[0]
        used[0] += 1
        assert W_ORDER[u] == mat
        w_copy(u).wait()
        body(wbuf.at[u % W_RING])
        if u + W_RING < len(W_ORDER):
            w_copy(u + W_RING).start()

    def with_a(body):
        u = used[1]
        used[1] += 1
        a_copy(u).wait()
        body(abuf.at[u % A_RING])
        if u + A_RING < len(a_order):
            a_copy(u + A_RING).start()

    def side(k, src, dst):
        return pltpu.make_async_copy(src, dst, s_l.at[k])

    def x_copy(i):
        return side(0, kept[i], xbuf.at[0 : kept[i].shape[0]])

    def n_copy(i):
        return side(1, kept[i], nbuf.at[0 : kept[i].shape[0]])

    def vrow(i):
        return vgr.at[i : i + 1]

    def take_two(which, copy, ring, total, body):
        u = used[which]
        used[which] += 2
        copy(u).wait()
        copy(u + 1).wait()
        body(lambda k: lax.rem(u + k, ring))
        for k in range(2):
            if u + k + ring < total:
                copy(u + k + ring).start()

    def two_w(mat, body):
        assert W_ORDER[used[0]] == mat
        take_two(0, w_copy, W_RING, len(W_ORDER), lambda slot: body(lambda k: wbuf.at[slot(k)]))

    def two_a(body):
        take_two(1, a_copy, A_RING, len(a_order), lambda slot: body(lambda k: abuf.at[slot(k)]))

    def feed(step, g, count, first_mat, first_vec, n_i):
        if step < 2:
            two_a(lambda a: both(lambda k: weight_grad(a(k), orow, count, g.at[k])))
            return
        first = 2 if step == 2 else 0
        if step == 2:
            n_copy(n_i).wait()

        def body(k, w, a):
            gelu_back(orow, w(k), a(k), count, pool.at[first + k], vgr.at[pl.ds(first_vec + first + k, 1)])
            weight_grad(nbuf, pool.at[first + k], count, g.at[k])

        two_w(first_mat + 4 + first, lambda w: two_a(lambda a: both(lambda k: body(k, w, a))))

    def feed_after(step, count, first_mat):
        first = 2 if step == 2 else 0
        if step == 2:
            dn[0:count, :] = jnp.zeros((count, D), F32)
        two_w(
            first_mat + first,
            lambda w: both(lambda k: back_through(pool.at[first + k], w(k), count, dn, True)),
        )

    def attend(part, *setting):
        g, count, padded, keys, padded_keys, out_ref, wo, q_i, lse_i, masked, bo, bq, bv = setting
        heads = partial(
            attention_backward_ref,
            pool.at[0], pool.at[1], pool.at[2], pool.at[3], lse, mask_ref if masked else None, padded, padded_keys,
            dq, dk.at[0:padded_keys], dv.at[0:padded_keys],
        )
        if part == 0:
            attend_start(*setting)
            heads(0, 3)
            return
        heads(3, 6)
        round_rows(dv, keys, pool.at[2])
        round_rows(dq, count, pool.at[0])
        round_rows(dk, keys, pool.at[1])
        sum_rows(dq, count, vrow(bq))
        sum_rows(dv, keys, vrow(bv))

    def attend_start(g, count, padded, keys, padded_keys, out_ref, wo, q_i, lse_i, masked, bo, bq, bv):
        cps = [side(2 + k, kept[q_i + k], pool.at[k, 0 : kept[q_i + k].shape[0]]) for k in range(3)]
        cps.append(side(5, kept[lse_i], lse.at[0 : kept[lse_i].shape[0]]))
        for cp in cps:
            cp.start()
        round_rows(out_ref, count, orow)
        sum_rows(out_ref, count, vrow(bo))
        with_a(lambda a: weight_grad(a, orow, count, g.at[1]))
        with_w(wo, lambda w: back_through(orow, w, count, pool.at[3], False))
        if padded > count:
            pool[3, count:padded, :] = jnp.zeros((padded - count, D), BF)
        for cp in cps:
            cp.wait()

    def start():
        o_copy = side(2, dcot, orow)
        o_copy.start()
        for u in range(A_RING):
            a_copy(u).start()
        for u in range(W_RING):
            w_copy(u).start()
        n_copy(25).start()
        x_copy(24).start()
        mem_copy = side(3, kept[10], mem)
        mem_copy.start()
        for i, v in enumerate((0, 5, 12, 17, 22, 28)):
            for k in range(6):
                gains[i : i + 1, k * LANES : (k + 1) * LANES] = v_ref[v // 8, v // 4 % 2, v // 2 % 2, v % 2, k : k + 1, :]
        o_copy.wait()
        mem_copy.wait()

    def widen():
        def body(r):
            outg[r, :] = orow[r, :].astype(F32)

        row_blocks(rows, body)
        sum_rows(outg, rows, vrow(28))

    def produce(t, part, g):
        if t < 4:
            feed(t, g, rows, 20, 24, 25)
            if t == 3:
                n_copy(18).start()
        elif t == 4:
            attend(part, g, rows, tall, frames, frames, outg, 19, 19, 23, False, 21, 19, 20)
            if part == 1:
                weight_grad(mem, pool.at[2], frames, g.at[0])
        elif t == 5:
            n_copy(18).wait()
            weight_grad(nbuf, pool.at[0], rows, g.at[0])
            weight_grad(mem, pool.at[1], frames, g.at[1])
            n_copy(11).start()
        elif t == 6:
            attend(part, g, rows, tall, rows, tall, outg, 15, 12, 16, True, 16, 14, 15)
            if part == 1:
                n_copy(11).wait()
                weight_grad(nbuf, pool.at[2], rows, g.at[0])
        elif t == 7:
            weight_grad(nbuf, pool.at[0], rows, g.at[0])
            weight_grad(nbuf, pool.at[1], rows, g.at[1])
            n_copy(7).start()
        elif t < 12:
            feed(t - 8, g, frames, 4, 7, 7)
            if t == 11:
                n_copy(0).start()
        elif t == 12:
            for half in range(2):
                attend(half, g, frames, frames, frames, frames, eoutg, 3, 1, 5, False, 4, 2, 3)
            n_copy(0).wait()
            weight_grad(nbuf, pool.at[2], frames, g.at[0])
        else:
            weight_grad(nbuf, pool.at[0], frames, g.at[0])
            weight_grad(nbuf, pool.at[1], frames, g.at[1])

    def after(t):
        if t in (2, 3):
            feed_after(t, rows, 20)
            if t == 2:
                widen()
                make_mask(seg_ref, seg_row, seg_col, mask_ref)
            if t == 3:
                x_copy(24).wait()
                norm_backward_ref(xbuf, gains.at[4:5], dn, rows, outg, vrow(22), vrow(23))
                x_copy(17).start()
        elif t == 5:
            with_w(16, lambda w: back_through(pool.at[0], w, rows, dn, False))
            with_w(17, lambda w: back_through(pool.at[1], w, frames, mgrad, False))
            with_w(18, lambda w: back_through(pool.at[2], w, frames, mgrad, True))
            x_copy(17).wait()
            norm_backward_ref(xbuf, gains.at[3:4], dn, rows, outg, vrow(17), vrow(18))
            x_copy(6).start()
        elif t == 7:
            cot = side(2, ecot, orow.at[0:frames])
            cot.start()
            with_w(12, lambda w: back_through(pool.at[0], w, rows, dn, False))
            with_w(13, lambda w: back_through(pool.at[1], w, rows, dn, True))
            with_w(14, lambda w: back_through(pool.at[2], w, rows, dn, True))
            with_a(lambda a: norm_backward_ref(a, gains.at[2:3], dn, rows, outg, vrow(12), vrow(13)))
            pltpu.make_async_copy(outg, tgrad, s_o.at[0]).start()
            cot.wait()

            def body(r):
                total = orow[r, :].astype(F32) + mgrad[r, :]
                eoutg[r, :] = total
                orow[r, :] = total.astype(BF)

            row_blocks(frames, body)
        elif t == 9:
            sum_rows(eoutg, frames, vrow(11))
        elif t in (10, 11):
            feed_after(t - 8, frames, 4)
            if t == 11:
                x_copy(6).wait()
                norm_backward_ref(xbuf, gains.at[1:2], dn, frames, eoutg, vrow(5), vrow(6))
                x_copy(24).start()
        elif t in (14, 15):
            if t == 14:
                x_copy(24).wait()
                row_blocks(rows, lambda r: add_row(dn, xbuf, gains.at[5:6], r))
            two_w(
                24 + 2 * (t - 14),
                lambda w: two_a(lambda a: both(lambda k: accumulate(a(k), w(k), rows, dn))),
            )
            if t == 15:
                round_rows(dn, rows, orow)
                pltpu.make_async_copy(orow, dout, s_o.at[2]).start()
        elif t == 13:
            with_w(0, lambda w: back_through(pool.at[0], w, frames, dn, False))
            with_w(1, lambda w: back_through(pool.at[1], w, frames, dn, True))
            with_w(2, lambda w: back_through(pool.at[2], w, frames, dn, True))
            with_a(lambda a: norm_backward_ref(a, gains.at[0:1], dn, frames, eoutg, vrow(0), vrow(1)))
            pltpu.make_async_copy(eoutg, fgrad, s_o.at[1]).start()
            for v in range(32):
                at = (v // 8, v // 4 % 2, v // 2 % 2, v % 2)
                if v < N_VEC:
                    vg[at + (slice(6, 8), slice(None))] = jnp.zeros((2, LANES), F32)
                    for k in range(6):
                        vg[at + (slice(k, k + 1), slice(None))] = vgr[v : v + 1, k * LANES : (k + 1) * LANES]
                else:
                    vg[at] = jnp.zeros((8, LANES), F32)

    scatter_kernel(n, start, produce, after, early, vg, gbuf, oe_ref, od_ref, norm_ref, *comm)
    pltpu.make_async_copy(outg, tgrad, s_o.at[0]).wait()
    pltpu.make_async_copy(eoutg, fgrad, s_o.at[1]).wait()
    pltpu.make_async_copy(orow, dout, s_o.at[2]).wait()


def backward_pass(weights, vectors, kept, early, ein, din, ecot, dcot, segments, n):
    (_, re, ne, ge), (_, rd, nd, gd) = sizes(ENC, n), sizes(DEC, n)
    frames, rows = ein.shape[0], din.shape[0]
    tall = -(-rows // 128) * 128
    dma = pltpu.SemaphoreType.DMA
    vmem, hbm = pl.BlockSpec(memory_space=pltpu.VMEM), pl.BlockSpec(memory_space=pl.ANY)
    return pl.pallas_call(
        partial(backward_kernel, n, rows, frames),
        out_shape=(
            jax.ShapeDtypeStruct((re, LANES), F32),
            jax.ShapeDtypeStruct((rd, LANES), F32),
            jax.ShapeDtypeStruct((8, LANES), F32),
            jax.ShapeDtypeStruct((frames, D), F32),
            jax.ShapeDtypeStruct((rows, D), F32),
            jax.ShapeDtypeStruct((rows, D), BF),
        ),
        in_specs=[hbm] + [vmem] * 2 + [hbm] * (5 + N_SAVED),
        out_specs=(hbm, hbm, vmem, hbm, hbm, hbm),
        scratch_shapes=[
            pltpu.VMEM((RING_C, 4, 2, 2, UNIT, D), BF),
            pltpu.VMEM((N_PAIR, 4, 2, UNIT, D), BF),
            pltpu.VMEM((N_PAIR, 4, UNIT, D), BF),
            pltpu.VMEM((N_PAIR, 3, UNIT, D), BF),
            pltpu.VMEM((N_PAIR, UNIT, D), BF),
            pltpu.VMEM((8, LANES), F32),
            pltpu.VMEM((4, 2, 2, 8, LANES), F32),
            pltpu.VMEM((4, 2, 8, LANES), F32),
            pltpu.VMEM((4, 8, LANES), F32),
            pltpu.VMEM((3, 8, LANES), F32),
            pltpu.VMEM((FRONT + re + BACK, LANES), F32),
            pltpu.VMEM((FRONT + rd + BACK, LANES), F32),
            pltpu.VMEM((ne, UNIT, D), BF),
            pltpu.VMEM((nd, UNIT, D), BF),
            pltpu.VMEM((ge, 4, UNIT, D), BF),
            pltpu.VMEM((gd, 4, UNIT, D), BF),
            pltpu.VMEM((N_VEC, 8, LANES), F32),
            pltpu.VMEM((8, LANES), F32),
            pltpu.VMEM((n, 8, LANES), F32),
            dma((N_PAIR,)),
            dma((N_PAIR,)),
            pltpu.SemaphoreType.REGULAR,
            dma((N_PAIR, 5)),
            dma((N_PAIR, 5)),
            dma((N_PAIR, 2)),
            dma((2, max(ne, nd))),
            dma((2, max(ge, gd), 4)),
            dma((6,)),
            dma((6,)),
            dma((2,)),
            dma((N_VEC,)),
            dma((n,)),
            dma((n,)),
            dma((2,)),
            pltpu.VMEM((RING, 2, 4, 2, 2, UNIT, D), BF),
            pltpu.VMEM((4, 2, 2, 2, 8, LANES), F32),
            pltpu.VMEM((32, D), F32),
            pltpu.VMEM((8, D), F32),
            pltpu.VMEM((W_RING, D, D), BF),
            pltpu.VMEM((rows, D), F32),
            pltpu.VMEM((frames, D), F32),
            pltpu.VMEM((rows, D), F32),
            pltpu.VMEM((4, tall, D), BF),
            pltpu.VMEM((A_RING, rows, D), BF),
            pltpu.VMEM((rows, D), BF),
            pltpu.VMEM((rows, D), F32),
            pltpu.VMEM((tall, D), F32),
            pltpu.VMEM((tall, D), F32),
            pltpu.VMEM((tall, D), F32),
            pltpu.VMEM((tall, tall), F32),
            pltpu.VMEM((8, tall), F32),
            pltpu.VMEM((tall, LANES), F32),
            pltpu.VMEM((tall // 128, 8, 2 * LANES), F32),
            pltpu.VMEM((rows, D), BF),
            pltpu.VMEM((frames, D), BF),
            pltpu.VMEM((frames, D), F32),
            dma((6,)),
            dma((W_RING,)),
            dma((A_RING,)),
            dma((3,)),
        ],
        compiler_params=pltpu.CompilerParams(collective_id=1, has_side_effects=True, vmem_limit_bytes=61 << 20),
        name="backward",
    )(weights, vectors, segments, ein, din, ecot, dcot, early, *kept)


def attention_plan(prefix, width):
    return [
        (prefix + "wq", width, width),
        (prefix + "bq", width, 0),
        (prefix + "wk", width, width),
        (prefix + "wv", width, width),
        (prefix + "bv", width, 0),
        (prefix + "wo", width, width),
        (prefix + "bo", width, 0),
    ]


def feed_plan(width, hidden):
    return [
        ("fc1_weight", width, hidden),
        ("fc1_bias", hidden, 0),
        ("fc2_weight", hidden, width),
        ("fc2_bias", width, 0),
    ]


def encoder_layout(width, hidden):
    return (
        [("ln1_gain", width, 0), ("ln1_bias", width, 0)]
        + attention_plan("att_", width)
        + [("ln2_gain", width, 0), ("ln2_bias", width, 0)]
        + feed_plan(width, hidden)
    )


def decoder_layout(width, hidden):
    return (
        [("ln1_gain", width, 0), ("ln1_bias", width, 0)]
        + attention_plan("self_", width)
        + [("ln2_gain", width, 0), ("ln2_bias", width, 0)]
        + attention_plan("cross_", width)
        + [("ln3_gain", width, 0), ("ln3_bias", width, 0)]
        + feed_plan(width, hidden)
    )


def unpack(flat, layout):
    params = {}
    offset = 0
    for name, rows, cols in layout:
        count = rows * cols if cols > 0 else rows
        piece = flat[offset : offset + count]
        params[name] = piece.reshape(rows, cols) if cols > 0 else piece
        offset = offset + count
    return params


def pack(grads, layout):
    return jnp.concatenate([grads[name].reshape(-1) for name, rows, cols in layout])


def dot_plain(left, right):
    return jnp.dot(left, right, preferred_element_type=jnp.float32)


def dot_left(left, right):
    return lax.dot_general(
        left, right, (((0,), (0,)), ((), ())), preferred_element_type=jnp.float32
    )


def dot_right(left, right):
    return lax.dot_general(
        left, right, (((1,), (1,)), ((), ())), preferred_element_type=jnp.float32
    )


def layer_norm(values, gain, shift):
    centred = values - jnp.mean(values, axis=-1, keepdims=True)
    spread = jnp.mean(centred * centred, axis=-1, keepdims=True)
    return centred * lax.rsqrt(spread + 1e-05) * gain + shift


def norm_forward(params, prefix, values):
    gain = params[prefix + "_gain"].astype(jnp.float32)
    shift = params[prefix + "_bias"].astype(jnp.float32)
    return layer_norm(values, gain, shift).astype(jnp.bfloat16)


def norm_backward(params, prefix, values, grad):
    gain = params[prefix + "_gain"].astype(jnp.float32)
    shift = params[prefix + "_bias"].astype(jnp.float32)
    unused, pullback = jax.vjp(layer_norm, values, gain, shift)
    value_grad, gain_grad, shift_grad = pullback(grad)
    return (value_grad, {prefix + "_gain": gain_grad, prefix + "_bias": shift_grad})


def block_rows(total):
    return total if total <= 1024 else 512


def attend_forward(queries, keys_low, values, allowed_fn):
    total, width = queries.shape
    heads = width // HEAD_DIM
    rows = block_rows(total)
    blocks = total // rows
    scale = HEAD_DIM ** (-0.5)
    query_heads = queries.reshape(blocks, rows, heads, HEAD_DIM)
    key_heads = keys_low.reshape(keys_low.shape[0], heads, HEAD_DIM)
    value_heads = values.reshape(values.shape[0], heads, HEAD_DIM)
    starts = jnp.arange(blocks, dtype=jnp.int32) * rows

    def one_block(inputs):
        block, start = inputs
        scores = (
            jnp.einsum("qhd,khd->hqk", block, key_heads, preferred_element_type=jnp.float32) * scale
        )
        if allowed_fn is not None:
            scores = jnp.where(allowed_fn(start, rows)[None], scores, -1000000000.0)
        peak = jnp.max(scores, axis=-1, keepdims=True)
        weights = jnp.exp(scores - peak)
        totals = jnp.sum(weights, axis=-1, keepdims=True)
        probs = (weights / totals).astype(jnp.bfloat16)
        mixed = jnp.einsum("hqk,khd->qhd", probs, value_heads, preferred_element_type=jnp.float32)
        return (mixed.reshape(rows, width).astype(jnp.bfloat16), (peak + jnp.log(totals))[..., 0])

    mixed, logsum = lax.map(one_block, (query_heads, starts))
    return (mixed.reshape(total, width), logsum)


def attend_backward(queries, keys_low, values, logsum, mixed_grad, allowed_fn):
    total, width = queries.shape
    heads = width // HEAD_DIM
    rows = block_rows(total)
    blocks = total // rows
    scale = HEAD_DIM ** (-0.5)
    query_heads = queries.reshape(blocks, rows, heads, HEAD_DIM)
    grad_heads = mixed_grad.reshape(blocks, rows, heads, HEAD_DIM)
    key_heads = keys_low.reshape(keys_low.shape[0], heads, HEAD_DIM)
    value_heads = values.reshape(values.shape[0], heads, HEAD_DIM)
    starts = jnp.arange(blocks, dtype=jnp.int32) * rows

    def one_block(carry, inputs):
        key_grad, value_grad = carry
        block, grad_block, block_sum, start = inputs
        scores = (
            jnp.einsum("qhd,khd->hqk", block, key_heads, preferred_element_type=jnp.float32) * scale
        )
        if allowed_fn is not None:
            scores = jnp.where(allowed_fn(start, rows)[None], scores, -1000000000.0)
        probs = jnp.exp(scores - block_sum[..., None])
        prob_grad = jnp.einsum(
            "qhd,khd->hqk", grad_block, value_heads, preferred_element_type=jnp.float32
        )
        value_grad = value_grad + jnp.einsum(
            "hqk,qhd->khd",
            probs.astype(jnp.bfloat16),
            grad_block,
            preferred_element_type=jnp.float32,
        )
        score_grad = probs * (prob_grad - jnp.sum(probs * prob_grad, axis=-1, keepdims=True))
        raw_grad = (score_grad * scale).astype(jnp.bfloat16)
        query_grad = jnp.einsum(
            "hqk,khd->qhd", raw_grad, key_heads, preferred_element_type=jnp.float32
        )
        key_grad = key_grad + jnp.einsum(
            "hqk,qhd->khd", raw_grad, block, preferred_element_type=jnp.float32
        )
        return ((key_grad, value_grad), query_grad.reshape(rows, width))

    zeros = jnp.zeros(key_heads.shape, jnp.float32)
    (key_grad, value_grad), query_grad = lax.scan(
        one_block, (zeros, zeros), (query_heads, grad_heads, logsum, starts)
    )
    return (
        query_grad.reshape(total, width),
        key_grad.reshape(keys_low.shape[0], width),
        value_grad.reshape(values.shape[0], width),
    )


def attention_forward(params, prefix, query_rows, key_rows, allowed_fn):
    queries = (dot_plain(query_rows, params[prefix + "wq"]) + params[prefix + "bq"]).astype(
        jnp.bfloat16
    )
    keys_low = dot_plain(key_rows, params[prefix + "wk"]).astype(jnp.bfloat16)
    values = (dot_plain(key_rows, params[prefix + "wv"]) + params[prefix + "bv"]).astype(
        jnp.bfloat16
    )
    mixed, logsum = attend_forward(queries, keys_low, values, allowed_fn)
    output = dot_plain(mixed, params[prefix + "wo"]) + params[prefix + "bo"]
    return (output, (queries, keys_low, values, mixed, logsum))


def attention_backward(params, prefix, query_rows, key_rows, kept, out_grad, allowed_fn):
    queries, keys_low, values, mixed, logsum = kept
    out_round = out_grad.astype(jnp.bfloat16)
    mixed_grad = dot_right(out_round, params[prefix + "wo"]).astype(jnp.bfloat16)
    query_grad, key_grad, value_grad = attend_backward(
        queries, keys_low, values, logsum, mixed_grad, allowed_fn
    )
    query_round = query_grad.astype(jnp.bfloat16)
    key_round = key_grad.astype(jnp.bfloat16)
    value_round = value_grad.astype(jnp.bfloat16)
    grads = {
        prefix + "wq": dot_left(query_rows, query_round),
        prefix + "bq": jnp.sum(query_grad, axis=0),
        prefix + "wk": dot_left(key_rows, key_round),
        prefix + "wv": dot_left(key_rows, value_round),
        prefix + "bv": jnp.sum(value_grad, axis=0),
        prefix + "wo": dot_left(mixed, out_round),
        prefix + "bo": jnp.sum(out_grad, axis=0),
    }
    query_side = dot_right(query_round, params[prefix + "wq"])
    key_side = dot_right(key_round, params[prefix + "wk"]) + dot_right(
        value_round, params[prefix + "wv"]
    )
    return (grads, query_side, key_side)


def feed_forward(params, normed):
    pre = dot_plain(normed, params["fc1_weight"]) + params["fc1_bias"]
    activated = jax.nn.gelu(pre, approximate=False).astype(jnp.bfloat16)
    return (dot_plain(activated, params["fc2_weight"]) + params["fc2_bias"], (pre, activated))


def feed_backward(params, normed, kept, out_grad):
    pre, activated = kept
    out_round = out_grad.astype(jnp.bfloat16)
    act_grad = dot_right(out_round, params["fc2_weight"])
    unused, gelu_back = jax.vjp(partial(jax.nn.gelu, approximate=False), pre)
    pre_grad = gelu_back(act_grad)[0]
    pre_round = pre_grad.astype(jnp.bfloat16)
    grads = {
        "fc1_weight": dot_left(normed, pre_round),
        "fc1_bias": jnp.sum(pre_grad, axis=0),
        "fc2_weight": dot_left(activated, out_round),
        "fc2_bias": jnp.sum(out_grad, axis=0),
    }
    return (grads, dot_right(pre_round, params["fc1_weight"]))


def encoder_forward(params, frames):
    normed = norm_forward(params, "ln1", frames)
    attended, attend_kept = attention_forward(params, "att_", normed, normed, None)
    after = frames + attended
    normed_two = norm_forward(params, "ln2", after)
    fed, feed_kept = feed_forward(params, normed_two)
    return (after + fed, (normed, attend_kept, after, normed_two, feed_kept))


def encoder_backward(params, frames, kept, out_grad):
    normed, attend_kept, after, normed_two, feed_kept = kept
    grads, normed_grad = feed_backward(params, normed_two, feed_kept, out_grad)
    part, norm_grads = norm_backward(params, "ln2", after, normed_grad)
    grads.update(norm_grads)
    after_grad = out_grad + part
    attend_grads, query_side, key_side = attention_backward(
        params, "att_", normed, normed, attend_kept, after_grad, None
    )
    grads.update(attend_grads)
    part, norm_grads = norm_backward(params, "ln1", frames, query_side + key_side)
    grads.update(norm_grads)
    return (grads, after_grad + part)


def decoder_forward(params, tokens, memory_low, allowed_fn):
    normed = norm_forward(params, "ln1", tokens)
    attended, self_kept = attention_forward(params, "self_", normed, normed, allowed_fn)
    after = tokens + attended
    normed_two = norm_forward(params, "ln2", after)
    crossed, cross_kept = attention_forward(params, "cross_", normed_two, memory_low, None)
    after_two = after + crossed
    normed_three = norm_forward(params, "ln3", after_two)
    fed, feed_kept = feed_forward(params, normed_three)
    return (
        after_two + fed,
        (normed, self_kept, after, normed_two, cross_kept, after_two, normed_three, feed_kept),
    )


def decoder_backward(params, tokens, memory_low, kept, out_grad, allowed_fn):
    normed, self_kept, after, normed_two, cross_kept, after_two, normed_three, feed_kept = kept
    grads, normed_grad = feed_backward(params, normed_three, feed_kept, out_grad)
    part, norm_grads = norm_backward(params, "ln3", after_two, normed_grad)
    grads.update(norm_grads)
    after_two_grad = out_grad + part
    cross_grads, query_side, memory_grad = attention_backward(
        params, "cross_", normed_two, memory_low, cross_kept, after_two_grad, None
    )
    grads.update(cross_grads)
    part, norm_grads = norm_backward(params, "ln2", after, query_side)
    grads.update(norm_grads)
    after_grad = after_two_grad + part
    self_grads, query_side, key_side = attention_backward(
        params, "self_", normed, normed, self_kept, after_grad, allowed_fn
    )
    grads.update(self_grads)
    part, norm_grads = norm_backward(params, "ln1", tokens, query_side + key_side)
    grads.update(norm_grads)
    return (grads, after_grad + part, memory_grad)


def adamw(master, first, second, grad, factor, correction):
    clipped = grad * factor
    moment = 0.5 * first + 0.5 * clipped
    variance = 0.5 * second + 0.5 * clipped * clipped
    update = moment / correction / (jnp.sqrt(variance / correction) + 1e-08) + 0.01 * master
    weights = master - 0.02 * update
    return (weights, moment, variance, weights.astype(jnp.bfloat16))


def shards_native(
    encoder_input,
    decoder_input,
    segments,
    encoder_cotangent,
    decoder_cotangent,
    encoder_master,
    encoder_first,
    encoder_second,
    decoder_master,
    decoder_first,
    decoder_second,
    step_count,
):
    encoder_plan = encoder_layout(D, FF)
    decoder_plan = decoder_layout(D, FF)
    encoder_params = unpack(
        lax.all_gather(encoder_master.astype(jnp.bfloat16), ("wide", "narrow"), axis=0, tiled=True),
        encoder_plan,
    )
    frames = encoder_input[0].astype(jnp.float32)
    memory, encoder_kept = encoder_forward(encoder_params, frames)
    memory_low = memory.astype(jnp.bfloat16)
    decoder_params = unpack(
        lax.all_gather(decoder_master.astype(jnp.bfloat16), ("wide", "narrow"), axis=0, tiled=True),
        decoder_plan,
    )
    tokens = decoder_input[0].astype(jnp.float32)
    segment_row = segments[0]
    length = segment_row.shape[0]

    def allowed_fn(start, count):
        places = start + jnp.arange(count, dtype=jnp.int32)
        row_segments = lax.dynamic_slice_in_dim(segment_row, start, count)
        columns = jnp.arange(length, dtype=jnp.int32)
        return (row_segments[:, None] == segment_row[None, :]) & (
            columns[None, :] <= places[:, None]
        )

    decoded, decoder_kept = decoder_forward(decoder_params, tokens, memory_low, allowed_fn)
    decoder_again = unpack(
        lax.all_gather(decoder_master.astype(jnp.bfloat16), ("wide", "narrow"), axis=0, tiled=True),
        decoder_plan,
    )
    decoder_grads, token_grad, memory_grad = decoder_backward(
        decoder_again,
        tokens,
        memory_low,
        decoder_kept,
        decoder_cotangent[0].astype(jnp.float32),
        allowed_fn,
    )
    decoder_total = pack(decoder_grads, decoder_plan)
    decoder_owned = lax.psum_scatter(
        decoder_total, ("wide", "narrow"), scatter_dimension=0, tiled=True
    )
    encoder_again = unpack(
        lax.all_gather(encoder_master.astype(jnp.bfloat16), ("wide", "narrow"), axis=0, tiled=True),
        encoder_plan,
    )
    memory_total = encoder_cotangent[0].astype(jnp.float32) + memory_grad
    encoder_grads, frame_grad = encoder_backward(encoder_again, frames, encoder_kept, memory_total)
    encoder_total = pack(encoder_grads, encoder_plan)
    encoder_owned = lax.psum_scatter(
        encoder_total, ("wide", "narrow"), scatter_dimension=0, tiled=True
    )
    local_squares = jnp.sum(encoder_owned * encoder_owned) + jnp.sum(decoder_owned * decoder_owned)
    gradient_norm = jnp.sqrt(lax.psum(local_squares, ("wide", "narrow")))
    factor = 1.0 / jnp.maximum(gradient_norm, 1.0)
    correction = 1.0 - jnp.power(0.5, step_count.astype(jnp.float32))
    encoder_new = adamw(
        encoder_master, encoder_first, encoder_second, encoder_owned, factor, correction
    )
    decoder_new = adamw(
        decoder_master, decoder_first, decoder_second, decoder_owned, factor, correction
    )
    return (
        memory_low[None],
        decoded.astype(jnp.bfloat16)[None],
        frame_grad[None],
        token_grad[None],
        gradient_norm,
        encoder_new[0],
        encoder_new[1],
        encoder_new[2],
        encoder_new[3],
        decoder_new[0],
        decoder_new[1],
        decoder_new[2],
        decoder_new[3],
    )


def shards(
    encoder_input,
    decoder_input,
    segments,
    encoder_cotangent,
    decoder_cotangent,
    encoder_master,
    encoder_first,
    encoder_second,
    decoder_master,
    decoder_first,
    decoder_second,
    step_count,
):
    n = 32
    weights, vectors, *kept, early = forward_pass(
        encoder_master, decoder_master, encoder_input[0], decoder_input[0], segments, decoder_cotangent[0], n
    )
    encoder_flat, decoder_flat, norm, frame_grad, token_grad, decoded = backward_pass(
        weights, vectors, kept, early, encoder_input[0], decoder_input[0], encoder_cotangent[0], decoder_cotangent[0], segments, n
    )
    gradient_norm = norm[0, 0]
    factor = 1.0 / jnp.maximum(gradient_norm, 1.0)
    correction = 1.0 - jnp.power(0.5, step_count.astype(jnp.float32))
    encoder_owned = encoder_flat.reshape(-1)[: encoder_master.shape[0]]
    decoder_owned = decoder_flat.reshape(-1)[: decoder_master.shape[0]]
    encoder_new = adamw(encoder_master, encoder_first, encoder_second, encoder_owned, factor, correction)
    decoder_new = adamw(decoder_master, decoder_first, decoder_second, decoder_owned, factor, correction)
    return (
        kept[10][None],
        decoded[None],
        frame_grad[None],
        token_grad[None],
        gradient_norm,
        *encoder_new,
        *decoder_new,
    )


def solution(mesh):
    placed = (
        P(("wide", "narrow"), None, None),
        P(("wide", "narrow"), None, None),
        P(("wide", "narrow"), None),
        P(("wide", "narrow"), None, None),
        P(("wide", "narrow"), None, None),
        P(("wide", "narrow")),
        P(("wide", "narrow")),
        P(("wide", "narrow")),
        P(("wide", "narrow")),
        P(("wide", "narrow")),
        P(("wide", "narrow")),
        P(),
    )
    return jax.shard_map(
        shards if tuple(mesh.shape.values()) == (8, 4) else shards_native,
        mesh=mesh,
        in_specs=placed,
        out_specs=(
            P(("wide", "narrow"), None, None),
            P(("wide", "narrow"), None, None),
            P(("wide", "narrow"), None, None),
            P(("wide", "narrow"), None, None),
            P(),
            P(("wide", "narrow")),
            P(("wide", "narrow")),
            P(("wide", "narrow")),
            P(("wide", "narrow")),
            P(("wide", "narrow")),
            P(("wide", "narrow")),
            P(("wide", "narrow")),
            P(("wide", "narrow")),
        ),
        check_vma=False,
    )
```
